32 devices in a mesh: blk: 8 (over z, y), chan: 4 (over x, core).
Axes of the slice: x: 2, y: 2, z: 4, core: 2. Of those that a mesh axis runs over, the one named last changes fastest.
Arguments:
- hidden_in: bfloat16 [2, 1, 2048, 768], P(None, None, ('blk', 'chan')), may hold values from -6 to 6
- cotangent: bfloat16 [2, 1, 2048, 768], P(None, None, ('blk', 'chan')), may hold values from -6 to 6
- mixer_input_weight: bfloat16 [768, 2304], P(None, ('blk', 'chan')), may hold values from -0.21875 to 0.21875
- mixer_output_weight: bfloat16 [768, 768], P(None, ('blk', 'chan')), may hold values from -0.21875 to 0.21875
- feedforward_up: bfloat16 [768, 3072], P(None, ('blk', 'chan')), may hold values from -0.21875 to 0.21875
- feedforward_down: bfloat16 [3072, 768], P(('blk', 'chan')), may hold values from -0.109375 to 0.109375
- first_gain: bfloat16 [768], P(('blk', 'chan')), may hold values from 0.5 to 1.5
- first_shift: bfloat16 [768], P(('blk', 'chan')), may hold values from -3 to 3
- second_gain: bfloat16 [768], P(('blk', 'chan')), may hold values from 0.5 to 1.5
- second_shift: bfloat16 [768], P(('blk', 'chan')), may hold values from -3 to 3
- short_taps: bfloat16 [3, 3, 768], P(None, None, ('blk', 'chan')), may hold values from -4 to 4
- short_bias: bfloat16 [3, 768], P(None, ('blk', 'chan')), may hold values from -3 to 3
- skip_scale: bfloat16 [768], P(('blk', 'chan')), may hold values from -4 to 4
- filter_out: bfloat16 [64, 768], P(None, ('blk', 'chan')), may hold values from -0.023925781 to 0.023925781
- pos_weight: bfloat16 [33, 64], replicated, may hold values from -1 to 1
- pos_bias: bfloat16 [64], replicated, may hold values from -4 to 4
- mid_weight: bfloat16 [64, 64], replicated, may hold values from -0.75 to 0.75
- mid_bias: bfloat16 [64], replicated, may hold values from -4 to 4
- sine_freq: bfloat16 [64], replicated, may hold values from 2 to 16
- decay_rate: bfloat16 [768], P(('blk', 'chan')), may hold values from 0.00024414062 to 0.029907227
Outputs:
- hidden_out: bfloat16 [2, 1, 2048, 768], P(None, None, ('blk', 'chan'))
- grad_hidden: bfloat16 [2, 1, 2048, 768], P(None, None, ('blk', 'chan'))
- grad_mixer_in: float32 [768, 2304], P(None, ('blk', 'chan'))
- grad_mixer_out: float32 [768, 768], P(None, ('blk', 'chan'))
- grad_mlp_up: float32 [768, 3072], P(None, ('blk', 'chan'))
- grad_mlp_down: float32 [3072, 768], P(('blk', 'chan'))
- grad_first_gain: float32 [768], P(('blk', 'chan'))
- grad_first_shift: float32 [768], P(('blk', 'chan'))
- grad_second_gain: float32 [768], P(('blk', 'chan'))
- grad_second_shift: float32 [768], P(('blk', 'chan'))
- grad_short_taps: float32 [3, 3, 768], P(None, None, ('blk', 'chan'))
- grad_short_bias: float32 [3, 768], P(None, ('blk', 'chan'))
- grad_skip_scale: float32 [768], P(('blk', 'chan'))
- grad_filter_out: float32 [64, 768], P(None, ('blk', 'chan'))
- grad_pos_weight: float32 [33, 64], replicated
- grad_pos_bias: float32 [64], replicated
- grad_mid_weight: float32 [64, 64], replicated
- grad_mid_bias: float32 [64], replicated
- grad_sine_freq: float32 [64], replicated
The draws below stay inside these ranges and needn't reach their ends.
All inputs are finite; a program needn't handle non-finite values.
Results may differ from the reference program's by a relative error of at most 0.012.
Values may be sent and summed in bfloat16 or wider, within the bound.
A program may use at most 320 MiB of HBM per device.

```python
import math
import jax
import jax.numpy as jnp
from jax import lax

D = 768
FF = 3072
ORDER = 64
BANDS = 16
SEQS = 1
MICRO = 2
EMB = 33
SEQ_LEN = 2048


def level_of(rng, extent, split, low, high):
    def one(dim, blocks):
        steps = jax.random.uniform(jax.random.fold_in(jax.random.fold_in(rng, 6), dim), (blocks,), jnp.float32, low / len(split), high / len(split))
        return jnp.repeat(jnp.exp(steps), extent[dim] // blocks).reshape((-1,) + (1,) * (len(extent) - dim - 1))

    loudness = one(*split[0])
    for cut in split[1:]:
        loudness = loudness * one(*cut)
    return loudness


def scatter_about(rng, dims, deviation, bound, cuts=(), held_as=jnp.bfloat16):
    level = level_of(rng, dims, cuts, -0.22, 0.18) if cuts else 1.0
    entries = jax.random.normal(rng, dims, jnp.float32) * deviation * level
    return jnp.minimum(jnp.maximum(entries, -bound), bound).astype(held_as)


def setup_inputs(seed: int = 0) -> dict:
    arg_keys = jax.random.split(jax.random.key(seed), 21)
    hidden_in = scatter_about(arg_keys[0], (MICRO, SEQS, SEQ_LEN, D), 1.0, 6.0, ((2, 32),))
    cotangent = scatter_about(arg_keys[1], (MICRO, SEQS, SEQ_LEN, D), 1.0, 6.0, ((2, 32),))
    mixer_input_weight = scatter_about(arg_keys[2], (D, 3 * D), D ** -0.5, 0.21875, ((1, 32),))
    mixer_output_weight = scatter_about(arg_keys[3], (D, D), D ** -0.5, 0.21875, ((1, 32),))
    feedforward_up = scatter_about(arg_keys[4], (D, FF), D ** -0.5, 0.21875, ((1, 32),))
    feedforward_down = scatter_about(arg_keys[5], (FF, D), FF ** -0.5, 0.109375, ((0, 32),))
    first_gain = jnp.clip(1.0 + 0.1 * jax.random.normal(arg_keys[6], (D,), jnp.float32), 0.5, 1.5).astype(jnp.bfloat16)
    first_shift = scatter_about(arg_keys[7], (D,), 0.3, 3.0, ((0, 32),))
    second_gain = jnp.clip(1.0 + 0.1 * jax.random.normal(arg_keys[8], (D,), jnp.float32), 0.5, 1.5).astype(jnp.bfloat16)
    second_shift = scatter_about(arg_keys[9], (D,), 0.3, 3.0, ((0, 32),))
    short_taps = scatter_about(arg_keys[10], (3, 3, D), 0.6, 4.0, ((2, 32),))
    short_bias = scatter_about(arg_keys[11], (3, D), 0.3, 3.0, ((1, 32),))
    skip_scale = scatter_about(arg_keys[12], (D,), 1.0, 4.0, ((0, 32),))
    filter_out = scatter_about(arg_keys[13], (ORDER, D), 0.004, 0.023925781, ((1, 32),))
    pos_weight = scatter_about(arg_keys[14], (EMB, ORDER), EMB ** -0.5, 1.0)
    pos_bias = scatter_about(arg_keys[15], (ORDER,), 1.0, 4.0)
    mid_weight = scatter_about(arg_keys[16], (ORDER, ORDER), ORDER ** -0.5, 0.75)
    mid_bias = scatter_about(arg_keys[17], (ORDER,), 1.0, 4.0)
    sine_freq = jnp.clip(jnp.exp(jax.random.uniform(arg_keys[18], (ORDER,), jnp.float32, math.log(2.0), math.log(16.0))), 2.0, 16.0).astype(jnp.bfloat16)
    decay_rate = jnp.clip(jnp.exp(math.log(0.029907227) - 4.808111 * jax.random.uniform(arg_keys[19], (D,), jnp.float32) ** level_of(arg_keys[19], (D,), ((0, 32),), -0.2, 0.2)), 0.00024414062, 0.029907227).astype(jnp.bfloat16)
    return {"hidden_in": hidden_in, "cotangent": cotangent, "mixer_input_weight": mixer_input_weight, "mixer_output_weight": mixer_output_weight, "feedforward_up": feedforward_up, "feedforward_down": feedforward_down, "first_gain": first_gain, "first_shift": first_shift, "second_gain": second_gain, "second_shift": second_shift, "short_taps": short_taps, "short_bias": short_bias, "skip_scale": skip_scale, "filter_out": filter_out, "pos_weight": pos_weight, "pos_bias": pos_bias, "mid_weight": mid_weight, "mid_bias": mid_bias, "sine_freq": sine_freq, "decay_rate": decay_rate}


EPS = 1e-05
PRECISION_LEVEL = lax.Precision.HIGHEST

@jax.custom_vjp
def reduced_copy(v):
    return lax.optimization_barrier(v.astype(jnp.bfloat16)).astype(jnp.float32)

@jax.custom_vjp
def reduced_backward(v):
    return v

def low_keep(v):
    return (reduced_copy(v), None)

def low_pass(kept, grad):
    return (grad,)

def back_keep(v):
    return (v, None)

def back_low(kept, grad):
    return (reduced_copy(grad),)
reduced_copy.defvjp(low_keep, low_pass)
reduced_backward.defvjp(back_keep, back_low)

def layer_norm(values, gain, shift):
    center = values - lax.optimization_barrier(jnp.mean(values, -1, keepdims=True))
    spread = lax.optimization_barrier(jnp.mean(center * center, -1, keepdims=True))
    return center * lax.rsqrt(spread + EPS) * gain + shift

def positions(lags, length):
    band_freq = 0.0001 + (BANDS - 1 - 0.0001) * jnp.arange(BANDS).astype(jnp.float32) / (BANDS - 1)
    phase = 2.0 * math.pi / length * lags[:, None] * band_freq[None, :]
    return jnp.concatenate([lags[:, None] / (length - 1), jnp.cos(phase), -jnp.sin(phase)], 1)

def filter_values(lags, length, params, decay_rates):
    first_w, first_b, middle_w, middle_b, final_w, sine_rate = params
    layer_one = jnp.sin(sine_rate * (jnp.dot(positions(lags, length), first_w, precision=PRECISION_LEVEL) + first_b))
    layer_two = jnp.sin(sine_rate * (jnp.dot(layer_one, middle_w, precision=PRECISION_LEVEL) + middle_b))
    return jnp.dot(layer_two, final_w, precision=PRECISION_LEVEL) * jnp.exp(-lags[:, None] * decay_rates)

def forward(hidden, weights, decay_rates):
    mixer_input_weight, mixer_output_weight, feedforward_up, feedforward_down, first_gain, first_shift, second_gain, second_shift, short_taps, short_bias, skip_scale, filter_out, pos_weight, pos_bias, mid_weight, mid_bias, sine_freq = weights
    lags = jnp.arange(SEQ_LEN).astype(jnp.float32)
    kernel = filter_values(lags, SEQ_LEN, (pos_weight, pos_bias, mid_weight, mid_bias, filter_out, sine_freq), decay_rates)
    kernel_spec = jnp.fft.rfft(kernel, n=2 * SEQ_LEN, axis=0)
    collected_results = []
    for micro in range(MICRO):
        values = hidden[micro]
        normalized_input = reduced_copy(layer_norm(values, first_gain, first_shift))
        projected_tokens = reduced_copy(reduced_backward(jnp.einsum('iyp,pm->iym', normalized_input, mixer_input_weight, precision=PRECISION_LEVEL)))
        projected_tokens = projected_tokens.reshape(SEQS, SEQ_LEN, 3, D)
        padded = jnp.pad(projected_tokens, ((0, 0), (2, 0), (0, 0), (0, 0)))
        conv = short_taps[0] * projected_tokens + short_taps[1] * padded[:, 1:-1] + short_taps[2] * padded[:, :-2] + short_bias
        gate_out = conv[:, :, 0]
        gate_in = conv[:, :, 1]
        signal = conv[:, :, 2]
        gated = signal * gate_in
        spectrum = jnp.fft.rfft(gated, n=2 * SEQ_LEN, axis=1) * kernel_spec[None]
        long_out = jnp.fft.irfft(spectrum, n=2 * SEQ_LEN, axis=1)[:, :SEQ_LEN]
        mixer_result = reduced_copy(reduced_backward((long_out + skip_scale * gated) * gate_out))
        branch_output = reduced_backward(jnp.einsum('iyp,pm->iym', mixer_result, mixer_output_weight, precision=PRECISION_LEVEL))
        residual_stream = values + branch_output
        second_branch = reduced_copy(layer_norm(residual_stream, second_gain, second_shift))
        upper_branch = reduced_backward(jnp.einsum('iyp,pm->iym', second_branch, feedforward_up, precision=PRECISION_LEVEL))
        activated_hidden = reduced_copy(jax.nn.gelu(upper_branch, approximate=True))
        collected_results.append(residual_stream + jnp.einsum('kix,xn->kin', activated_hidden, feedforward_down, precision=PRECISION_LEVEL))
    return jnp.stack(collected_results)

def reference(hidden_in, cotangent, mixer_input_weight, mixer_output_weight, feedforward_up, feedforward_down, first_gain, first_shift, second_gain, second_shift, short_taps, short_bias, skip_scale, filter_out, pos_weight, pos_bias, mid_weight, mid_bias, sine_freq, decay_rate):
    decay_rates = decay_rate.astype(jnp.float32)
    weights = tuple((param.astype(jnp.float32) for param in (mixer_input_weight, mixer_output_weight, feedforward_up, feedforward_down, first_gain, first_shift, second_gain, second_shift, short_taps, short_bias, skip_scale, filter_out, pos_weight, pos_bias, mid_weight, mid_bias, sine_freq)))

    def layer(hidden, params):
        return forward(hidden, params, decay_rates)
    result, pullback = jax.vjp(layer, hidden_in.astype(jnp.float32), weights)
    grad_hidden, grads = pullback(cotangent.astype(jnp.float32))
    return (result.astype(jnp.bfloat16), grad_hidden.astype(jnp.bfloat16), grads[0], grads[1], grads[2], grads[3], grads[4], grads[5], grads[6], grads[7], grads[8], grads[9], grads[10], grads[11], grads[12], grads[13], grads[14], grads[15], grads[16])
```

```python
import math

import jax
import jax.numpy as jnp
from jax import lax
from jax.sharding import PartitionSpec as P

EPS = 1e-05
BANDS = 16
EXACT = lax.Precision.HIGHEST
AXES = ("blk", "chan")
F32 = jnp.float32
BF16 = jnp.bfloat16


def contract(a, b, dim_a, dim_b, precision=None):
    return lax.dot_general(
        a, b, (((dim_a,), (dim_b,)), ((), ())), precision=precision, preferred_element_type=F32
    )


def positions(length):
    lags = jnp.arange(length).astype(F32)
    band_freq = 0.0001 + (BANDS - 1 - 0.0001) * jnp.arange(BANDS).astype(F32) / (BANDS - 1)
    phase = 2.0 * math.pi / length * lags[None, :] * band_freq[:, None]
    return lags, jnp.concatenate([lags[None, :] / (length - 1), jnp.cos(phase), -jnp.sin(phase)], 0)


def filter_hidden(length, pos_weight, pos_bias, mid_weight, mid_bias, sine_freq):
    lags, features = positions(length)
    freq = sine_freq[:, None]
    first_sum = contract(pos_weight, features, 0, 0, EXACT) + pos_bias[:, None]
    first = jnp.sin(freq * first_sum)
    second_sum = contract(mid_weight, first, 0, 0, EXACT) + mid_bias[:, None]
    second = jnp.sin(freq * second_sum)
    return lags, features, first_sum, first, second_sum, second


def block_table(block):
    spot = lax.broadcasted_iota(jnp.int32, (block, block), 0)
    freq = lax.broadcasted_iota(jnp.int32, (block, block), 1)
    phase = (math.pi / block) * (spot * freq % (2 * block)).astype(F32)
    parity = 1.0 - 2.0 * (spot % 2).astype(F32)
    imag = jnp.where(freq == 0, parity, -jnp.sin(phase))
    return jnp.concatenate([jnp.cos(phase), imag], 1)


def to_spectrum(blocks, table):
    spec = lax.dot_general(
        blocks, table, (((blocks.ndim - 1,), (0,)), ((), ())), precision=EXACT, preferred_element_type=F32
    )
    half = table.shape[0]
    return spec[..., :half], spec[..., half:]


def from_spectrum(real, imag, table):
    half = table.shape[0]
    weight = jnp.where(lax.iota(jnp.int32, half) == 0, 0.5 / half, 1.0 / half)
    spec = jnp.concatenate([real * weight, imag * weight], -1)
    return lax.dot_general(
        spec, table, (((spec.ndim - 1,), (1,)), ((), ())), precision=EXACT, preferred_element_type=F32
    )


def packed_kernel(real, imag):
    first = lax.iota(jnp.int32, real.shape[-1]) == 0
    return real, jnp.where(first, imag, real), jnp.where(first, 0.0, imag)


def layer_norm(values, gain, shift):
    center = values - jnp.mean(values, -1, keepdims=True)
    scale_inv = lax.rsqrt(jnp.mean(center * center, -1, keepdims=True) + EPS)
    normal = center * scale_inv
    return normal * gain + shift, normal, scale_inv


def layer_norm_back(grad_out, normal, scale_inv, gain):
    grad_normal = grad_out * gain
    inner = grad_normal - jnp.mean(grad_normal, -1, keepdims=True)
    inner = inner - normal * jnp.mean(grad_normal * normal, -1, keepdims=True)
    return inner * scale_inv, jnp.sum(grad_out * normal, 0), jnp.sum(grad_out, 0)


def gelu_parts(v):
    root = math.sqrt(2.0 / math.pi)
    inner = root * (v + 0.044715 * v * v * v)
    t = jnp.tanh(inner)
    value = 0.5 * v * (1.0 + t)
    slope = 0.5 * (1.0 + t) + 0.5 * v * (1.0 - t * t) * root * (1.0 + 3.0 * 0.044715 * v * v)
    return value, slope


def delayed(values, steps):
    if steps == 0:
        return values
    pad = jnp.zeros(values.shape[:-1] + (steps,), values.dtype)
    return jnp.concatenate([pad, values[..., :-steps]], -1)


def advanced(values, steps):
    if steps == 0:
        return values
    pad = jnp.zeros(values.shape[:-1] + (steps,), values.dtype)
    return jnp.concatenate([values[..., steps:], pad], -1)


def exchange(values):
    return lax.all_to_all(values, AXES, split_axis=0, concat_axis=0, tiled=True)


def shards(
    hidden_in,
    cotangent,
    mixer_input_weight,
    mixer_output_weight,
    feedforward_up,
    feedforward_down,
    first_gain,
    first_shift,
    second_gain,
    second_shift,
    short_taps,
    short_bias,
    skip_scale,
    filter_out,
    pos_weight,
    pos_bias,
    mid_weight,
    mid_bias,
    sine_freq,
    decay_rate,
):
    devices = lax.axis_size(AXES)
    micro, seq_count, tok, width = hidden_in.shape
    seqs = micro * seq_count
    tokens = seqs * tok
    length = tok * devices
    chans = width // devices
    block = tok * lax.axis_size("chan")
    blocks = length // block

    def gather(shard):
        return lax.all_gather(shard, AXES, axis=0, tiled=True)

    rows_in, rows_out, rows_up = (w.shape[1] for w in (mixer_input_weight, mixer_output_weight, feedforward_up))
    weight_in = gather(mixer_input_weight.T)
    weight_out = gather(mixer_output_weight.T)
    weight_up = gather(feedforward_up.T)
    weight_down = gather(feedforward_down)
    norms = jnp.stack([first_gain, first_shift, second_gain, second_shift])
    norms = lax.all_gather(norms, AXES, axis=1, tiled=True).astype(F32)
    gain_one, shift_one, gain_two, shift_two = norms[0], norms[1], norms[2], norms[3]

    freq = sine_freq.astype(F32)
    w_pos, w_mid, w_fil = pos_weight.astype(F32), mid_weight.astype(F32), filter_out.astype(F32)
    lags, features, first_sum, first_act, second_sum, second_act = filter_hidden(
        length, w_pos, pos_bias.astype(F32), w_mid, mid_bias.astype(F32), freq
    )
    decay = jnp.exp(-lags[None, :] * decay_rate.astype(F32)[:, None])
    kernel = contract(w_fil, second_act, 0, 0, EXACT) * decay
    table = block_table(block)
    sign = 1.0 - 2.0 * (lax.iota(jnp.int32, block) % 2).astype(F32)
    ker_re, ker_im = to_spectrum(kernel.reshape(chans, blocks, block), table)

    def with_previous(spec):
        before = jnp.concatenate([jnp.zeros_like(spec[:, :1]), spec[:, :-1]], 1)
        return spec + sign * before

    k_re, k_alt, k_im = packed_kernel(with_previous(ker_re), with_previous(ker_im))

    values = hidden_in.reshape(tokens, width).astype(F32)
    normed, normal_one, inv_one = layer_norm(values, gain_one, shift_one)
    normed = normed.astype(BF16)
    projected = contract(weight_in, normed, 1, 1).astype(BF16)
    projected = projected.reshape(3, devices, chans, tokens).transpose(1, 0, 2, 3)
    arrived = exchange(projected)

    def by_sequence(values):
        parts = values.shape[1]
        values = values.reshape(devices, parts, chans, seqs, tok)
        return values.transpose(1, 3, 2, 0, 4).reshape(parts, seqs, chans, length)

    def by_device(values):
        parts = values.shape[0]
        values = values.reshape(parts, seqs, chans, devices, tok)
        return values.transpose(3, 0, 2, 1, 4).reshape(devices, parts, chans, tokens)

    steps = by_sequence(arrived).astype(F32)
    taps = short_taps.astype(F32)[:, :, None, :, None]
    conv = short_bias.astype(F32)[:, None, :, None]
    for i in range(3):
        conv = conv + taps[i] * delayed(steps, i)
    gate_out, gate_in, signal = conv[0], conv[1], conv[2]
    gated = signal * gate_in
    sig_re, sig_im = to_spectrum(gated.reshape(seqs, chans, blocks, block), table)

    def shifted_sum(make):
        total = None
        for d in range(blocks):
            term = make(d)
            total = term if total is None else tuple(a + b for a, b in zip(total, term))
        return total

    def ahead(x, d):
        return x if d == 0 else jnp.pad(x[:, :, :-d], ((0, 0), (0, 0), (d, 0), (0, 0)))

    def back(x, d):
        return x if d == 0 else jnp.pad(x[:, :, d:], ((0, 0), (0, 0), (0, d), (0, 0)))

    def forward_term(d):
        re, im = ahead(sig_re, d), ahead(sig_im, d)
        kr, ka, ki = k_re[:, d : d + 1], k_alt[:, d : d + 1], k_im[:, d : d + 1]
        return re * kr - im * ki, re * ki + im * ka

    out_re, out_im = shifted_sum(forward_term)
    long_out = from_spectrum(out_re, out_im, table).reshape(seqs, chans, length)
    skip = skip_scale.astype(F32)[None, :, None]
    long_total = long_out + skip * gated
    mixed = (long_total * gate_out).astype(BF16)
    mixed = exchange(by_device(mixed[None])).reshape(width, tokens)

    resid = values + contract(mixed, weight_out, 0, 1)
    second, normal_two, inv_two = layer_norm(resid, gain_two, shift_two)
    second = second.astype(BF16)
    upper = contract(second, weight_up, 1, 1)
    active, slope = gelu_parts(upper)
    active = active.astype(BF16)
    result = resid + contract(active, weight_down, 1, 0)

    cot = cotangent.reshape(tokens, width)
    grad_down = contract(active, cot, 0, 0)
    grad_upper = (contract(cot, weight_down, 1, 1) * slope).astype(BF16)
    grad_up = contract(grad_upper, second, 0, 0)
    grad_second = contract(grad_upper, weight_up, 1, 0)
    resid_term, grad_gain_two, grad_shift_two = layer_norm_back(grad_second, normal_two, inv_two, gain_two)
    grad_resid = cot.astype(F32) + resid_term
    grad_branch = grad_resid.astype(BF16)
    grad_out_w = contract(grad_branch, mixed, 0, 1)
    grad_mixed = contract(weight_out, grad_branch, 0, 1).astype(BF16)
    grad_mixed = exchange(grad_mixed.reshape(devices, 1, chans, tokens))
    grad_mixed = by_sequence(grad_mixed)[0].astype(F32)

    grad_gate_out = grad_mixed * long_total
    grad_long = grad_mixed * gate_out
    grad_skip = jnp.sum(grad_long * gated, (0, 2))
    gl_re, gl_im = to_spectrum(grad_long.reshape(seqs, chans, blocks, block), table)

    def signal_term(d):
        re, im = back(gl_re, d), back(gl_im, d)
        kr, ka, ki = k_re[:, d : d + 1], k_alt[:, d : d + 1], k_im[:, d : d + 1]
        return re * kr + im * ki, im * ka - re * ki

    gg_re, gg_im = shifted_sum(signal_term)
    grad_gated = from_spectrum(gg_re, gg_im, table).reshape(seqs, chans, length) + skip * grad_long

    first_slot = lax.iota(jnp.int32, block) == 0
    kg_re, kg_im = [], []
    for d in range(blocks):
        s_re, s_im = sig_re[:, :, : blocks - d], sig_im[:, :, : blocks - d]
        g_re, g_im = gl_re[:, :, d:], gl_im[:, :, d:]
        same, other = g_re * s_re, g_im * s_im
        kg_re.append(jnp.sum(jnp.where(first_slot, same, same + other), (0, 2)))
        kg_im.append(jnp.sum(jnp.where(first_slot, other, g_im * s_re - g_re * s_im), (0, 2)))
    kg_re, kg_im = jnp.stack(kg_re, 1), jnp.stack(kg_im, 1)

    def with_next(spec):
        after = jnp.concatenate([spec[:, 1:], jnp.zeros_like(spec[:, :1])], 1)
        return spec + sign * after

    grad_kernel = from_spectrum(with_next(kg_re), with_next(kg_im), table).reshape(chans, length)

    grad_conv = jnp.stack([grad_gate_out, grad_gated * signal, grad_gated * gate_in])
    grad_bias = jnp.sum(grad_conv, (1, 3))
    grad_taps = jnp.stack([jnp.sum(grad_conv * delayed(steps, i), (1, 3)) for i in range(3)])
    grad_steps = taps[0] * grad_conv
    for i in (1, 2):
        grad_steps = grad_steps + taps[i] * advanced(grad_conv, i)
    grad_proj = exchange(by_device(grad_steps.astype(BF16)))
    grad_proj = grad_proj.transpose(1, 0, 2, 3).reshape(3 * width, tokens)

    fade = grad_kernel * decay
    grad_filter = contract(second_act, fade, 1, 1, EXACT)
    grad_two = contract(w_fil, fade, 1, 0, EXACT) * jnp.cos(freq[:, None] * second_sum)
    grad_freq = jnp.sum(grad_two * second_sum, 1)
    grad_two = grad_two * freq[:, None]
    grad_mid = contract(first_act, grad_two, 1, 1, EXACT)
    grad_one = contract(w_mid, grad_two, 1, 0, EXACT) * jnp.cos(freq[:, None] * first_sum)
    grad_freq = grad_freq + jnp.sum(grad_one * first_sum, 1)
    grad_one = grad_one * freq[:, None]
    grad_pos = contract(features, grad_one, 1, 1, EXACT)
    small = lax.psum(
        jnp.concatenate([grad_pos, jnp.sum(grad_one, 1)[None], grad_mid, jnp.sum(grad_two, 1)[None], grad_freq[None]]),
        AXES,
    )
    emb, order = pos_weight.shape

    grad_in = contract(grad_proj, normed, 1, 0)
    grad_normed = contract(grad_proj, weight_in, 0, 0)
    input_term, grad_gain_one, grad_shift_one = layer_norm_back(grad_normed, normal_one, inv_one, gain_one)
    grad_hidden = (grad_resid + input_term).astype(BF16)

    def reduce_rows(partial):
        return lax.psum_scatter(partial.astype(BF16), AXES, scatter_dimension=0, tiled=True).astype(F32)

    norm_grads = jnp.stack([grad_gain_one, grad_shift_one, grad_gain_two, grad_shift_two])
    norm_grads = lax.psum_scatter(norm_grads, AXES, scatter_dimension=1, tiled=True)
    return (
        result.astype(BF16).reshape(hidden_in.shape),
        grad_hidden.reshape(hidden_in.shape),
        reduce_rows(grad_in).T,
        reduce_rows(grad_out_w).T,
        reduce_rows(grad_up).T,
        reduce_rows(grad_down),
        norm_grads[0],
        norm_grads[1],
        norm_grads[2],
        norm_grads[3],
        grad_taps,
        grad_bias,
        grad_skip,
        grad_filter,
        small[:emb],
        small[emb],
        small[emb + 1 : emb + 1 + order],
        small[emb + 1 + order],
        small[emb + 2 + order],
    )


def solution(mesh):
    rows, spread, tokens = P(AXES), P(None, AXES), P(None, None, AXES, None)
    params = (rows, rows, rows, rows, P(None, None, AXES), spread, rows, spread, P(), P(), P(), P(), P())
    return jax.shard_map(
        shards,
        mesh=mesh,
        in_specs=(tokens, tokens, spread, spread, spread, P(AXES, None)) + params + (rows,),
        out_specs=(tokens, tokens, spread, spread, spread, P(AXES, None)) + params,
        check_vma=False,
    )
```

```python
import functools
import math

import jax
import jax.numpy as jnp
from jax import lax
from jax.experimental import pallas as pl
from jax.experimental.pallas import tpu as pltpu
from jax.sharding import PartitionSpec as P

EPS = 1e-05
BANDS = 16
EXACT = lax.Precision.HIGHEST
AXES = ("blk", "chan")
F32 = jnp.float32
BF16 = jnp.bfloat16
MESH = pl.DeviceIdType.MESH
KERNEL_VMEM = 60 << 20


def contract(a, b, dim_a, dim_b, precision=None):
    return lax.dot_general(
        a, b, (((dim_a,), (dim_b,)), ((), ())), precision=precision, preferred_element_type=F32
    )


def positions(length):
    lags = jnp.arange(length).astype(F32)
    band_freq = 0.0001 + (BANDS - 1 - 0.0001) * jnp.arange(BANDS).astype(F32) / (BANDS - 1)
    phase = 2.0 * math.pi / length * lags[None, :] * band_freq[:, None]
    return lags, jnp.concatenate([lags[None, :] / (length - 1), jnp.cos(phase), -jnp.sin(phase)], 0)


def filter_hidden(length, pos_weight, pos_bias, mid_weight, mid_bias, sine_freq):
    lags, features = positions(length)
    freq = sine_freq[:, None]
    first_sum = contract(pos_weight, features, 0, 0, EXACT) + pos_bias[:, None]
    first = jnp.sin(freq * first_sum)
    second_sum = contract(mid_weight, first, 0, 0, EXACT) + mid_bias[:, None]
    second = jnp.sin(freq * second_sum)
    return lags, features, first_sum, first, second_sum, second


def block_table(block):
    spot = lax.broadcasted_iota(jnp.int32, (block, block), 0)
    freq = lax.broadcasted_iota(jnp.int32, (block, block), 1)
    phase = (math.pi / block) * (spot * freq % (2 * block)).astype(F32)
    parity = 1.0 - 2.0 * (spot % 2).astype(F32)
    imag = jnp.where(freq == 0, parity, -jnp.sin(phase))
    return jnp.concatenate([jnp.cos(phase), imag], 1)


def to_spectrum(blocks, table):
    spec = lax.dot_general(
        blocks, table, (((blocks.ndim - 1,), (0,)), ((), ())), precision=EXACT, preferred_element_type=F32
    )
    half = table.shape[0]
    return spec[..., :half], spec[..., half:]


def from_spectrum(real, imag, table):
    half = table.shape[0]
    weight = jnp.where(lax.iota(jnp.int32, half) == 0, 0.5 / half, 1.0 / half)
    spec = jnp.concatenate([real * weight, imag * weight], -1)
    return lax.dot_general(
        spec, table, (((spec.ndim - 1,), (1,)), ((), ())), precision=EXACT, preferred_element_type=F32
    )


def packed_kernel(real, imag):
    first = lax.iota(jnp.int32, real.shape[-1]) == 0
    return real, jnp.where(first, imag, real), jnp.where(first, 0.0, imag)


def layer_norm(values, gain, shift):
    center = values - jnp.mean(values, -1, keepdims=True)
    scale_inv = lax.rsqrt(jnp.mean(center * center, -1, keepdims=True) + EPS)
    normal = center * scale_inv
    return normal * gain + shift, normal, scale_inv


def layer_norm_back(grad_out, normal, scale_inv, gain):
    grad_normal = grad_out * gain
    inner = grad_normal - jnp.mean(grad_normal, -1, keepdims=True)
    inner = inner - normal * jnp.mean(grad_normal * normal, -1, keepdims=True)
    return inner * scale_inv, jnp.sum(grad_out * normal, 0), jnp.sum(grad_out, 0)


def gelu_parts(v):
    root = math.sqrt(2.0 / math.pi)
    inner = root * (v + 0.044715 * v * v * v)
    t = jnp.tanh(inner)
    value = 0.5 * v * (1.0 + t)
    slope = 0.5 * (1.0 + t) + 0.5 * v * (1.0 - t * t) * root * (1.0 + 3.0 * 0.044715 * v * v)
    return value, slope


def delayed(values, steps):
    if steps == 0:
        return values
    pad = jnp.zeros(values.shape[:-1] + (steps,), values.dtype)
    return jnp.concatenate([pad, values[..., :-steps]], -1)


def advanced(values, steps):
    if steps == 0:
        return values
    pad = jnp.zeros(values.shape[:-1] + (steps,), values.dtype)
    return jnp.concatenate([values[..., steps:], pad], -1)


def exchange(values):
    return lax.all_to_all(values, AXES, split_axis=0, concat_axis=0, tiled=True)


def spot():
    b, c = lax.axis_index("blk"), lax.axis_index("chan")
    return b // 2, b % 2, c // 2, c % 2


def at(z, y, x, k):
    return {"blk": z * 2 + y, "chan": x * 2 + k}


def flat(z, y, x, k):
    return ((z * 2 + y) * 2 + x) * 2 + k


def when(condition, act):
    pl.when(condition)(act)


def send(src, dst, send_sem, recv_sem, place):
    return pltpu.make_async_remote_copy(
        src_ref=src, dst_ref=dst, send_sem=send_sem, recv_sem=recv_sem, device_id=at(*place), device_id_type=MESH
    )


def greet_all(count):
    b, c = lax.axis_index("blk"), lax.axis_index("chan")
    chan = lax.axis_size("chan")
    me = b * chan + c
    barrier = pltpu.get_barrier_semaphore()

    def one(i, carry):
        other = lax.rem(me + i, count)
        pl.semaphore_signal(
            barrier, inc=1, device_id={"blk": other // chan, "chan": other % chan}, device_id_type=MESH
        )
        return carry

    lax.fori_loop(1, count, one, 0)
    pl.semaphore_wait(barrier, count - 1)


def greet_near(line):
    z, y, x, k = spot()
    barrier = pltpu.get_barrier_semaphore()

    def hello(*place):
        pl.semaphore_signal(barrier, inc=1, device_id=at(*place), device_id_type=MESH)

    hello(z, 1 - y, x, k)
    hello(z, y, 1 - x, k)
    hello(z, y, x, 1 - k)
    when(z > 0, lambda: hello(z - 1, y, x, k))
    when(z < line - 1, lambda: hello(z + 1, y, x, k))
    pl.semaphore_wait(barrier, 3 + jnp.minimum(z, 1) + jnp.minimum(line - 1 - z, 1))


def low_rows(rows):
    return max(rows // 16 * 8, 8) if rows > 8 else rows


class Gather:
    def __init__(self, line, shard, full, sends, recvs, local):
        self.line, self.shard, self.full, self.s, self.r, self.local = line, shard, full, sends, recvs, local
        self.rows = shard.shape[0]
        self.low = low_rows(self.rows)
        self.z, self.y, self.x, self.k = spot()

    def copy(self, kind, index, shard, place, rows=None):
        ref = self.full.at[shard] if rows is None else self.full.at[shard, pl.ds(*rows)]
        return send(ref, ref, self.s.at[kind, index], self.r.at[kind, index], place)

    def up(self, zo):
        return self.copy(0, zo, flat(zo, self.y, self.x, self.k), (self.z + 1, self.y, self.x, self.k))

    def down(self, zo):
        return self.copy(1, zo, flat(zo, self.y, self.x, self.k), (self.z - 1, self.y, self.x, self.k))

    def to_x(self, zo):
        return self.copy(2, zo, flat(zo, self.y, self.x, self.k), (self.z, self.y, 1 - self.x, self.k))

    def to_y(self, zo):
        return self.copy(3, zo, flat(zo, self.y, self.x, self.k), (self.z, 1 - self.y, self.x, self.k))

    def low_y(self, zo, other_y=False):
        shard = flat(zo, 1 - self.y if other_y else self.y, 1 - self.x, self.k)
        return self.copy(4, zo, shard, (self.z, 1 - self.y, self.x, self.k), (0, self.low))

    def high_x(self, zo, other_x=False):
        shard = flat(zo, 1 - self.y, 1 - self.x if other_x else self.x, self.k)
        return self.copy(5, zo, shard, (self.z, self.y, 1 - self.x, self.k), (self.low, self.rows - self.low))

    def core(self, zo, yo, xo, k):
        return self.copy(6, (zo * 2 + yo) * 2 + xo, flat(zo, yo, xo, k), (self.z, self.y, self.x, 1 - self.k))

    def line_has(self, zo):
        self.to_x(zo).start()
        self.to_y(zo).start()
        self.core(zo, self.y, self.x, self.k).start()

    def begin(self):
        own = self.full.at[flat(self.z, self.y, self.x, self.k)]
        copy = pltpu.make_async_copy(self.shard, own, self.local)
        copy.start()
        copy.wait()
        when(self.z < self.line - 1, lambda: self.up(self.z).start())
        when(self.z > 0, lambda: self.down(self.z).start())
        self.line_has(self.z)

    def each(self, distance, act):
        if distance == 0:
            act(self.z)
        else:
            when(self.z - distance >= 0, lambda: act(self.z - distance))
            when(self.z + distance < self.line, lambda: act(self.z + distance))

    def along(self, distance):
        def from_below():
            zo = self.z - distance
            self.up(zo).wait_recv()
            when(self.z < self.line - 1, lambda: self.up(zo).start())
            self.line_has(zo)

        def from_above():
            zo = self.z + distance
            self.down(zo).wait_recv()
            when(self.z > 0, lambda: self.down(zo).start())
            self.line_has(zo)

        when(self.z - distance >= 0, from_below)
        when(self.z + distance < self.line, from_above)

    def plane(self, distance):
        def act(zo):
            self.to_x(zo).wait_recv()
            self.low_y(zo).start()
            self.core(zo, self.y, 1 - self.x, self.k).start()
            self.to_y(zo).wait_recv()
            if self.low < self.rows:
                self.high_x(zo).start()
            self.core(zo, 1 - self.y, self.x, self.k).start()

        self.each(distance, act)

    def corner(self, distance):
        def act(zo):
            self.low_y(zo, True).wait_recv()
            if self.low < self.rows:
                self.high_x(zo, True).wait_recv()
            self.core(zo, 1 - self.y, 1 - self.x, self.k).start()

        self.each(distance, act)

    def finish(self):
        for zo in range(self.line):
            for yo in range(2):
                for xo in range(2):
                    self.core(zo, yo, xo, 1 - self.k).wait_recv()

    def drain(self):
        for zo in range(self.line):
            when(jnp.logical_and(self.z < self.line - 1, zo <= self.z), lambda: self.up(zo).wait_send())
            when(jnp.logical_and(self.z > 0, zo >= self.z), lambda: self.down(zo).wait_send())
            self.to_x(zo).wait_send()
            self.to_y(zo).wait_send()
            self.low_y(zo).wait_send()
            if self.low < self.rows:
                self.high_x(zo).wait_send()
            for yo in range(2):
                for xo in range(2):
                    self.core(zo, yo, xo, self.k).wait_send()


def gather_kernel(line, count, *refs):
    shards, fulls = refs[:count], refs[count : 2 * count]
    sends, recvs, local = refs[2 * count :]
    greet_near(line)
    pieces = [Gather(line, shards[p], fulls[p], sends.at[p], recvs.at[p], local) for p in range(count)]
    for piece in pieces:
        piece.begin()
    for distance in range(1, line):
        for piece in pieces:
            piece.along(distance)
            piece.plane(distance - 1)
            if distance > 1:
                piece.corner(distance - 2)
    for piece in pieces:
        piece.plane(line - 1)
        if line > 1:
            piece.corner(line - 2)
    for piece in pieces:
        piece.corner(line - 1)
    for piece in pieces:
        piece.finish()
        piece.drain()


def gather_pieces(shards, line):
    count, devices = len(shards), line * 8
    vmem = pl.BlockSpec(memory_space=pltpu.VMEM)
    return pl.pallas_call(
        functools.partial(gather_kernel, line, count),
        name="gather_weights",
        out_shape=[jax.ShapeDtypeStruct((devices,) + s.shape, s.dtype) for s in shards],
        in_specs=[vmem] * count,
        out_specs=[vmem] * count,
        scratch_shapes=[
            pltpu.SemaphoreType.DMA((count, 7, line * 4)),
            pltpu.SemaphoreType.DMA((count, 7, line * 4)),
            pltpu.SemaphoreType.DMA,
        ],
        compiler_params=pltpu.CompilerParams(
            collective_id=0, has_side_effects=True, vmem_limit_bytes=KERNEL_VMEM
        ),
    )(*shards)


class Reduce:
    def __init__(self, line, part, out, chip, low_y, high_x, by_x, by_y, up, down, sends, recvs):
        self.line, self.part, self.out, self.chip = line, part, out, chip
        self.low_buf, self.high_buf, self.x_buf, self.y_buf, self.up_buf, self.down_buf = (
            low_y, high_x, by_x, by_y, up, down,
        )
        self.s, self.r = sends, recvs
        self.rows = part.shape[1]
        self.low = low_rows(self.rows)
        self.z, self.y, self.x, self.k = spot()

    def index(self, zo, yo, xo):
        return (zo * 2 + yo) * 2 + xo

    def copy(self, kind, index, src, dst, place):
        return send(src, dst, self.s.at[kind, index], self.r.at[kind, index], place)

    def core(self, zo, yo, xo):
        i = self.index(zo, yo, xo)
        src = self.part.at[flat(zo, yo, xo, 1 - self.k)]
        return self.copy(6, i, src, self.chip.at[i], (self.z, self.y, self.x, 1 - self.k))

    def low_y(self, zo):
        i = self.index(zo, 1 - self.y, 1 - self.x)
        src = self.chip.at[i, pl.ds(0, self.low)]
        return self.copy(4, zo, src, self.low_buf.at[zo], (self.z, 1 - self.y, self.x, self.k))

    def high_x(self, zo):
        i = self.index(zo, 1 - self.y, 1 - self.x)
        src = self.chip.at[i, pl.ds(self.low, self.rows - self.low)]
        return self.copy(5, zo, src, self.high_buf.at[zo], (self.z, self.y, 1 - self.x, self.k))

    def to_x(self, zo):
        src = self.chip.at[self.index(zo, self.y, 1 - self.x)]
        return self.copy(2, zo, src, self.x_buf.at[zo], (self.z, self.y, 1 - self.x, self.k))

    def to_y(self, zo):
        src = self.chip.at[self.index(zo, 1 - self.y, self.x)]
        return self.copy(3, zo, src, self.y_buf.at[zo], (self.z, 1 - self.y, self.x, self.k))

    def up(self, zo):
        src = self.chip.at[self.index(zo, self.y, self.x)]
        return self.copy(0, zo, src, self.up_buf.at[zo], (self.z + 1, self.y, self.x, self.k))

    def down(self, zo):
        src = self.chip.at[self.index(zo, self.y, self.x)]
        return self.copy(1, zo, src, self.down_buf.at[zo], (self.z - 1, self.y, self.x, self.k))

    def add(self, i, other, rows=None):
        if rows is None:
            self.chip[i] = self.chip[i] + other
        else:
            self.chip[i, pl.ds(*rows)] = self.chip[i, pl.ds(*rows)] + other

    def each(self, distance, act):
        if distance == 0:
            act(self.z)
        else:
            when(self.z - distance >= 0, lambda: act(self.z - distance))
            when(self.z + distance < self.line, lambda: act(self.z + distance))

    def begin(self, distance):
        def act(zo):
            for yo, xo in ((1 - self.y, 1 - self.x), (self.y, 1 - self.x), (1 - self.y, self.x), (self.y, self.x)):
                self.core(zo, yo, xo).start()

        self.each(distance, act)

    def corner(self, distance):
        def act(zo):
            for yo, xo in ((1 - self.y, 1 - self.x), (self.y, 1 - self.x), (1 - self.y, self.x), (self.y, self.x)):
                self.core(zo, yo, xo).wait_recv()
                self.add(self.index(zo, yo, xo), self.part[flat(zo, yo, xo, self.k)])
                if yo is not self.y and xo is not self.x:
                    self.low_y(zo).start()
                    if self.low < self.rows:
                        self.high_x(zo).start()

        self.each(distance, act)

    def plane(self, distance):
        def act(zo):
            self.low_y(zo).wait_recv()
            self.add(self.index(zo, self.y, 1 - self.x), self.low_buf[zo], (0, self.low))
            self.to_x(zo).start()
            if self.low < self.rows:
                self.high_x(zo).wait_recv()
                self.add(
                    self.index(zo, 1 - self.y, self.x), self.high_buf[zo], (self.low, self.rows - self.low)
                )
            self.to_y(zo).start()

        self.each(distance, act)

    def along(self, distance):
        own = self.index

        def joined(zo):
            self.to_x(zo).wait_recv()
            self.to_y(zo).wait_recv()
            i = own(zo, self.y, self.x)
            total = self.x_buf[zo].astype(F32) + self.y_buf[zo].astype(F32) + self.chip[i].astype(F32)
            return i, total

        def from_below(zo):
            self.up(zo).wait_recv()
            i = own(zo, self.y, self.x)
            self.add(i, self.up_buf[zo])

        def from_above(zo):
            self.down(zo).wait_recv()
            i = own(zo, self.y, self.x)
            self.add(i, self.down_buf[zo])

        def rising():
            zo = self.z + distance
            i, total = joined(zo)
            self.chip[i] = total.astype(self.chip.dtype)
            when(self.z > 0, lambda: from_below(zo))
            self.up(zo).start()

        def falling():
            zo = self.z - distance
            i, total = joined(zo)
            self.chip[i] = total.astype(self.chip.dtype)
            when(self.z < self.line - 1, lambda: from_above(zo))
            self.down(zo).start()

        if distance:
            when(self.z + distance < self.line, rising)
            when(self.z - distance >= 0, falling)
        else:
            _, total = joined(self.z)
            self.out[...] = total

            def below():
                self.up(self.z).wait_recv()
                self.out[...] += self.up_buf[self.z].astype(F32)

            def above():
                self.down(self.z).wait_recv()
                self.out[...] += self.down_buf[self.z].astype(F32)

            when(self.z > 0, below)
            when(self.z < self.line - 1, above)

    def drain(self):
        for zo in range(self.line):
            when(zo > self.z, lambda: self.up(zo).wait_send())
            when(zo < self.z, lambda: self.down(zo).wait_send())
            self.to_x(zo).wait_send()
            self.to_y(zo).wait_send()
            self.low_y(zo).wait_send()
            if self.low < self.rows:
                self.high_x(zo).wait_send()
            for yo in range(2):
                for xo in range(2):
                    self.core(zo, yo, xo).wait_send()


BUFFERS = 7


def reduce_scratch(line, part):
    _, rows, width = part.shape
    low = low_rows(rows)
    high = max(rows - low, 8)
    sizes = [(line * 4, rows), (line, low), (line, high), (line, rows), (line, rows), (line, rows), (line, rows)]
    return [pltpu.VMEM(s + (width,), part.dtype) for s in sizes]


def reduce_kernel(line, count, *refs):
    parts, outs, everyone = refs[:count], refs[count : 2 * count], refs[2 * count]
    sends, recvs, share_send, share_recv, local = refs[2 * count + 1 : 2 * count + 6]
    buffers = refs[2 * count + 6 :]
    devices = line * 8
    greet_all(devices)
    pieces = [
        Reduce(
            line, parts[p], outs[p], *buffers[p * BUFFERS : (p + 1) * BUFFERS], sends.at[p], recvs.at[p]
        )
        for p in range(count)
    ]
    for distance in range(line - 1, -1, -1):
        for piece in pieces:
            piece.begin(distance)
    for step in range(line + 2):
        for piece in pieces:
            if step < line:
                piece.corner(line - 1 - step)
            if 1 <= step <= line:
                piece.plane(line - step)
            if step >= 2:
                piece.along(line + 1 - step)
    mine = flat(*spot())
    last = outs[count - 1]

    def share(i):
        other = lax.rem(mine + i, devices)
        return send(
            last,
            everyone.at[mine],
            share_send.at[i],
            share_recv.at[i],
            (other // 8, other // 4 % 2, other // 2 % 2, other % 2),
        )

    keep = pltpu.make_async_copy(last, everyone.at[mine], local)
    keep.start()
    lax.fori_loop(1, devices, lambda i, c: (share(i).start(), c)[1], 0)
    for piece in pieces:
        piece.drain()
    keep.wait()

    def settle(i, carry):
        share(i).wait_recv()
        share(i).wait_send()
        return carry

    lax.fori_loop(1, devices, settle, 0)


def reduce_pieces(parts, line):
    count, devices = len(parts), line * 8
    vmem = pl.BlockSpec(memory_space=pltpu.VMEM)
    return pl.pallas_call(
        functools.partial(reduce_kernel, line, count),
        name="reduce_gradients",
        out_shape=[jax.ShapeDtypeStruct(p.shape[1:], F32) for p in parts]
        + [jax.ShapeDtypeStruct(parts[-1].shape, F32)],
        in_specs=[vmem] * count,
        out_specs=[vmem] * (count + 1),
        scratch_shapes=[
            pltpu.SemaphoreType.DMA((count, 7, line * 4)),
            pltpu.SemaphoreType.DMA((count, 7, line * 4)),
            pltpu.SemaphoreType.DMA((devices,)),
            pltpu.SemaphoreType.DMA((devices,)),
            pltpu.SemaphoreType.DMA,
        ]
        + [buffer for part in parts for buffer in reduce_scratch(line, part)],
        compiler_params=pltpu.CompilerParams(
            collective_id=1, has_side_effects=True, vmem_limit_bytes=KERNEL_VMEM
        ),
    )(*parts)


def shards(
    hidden_in,
    cotangent,
    mixer_input_weight,
    mixer_output_weight,
    feedforward_up,
    feedforward_down,
    first_gain,
    first_shift,
    second_gain,
    second_shift,
    short_taps,
    short_bias,
    skip_scale,
    filter_out,
    pos_weight,
    pos_bias,
    mid_weight,
    mid_bias,
    sine_freq,
    decay_rate,
):
    devices = lax.axis_size(AXES)
    micro, seq_count, tok, width = hidden_in.shape
    seqs = micro * seq_count
    tokens = seqs * tok
    length = tok * devices
    chans = width // devices
    block = tok * lax.axis_size("chan")
    blocks = length // block

    line = lax.axis_size("blk") // 2
    paired = devices == 32 and lax.axis_size("chan") == 4
    norms = jnp.stack([first_gain, first_shift, second_gain, second_shift])
    own = [mixer_input_weight.T, feedforward_up.T, feedforward_down, mixer_output_weight.T]
    if paired:
        norms = jnp.pad(norms, ((0, 4), (0, 128 - chans)))
        *full, norms = gather_pieces(own + [norms], line)
        norms = norms[:, :4, :chans].transpose(1, 0, 2).reshape(4, width)
        full = [w.reshape(-1, width) for w in full]
    else:
        full = [lax.all_gather(shard, AXES, axis=0, tiled=True) for shard in own]
        norms = lax.all_gather(norms, AXES, axis=1, tiled=True)
    weight_in, weight_up, weight_down, weight_out = full
    norms = norms.astype(F32)
    gain_one, shift_one, gain_two, shift_two = norms[0], norms[1], norms[2], norms[3]

    freq = sine_freq.astype(F32)
    w_pos, w_mid, w_fil = pos_weight.astype(F32), mid_weight.astype(F32), filter_out.astype(F32)
    lags, features, first_sum, first_act, second_sum, second_act = filter_hidden(
        length, w_pos, pos_bias.astype(F32), w_mid, mid_bias.astype(F32), freq
    )
    decay = jnp.exp(-lags[None, :] * decay_rate.astype(F32)[:, None])
    kernel = contract(w_fil, second_act, 0, 0, EXACT) * decay
    table = block_table(block)
    sign = 1.0 - 2.0 * (lax.iota(jnp.int32, block) % 2).astype(F32)
    ker_re, ker_im = to_spectrum(kernel.reshape(chans, blocks, block), table)

    def with_previous(spec):
        before = jnp.concatenate([jnp.zeros_like(spec[:, :1]), spec[:, :-1]], 1)
        return spec + sign * before

    k_re, k_alt, k_im = packed_kernel(with_previous(ker_re), with_previous(ker_im))

    values = hidden_in.reshape(tokens, width).astype(F32)
    normed, normal_one, inv_one = layer_norm(values, gain_one, shift_one)
    normed = normed.astype(BF16)
    projected = contract(weight_in, normed, 1, 1).astype(BF16)
    projected = projected.reshape(3, devices, chans, tokens).transpose(1, 0, 2, 3)
    arrived = exchange(projected)

    def by_sequence(values):
        parts = values.shape[1]
        values = values.reshape(devices, parts, chans, seqs, tok)
        return values.transpose(1, 3, 2, 0, 4).reshape(parts, seqs, chans, length)

    def by_device(values):
        parts = values.shape[0]
        values = values.reshape(parts, seqs, chans, devices, tok)
        return values.transpose(3, 0, 2, 1, 4).reshape(devices, parts, chans, tokens)

    steps = by_sequence(arrived).astype(F32)
    taps = short_taps.astype(F32)[:, :, None, :, None]
    conv = short_bias.astype(F32)[:, None, :, None]
    for i in range(3):
        conv = conv + taps[i] * delayed(steps, i)
    gate_out, gate_in, signal = conv[0], conv[1], conv[2]
    gated = signal * gate_in
    sig_re, sig_im = to_spectrum(gated.reshape(seqs, chans, blocks, block), table)

    def shifted_sum(make):
        total = None
        for d in range(blocks):
            term = make(d)
            total = term if total is None else tuple(a + b for a, b in zip(total, term))
        return total

    def ahead(x, d):
        return x if d == 0 else jnp.pad(x[:, :, :-d], ((0, 0), (0, 0), (d, 0), (0, 0)))

    def back(x, d):
        return x if d == 0 else jnp.pad(x[:, :, d:], ((0, 0), (0, 0), (0, d), (0, 0)))

    def forward_term(d):
        re, im = ahead(sig_re, d), ahead(sig_im, d)
        kr, ka, ki = k_re[:, d : d + 1], k_alt[:, d : d + 1], k_im[:, d : d + 1]
        return re * kr - im * ki, re * ki + im * ka

    out_re, out_im = shifted_sum(forward_term)
    long_out = from_spectrum(out_re, out_im, table).reshape(seqs, chans, length)
    skip = skip_scale.astype(F32)[None, :, None]
    long_total = long_out + skip * gated
    mixed = (long_total * gate_out).astype(BF16)
    mixed = exchange(by_device(mixed[None])).reshape(width, tokens)

    resid = values + contract(mixed, weight_out, 0, 1)
    second, normal_two, inv_two = layer_norm(resid, gain_two, shift_two)
    second = second.astype(BF16)
    upper = contract(second, weight_up, 1, 1)
    active, slope = gelu_parts(upper)
    active = active.astype(BF16)
    result = resid + contract(active, weight_down, 1, 0)

    cot = cotangent.reshape(tokens, width)
    grad_down = contract(active, cot, 0, 0)
    grad_upper = (contract(cot, weight_down, 1, 1) * slope).astype(BF16)
    grad_up = contract(grad_upper, second, 0, 0)
    grad_second = contract(grad_upper, weight_up, 1, 0)
    resid_term, grad_gain_two, grad_shift_two = layer_norm_back(grad_second, normal_two, inv_two, gain_two)
    grad_resid = cot.astype(F32) + resid_term
    grad_branch = grad_resid.astype(BF16)
    grad_out_w = contract(grad_branch, mixed, 0, 1)
    grad_mixed = contract(weight_out, grad_branch, 0, 1).astype(BF16)
    grad_mixed = exchange(grad_mixed.reshape(devices, 1, chans, tokens))
    grad_mixed = by_sequence(grad_mixed)[0].astype(F32)

    grad_gate_out = grad_mixed * long_total
    grad_long = grad_mixed * gate_out
    grad_skip = jnp.sum(grad_long * gated, (0, 2))
    gl_re, gl_im = to_spectrum(grad_long.reshape(seqs, chans, blocks, block), table)

    def signal_term(d):
        re, im = back(gl_re, d), back(gl_im, d)
        kr, ka, ki = k_re[:, d : d + 1], k_alt[:, d : d + 1], k_im[:, d : d + 1]
        return re * kr + im * ki, im * ka - re * ki

    gg_re, gg_im = shifted_sum(signal_term)
    grad_gated = from_spectrum(gg_re, gg_im, table).reshape(seqs, chans, length) + skip * grad_long

    first_slot = lax.iota(jnp.int32, block) == 0
    kg_re, kg_im = [], []
    for d in range(blocks):
        s_re, s_im = sig_re[:, :, : blocks - d], sig_im[:, :, : blocks - d]
        g_re, g_im = gl_re[:, :, d:], gl_im[:, :, d:]
        same, other = g_re * s_re, g_im * s_im
        kg_re.append(jnp.sum(jnp.where(first_slot, same, same + other), (0, 2)))
        kg_im.append(jnp.sum(jnp.where(first_slot, other, g_im * s_re - g_re * s_im), (0, 2)))
    kg_re, kg_im = jnp.stack(kg_re, 1), jnp.stack(kg_im, 1)

    def with_next(spec):
        after = jnp.concatenate([spec[:, 1:], jnp.zeros_like(spec[:, :1])], 1)
        return spec + sign * after

    grad_kernel = from_spectrum(with_next(kg_re), with_next(kg_im), table).reshape(chans, length)

    grad_conv = jnp.stack([grad_gate_out, grad_gated * signal, grad_gated * gate_in])
    grad_bias = jnp.sum(grad_conv, (1, 3))
    grad_taps = jnp.stack([jnp.sum(grad_conv * delayed(steps, i), (1, 3)) for i in range(3)])
    grad_steps = taps[0] * grad_conv
    for i in (1, 2):
        grad_steps = grad_steps + taps[i] * advanced(grad_conv, i)
    grad_proj = exchange(by_device(grad_steps.astype(BF16)))
    grad_proj = grad_proj.transpose(1, 0, 2, 3).reshape(3 * width, tokens)

    fade = grad_kernel * decay
    grad_filter = contract(second_act, fade, 1, 1, EXACT)
    grad_two = contract(w_fil, fade, 1, 0, EXACT) * jnp.cos(freq[:, None] * second_sum)
    grad_freq = jnp.sum(grad_two * second_sum, 1)
    grad_two = grad_two * freq[:, None]
    grad_mid = contract(first_act, grad_two, 1, 1, EXACT)
    grad_one = contract(w_mid, grad_two, 1, 0, EXACT) * jnp.cos(freq[:, None] * first_sum)
    grad_freq = grad_freq + jnp.sum(grad_one * first_sum, 1)
    grad_one = grad_one * freq[:, None]
    grad_pos = contract(features, grad_one, 1, 1, EXACT)
    small = jnp.concatenate(
        [grad_pos, jnp.sum(grad_one, 1)[None], grad_mid, jnp.sum(grad_two, 1)[None], grad_freq[None]]
    )
    emb, order = pos_weight.shape

    grad_in = contract(grad_proj, normed, 1, 0)
    grad_normed = contract(grad_proj, weight_in, 0, 0)
    input_term, grad_gain_one, grad_shift_one = layer_norm_back(grad_normed, normal_one, inv_one, gain_one)
    grad_hidden = (grad_resid + input_term).astype(BF16)

    norm_grads = jnp.stack([grad_gain_one, grad_shift_one, grad_gain_two, grad_shift_two])
    sums = [grad_in, grad_up, grad_down, grad_out_w]
    if paired:
        sums = [g.astype(BF16).reshape(devices, -1, width) for g in sums]
        norm_grads = norm_grads.reshape(4, devices, chans).transpose(1, 0, 2)
        norm_grads = jnp.pad(norm_grads, ((0, 0), (0, 0), (0, 128 - chans)))
        count = small.size
        share = -(-count // (devices * 128))
        small = jnp.pad(small.reshape(-1, 128), ((0, devices * share - count // 128), (0, 0)))
        small = jnp.pad(small.reshape(devices, share, 128), ((0, 0), (0, 4 - share), (0, 0)))
        *sums, norm_grads, small = reduce_pieces(sums + [jnp.concatenate([norm_grads, small], 1)], line)
        norm_grads = norm_grads[:4, :chans]
        small = small[:, 4 : 4 + share].reshape(-1)[:count].reshape(-1, order)
    else:
        sums = [
            lax.psum_scatter(g.astype(BF16), AXES, scatter_dimension=0, tiled=True).astype(F32) for g in sums
        ]
        norm_grads = lax.psum_scatter(norm_grads, AXES, scatter_dimension=1, tiled=True)
        small = lax.psum(small, AXES)
    return (
        result.astype(BF16).reshape(hidden_in.shape),
        grad_hidden.reshape(hidden_in.shape),
        sums[0].T,
        sums[3].T,
        sums[1].T,
        sums[2],
        norm_grads[0],
        norm_grads[1],
        norm_grads[2],
        norm_grads[3],
        grad_taps,
        grad_bias,
        grad_skip,
        grad_filter,
        small[:emb],
        small[emb],
        small[emb + 1 : emb + 1 + order],
        small[emb + 1 + order],
        small[emb + 2 + order],
    )


def solution(mesh):
    rows, spread, tokens = P(AXES), P(None, AXES), P(None, None, AXES, None)
    params = (rows, rows, rows, rows, P(None, None, AXES), spread, rows, spread, P(), P(), P(), P(), P())
    return jax.shard_map(
        shards,
        mesh=mesh,
        in_specs=(tokens, tokens, spread, spread, spread, P(AXES, None)) + params + (rows,),
        out_specs=(tokens, tokens, spread, spread, spread, P(AXES, None)) + params,
        check_vma=False,
    )
```

```python
import functools
import math

import jax
import jax.numpy as jnp
import numpy as np
from jax import lax
from jax.experimental import pallas as pl
from jax.experimental.pallas import tpu as pltpu
from jax.sharding import PartitionSpec as P

EPS = 1e-05
BANDS = 16
EXACT = lax.Precision.HIGHEST
AXES = ("blk", "chan")
F32 = jnp.float32
BF16 = jnp.bfloat16
MESH = pl.DeviceIdType.MESH
KERNEL_VMEM = 60 << 20


def contract(a, b, dim_a, dim_b, precision=None):
    return lax.dot_general(
        a, b, (((dim_a,), (dim_b,)), ((), ())), precision=precision, preferred_element_type=F32
    )


def positions(length):
    lags = jnp.arange(length).astype(F32)
    band_freq = 0.0001 + (BANDS - 1 - 0.0001) * jnp.arange(BANDS).astype(F32) / (BANDS - 1)
    phase = 2.0 * math.pi / length * lags[None, :] * band_freq[:, None]
    return lags, jnp.concatenate([lags[None, :] / (length - 1), jnp.cos(phase), -jnp.sin(phase)], 0)


def feature_blocks(length, block):
    lags = np.arange(length).astype(np.float32)
    bands = np.arange(BANDS).astype(np.float32)
    band_freq = np.float32(0.0001) + np.float32(BANDS - 1 - 0.0001) * bands / np.float32(BANDS - 1)
    phase = np.float32(2.0 * math.pi / length) * lags[None, :] * band_freq[:, None]
    ramp = lags[None, :] / np.float32(length - 1)
    rows = np.concatenate([ramp, np.cos(phase), -np.sin(phase), np.ones_like(ramp)])
    rows = np.pad(rows, ((0, -len(rows) % 8), (0, 0))).astype(np.float32)
    return np.ascontiguousarray(rows.reshape(len(rows), -1, block).transpose(1, 0, 2))


def fixed_table(block):
    spot, freq = np.arange(block)[:, None], np.arange(block)[None, :]
    phase = (np.pi / block) * (spot * freq % (2 * block))
    imag = np.where(freq == 0, 1.0 - 2.0 * (spot % 2), -np.sin(phase))
    return np.concatenate([np.cos(phase), imag], 1).astype(np.float32)


def filter_hidden(length, pos_weight, pos_bias, mid_weight, mid_bias, sine_freq):
    lags, features = positions(length)
    freq = sine_freq[:, None]
    first_sum = contract(pos_weight, features, 0, 0, EXACT) + pos_bias[:, None]
    first = jnp.sin(freq * first_sum)
    second_sum = contract(mid_weight, first, 0, 0, EXACT) + mid_bias[:, None]
    second = jnp.sin(freq * second_sum)
    return lags, features, first_sum, first, second_sum, second


def block_table(block):
    spot = lax.broadcasted_iota(jnp.int32, (block, block), 0)
    freq = lax.broadcasted_iota(jnp.int32, (block, block), 1)
    phase = (math.pi / block) * (spot * freq % (2 * block)).astype(F32)
    parity = 1.0 - 2.0 * (spot % 2).astype(F32)
    imag = jnp.where(freq == 0, parity, -jnp.sin(phase))
    return jnp.concatenate([jnp.cos(phase), imag], 1)


def to_spectrum(blocks, table):
    spec = lax.dot_general(
        blocks, table, (((blocks.ndim - 1,), (0,)), ((), ())), precision=EXACT, preferred_element_type=F32
    )
    half = table.shape[0]
    return spec[..., :half], spec[..., half:]


def from_spectrum(real, imag, table):
    half = table.shape[0]
    weight = jnp.where(lax.iota(jnp.int32, half) == 0, 0.5 / half, 1.0 / half)
    spec = jnp.concatenate([real * weight, imag * weight], -1)
    return lax.dot_general(
        spec, table, (((spec.ndim - 1,), (1,)), ((), ())), precision=EXACT, preferred_element_type=F32
    )


def packed_kernel(real, imag):
    first = lax.iota(jnp.int32, real.shape[-1]) == 0
    return real, jnp.where(first, imag, real), jnp.where(first, 0.0, imag)


def layer_norm(values, gain, shift):
    center = values - jnp.mean(values, -1, keepdims=True)
    scale_inv = lax.rsqrt(jnp.mean(center * center, -1, keepdims=True) + EPS)
    normal = center * scale_inv
    return normal * gain + shift, normal, scale_inv


def layer_norm_back(grad_out, normal, scale_inv, gain):
    grad_normal = grad_out * gain
    inner = grad_normal - jnp.mean(grad_normal, -1, keepdims=True)
    inner = inner - normal * jnp.mean(grad_normal * normal, -1, keepdims=True)
    return inner * scale_inv, jnp.sum(grad_out * normal, 0), jnp.sum(grad_out, 0)


def gelu_parts(v):
    root = math.sqrt(2.0 / math.pi)
    inner = root * (v + 0.044715 * v * v * v)
    t = jnp.tanh(inner)
    value = 0.5 * v * (1.0 + t)
    slope = 0.5 * (1.0 + t) + 0.5 * v * (1.0 - t * t) * root * (1.0 + 3.0 * 0.044715 * v * v)
    return value, slope


def delayed(values, steps):
    if steps == 0:
        return values
    pad = jnp.zeros(values.shape[:-1] + (steps,), values.dtype)
    return jnp.concatenate([pad, values[..., :-steps]], -1)


def advanced(values, steps):
    if steps == 0:
        return values
    pad = jnp.zeros(values.shape[:-1] + (steps,), values.dtype)
    return jnp.concatenate([values[..., steps:], pad], -1)


def exchange(values):
    return lax.all_to_all(values, AXES, split_axis=0, concat_axis=0, tiled=True)


def spot():
    b, c = lax.axis_index("blk"), lax.axis_index("chan")
    return b // 2, b % 2, c // 2, c % 2


def at(z, y, x, k):
    return {"blk": z * 2 + y, "chan": x * 2 + k}


def flat(z, y, x, k):
    return ((z * 2 + y) * 2 + x) * 2 + k


def when(condition, act):
    pl.when(condition)(act)


def send(src, dst, send_sem, recv_sem, place):
    return pltpu.make_async_remote_copy(
        src_ref=src, dst_ref=dst, send_sem=send_sem, recv_sem=recv_sem, device_id=at(*place), device_id_type=MESH
    )


def greet_all(count):
    b, c = lax.axis_index("blk"), lax.axis_index("chan")
    chan = lax.axis_size("chan")
    me = b * chan + c
    barrier = pltpu.get_barrier_semaphore()

    def one(i, carry):
        other = lax.rem(me + i, count)
        pl.semaphore_signal(
            barrier, inc=1, device_id={"blk": other // chan, "chan": other % chan}, device_id_type=MESH
        )
        return carry

    lax.fori_loop(1, count, one, 0)
    pl.semaphore_wait(barrier, count - 1)


def greet_near(line):
    z, y, x, k = spot()
    barrier = pltpu.get_barrier_semaphore()

    def hello(*place):
        pl.semaphore_signal(barrier, inc=1, device_id=at(*place), device_id_type=MESH)

    hello(z, 1 - y, x, k)
    hello(z, y, 1 - x, k)
    hello(z, y, x, 1 - k)
    when(z > 0, lambda: hello(z - 1, y, x, k))
    when(z < line - 1, lambda: hello(z + 1, y, x, k))
    pl.semaphore_wait(barrier, 3 + jnp.minimum(z, 1) + jnp.minimum(line - 1 - z, 1))


def low_rows(rows):
    return max(rows // 16 * 8, 8) if rows > 8 else rows


class Gather:
    def __init__(self, line, shard, full, sends, recvs, local):
        self.line, self.shard, self.full, self.s, self.r, self.local = line, shard, full, sends, recvs, local
        self.rows = shard.shape[0]
        self.low = low_rows(self.rows)
        self.z, self.y, self.x, self.k = spot()

    def copy(self, kind, index, shard, place, rows=None):
        ref = self.full.at[shard] if rows is None else self.full.at[shard, pl.ds(*rows)]
        return send(ref, ref, self.s.at[kind, index], self.r.at[kind, index], place)

    def up(self, zo):
        return self.copy(0, zo, flat(zo, self.y, self.x, self.k), (self.z + 1, self.y, self.x, self.k))

    def down(self, zo):
        return self.copy(1, zo, flat(zo, self.y, self.x, self.k), (self.z - 1, self.y, self.x, self.k))

    def to_x(self, zo):
        return self.copy(2, zo, flat(zo, self.y, self.x, self.k), (self.z, self.y, 1 - self.x, self.k))

    def to_y(self, zo):
        return self.copy(3, zo, flat(zo, self.y, self.x, self.k), (self.z, 1 - self.y, self.x, self.k))

    def low_y(self, zo, other_y=False):
        shard = flat(zo, 1 - self.y if other_y else self.y, 1 - self.x, self.k)
        return self.copy(4, zo, shard, (self.z, 1 - self.y, self.x, self.k), (0, self.low))

    def high_x(self, zo, other_x=False):
        shard = flat(zo, 1 - self.y, 1 - self.x if other_x else self.x, self.k)
        return self.copy(5, zo, shard, (self.z, self.y, 1 - self.x, self.k), (self.low, self.rows - self.low))

    def core(self, zo, yo, xo, k):
        return self.copy(6, (zo * 2 + yo) * 2 + xo, flat(zo, yo, xo, k), (self.z, self.y, self.x, 1 - self.k))

    def line_has(self, zo):
        self.to_x(zo).start()
        self.to_y(zo).start()
        self.core(zo, self.y, self.x, self.k).start()

    def begin(self):
        own = self.full.at[flat(self.z, self.y, self.x, self.k)]
        copy = pltpu.make_async_copy(self.shard, own, self.local)
        copy.start()
        copy.wait()
        when(self.z < self.line - 1, lambda: self.up(self.z).start())
        when(self.z > 0, lambda: self.down(self.z).start())
        self.line_has(self.z)

    def each(self, distance, act):
        if distance == 0:
            act(self.z)
        else:
            when(self.z - distance >= 0, lambda: act(self.z - distance))
            when(self.z + distance < self.line, lambda: act(self.z + distance))

    def along(self, distance):
        def from_below():
            zo = self.z - distance
            self.up(zo).wait_recv()
            when(self.z < self.line - 1, lambda: self.up(zo).start())
            self.line_has(zo)

        def from_above():
            zo = self.z + distance
            self.down(zo).wait_recv()
            when(self.z > 0, lambda: self.down(zo).start())
            self.line_has(zo)

        when(self.z - distance >= 0, from_below)
        when(self.z + distance < self.line, from_above)

    def plane(self, distance):
        def act(zo):
            self.to_x(zo).wait_recv()
            self.low_y(zo).start()
            self.core(zo, self.y, 1 - self.x, self.k).start()
            self.to_y(zo).wait_recv()
            if self.low < self.rows:
                self.high_x(zo).start()
            self.core(zo, 1 - self.y, self.x, self.k).start()

        self.each(distance, act)

    def corner(self, distance):
        def act(zo):
            self.low_y(zo, True).wait_recv()
            if self.low < self.rows:
                self.high_x(zo, True).wait_recv()
            self.core(zo, 1 - self.y, 1 - self.x, self.k).start()

        self.each(distance, act)

    def finish(self):
        for zo in range(self.line):
            for yo in range(2):
                for xo in range(2):
                    self.core(zo, yo, xo, 1 - self.k).wait_recv()

    def drain(self):
        for zo in range(self.line):
            when(jnp.logical_and(self.z < self.line - 1, zo <= self.z), lambda: self.up(zo).wait_send())
            when(jnp.logical_and(self.z > 0, zo >= self.z), lambda: self.down(zo).wait_send())
            self.to_x(zo).wait_send()
            self.to_y(zo).wait_send()
            self.low_y(zo).wait_send()
            if self.low < self.rows:
                self.high_x(zo).wait_send()
            for yo in range(2):
                for xo in range(2):
                    self.core(zo, yo, xo, self.k).wait_send()


def gather_kernel(line, count, *refs):
    shards, fulls = refs[:count], refs[count : 2 * count]
    sends, recvs, local = refs[2 * count :]
    greet_near(line)
    pieces = [Gather(line, shards[p], fulls[p], sends.at[p], recvs.at[p], local) for p in range(count)]
    for piece in pieces:
        piece.begin()
    for distance in range(1, line):
        for piece in pieces:
            piece.along(distance)
            piece.plane(distance - 1)
            if distance > 1:
                piece.corner(distance - 2)
    for piece in pieces:
        piece.plane(line - 1)
        if line > 1:
            piece.corner(line - 2)
    for piece in pieces:
        piece.corner(line - 1)
    for piece in pieces:
        piece.finish()
        piece.drain()


def gather_pieces(shards, line):
    count, devices = len(shards), line * 8
    vmem = pl.BlockSpec(memory_space=pltpu.VMEM)
    return pl.pallas_call(
        functools.partial(gather_kernel, line, count),
        name="gather_weights",
        out_shape=[jax.ShapeDtypeStruct((devices,) + s.shape, s.dtype) for s in shards],
        in_specs=[vmem] * count,
        out_specs=[vmem] * count,
        scratch_shapes=[
            pltpu.SemaphoreType.DMA((count, 7, line * 4)),
            pltpu.SemaphoreType.DMA((count, 7, line * 4)),
            pltpu.SemaphoreType.DMA,
        ],
        compiler_params=pltpu.CompilerParams(
            collective_id=0, has_side_effects=True, vmem_limit_bytes=KERNEL_VMEM
        ),
    )(*shards)


class Reduce:
    def __init__(self, line, part, out, chip, low_y, high_x, by_x, by_y, up, down, sends, recvs):
        self.line, self.part, self.out, self.chip = line, part, out, chip
        self.low_buf, self.high_buf, self.x_buf, self.y_buf, self.up_buf, self.down_buf = (
            low_y, high_x, by_x, by_y, up, down,
        )
        self.s, self.r = sends, recvs
        self.rows = part.shape[1]
        self.low = low_rows(self.rows)
        self.z, self.y, self.x, self.k = spot()

    def index(self, zo, yo, xo):
        return (zo * 2 + yo) * 2 + xo

    def copy(self, kind, index, src, dst, place):
        return send(src, dst, self.s.at[kind, index], self.r.at[kind, index], place)

    def core(self, zo, yo, xo):
        i = self.index(zo, yo, xo)
        src = self.part.at[flat(zo, yo, xo, 1 - self.k)]
        return self.copy(6, i, src, self.chip.at[i], (self.z, self.y, self.x, 1 - self.k))

    def low_y(self, zo):
        i = self.index(zo, 1 - self.y, 1 - self.x)
        src = self.chip.at[i, pl.ds(0, self.low)]
        return self.copy(4, zo, src, self.low_buf.at[zo], (self.z, 1 - self.y, self.x, self.k))

    def high_x(self, zo):
        i = self.index(zo, 1 - self.y, 1 - self.x)
        src = self.chip.at[i, pl.ds(self.low, self.rows - self.low)]
        return self.copy(5, zo, src, self.high_buf.at[zo], (self.z, self.y, 1 - self.x, self.k))

    def to_x(self, zo):
        src = self.chip.at[self.index(zo, self.y, 1 - self.x)]
        return self.copy(2, zo, src, self.x_buf.at[zo], (self.z, self.y, 1 - self.x, self.k))

    def to_y(self, zo):
        src = self.chip.at[self.index(zo, 1 - self.y, self.x)]
        return self.copy(3, zo, src, self.y_buf.at[zo], (self.z, 1 - self.y, self.x, self.k))

    def up(self, zo):
        src = self.chip.at[self.index(zo, self.y, self.x)]
        return self.copy(0, zo, src, self.up_buf.at[zo], (self.z + 1, self.y, self.x, self.k))

    def down(self, zo):
        src = self.chip.at[self.index(zo, self.y, self.x)]
        return self.copy(1, zo, src, self.down_buf.at[zo], (self.z - 1, self.y, self.x, self.k))

    def add(self, i, other, rows=None):
        if rows is None:
            self.chip[i] = self.chip[i] + other
        else:
            self.chip[i, pl.ds(*rows)] = self.chip[i, pl.ds(*rows)] + other

    def each(self, distance, act):
        if distance == 0:
            act(self.z)
        else:
            when(self.z - distance >= 0, lambda: act(self.z - distance))
            when(self.z + distance < self.line, lambda: act(self.z + distance))

    def begin(self, distance):
        def act(zo):
            for yo, xo in ((1 - self.y, 1 - self.x), (self.y, 1 - self.x), (1 - self.y, self.x), (self.y, self.x)):
                self.core(zo, yo, xo).start()

        self.each(distance, act)

    def corner(self, distance):
        def act(zo):
            for yo, xo in ((1 - self.y, 1 - self.x), (self.y, 1 - self.x), (1 - self.y, self.x), (self.y, self.x)):
                self.core(zo, yo, xo).wait_recv()
                self.add(self.index(zo, yo, xo), self.part[flat(zo, yo, xo, self.k)])
                if yo is not self.y and xo is not self.x:
                    self.low_y(zo).start()
                    if self.low < self.rows:
                        self.high_x(zo).start()

        self.each(distance, act)

    def plane(self, distance):
        def act(zo):
            self.low_y(zo).wait_recv()
            self.add(self.index(zo, self.y, 1 - self.x), self.low_buf[zo], (0, self.low))
            self.to_x(zo).start()
            if self.low < self.rows:
                self.high_x(zo).wait_recv()
                self.add(
                    self.index(zo, 1 - self.y, self.x), self.high_buf[zo], (self.low, self.rows - self.low)
                )
            self.to_y(zo).start()

        self.each(distance, act)

    def along(self, distance):
        own = self.index

        def joined(zo):
            self.to_x(zo).wait_recv()
            self.to_y(zo).wait_recv()
            i = own(zo, self.y, self.x)
            total = self.x_buf[zo].astype(F32) + self.y_buf[zo].astype(F32) + self.chip[i].astype(F32)
            return i, total

        def from_below(zo):
            self.up(zo).wait_recv()
            i = own(zo, self.y, self.x)
            self.add(i, self.up_buf[zo])

        def from_above(zo):
            self.down(zo).wait_recv()
            i = own(zo, self.y, self.x)
            self.add(i, self.down_buf[zo])

        def rising():
            zo = self.z + distance
            i, total = joined(zo)
            self.chip[i] = total.astype(self.chip.dtype)
            when(self.z > 0, lambda: from_below(zo))
            self.up(zo).start()

        def falling():
            zo = self.z - distance
            i, total = joined(zo)
            self.chip[i] = total.astype(self.chip.dtype)
            when(self.z < self.line - 1, lambda: from_above(zo))
            self.down(zo).start()

        if distance:
            when(self.z + distance < self.line, rising)
            when(self.z - distance >= 0, falling)
        else:
            _, total = joined(self.z)
            self.out[...] = total

            def below():
                self.up(self.z).wait_recv()
                self.out[...] += self.up_buf[self.z].astype(F32)

            def above():
                self.down(self.z).wait_recv()
                self.out[...] += self.down_buf[self.z].astype(F32)

            when(self.z > 0, below)
            when(self.z < self.line - 1, above)

    def drain(self):
        for zo in range(self.line):
            when(zo > self.z, lambda: self.up(zo).wait_send())
            when(zo < self.z, lambda: self.down(zo).wait_send())
            self.to_x(zo).wait_send()
            self.to_y(zo).wait_send()
            self.low_y(zo).wait_send()
            if self.low < self.rows:
                self.high_x(zo).wait_send()
            for yo in range(2):
                for xo in range(2):
                    self.core(zo, yo, xo).wait_send()


BUFFERS = 7


def reduce_scratch(line, part):
    _, rows, width = part.shape
    low = low_rows(rows)
    high = max(rows - low, 8)
    sizes = [(line * 4, rows), (line, low), (line, high), (line, rows), (line, rows), (line, rows), (line, rows)]
    return [pltpu.VMEM(s + (width,), part.dtype) for s in sizes]


def reduce_kernel(line, count, *refs):
    parts, outs, everyone = refs[:count], refs[count : 2 * count], refs[2 * count]
    sends, recvs, share_send, share_recv, local = refs[2 * count + 1 : 2 * count + 6]
    buffers = refs[2 * count + 6 :]
    devices = line * 8
    greet_all(devices)
    pieces = [
        Reduce(
            line, parts[p], outs[p], *buffers[p * BUFFERS : (p + 1) * BUFFERS], sends.at[p], recvs.at[p]
        )
        for p in range(count)
    ]
    for distance in range(line - 1, -1, -1):
        for piece in pieces:
            piece.begin(distance)
    for step in range(line + 2):
        for piece in pieces:
            if step < line:
                piece.corner(line - 1 - step)
            if 1 <= step <= line:
                piece.plane(line - step)
            if step >= 2:
                piece.along(line + 1 - step)
    mine = flat(*spot())
    last = outs[count - 1]

    def share(i):
        other = lax.rem(mine + i, devices)
        return send(
            last,
            everyone.at[mine],
            share_send.at[i],
            share_recv.at[i],
            (other // 8, other // 4 % 2, other // 2 % 2, other % 2),
        )

    keep = pltpu.make_async_copy(last, everyone.at[mine], local)
    keep.start()
    lax.fori_loop(1, devices, lambda i, c: (share(i).start(), c)[1], 0)
    for piece in pieces:
        piece.drain()
    keep.wait()

    def settle(i, carry):
        share(i).wait_recv()
        share(i).wait_send()
        return carry

    lax.fori_loop(1, devices, settle, 0)


def reduce_pieces(parts, line):
    count, devices = len(parts), line * 8
    vmem = pl.BlockSpec(memory_space=pltpu.VMEM)
    return pl.pallas_call(
        functools.partial(reduce_kernel, line, count),
        name="reduce_gradients",
        out_shape=[jax.ShapeDtypeStruct(p.shape[1:], F32) for p in parts]
        + [jax.ShapeDtypeStruct(parts[-1].shape, F32)],
        in_specs=[vmem] * count,
        out_specs=[vmem] * (count + 1),
        scratch_shapes=[
            pltpu.SemaphoreType.DMA((count, 7, line * 4)),
            pltpu.SemaphoreType.DMA((count, 7, line * 4)),
            pltpu.SemaphoreType.DMA((devices,)),
            pltpu.SemaphoreType.DMA((devices,)),
            pltpu.SemaphoreType.DMA,
        ]
        + [buffer for part in parts for buffer in reduce_scratch(line, part)],
        compiler_params=pltpu.CompilerParams(
            collective_id=1, has_side_effects=True, vmem_limit_bytes=KERNEL_VMEM
        ),
    )(*parts)


def dot_rows(a, b, precision=None):
    return lax.dot_general(a, b, (((1,), (1,)), ((), ())), precision=precision, preferred_element_type=F32)


def dot_plain(a, b, precision=None):
    return lax.dot_general(a, b, (((1,), (0,)), ((), ())), precision=precision, preferred_element_type=F32)


def eighths(value):
    return pl.multiple_of(value, 8)


class Exchange:
    def __init__(self, src, dst, sends, recvs, devices):
        self.src, self.dst, self.s, self.r, self.devices = src, dst, sends, recvs, devices
        self.me = flat(*spot())

    def copy(self, i):
        other = lax.rem(self.me + i, self.devices)
        place = (other // 8, other // 4 % 2, other // 2 % 2, other % 2)
        return send(self.src.at[other], self.dst.at[self.me], self.s.at[i], self.r.at[i], place)

    def start(self):
        lax.fori_loop(1, self.devices, lambda i, c: (self.copy(i).start(), c)[1], 0)
        self.dst[self.me] = self.src[self.me]

    def arrive(self):
        lax.fori_loop(1, self.devices, lambda i, c: (self.copy(i).wait_recv(), c)[1], 0)

    def drain(self):
        lax.fori_loop(1, self.devices, lambda i, c: (self.copy(i).wait_send(), c)[1], 0)


def low_lanes(shape):
    return lax.broadcasted_iota(jnp.int32, shape, 1) < 64


def merge_halves(first, second):
    low = low_lanes(first.shape)
    return (
        jnp.where(low, first, pltpu.roll(second, 64, 1)),
        jnp.where(low, pltpu.roll(first, 64, 1), second),
    )


def lane_norm(values, gain, shift):
    center = values - jnp.mean(values, 1, keepdims=True)
    scale_inv = lax.rsqrt(jnp.mean(center * center, 1, keepdims=True) + EPS)
    normal = center * scale_inv
    return normal * gain + shift, normal, scale_inv


def slot_zero(shape):
    return lax.broadcasted_iota(jnp.int32, shape, 1) == 0


def slot_sign(shape):
    return 1.0 - 2.0 * (lax.broadcasted_iota(jnp.int32, shape, 1) % 2).astype(F32)


def slot_weight(shape):
    return jnp.where(slot_zero(shape), 0.5 / shape[1], 1.0 / shape[1])


def column(params, index):
    return params[:, index : index + 1]


def norm_rows(stack, count, chans, width):
    total = None
    for j in range(count):
        tile = stack(j).astype(F32)[:, :128]
        tile = jnp.where(lax.broadcasted_iota(jnp.int32, tile.shape, 1) < chans, tile, 0.0)
        wide = jnp.concatenate([tile, jnp.zeros((tile.shape[0], width - 128), F32)], 1)
        wide = pltpu.roll(wide, j * chans, 1) if j else wide
        total = wide if total is None else total + wide
    return total


def front_kernel(dims, *refs):
    line, devices, chans, seqs, block, blocks, width = dims
    (own_in, own_out, own_up, own_down, hidden, params, feats, pos_t, mid_t, fil_t, cols, table) = refs[:12]
    (full_in, full_out, full_up, full_down, mixed_in, norms_out, steps, conv, spec, total, k_re, k_alt, k_im) = refs[12:25]
    (one, cos_one, two, cos_two) = refs[25:29]
    (proj_send, proj_recv, mix_send, kernel_buf, gated, sums) = refs[29:35]
    (sends, recvs, local, send_a, recv_a, send_b, recv_b) = refs[35:]
    rows = chans * seqs
    greet_all(devices)
    pieces = [
        Gather(line, shard, full, sends.at[p], recvs.at[p], local)
        for p, (shard, full) in enumerate(
            ((own_in, full_in), (own_out, full_out), (own_up, full_up), (own_down, full_down))
        )
    ]
    late = (0, 1, 2, 3)

    def tick(now):
        for piece, offset in zip(pieces, late):
            step = now - offset
            if step == 0:
                piece.begin()
            if 1 <= step < line:
                piece.along(step)
            if 1 <= step <= line:
                piece.plane(step - 1)
            if 2 <= step <= line + 1:
                piece.corner(step - 2)

    def filter_part(n, carry):
        sum_one = dot_plain(pos_t[...], feats[n], EXACT)
        phase = column(cols[...], 0) * sum_one
        act_one = jnp.sin(phase)
        one[n] = act_one
        cos_one[n] = jnp.cos(phase)
        phase = column(cols[...], 0) * (dot_plain(mid_t[...], act_one, EXACT) + column(cols[...], 1))
        act_two = jnp.sin(phase)
        two[n] = act_two
        cos_two[n] = jnp.cos(phase)
        lag = lax.broadcasted_iota(jnp.int32, (chans, block), 1) + n * block
        fade = jnp.exp(-lag.astype(F32) * column(params[...], 13))
        kernel_buf[pl.ds(eighths(n * chans), chans), :] = dot_plain(fil_t[...], act_two, EXACT) * fade
        return carry

    def filters(first, last):
        lax.fori_loop(first, last, filter_part, 0)

    def kernel_spectrum():
        ker = dot_plain(kernel_buf[...], table[...], EXACT)
        before = jnp.concatenate([jnp.zeros((chans, 2 * block), F32), ker[:-chans]], 0)
        sign = slot_sign((chans * blocks, block))
        real = ker[:, :block] + sign * before[:, :block]
        imag = ker[:, block:] + sign * before[:, block:]
        zero = slot_zero(real.shape)
        k_re[...] = real
        k_alt[...] = jnp.where(zero, imag, real)
        k_im[...] = jnp.where(zero, 0.0, imag)

    tick(0)
    filters(0, blocks // 4)
    tick(1)
    filters(blocks // 4, blocks // 2)
    tick(2)
    filters(blocks // 2, 3 * blocks // 4)
    tick(3)
    filters(3 * blocks // 4, blocks)
    tick(4)
    kernel_spectrum()
    tick(5)
    pieces[0].finish()

    in_rows = full_in.shape[1]
    norms = norm_rows(lambda j: full_in[j, in_rows - 8 :], devices, chans, width)
    norms_out[...] = norms
    normed, _, _ = lane_norm(hidden[...].astype(F32), norms[0:1], norms[1:2])
    projected = dot_rows(full_in[...].reshape(devices * in_rows, width), normed.astype(BF16))
    projected = projected.reshape(devices, in_rows, 128)
    for j in range(devices):
        for i in range(3):
            unit = 3 * j + i
            proj_send[unit % devices, unit // devices] = projected[j, i * chans : (i + 1) * chans].astype(BF16)
    moved = Exchange(proj_send, proj_recv, send_a, recv_a, devices)
    moved.start()
    tick(6)
    moved.arrive()

    def assemble(j, carry):
        lanes = pl.ds(pl.multiple_of(j * 128, 128), 128)
        for p in range(3):
            pair = merge_halves(proj_recv[2 * j, p].astype(F32), proj_recv[2 * j + 1, p].astype(F32))
            for s in range(seqs):
                steps[p, s, :, lanes] = pair[s]
        return carry

    lax.fori_loop(0, devices // 2, assemble, 0)
    length = block * blocks
    for s in range(seqs):
        for c in range(0, chans, 8):
            spots = lax.broadcasted_iota(jnp.int32, (8, length), 1)
            parts = []
            for p in range(3):
                x = steps[p, s, c : c + 8, :]
                local_params = params[c : c + 8, :]
                value = column(local_params, 9 + p) + column(local_params, p) * x
                for i in (1, 2):
                    value += column(local_params, 3 * i + p) * jnp.where(spots < i, 0.0, pltpu.roll(x, i, 1))
                parts.append(value)
            product = parts[1] * parts[2]
            for n in range(blocks):
                at_rows = (n * seqs + s) * chans + c
                lanes = slice(n * block, (n + 1) * block)
                gated[at_rows : at_rows + 8, :] = product[:, lanes]
                for p in range(3):
                    conv[p, at_rows : at_rows + 8, :] = parts[p][:, lanes]
    tick(7)

    spec[...] = dot_plain(gated[...], table[...], EXACT)
    weight = slot_weight((chans, block))

    def output_block(m, carry):
        def add(n, acc):
            at_kernel = pl.ds(eighths((m - n) * chans), chans)
            kr, ka, ki = k_re[at_kernel, :], k_alt[at_kernel, :], k_im[at_kernel, :]
            result = []
            for s in range(seqs):
                at_signal = pl.ds(eighths((n * seqs + s) * chans), chans)
                re, im = spec[at_signal, :block], spec[at_signal, block:]
                result.append(acc[2 * s] + re * kr - im * ki)
                result.append(acc[2 * s + 1] + re * ki + im * ka)
            return tuple(result)

        acc = lax.fori_loop(0, m + 1, add, tuple(jnp.zeros((chans, block), F32) for _ in range(2 * seqs)))
        for s in range(seqs):
            at_signal = pl.ds(eighths((m * seqs + s) * chans), chans)
            sums[at_signal, :block] = acc[2 * s] * weight
            sums[at_signal, block:] = acc[2 * s + 1] * weight
        return carry

    lax.fori_loop(0, blocks, output_block, 0)
    tick(8)
    total[...] = dot_rows(sums[...], table[...], EXACT)

    def mix(m, carry):
        mixed = []
        for s in range(seqs):
            at_signal = pl.ds(eighths((m * seqs + s) * chans), chans)
            value = total[at_signal, :] + column(params[...], 12) * gated[at_signal, :]
            total[at_signal, :] = value
            mixed.append(value * conv[0, at_signal, :])
        for h in range(block // 128):
            pair = merge_halves(*(v[:, h * 128 : (h + 1) * 128] for v in mixed))
            for q in range(2):
                mix_send[m * (block // 64) + 2 * h + q] = pair[q].astype(BF16)
        return carry

    lax.fori_loop(0, blocks, mix, 0)
    back = Exchange(mix_send, mixed_in, send_b, recv_b, devices)
    back.start()
    for piece in pieces[1:]:
        piece.finish()
    back.arrive()
    for piece in pieces:
        piece.drain()
    moved.drain()
    back.drain()


def front(shards, hidden, params, feats, pos_t, mid_t, fil_t, cols, table, dims):
    line, devices, chans, seqs, block, blocks, width = dims
    order = pos_t.shape[0]
    rows = blocks * seqs * chans
    shape = jax.ShapeDtypeStruct
    vmem = pl.BlockSpec(memory_space=pltpu.VMEM)
    outs = [shape((devices,) + s.shape, BF16) for s in shards] + [
        shape((devices, chans, 128), BF16),
        shape((8, width), F32),
        shape((3, seqs, chans, block * blocks), F32),
        shape((3, rows, block), F32),
        shape((rows, 2 * block), F32),
        shape((rows, block), F32),
    ]
    outs += [shape((blocks * chans, block), F32)] * 3 + [shape((blocks, order, block), F32)] * 4
    operands = [*shards, hidden, params, feats, pos_t, mid_t, fil_t, cols, table]
    dma = pltpu.SemaphoreType.DMA
    return pl.pallas_call(
        functools.partial(front_kernel, dims),
        name="front",
        out_shape=outs,
        in_specs=[vmem] * len(operands),
        out_specs=[vmem] * len(outs),
        scratch_shapes=[
            pltpu.VMEM((devices, 3, chans, 128), BF16),
            pltpu.VMEM((devices, 3, chans, 128), BF16),
            pltpu.VMEM((devices, chans, 128), BF16),
            pltpu.VMEM((blocks * chans, block), F32),
            pltpu.VMEM((rows, block), F32),
            pltpu.VMEM((rows, 2 * block), F32),
            dma((4, 7, line * 4)),
            dma((4, 7, line * 4)),
            dma,
            dma((devices,)),
            dma((devices,)),
            dma((devices,)),
            dma((devices,)),
        ],
        compiler_params=pltpu.CompilerParams(collective_id=0, has_side_effects=True, vmem_limit_bytes=KERNEL_VMEM),
    )(*operands)


def shards(
    hidden_in,
    cotangent,
    mixer_input_weight,
    mixer_output_weight,
    feedforward_up,
    feedforward_down,
    first_gain,
    first_shift,
    second_gain,
    second_shift,
    short_taps,
    short_bias,
    skip_scale,
    filter_out,
    pos_weight,
    pos_bias,
    mid_weight,
    mid_bias,
    sine_freq,
    decay_rate,
):
    devices = lax.axis_size(AXES)
    micro, seq_count, tok, width = hidden_in.shape
    seqs = micro * seq_count
    tokens = seqs * tok
    length = tok * devices
    chans = width // devices
    block = tok * lax.axis_size("chan")
    blocks = length // block

    line = lax.axis_size("blk") // 2
    paired = devices == 32 and lax.axis_size("chan") == 4
    norms = jnp.stack([first_gain, first_shift, second_gain, second_shift])
    own = [mixer_input_weight.T, feedforward_up.T, feedforward_down, mixer_output_weight.T]
    if paired:
        norms = jnp.pad(norms, ((0, 4), (0, width - chans)))
        local = jnp.concatenate(
            [short_taps.reshape(9, chans), short_bias, skip_scale[None], decay_rate[None]]
        ).astype(F32)
        params = jnp.pad(local.T, ((0, 0), (0, 128 - 14)))
        features = feature_blocks(length, block)
        emb, order = pos_weight.shape
        pos_t = jnp.concatenate([pos_weight, pos_bias[None]]).astype(F32).T
        pos_t = jnp.pad(pos_t, ((0, 0), (0, -(emb + 1) % 8)))
        cols = jnp.pad(jnp.stack([sine_freq, mid_bias], 1).astype(F32), ((0, 0), (0, 126)))
        front_outs = front(
            [jnp.concatenate([own[0], norms]), own[3], own[1], own[2]],
            hidden_in.reshape(tokens, width),
            params,
            jnp.asarray(features),
            pos_t,
            mid_weight.astype(F32).T,
            filter_out.astype(F32).T,
            cols,
            jnp.asarray(fixed_table(block)),
            (line, devices, chans, seqs, block, blocks, width),
        )
        full = [front_outs[0][:, :-8], front_outs[2], front_outs[3], front_outs[1]]
        full = [w.reshape(-1, width) for w in full]
        norms = front_outs[5][:4]
    else:
        full = [lax.all_gather(shard, AXES, axis=0, tiled=True) for shard in own]
        norms = lax.all_gather(norms, AXES, axis=1, tiled=True)
    weight_in, weight_up, weight_down, weight_out = full
    norms = norms.astype(F32)
    gain_one, shift_one, gain_two, shift_two = norms[0], norms[1], norms[2], norms[3]

    freq = sine_freq.astype(F32)
    w_pos, w_mid, w_fil = pos_weight.astype(F32), mid_weight.astype(F32), filter_out.astype(F32)
    lags, features, first_sum, first_act, second_sum, second_act = filter_hidden(
        length, w_pos, pos_bias.astype(F32), w_mid, mid_bias.astype(F32), freq
    )
    decay = jnp.exp(-lags[None, :] * decay_rate.astype(F32)[:, None])
    kernel = contract(w_fil, second_act, 0, 0, EXACT) * decay
    table = block_table(block)
    sign = 1.0 - 2.0 * (lax.iota(jnp.int32, block) % 2).astype(F32)
    ker_re, ker_im = to_spectrum(kernel.reshape(chans, blocks, block), table)

    def with_previous(spec):
        before = jnp.concatenate([jnp.zeros_like(spec[:, :1]), spec[:, :-1]], 1)
        return spec + sign * before

    k_re, k_alt, k_im = packed_kernel(with_previous(ker_re), with_previous(ker_im))

    values = hidden_in.reshape(tokens, width).astype(F32)
    normed, normal_one, inv_one = layer_norm(values, gain_one, shift_one)
    normed = normed.astype(BF16)
    projected = contract(weight_in, normed, 1, 1).astype(BF16)
    projected = projected.reshape(3, devices, chans, tokens).transpose(1, 0, 2, 3)
    arrived = exchange(projected)

    def by_sequence(values):
        parts = values.shape[1]
        values = values.reshape(devices, parts, chans, seqs, tok)
        return values.transpose(1, 3, 2, 0, 4).reshape(parts, seqs, chans, length)

    def by_device(values):
        parts = values.shape[0]
        values = values.reshape(parts, seqs, chans, devices, tok)
        return values.transpose(3, 0, 2, 1, 4).reshape(devices, parts, chans, tokens)

    steps = by_sequence(arrived).astype(F32)
    taps = short_taps.astype(F32)[:, :, None, :, None]
    conv = short_bias.astype(F32)[:, None, :, None]
    for i in range(3):
        conv = conv + taps[i] * delayed(steps, i)
    gate_out, gate_in, signal = conv[0], conv[1], conv[2]
    gated = signal * gate_in
    sig_re, sig_im = to_spectrum(gated.reshape(seqs, chans, blocks, block), table)

    def shifted_sum(make):
        total = None
        for d in range(blocks):
            term = make(d)
            total = term if total is None else tuple(a + b for a, b in zip(total, term))
        return total

    def ahead(x, d):
        return x if d == 0 else jnp.pad(x[:, :, :-d], ((0, 0), (0, 0), (d, 0), (0, 0)))

    def back(x, d):
        return x if d == 0 else jnp.pad(x[:, :, d:], ((0, 0), (0, 0), (0, d), (0, 0)))

    def forward_term(d):
        re, im = ahead(sig_re, d), ahead(sig_im, d)
        kr, ka, ki = k_re[:, d : d + 1], k_alt[:, d : d + 1], k_im[:, d : d + 1]
        return re * kr - im * ki, re * ki + im * ka

    out_re, out_im = shifted_sum(forward_term)
    long_out = from_spectrum(out_re, out_im, table).reshape(seqs, chans, length)
    skip = skip_scale.astype(F32)[None, :, None]
    long_total = long_out + skip * gated
    mixed = (long_total * gate_out).astype(BF16)
    mixed = exchange(by_device(mixed[None])).reshape(width, tokens)

    if paired:
        def sequences(x):
            return x.reshape(blocks, seqs, chans, block).transpose(1, 2, 0, 3)

        mixed = front_outs[4].reshape(width, tokens)
        steps = front_outs[6]
        gate_out, gate_in, signal = [sequences(c).reshape(seqs, chans, length) for c in front_outs[7]]
        gated = signal * gate_in
        sig_re, sig_im = sequences(front_outs[8][:, :block]), sequences(front_outs[8][:, block:])
        long_total = sequences(front_outs[9]).reshape(seqs, chans, length)
        k_re, k_alt, k_im = [k.reshape(blocks, chans, block).transpose(1, 0, 2) for k in front_outs[10:13]]
        first_act, cos_one_, second_act, cos_two_ = [k.transpose(1, 0, 2).reshape(-1, length) for k in front_outs[13:17]]

    resid = values + contract(mixed, weight_out, 0, 1)
    second, normal_two, inv_two = layer_norm(resid, gain_two, shift_two)
    second = second.astype(BF16)
    upper = contract(second, weight_up, 1, 1)
    active, slope = gelu_parts(upper)
    active = active.astype(BF16)
    result = resid + contract(active, weight_down, 1, 0)

    cot = cotangent.reshape(tokens, width)
    grad_down = contract(active, cot, 0, 0)
    grad_upper = (contract(cot, weight_down, 1, 1) * slope).astype(BF16)
    grad_up = contract(grad_upper, second, 0, 0)
    grad_second = contract(grad_upper, weight_up, 1, 0)
    resid_term, grad_gain_two, grad_shift_two = layer_norm_back(grad_second, normal_two, inv_two, gain_two)
    grad_resid = cot.astype(F32) + resid_term
    grad_branch = grad_resid.astype(BF16)
    grad_out_w = contract(grad_branch, mixed, 0, 1)
    grad_mixed = contract(weight_out, grad_branch, 0, 1).astype(BF16)
    grad_mixed = exchange(grad_mixed.reshape(devices, 1, chans, tokens))
    grad_mixed = by_sequence(grad_mixed)[0].astype(F32)

    grad_gate_out = grad_mixed * long_total
    grad_long = grad_mixed * gate_out
    grad_skip = jnp.sum(grad_long * gated, (0, 2))
    gl_re, gl_im = to_spectrum(grad_long.reshape(seqs, chans, blocks, block), table)

    def signal_term(d):
        re, im = back(gl_re, d), back(gl_im, d)
        kr, ka, ki = k_re[:, d : d + 1], k_alt[:, d : d + 1], k_im[:, d : d + 1]
        return re * kr + im * ki, im * ka - re * ki

    gg_re, gg_im = shifted_sum(signal_term)
    grad_gated = from_spectrum(gg_re, gg_im, table).reshape(seqs, chans, length) + skip * grad_long

    first_slot = lax.iota(jnp.int32, block) == 0
    kg_re, kg_im = [], []
    for d in range(blocks):
        s_re, s_im = sig_re[:, :, : blocks - d], sig_im[:, :, : blocks - d]
        g_re, g_im = gl_re[:, :, d:], gl_im[:, :, d:]
        same, other = g_re * s_re, g_im * s_im
        kg_re.append(jnp.sum(jnp.where(first_slot, same, same + other), (0, 2)))
        kg_im.append(jnp.sum(jnp.where(first_slot, other, g_im * s_re - g_re * s_im), (0, 2)))
    kg_re, kg_im = jnp.stack(kg_re, 1), jnp.stack(kg_im, 1)

    def with_next(spec):
        after = jnp.concatenate([spec[:, 1:], jnp.zeros_like(spec[:, :1])], 1)
        return spec + sign * after

    grad_kernel = from_spectrum(with_next(kg_re), with_next(kg_im), table).reshape(chans, length)

    grad_conv = jnp.stack([grad_gate_out, grad_gated * signal, grad_gated * gate_in])
    grad_bias = jnp.sum(grad_conv, (1, 3))
    grad_taps = jnp.stack([jnp.sum(grad_conv * delayed(steps, i), (1, 3)) for i in range(3)])
    grad_steps = taps[0] * grad_conv
    for i in (1, 2):
        grad_steps = grad_steps + taps[i] * advanced(grad_conv, i)
    grad_proj = exchange(by_device(grad_steps.astype(BF16)))
    grad_proj = grad_proj.transpose(1, 0, 2, 3).reshape(3 * width, tokens)

    fade = grad_kernel * decay
    grad_filter = contract(second_act, fade, 1, 1, EXACT)
    grad_two = contract(w_fil, fade, 1, 0, EXACT) * jnp.cos(freq[:, None] * second_sum)
    grad_freq = jnp.sum(grad_two * second_sum, 1)
    grad_two = grad_two * freq[:, None]
    grad_mid = contract(first_act, grad_two, 1, 1, EXACT)
    grad_one = contract(w_mid, grad_two, 1, 0, EXACT) * jnp.cos(freq[:, None] * first_sum)
    grad_freq = grad_freq + jnp.sum(grad_one * first_sum, 1)
    grad_one = grad_one * freq[:, None]
    grad_pos = contract(features, grad_one, 1, 1, EXACT)
    small = jnp.concatenate(
        [grad_pos, jnp.sum(grad_one, 1)[None], grad_mid, jnp.sum(grad_two, 1)[None], grad_freq[None]]
    )
    emb, order = pos_weight.shape

    grad_in = contract(grad_proj, normed, 1, 0)
    grad_normed = contract(grad_proj, weight_in, 0, 0)
    input_term, grad_gain_one, grad_shift_one = layer_norm_back(grad_normed, normal_one, inv_one, gain_one)
    grad_hidden = (grad_resid + input_term).astype(BF16)

    norm_grads = jnp.stack([grad_gain_one, grad_shift_one, grad_gain_two, grad_shift_two])
    sums = [grad_in, grad_up, grad_down, grad_out_w]
    if paired:
        sums = [g.astype(BF16).reshape(devices, -1, width) for g in sums]
        norm_grads = norm_grads.reshape(4, devices, chans).transpose(1, 0, 2)
        norm_grads = jnp.pad(norm_grads, ((0, 0), (0, 0), (0, 128 - chans)))
        count = small.size
        share = -(-count // (devices * 128))
        small = jnp.pad(small.reshape(-1, 128), ((0, devices * share - count // 128), (0, 0)))
        small = jnp.pad(small.reshape(devices, share, 128), ((0, 0), (0, 4 - share), (0, 0)))
        *sums, norm_grads, small = reduce_pieces(sums + [jnp.concatenate([norm_grads, small], 1)], line)
        norm_grads = norm_grads[:4, :chans]
        small = small[:, 4 : 4 + share].reshape(-1)[:count].reshape(-1, order)
    else:
        sums = [
            lax.psum_scatter(g.astype(BF16), AXES, scatter_dimension=0, tiled=True).astype(F32) for g in sums
        ]
        norm_grads = lax.psum_scatter(norm_grads, AXES, scatter_dimension=1, tiled=True)
        small = lax.psum(small, AXES)
    return (
        result.astype(BF16).reshape(hidden_in.shape),
        grad_hidden.reshape(hidden_in.shape),
        sums[0].T,
        sums[3].T,
        sums[1].T,
        sums[2],
        norm_grads[0],
        norm_grads[1],
        norm_grads[2],
        norm_grads[3],
        grad_taps,
        grad_bias,
        grad_skip,
        grad_filter,
        small[:emb],
        small[emb],
        small[emb + 1 : emb + 1 + order],
        small[emb + 1 + order],
        small[emb + 2 + order],
    )


def solution(mesh):
    rows, spread, tokens = P(AXES), P(None, AXES), P(None, None, AXES, None)
    params = (rows, rows, rows, rows, P(None, None, AXES), spread, rows, spread, P(), P(), P(), P(), P())
    return jax.shard_map(
        shards,
        mesh=mesh,
        in_specs=(tokens, tokens, spread, spread, spread, P(AXES, None)) + params + (rows,),
        out_specs=(tokens, tokens, spread, spread, spread, P(AXES, None)) + params,
        check_vma=False,
    )
```

```python
import functools
import math

import jax
import jax.numpy as jnp
import numpy as np
from jax import lax
from jax.experimental import pallas as pl
from jax.experimental.pallas import tpu as pltpu
from jax.sharding import PartitionSpec as P

EPS = 1e-05
BANDS = 16
EXACT = lax.Precision.HIGHEST
AXES = ("blk", "chan")
F32 = jnp.float32
BF16 = jnp.bfloat16
MESH = pl.DeviceIdType.MESH
KERNEL_VMEM = 62 << 20


def contract(a, b, dim_a, dim_b, precision=None):
    return lax.dot_general(
        a, b, (((dim_a,), (dim_b,)), ((), ())), precision=precision, preferred_element_type=F32
    )


def positions(length):
    lags = jnp.arange(length).astype(F32)
    band_freq = 0.0001 + (BANDS - 1 - 0.0001) * jnp.arange(BANDS).astype(F32) / (BANDS - 1)
    phase = 2.0 * math.pi / length * lags[None, :] * band_freq[:, None]
    return lags, jnp.concatenate([lags[None, :] / (length - 1), jnp.cos(phase), -jnp.sin(phase)], 0)


def feature_blocks(length, block):
    lags = np.arange(length).astype(np.float32)
    bands = np.arange(BANDS).astype(np.float32)
    band_freq = np.float32(0.0001) + np.float32(BANDS - 1 - 0.0001) * bands / np.float32(BANDS - 1)
    phase = np.float32(2.0 * math.pi / length) * lags[None, :] * band_freq[:, None]
    ramp = lags[None, :] / np.float32(length - 1)
    rows = np.concatenate([ramp, np.cos(phase), -np.sin(phase), np.ones_like(ramp)])
    rows = np.pad(rows, ((0, -len(rows) % 8), (0, 0))).astype(np.float32)
    return np.ascontiguousarray(rows.reshape(len(rows), -1, block).transpose(1, 0, 2))


def fixed_table(block):
    spot, freq = np.arange(block)[:, None], np.arange(block)[None, :]
    phase = (np.pi / block) * (spot * freq % (2 * block))
    imag = np.where(freq == 0, 1.0 - 2.0 * (spot % 2), -np.sin(phase))
    return np.concatenate([np.cos(phase), imag], 1).astype(np.float32)


def filter_hidden(length, pos_weight, pos_bias, mid_weight, mid_bias, sine_freq):
    lags, features = positions(length)
    freq = sine_freq[:, None]
    first_sum = contract(pos_weight, features, 0, 0, EXACT) + pos_bias[:, None]
    first = jnp.sin(freq * first_sum)
    second_sum = contract(mid_weight, first, 0, 0, EXACT) + mid_bias[:, None]
    second = jnp.sin(freq * second_sum)
    return lags, features, first_sum, first, second_sum, second


def block_table(block):
    spot = lax.broadcasted_iota(jnp.int32, (block, block), 0)
    freq = lax.broadcasted_iota(jnp.int32, (block, block), 1)
    phase = (math.pi / block) * (spot * freq % (2 * block)).astype(F32)
    parity = 1.0 - 2.0 * (spot % 2).astype(F32)
    imag = jnp.where(freq == 0, parity, -jnp.sin(phase))
    return jnp.concatenate([jnp.cos(phase), imag], 1)


def to_spectrum(blocks, table):
    spec = lax.dot_general(
        blocks, table, (((blocks.ndim - 1,), (0,)), ((), ())), precision=EXACT, preferred_element_type=F32
    )
    half = table.shape[0]
    return spec[..., :half], spec[..., half:]


def from_spectrum(real, imag, table):
    half = table.shape[0]
    weight = jnp.where(lax.iota(jnp.int32, half) == 0, 0.5 / half, 1.0 / half)
    spec = jnp.concatenate([real * weight, imag * weight], -1)
    return lax.dot_general(
        spec, table, (((spec.ndim - 1,), (1,)), ((), ())), precision=EXACT, preferred_element_type=F32
    )


def packed_kernel(real, imag):
    first = lax.iota(jnp.int32, real.shape[-1]) == 0
    return real, jnp.where(first, imag, real), jnp.where(first, 0.0, imag)


def layer_norm(values, gain, shift):
    center = values - jnp.mean(values, -1, keepdims=True)
    scale_inv = lax.rsqrt(jnp.mean(center * center, -1, keepdims=True) + EPS)
    normal = center * scale_inv
    return normal * gain + shift, normal, scale_inv


def layer_norm_back(grad_out, normal, scale_inv, gain):
    grad_normal = grad_out * gain
    inner = grad_normal - jnp.mean(grad_normal, -1, keepdims=True)
    inner = inner - normal * jnp.mean(grad_normal * normal, -1, keepdims=True)
    return inner * scale_inv, jnp.sum(grad_out * normal, 0), jnp.sum(grad_out, 0)


def gelu_parts(v):
    root = math.sqrt(2.0 / math.pi)
    inner = root * (v + 0.044715 * v * v * v)
    t = jnp.tanh(inner)
    value = 0.5 * v * (1.0 + t)
    slope = 0.5 * (1.0 + t) + 0.5 * v * (1.0 - t * t) * root * (1.0 + 3.0 * 0.044715 * v * v)
    return value, slope


def delayed(values, steps):
    if steps == 0:
        return values
    pad = jnp.zeros(values.shape[:-1] + (steps,), values.dtype)
    return jnp.concatenate([pad, values[..., :-steps]], -1)


def advanced(values, steps):
    if steps == 0:
        return values
    pad = jnp.zeros(values.shape[:-1] + (steps,), values.dtype)
    return jnp.concatenate([values[..., steps:], pad], -1)


def exchange(values):
    return lax.all_to_all(values, AXES, split_axis=0, concat_axis=0, tiled=True)


def spot():
    b, c = lax.axis_index("blk"), lax.axis_index("chan")
    return b // 2, b % 2, c // 2, c % 2


def at(z, y, x, k):
    return {"blk": z * 2 + y, "chan": x * 2 + k}


def flat(z, y, x, k):
    return ((z * 2 + y) * 2 + x) * 2 + k


def when(condition, act):
    pl.when(condition)(act)


def send(src, dst, send_sem, recv_sem, place):
    return pltpu.make_async_remote_copy(
        src_ref=src, dst_ref=dst, send_sem=send_sem, recv_sem=recv_sem, device_id=at(*place), device_id_type=MESH
    )


def greet_all(count):
    b, c = lax.axis_index("blk"), lax.axis_index("chan")
    chan = lax.axis_size("chan")
    me = b * chan + c
    barrier = pltpu.get_barrier_semaphore()

    def one(i, carry):
        other = lax.rem(me + i, count)
        pl.semaphore_signal(
            barrier, inc=1, device_id={"blk": other // chan, "chan": other % chan}, device_id_type=MESH
        )
        return carry

    lax.fori_loop(1, count, one, 0)
    pl.semaphore_wait(barrier, count - 1)


def greet_near(line):
    z, y, x, k = spot()
    barrier = pltpu.get_barrier_semaphore()

    def hello(*place):
        pl.semaphore_signal(barrier, inc=1, device_id=at(*place), device_id_type=MESH)

    hello(z, 1 - y, x, k)
    hello(z, y, 1 - x, k)
    hello(z, y, x, 1 - k)
    when(z > 0, lambda: hello(z - 1, y, x, k))
    when(z < line - 1, lambda: hello(z + 1, y, x, k))
    pl.semaphore_wait(barrier, 3 + jnp.minimum(z, 1) + jnp.minimum(line - 1 - z, 1))


def low_rows(rows):
    return max(rows // 16 * 8, 8) if rows > 8 else rows


class Gather:
    def __init__(self, line, shard, full, sends, recvs, local):
        self.line, self.shard, self.full, self.s, self.r, self.local = line, shard, full, sends, recvs, local
        self.rows = shard.shape[0]
        self.low = low_rows(self.rows)
        self.z, self.y, self.x, self.k = spot()

    def copy(self, kind, index, shard, place, rows=None):
        ref = self.full.at[shard] if rows is None else self.full.at[shard, pl.ds(*rows)]
        return send(ref, ref, self.s.at[kind, index], self.r.at[kind, index], place)

    def up(self, zo):
        return self.copy(0, zo, flat(zo, self.y, self.x, self.k), (self.z + 1, self.y, self.x, self.k))

    def down(self, zo):
        return self.copy(1, zo, flat(zo, self.y, self.x, self.k), (self.z - 1, self.y, self.x, self.k))

    def to_x(self, zo):
        return self.copy(2, zo, flat(zo, self.y, self.x, self.k), (self.z, self.y, 1 - self.x, self.k))

    def to_y(self, zo):
        return self.copy(3, zo, flat(zo, self.y, self.x, self.k), (self.z, 1 - self.y, self.x, self.k))

    def low_y(self, zo, other_y=False):
        shard = flat(zo, 1 - self.y if other_y else self.y, 1 - self.x, self.k)
        return self.copy(4, zo, shard, (self.z, 1 - self.y, self.x, self.k), (0, self.low))

    def high_x(self, zo, other_x=False):
        shard = flat(zo, 1 - self.y, 1 - self.x if other_x else self.x, self.k)
        return self.copy(5, zo, shard, (self.z, self.y, 1 - self.x, self.k), (self.low, self.rows - self.low))

    def core(self, zo, yo, xo, k):
        return self.copy(6, (zo * 2 + yo) * 2 + xo, flat(zo, yo, xo, k), (self.z, self.y, self.x, 1 - self.k))

    def line_has(self, zo):
        self.to_x(zo).start()
        self.to_y(zo).start()
        self.core(zo, self.y, self.x, self.k).start()

    def begin(self):
        own = self.full.at[flat(self.z, self.y, self.x, self.k)]
        copy = pltpu.make_async_copy(self.shard, own, self.local)
        copy.start()
        copy.wait()
        when(self.z < self.line - 1, lambda: self.up(self.z).start())
        when(self.z > 0, lambda: self.down(self.z).start())
        self.line_has(self.z)

    def each(self, distance, act):
        if distance == 0:
            act(self.z)
        else:
            when(self.z - distance >= 0, lambda: act(self.z - distance))
            when(self.z + distance < self.line, lambda: act(self.z + distance))

    def along(self, distance):
        def from_below():
            zo = self.z - distance
            self.up(zo).wait_recv()
            when(self.z < self.line - 1, lambda: self.up(zo).start())
            self.line_has(zo)

        def from_above():
            zo = self.z + distance
            self.down(zo).wait_recv()
            when(self.z > 0, lambda: self.down(zo).start())
            self.line_has(zo)

        when(self.z - distance >= 0, from_below)
        when(self.z + distance < self.line, from_above)

    def plane(self, distance):
        def act(zo):
            self.to_x(zo).wait_recv()
            self.low_y(zo).start()
            self.core(zo, self.y, 1 - self.x, self.k).start()
            self.to_y(zo).wait_recv()
            if self.low < self.rows:
                self.high_x(zo).start()
            self.core(zo, 1 - self.y, self.x, self.k).start()

        self.each(distance, act)

    def corner(self, distance):
        def act(zo):
            self.low_y(zo, True).wait_recv()
            if self.low < self.rows:
                self.high_x(zo, True).wait_recv()
            self.core(zo, 1 - self.y, 1 - self.x, self.k).start()

        self.each(distance, act)

    def finish(self):
        for zo in range(self.line):
            for yo in range(2):
                for xo in range(2):
                    self.core(zo, yo, xo, 1 - self.k).wait_recv()

    def drain(self):
        for zo in range(self.line):
            when(jnp.logical_and(self.z < self.line - 1, zo <= self.z), lambda: self.up(zo).wait_send())
            when(jnp.logical_and(self.z > 0, zo >= self.z), lambda: self.down(zo).wait_send())
            self.to_x(zo).wait_send()
            self.to_y(zo).wait_send()
            self.low_y(zo).wait_send()
            if self.low < self.rows:
                self.high_x(zo).wait_send()
            for yo in range(2):
                for xo in range(2):
                    self.core(zo, yo, xo, self.k).wait_send()


class Reduce:
    def __init__(self, line, part, out, chip, low_y, high_x, by_x, by_y, by_z, sends, recvs):
        self.line, self.part, self.out, self.chip = line, part, out, chip
        self.low_buf, self.high_buf, self.x_buf, self.y_buf, self.z_buf = low_y, high_x, by_x, by_y, by_z
        self.s, self.r = sends, recvs
        self.rows = part.shape[1]
        self.low = low_rows(self.rows)
        self.z, self.y, self.x, self.k = spot()

    def index(self, zo, yo, xo):
        return (zo * 2 + yo) * 2 + xo

    def copy(self, kind, index, src, dst, place):
        return send(src, dst, self.s.at[kind, index], self.r.at[kind, index], place)

    def core(self, zo, yo, xo):
        i = self.index(zo, yo, xo)
        src = self.part.at[flat(zo, yo, xo, 1 - self.k)]
        return self.copy(6, i, src, self.chip.at[i], (self.z, self.y, self.x, 1 - self.k))

    def low_y(self, zo):
        i = self.index(zo, 1 - self.y, 1 - self.x)
        src = self.chip.at[i, pl.ds(0, self.low)]
        return self.copy(4, zo, src, self.low_buf.at[zo], (self.z, 1 - self.y, self.x, self.k))

    def high_x(self, zo):
        i = self.index(zo, 1 - self.y, 1 - self.x)
        src = self.chip.at[i, pl.ds(self.low, self.rows - self.low)]
        return self.copy(5, zo, src, self.high_buf.at[zo], (self.z, self.y, 1 - self.x, self.k))

    def to_x(self, zo):
        src = self.chip.at[self.index(zo, self.y, 1 - self.x)]
        return self.copy(2, zo, src, self.x_buf.at[zo], (self.z, self.y, 1 - self.x, self.k))

    def to_y(self, zo):
        src = self.chip.at[self.index(zo, 1 - self.y, self.x)]
        return self.copy(3, zo, src, self.y_buf.at[zo], (self.z, 1 - self.y, self.x, self.k))

    def up(self, zo):
        src = self.chip.at[self.index(zo, self.y, self.x)]
        return self.copy(0, zo, src, self.z_buf.at[zo + 1], (self.z + 1, self.y, self.x, self.k))

    def down(self, zo):
        src = self.chip.at[self.index(zo, self.y, self.x)]
        return self.copy(1, zo, src, self.z_buf.at[zo], (self.z - 1, self.y, self.x, self.k))

    def add(self, i, other, rows=None):
        if rows is None:
            self.chip[i] = self.chip[i] + other
        else:
            self.chip[i, pl.ds(*rows)] = self.chip[i, pl.ds(*rows)] + other

    def each(self, distance, act):
        if distance == 0:
            act(self.z)
        else:
            when(self.z - distance >= 0, lambda: act(self.z - distance))
            when(self.z + distance < self.line, lambda: act(self.z + distance))

    def begin_at(self, zo):
        for yo, xo in ((1 - self.y, 1 - self.x), (self.y, 1 - self.x), (1 - self.y, self.x), (self.y, self.x)):
            self.core(zo, yo, xo).start()

    def begin(self, distance):
        self.each(distance, self.begin_at)

    def corner(self, distance):
        def act(zo):
            for yo, xo in ((1 - self.y, 1 - self.x), (self.y, 1 - self.x), (1 - self.y, self.x), (self.y, self.x)):
                self.core(zo, yo, xo).wait_recv()
                self.add(self.index(zo, yo, xo), self.part[flat(zo, yo, xo, self.k)])
                if yo is not self.y and xo is not self.x:
                    self.low_y(zo).start()
                    if self.low < self.rows:
                        self.high_x(zo).start()

        self.each(distance, act)

    def plane(self, distance):
        def act(zo):
            self.low_y(zo).wait_recv()
            self.add(self.index(zo, self.y, 1 - self.x), self.low_buf[zo], (0, self.low))
            self.to_x(zo).start()
            if self.low < self.rows:
                self.high_x(zo).wait_recv()
                self.add(
                    self.index(zo, 1 - self.y, self.x), self.high_buf[zo], (self.low, self.rows - self.low)
                )
            self.to_y(zo).start()

        self.each(distance, act)

    def along(self, distance):
        own = self.index

        def joined(zo):
            self.to_x(zo).wait_recv()
            self.to_y(zo).wait_recv()
            i = own(zo, self.y, self.x)
            total = self.x_buf[zo].astype(F32) + self.y_buf[zo].astype(F32) + self.chip[i].astype(F32)
            return i, total

        def from_below(zo):
            self.up(zo).wait_recv()
            i = own(zo, self.y, self.x)
            self.add(i, self.z_buf[zo + 1])

        def from_above(zo):
            self.down(zo).wait_recv()
            i = own(zo, self.y, self.x)
            self.add(i, self.z_buf[zo])

        def rising():
            zo = self.z + distance
            i, total = joined(zo)
            self.chip[i] = total.astype(self.chip.dtype)
            when(self.z > 0, lambda: from_below(zo))
            self.up(zo).start()

        def falling():
            zo = self.z - distance
            i, total = joined(zo)
            self.chip[i] = total.astype(self.chip.dtype)
            when(self.z < self.line - 1, lambda: from_above(zo))
            self.down(zo).start()

        if distance:
            when(self.z + distance < self.line, rising)
            when(self.z - distance >= 0, falling)
        else:
            _, total = joined(self.z)
            self.out[...] = total

            def below():
                self.up(self.z).wait_recv()
                self.out[...] += self.z_buf[self.z + 1].astype(F32)

            def above():
                self.down(self.z).wait_recv()
                self.out[...] += self.z_buf[self.z].astype(F32)

            when(self.z > 0, below)
            when(self.z < self.line - 1, above)

    def drain(self):
        for zo in range(self.line):
            when(zo > self.z, lambda: self.up(zo).wait_send())
            when(zo < self.z, lambda: self.down(zo).wait_send())
            self.to_x(zo).wait_send()
            self.to_y(zo).wait_send()
            self.low_y(zo).wait_send()
            if self.low < self.rows:
                self.high_x(zo).wait_send()
            for yo in range(2):
                for xo in range(2):
                    self.core(zo, yo, xo).wait_send()


BUFFERS = 6


def reduce_scratch(line, part):
    _, rows, width = part.shape
    low = low_rows(rows)
    high = max(rows - low, 8)
    sizes = [(line * 4, rows), (line, low), (line, high), (line, rows), (line, rows), (line + 1, rows)]
    return [pltpu.VMEM(s + (width,), part.dtype) for s in sizes]


def dot_rows(a, b, precision=None):
    return lax.dot_general(a, b, (((1,), (1,)), ((), ())), precision=precision, preferred_element_type=F32)


def dot_plain(a, b, precision=None):
    return lax.dot_general(a, b, (((1,), (0,)), ((), ())), precision=precision, preferred_element_type=F32)


def eighths(value):
    return pl.multiple_of(value, 8)


class Exchange:
    def __init__(self, src, dst, sends, recvs, devices):
        self.src, self.dst, self.s, self.r, self.devices = src, dst, sends, recvs, devices
        self.me = flat(*spot())

    def copy(self, i):
        other = lax.rem(self.me + i, self.devices)
        place = (other // 8, other // 4 % 2, other // 2 % 2, other % 2)
        return send(self.src.at[other], self.dst.at[self.me], self.s.at[i], self.r.at[i], place)

    def start(self):
        lax.fori_loop(1, self.devices, lambda i, c: (self.copy(i).start(), c)[1], 0)
        self.dst[self.me] = self.src[self.me]

    def arrive(self):
        lax.fori_loop(1, self.devices, lambda i, c: (self.copy(i).wait_recv(), c)[1], 0)

    def drain(self):
        lax.fori_loop(1, self.devices, lambda i, c: (self.copy(i).wait_send(), c)[1], 0)


def low_lanes(shape):
    return lax.broadcasted_iota(jnp.int32, shape, 1) < 64


def merge_halves(first, second):
    low = low_lanes(first.shape)
    return (
        jnp.where(low, first, pltpu.roll(second, 64, 1)),
        jnp.where(low, pltpu.roll(first, 64, 1), second),
    )


def lane_norm(values, gain, shift):
    center = values - jnp.mean(values, 1, keepdims=True)
    scale_inv = lax.rsqrt(jnp.mean(center * center, 1, keepdims=True) + EPS)
    normal = center * scale_inv
    return normal * gain + shift, normal, scale_inv


def slot_zero(shape):
    return lax.broadcasted_iota(jnp.int32, shape, 1) == 0


def slot_sign(shape):
    return 1.0 - 2.0 * (lax.broadcasted_iota(jnp.int32, shape, 1) % 2).astype(F32)


def slot_weight(shape):
    return jnp.where(slot_zero(shape), 0.5 / shape[1], 1.0 / shape[1])


def column(params, index):
    return params[:, index : index + 1]


def norm_rows(stack, count, chans, width):
    total = None
    for j in range(count):
        tile = stack(j).astype(F32)[:, :128]
        tile = jnp.where(lax.broadcasted_iota(jnp.int32, tile.shape, 1) < chans, tile, 0.0)
        wide = jnp.concatenate([tile, jnp.zeros((tile.shape[0], width - 128), F32)], 1)
        wide = pltpu.roll(wide, j * chans, 1) if j else wide
        total = wide if total is None else total + wide
    return total


RAW = 14


def prepare(in_t, raw, own_in, desk, params, pos_t, mid_t, fil_t, cols):
    gain_one, shift_one, gain_two, shift_two, taps, bias, skip, decay, fil, pos, pos_bias, mid, rate, mid_bias = raw
    chans, order, emb = fil.shape[0], mid.shape[0], pos.shape[0]

    def put(row, values, wide):
        desk[row : row + values.shape[0], :wide] = values.astype(F32)

    desk[...] = jnp.zeros_like(desk)
    for i, ref in enumerate((gain_one, shift_one, gain_two, shift_two)):
        put(i, ref[...], chans)
    norms = jnp.concatenate([desk[:8, :], jnp.zeros((8, in_t.shape[1] - 128), F32)], 1)
    own_in[...] = jnp.concatenate([in_t[...].astype(F32), norms], 0).astype(BF16)
    for i in range(3):
        put(3 * i, taps[i], chans)
    put(9, bias[...], chans)
    put(12, skip[...], chans)
    put(13, decay[...], chans)
    params[...] = desk[...].T[:chans]
    desk[...] = jnp.zeros_like(desk)
    put(0, pos[...], order)
    put(emb, pos_bias[...], order)
    pos_t[...] = desk[...].T[:order, : pos_t.shape[1]]
    desk[...] = jnp.zeros_like(desk)
    put(0, mid[...], order)
    mid_t[...] = desk[...].T[:order, :order]
    desk[...] = jnp.zeros_like(desk)
    put(0, rate[...], order)
    put(1, mid_bias[...], order)
    cols[...] = desk[...].T[:order]
    fil_t[...] = fil[...].astype(F32)


def front_kernel(dims, *refs):
    line, devices, chans, seqs, block, blocks, width = dims
    (in_t, own_out, own_up, own_down, hidden, feats, table) = refs[:7]
    raw = refs[7 : 7 + RAW]
    refs = refs[7 + RAW :]
    (full_in, full_out, full_up, full_down, mixed_in, norms_out, steps, conv, spec, total, k_re, k_alt, k_im) = refs[:13]
    (one, cos_one, two, cos_two, params, pos_t, mid_t, fil_t, cols) = refs[13:22]
    (own_in, desk, proj_send, proj_recv, mix_send, kernel_buf, gated, sums) = refs[22:30]
    (sends, recvs, local, send_a, recv_a, send_b, recv_b) = refs[30:]
    prepare(in_t, raw, own_in, desk, params, pos_t, mid_t, fil_t, cols)
    greet_all(devices)
    pieces = [
        Gather(line, shard, full, sends.at[p], recvs.at[p], local)
        for p, (shard, full) in enumerate(
            ((own_in, full_in), (own_out, full_out), (own_up, full_up), (own_down, full_down))
        )
    ]
    late = (0, 1, 2, 3)

    def tick(now):
        for piece, offset in zip(pieces, late):
            step = now - offset
            if step == 0:
                piece.begin()
            if 1 <= step < line:
                piece.along(step)
            if 1 <= step <= line:
                piece.plane(step - 1)
            if 2 <= step <= line + 1:
                piece.corner(step - 2)

    def filter_part(n, carry):
        sum_one = dot_plain(pos_t[...], feats[n], EXACT)
        phase = column(cols[...], 0) * sum_one
        act_one = jnp.sin(phase)
        one[n] = act_one
        cos_one[n] = jnp.cos(phase)
        phase = column(cols[...], 0) * (dot_plain(mid_t[...], act_one, EXACT) + column(cols[...], 1))
        act_two = jnp.sin(phase)
        two[n] = act_two
        cos_two[n] = jnp.cos(phase)
        lag = lax.broadcasted_iota(jnp.int32, (chans, block), 1) + n * block
        fade = jnp.exp(-lag.astype(F32) * column(params[...], 13))
        kernel_buf[pl.ds(eighths(n * chans), chans), :] = dot_plain(fil_t[...], act_two, EXACT) * fade
        return carry

    def filters(first, last):
        lax.fori_loop(first, last, filter_part, 0)

    def kernel_spectrum():
        ker = dot_plain(kernel_buf[...], table[...], EXACT)
        before = jnp.concatenate([jnp.zeros((chans, 2 * block), F32), ker[:-chans]], 0)
        sign = slot_sign((chans * blocks, block))
        real = ker[:, :block] + sign * before[:, :block]
        imag = ker[:, block:] + sign * before[:, block:]
        zero = slot_zero(real.shape)
        k_re[...] = real
        k_alt[...] = jnp.where(zero, imag, real)
        k_im[...] = jnp.where(zero, 0.0, imag)

    tick(0)
    filters(0, blocks // 4)
    tick(1)
    filters(blocks // 4, blocks // 2)
    tick(2)
    filters(blocks // 2, 3 * blocks // 4)
    tick(3)
    filters(3 * blocks // 4, blocks)
    tick(4)
    kernel_spectrum()
    tick(5)
    pieces[0].finish()

    in_rows = full_in.shape[1]
    norms = norm_rows(lambda j: full_in[j, in_rows - 8 :], devices, chans, width)
    norms_out[...] = norms
    normed, _, _ = lane_norm(hidden[...].astype(F32), norms[0:1], norms[1:2])
    projected = dot_rows(full_in[...].reshape(devices * in_rows, width), normed.astype(BF16))
    projected = projected.reshape(devices, in_rows, 128)
    for j in range(devices):
        for i in range(3):
            unit = 3 * j + i
            proj_send[unit % devices, unit // devices] = projected[j, i * chans : (i + 1) * chans].astype(BF16)
    moved = Exchange(proj_send, proj_recv, send_a, recv_a, devices)
    moved.start()
    tick(6)
    moved.arrive()

    def assemble(j, carry):
        lanes = pl.ds(pl.multiple_of(j * 128, 128), 128)
        for p in range(3):
            pair = merge_halves(proj_recv[2 * j, p].astype(F32), proj_recv[2 * j + 1, p].astype(F32))
            for s in range(seqs):
                steps[p, s, :, lanes] = pair[s]
        return carry

    lax.fori_loop(0, devices // 2, assemble, 0)
    length = block * blocks
    for s in range(seqs):
        for c in range(0, chans, 8):
            spots = lax.broadcasted_iota(jnp.int32, (8, length), 1)
            parts = []
            for p in range(3):
                x = steps[p, s, c : c + 8, :]
                local_params = params[c : c + 8, :]
                value = column(local_params, 9 + p) + column(local_params, p) * x
                for i in (1, 2):
                    value += column(local_params, 3 * i + p) * jnp.where(spots < i, 0.0, pltpu.roll(x, i, 1))
                parts.append(value)
            product = parts[1] * parts[2]
            for n in range(blocks):
                at_rows = (n * seqs + s) * chans + c
                lanes = slice(n * block, (n + 1) * block)
                gated[at_rows : at_rows + 8, :] = product[:, lanes]
                for p in range(3):
                    conv[p, at_rows : at_rows + 8, :] = parts[p][:, lanes]
    tick(7)

    spec[...] = dot_plain(gated[...], table[...], EXACT)
    weight = slot_weight((chans, block))

    def output_block(m, carry):
        def add(n, acc):
            at_kernel = pl.ds(eighths((m - n) * chans), chans)
            kr, ka, ki = k_re[at_kernel, :], k_alt[at_kernel, :], k_im[at_kernel, :]
            result = []
            for s in range(seqs):
                at_signal = pl.ds(eighths((n * seqs + s) * chans), chans)
                re, im = spec[at_signal, :block], spec[at_signal, block:]
                result.append(acc[2 * s] + re * kr - im * ki)
                result.append(acc[2 * s + 1] + re * ki + im * ka)
            return tuple(result)

        acc = lax.fori_loop(0, m + 1, add, tuple(jnp.zeros((chans, block), F32) for _ in range(2 * seqs)))
        for s in range(seqs):
            at_signal = pl.ds(eighths((m * seqs + s) * chans), chans)
            sums[at_signal, :block] = acc[2 * s] * weight
            sums[at_signal, block:] = acc[2 * s + 1] * weight
        return carry

    lax.fori_loop(0, blocks, output_block, 0)
    tick(8)
    total[...] = dot_rows(sums[...], table[...], EXACT)

    def mix(m, carry):
        mixed = []
        for s in range(seqs):
            at_signal = pl.ds(eighths((m * seqs + s) * chans), chans)
            value = total[at_signal, :] + column(params[...], 12) * gated[at_signal, :]
            total[at_signal, :] = value
            mixed.append(value * conv[0, at_signal, :])
        for h in range(block // 128):
            pair = merge_halves(*(v[:, h * 128 : (h + 1) * 128] for v in mixed))
            for q in range(2):
                mix_send[m * (block // 64) + 2 * h + q] = pair[q].astype(BF16)
        return carry

    lax.fori_loop(0, blocks, mix, 0)
    back = Exchange(mix_send, mixed_in, send_b, recv_b, devices)
    back.start()
    for piece in pieces[1:]:
        piece.finish()
    back.arrive()
    for piece in pieces:
        piece.drain()
    moved.drain()
    back.drain()


def front(shards, hidden, feats, table, raw, dims):
    line, devices, chans, seqs, block, blocks, width = dims
    order = raw[-1].shape[1]
    rows = blocks * seqs * chans
    shape = jax.ShapeDtypeStruct
    vmem = pl.BlockSpec(memory_space=pltpu.VMEM)
    in_rows = shards[0].shape[0] + 8
    outs = [shape((devices, s.shape[0] + extra, width), BF16) for s, extra in zip(shards, (8, 0, 0, 0))] + [
        shape((devices, chans, 128), BF16),
        shape((8, width), F32),
        shape((3, seqs, chans, block * blocks), F32),
        shape((3, rows, block), F32),
        shape((rows, 2 * block), F32),
        shape((rows, block), F32),
    ]
    outs += [shape((blocks * chans, block), F32)] * 3 + [shape((blocks, order, block), F32)] * 4
    outs += [shape((chans, 128), F32), shape((order, feats.shape[1]), F32), shape((order, order), F32)]
    outs += [shape((chans, order), F32), shape((order, 128), F32)]
    operands = [*shards, hidden, feats, table, *raw]
    dma = pltpu.SemaphoreType.DMA
    return pl.pallas_call(
        functools.partial(front_kernel, dims),
        name="front",
        out_shape=outs,
        in_specs=[vmem] * len(operands),
        out_specs=[vmem] * len(outs),
        scratch_shapes=[
            pltpu.VMEM((in_rows, width), BF16),
            pltpu.VMEM((128, 128), F32),
            pltpu.VMEM((devices, 3, chans, 128), BF16),
            pltpu.VMEM((devices, 3, chans, 128), BF16),
            pltpu.VMEM((devices, chans, 128), BF16),
            pltpu.VMEM((blocks * chans, block), F32),
            pltpu.VMEM((rows, block), F32),
            pltpu.VMEM((rows, 2 * block), F32),
            dma((4, 7, line * 4)),
            dma((4, 7, line * 4)),
            dma,
            dma((devices,)),
            dma((devices,)),
            dma((devices,)),
            dma((devices,)),
        ],
        compiler_params=pltpu.CompilerParams(collective_id=0, has_side_effects=True, vmem_limit_bytes=KERNEL_VMEM),
    )(*operands)


def lane_norm_back(grad_out, normal, scale_inv, gain):
    grad_normal = grad_out * gain
    inner = grad_normal - jnp.mean(grad_normal, 1, keepdims=True)
    inner = inner - normal * jnp.mean(grad_normal * normal, 1, keepdims=True)
    return inner * scale_inv, jnp.sum(grad_out * normal, 0, keepdims=True), jnp.sum(grad_out, 0, keepdims=True)


def back_kernel(dims, *refs):
    line, devices, chans, seqs, block, blocks, width = dims
    (full_in, full_out, full_up, full_down) = refs[:4]
    (hidden, cot, mixed_in, norms, steps, conv, spec, total, k_re, k_alt, k_im) = refs[4:15]
    (one, cos_one, two, cos_two, params, feats, pos_t, mid_t, fil_t, rows_in, table) = refs[15:26]
    (result, grad_hidden, sum_up, sum_down, sum_out, sum_in, sum_tile, everyone, chan_grads, filter_grad) = refs[26:36]
    (w_in, w_out, w_up, w_down, w_flat, load_sem) = refs[36:42]
    (g_up, g_down, g_out, g_in, g_tile) = refs[42:47]
    (resid, value_sum, second_sum, mix_send, mix_recv, g_long, g_spec, g_sums, g_conv, k_sums) = refs[47:57]
    (proj_send, proj_recv, g_proj, small) = refs[57:61]
    (sends, recvs, share_send, share_recv, local, send_a, recv_a, send_b, recv_b) = refs[61:70]
    buffers = refs[70:]
    shards = full_up.shape[0] // line
    hidden_rows = full_up.shape[1]
    chunk = shards * hidden_rows
    in_rows = full_in.shape[1]

    load_in = pltpu.make_async_copy(full_in, w_in, load_sem.at[0])
    load_out = pltpu.make_async_copy(full_out, w_out, load_sem.at[1])

    def visit(i):
        z = lax.axis_index("blk") // 2
        return lax.rem(z + line // 2 + i, line)

    def load(i):
        slot = i % 2
        source = pl.ds(visit(i) * shards, shards)
        return (
            pltpu.make_async_copy(full_up.at[source], w_up.at[slot], load_sem.at[2 + slot]),
            pltpu.make_async_copy(full_down.at[source], w_down.at[slot], load_sem.at[4 + slot]),
        )

    load_out.start()
    for copy in load(0):
        copy.start()
    load_in.start()
    greet_all(devices)
    parts = (g_up, g_down, g_out, g_in, g_tile)
    outs = (sum_up, sum_down, sum_out, sum_in, sum_tile)
    pieces = [
        Reduce(line, parts[p], outs[p], *buffers[p * BUFFERS : (p + 1) * BUFFERS], sends.at[p], recvs.at[p])
        for p in range(5)
    ]

    def tick(group, step):
        for piece in group:
            if step < line:
                piece.corner(line - 1 - step)
            if 1 <= step <= line:
                piece.plane(line - step)
            if 2 <= step <= line + 1:
                piece.along(line + 1 - step)

    gain_two, shift_two = norms[2:3], norms[3:4]
    mixed = mixed_in[...].astype(F32).reshape(width, 128).T.astype(BF16)
    load_out.wait()
    w_flat[...] = w_out[...].astype(F32).reshape(width, width).astype(BF16)
    resid[...] = hidden[...].astype(F32) + dot_rows(mixed, w_flat[...])
    second, normal_two, inv_two = lane_norm(resid[...], gain_two, shift_two)
    second = second.astype(BF16)
    value_sum[...] = jnp.zeros_like(value_sum)
    second_sum[...] = jnp.zeros_like(second_sum)

    for i in range(line):
        slot = i % 2
        if i + 1 < line:
            for copy in load(i + 1):
                copy.start()
        for copy in load(i):
            copy.wait()
        up = w_up[slot].reshape(chunk, width)
        down = w_down[slot].reshape(chunk, width)
        active, slope = gelu_parts(dot_rows(up, second))
        active = active.astype(BF16)
        grad_upper = (dot_rows(down, cot[...]) * slope).astype(BF16)
        where_to = pl.ds(visit(i) * shards, shards)
        g_down[where_to] = dot_plain(active, cot[...]).astype(BF16).reshape(shards, hidden_rows, width)
        g_up[where_to] = dot_plain(grad_upper, second).astype(BF16).reshape(shards, hidden_rows, width)
        pieces[0].begin_at(visit(i))
        pieces[1].begin_at(visit(i))
        value_sum[...] += dot_plain(active.astype(F32).T.astype(BF16), down)
        second_sum[...] += dot_plain(grad_upper.astype(F32).T.astype(BF16), up)
    result[...] = (resid[...] + value_sum[...]).astype(BF16)
    resid_term, grad_gain_two, grad_shift_two = lane_norm_back(second_sum[...], normal_two, inv_two, gain_two)
    resid[...] = cot[...].astype(F32) + resid_term
    grad_mixed = dot_plain(resid[...].astype(BF16), w_flat[...])
    mix_send[...] = grad_mixed.T.reshape(devices, chans, 128).astype(BF16)
    moved = Exchange(mix_send, mix_recv, send_a, recv_a, devices)
    moved.start()
    grad_branch = resid[...].T.astype(BF16)
    g_out[...] = dot_plain(grad_branch, mixed).reshape(devices, chans, width).astype(BF16)
    for distance in range(line - 1, -1, -1):
        pieces[2].begin(distance)
    first_group = pieces[:3]
    tick(first_group, 0)
    moved.arrive()

    weight = slot_weight((chans, block))
    skip = column(params[...], 12)
    per_block = block // 64

    def arrange(m, carry):
        for h in range(block // 128):
            source = m * per_block + 2 * h
            pair = merge_halves(mix_recv[source].astype(F32), mix_recv[source + 1].astype(F32))
            lanes = slice(h * 128, (h + 1) * 128)
            for s in range(seqs):
                at_rows = pl.ds(eighths((m * seqs + s) * chans), chans)
                place = pl.ds(pl.multiple_of(m * block + h * 128, 128), 128)
                g_conv[0, s, :, place] = pair[s] * total[at_rows, lanes]
                grad = pair[s] * conv[0, at_rows, lanes]
                g_long[at_rows, lanes] = grad
                carry = carry + grad * conv[1, at_rows, lanes] * conv[2, at_rows, lanes]
        return carry

    skip_sum = lax.fori_loop(0, blocks, arrange, jnp.zeros((chans, 128), F32))
    g_spec[...] = dot_plain(g_long[...], table[...], EXACT)
    tick(first_group, 1)

    def signal_block(n, carry):
        def add(m, acc):
            at_kernel = pl.ds(eighths((m - n) * chans), chans)
            kr, ka, ki = k_re[at_kernel, :], k_alt[at_kernel, :], k_im[at_kernel, :]
            out = []
            for s in range(seqs):
                at_rows = pl.ds(eighths((m * seqs + s) * chans), chans)
                re, im = g_spec[at_rows, :block], g_spec[at_rows, block:]
                out.append(acc[2 * s] + re * kr + im * ki)
                out.append(acc[2 * s + 1] + im * ka - re * ki)
            return tuple(out)

        acc = lax.fori_loop(n, blocks, add, tuple(jnp.zeros((chans, block), F32) for _ in range(2 * seqs)))
        for s in range(seqs):
            at_rows = pl.ds(eighths((n * seqs + s) * chans), chans)
            g_sums[at_rows, :block] = acc[2 * s] * weight
            g_sums[at_rows, block:] = acc[2 * s + 1] * weight
        return carry

    lax.fori_loop(0, blocks, signal_block, 0)
    g_sums[:, :block] = dot_rows(g_sums[...], table[...], EXACT)

    def gate_grads(m, carry):
        for s in range(seqs):
            at_rows = pl.ds(eighths((m * seqs + s) * chans), chans)
            place = pl.ds(pl.multiple_of(m * block, block), block)
            grad = g_sums[at_rows, :block] + skip * g_long[at_rows, :]
            g_conv[1, s, :, place] = grad * conv[2, at_rows, :]
            g_conv[2, s, :, place] = grad * conv[1, at_rows, :]
        return carry

    lax.fori_loop(0, blocks, gate_grads, 0)
    tick(first_group, 2)

    length = block * blocks
    for c in range(0, chans, 8):
        col = lax.broadcasted_iota(jnp.int32, (8, 128), 1)
        spots = lax.broadcasted_iota(jnp.int32, (8, length), 1)
        found = jnp.where(col == 12, jnp.sum(skip_sum[c : c + 8], 1, keepdims=True), 0.0)
        local_params = params[c : c + 8, :]
        for p in range(3):
            for s in range(seqs):
                grad = g_conv[p, s, c : c + 8, :]
                x = steps[p, s, c : c + 8, :]
                value = jnp.zeros_like(grad)
                for i in range(3):
                    later = jnp.where(spots < length - i, pltpu.roll(grad, length - i, 1), 0.0) if i else grad
                    value += column(local_params, 3 * i + p) * later
                    found += jnp.where(col == 3 * i + p, jnp.sum(later * x, 1, keepdims=True), 0.0)
                found += jnp.where(col == 9 + p, jnp.sum(grad, 1, keepdims=True), 0.0)
                g_conv[p, s, c : c + 8, :] = value
        chan_grads[c : c + 8, :] = found

    def pack(j, carry):
        lanes = pl.ds(pl.multiple_of(j * 128, 128), 128)
        for p in range(3):
            pair = merge_halves(g_conv[p, 0, :, lanes], g_conv[p, 1, :, lanes])
            proj_send[2 * j, p] = pair[0].astype(BF16)
            proj_send[2 * j + 1, p] = pair[1].astype(BF16)
        return carry

    lax.fori_loop(0, devices // 2, pack, 0)
    home = Exchange(proj_send, proj_recv, send_b, recv_b, devices)
    home.start()
    tick(first_group, 3)

    def kernel_block(d, carry):
        def add(n, acc):
            real, imag = acc
            for s in range(seqs):
                at_signal = pl.ds(eighths((n * seqs + s) * chans), chans)
                at_grad = pl.ds(eighths(((n + d) * seqs + s) * chans), chans)
                s_re, s_im = spec[at_signal, :block], spec[at_signal, block:]
                g_re, g_im = g_spec[at_grad, :block], g_spec[at_grad, block:]
                zero = slot_zero((chans, block))
                same, other = g_re * s_re, g_im * s_im
                real = real + jnp.where(zero, same, same + other)
                imag = imag + jnp.where(zero, other, g_im * s_re - g_re * s_im)
            return real, imag

        empty = jnp.zeros((chans, block), F32)
        real, imag = lax.fori_loop(0, blocks - d, add, (empty, empty))
        at_kernel = pl.ds(eighths(d * chans), chans)
        k_sums[at_kernel, :block] = real
        k_sums[at_kernel, block:] = imag
        return carry

    lax.fori_loop(0, blocks, kernel_block, 0)
    after = jnp.concatenate([k_sums[chans:, :], jnp.zeros((chans, 2 * block), F32)], 0)
    shape = (chans * blocks, block)
    sign, scale = slot_sign(shape), slot_weight(shape)
    k_sums[:, :block] = (k_sums[:, :block] + sign * after[:, :block]) * scale
    k_sums[:, block:] = (k_sums[:, block:] + sign * after[:, block:]) * scale
    k_sums[:, :block] = dot_rows(k_sums[...], table[...], EXACT)
    tick(first_group, 4)

    order = pos_t.shape[0]
    emb = pos_t.shape[1]
    freq = column(rows_in[...], 0)

    def filter_block(n, carry):
        grad_fil, grad_pos, grad_mid, grad_bias = carry
        lag = lax.broadcasted_iota(jnp.int32, (chans, block), 1) + n * block
        fade = jnp.exp(-lag.astype(F32) * column(params[...], 13))
        grad = k_sums[pl.ds(eighths(n * chans), chans), :block] * fade
        grad_fil = grad_fil + dot_rows(grad, two[n], EXACT)
        grad_two = dot_plain(fil_t[...].T, grad, EXACT) * cos_two[n] * freq
        grad_mid = grad_mid + dot_rows(one[n], grad_two, EXACT)
        grad_bias = grad_bias + dot_rows(jnp.ones((8, block), F32), grad_two, EXACT)
        grad_one = dot_plain(mid_t[...].T, grad_two, EXACT) * cos_one[n] * freq
        grad_pos = grad_pos + dot_rows(feats[n], grad_one, EXACT)
        return grad_fil, grad_pos, grad_mid, grad_bias

    zeros = [jnp.zeros(s, F32) for s in ((chans, order), (emb, order), (order, order), (8, order))]
    grad_fil, grad_pos, grad_mid, grad_bias = lax.fori_loop(0, blocks, filter_block, tuple(zeros))
    filter_grad[...] = grad_fil
    rate_bias = rows_in[...].T
    grad_rate = jnp.sum(pos_t[...].T * grad_pos, 0, keepdims=True) + jnp.sum(mid_t[...].T * grad_mid, 0, keepdims=True)
    grad_rate = (grad_rate + rate_bias[1:2] * grad_bias[:1]) / rate_bias[0:1]
    small[...] = jnp.zeros_like(small)
    small[:emb, :order] = grad_pos
    small[emb : emb + order, :order] = grad_mid
    picked = lax.broadcasted_iota(jnp.int32, (8, order), 0)
    small[emb + order : emb + order + 8, :order] = jnp.where(
        picked == 0, grad_bias, jnp.where(picked == 1, grad_rate, 0.0)
    )
    tick(first_group, 5)

    gain_one, shift_one = norms[0:1], norms[1:2]
    normed, normal_one, inv_one = lane_norm(hidden[...].astype(F32), gain_one, shift_one)
    normed = normed.astype(BF16)
    g_proj[...] = jnp.zeros_like(g_proj)
    home.arrive()
    for j in range(devices):
        for i in range(3):
            unit = 3 * j + i
            at_rows = slice(j * in_rows + i * chans, j * in_rows + (i + 1) * chans)
            g_proj[at_rows, :] = proj_recv[unit % devices, unit // devices].astype(F32)
    for i in range(line):
        zo = visit(i)
        group = shards * in_rows
        grads = dot_plain(g_proj[pl.ds(eighths(zo * group), group), :].astype(BF16), normed)
        g_in[pl.ds(zo * shards, shards)] = grads.reshape(shards, in_rows, width)[:, : 3 * chans].astype(BF16)
        pieces[3].begin_at(zo)
    load_in.wait()
    tick(pieces[3:4], 0)
    grad_normed = dot_plain(g_proj[...].T.astype(BF16), w_in[...].reshape(devices * in_rows, width))
    input_term, grad_gain_one, grad_shift_one = lane_norm_back(grad_normed, normal_one, inv_one, gain_one)
    grad_hidden[...] = (resid[...] + input_term).astype(BF16)
    norm_grads = jnp.concatenate(
        [grad_gain_one, grad_shift_one, grad_gain_two, grad_shift_two, jnp.zeros((4, width), F32)], 0
    )
    for j in range(devices):
        turned = pltpu.roll(norm_grads, width - j * chans, 1) if j else norm_grads
        g_tile[j, 0:4, :] = turned[0:4, :128]
        g_tile[j, 4:8, :] = small[4 * j : 4 * j + 4, :]
    for distance in range(line - 1, -1, -1):
        pieces[4].begin(distance)
    tick(pieces[4:5], 0)
    for step in range(1, line + 2):
        tick(pieces[3:], step)

    mine = flat(*spot())

    def share(i):
        other = lax.rem(mine + i, devices)
        place = (other // 8, other // 4 % 2, other // 2 % 2, other % 2)
        return send(sum_tile, everyone.at[mine], share_send.at[i], share_recv.at[i], place)

    keep = pltpu.make_async_copy(sum_tile, everyone.at[mine], local)
    keep.start()
    lax.fori_loop(1, devices, lambda i, c: (share(i).start(), c)[1], 0)
    for piece in pieces:
        piece.drain()
    moved.drain()
    home.drain()
    keep.wait()

    def settle(i, carry):
        share(i).wait_recv()
        share(i).wait_send()
        return carry

    lax.fori_loop(1, devices, settle, 0)


def back(fulls, operands, dims):
    line, devices, chans, seqs, block, blocks, width = dims
    full_in, full_out, full_up, full_down = fulls
    pos_t = operands[17]
    order = pos_t.shape[0]
    rows = blocks * seqs * chans
    shards, hidden_rows = devices // line, full_up.shape[1]
    shape = jax.ShapeDtypeStruct
    vmem = pl.BlockSpec(memory_space=pltpu.VMEM)
    dma = pltpu.SemaphoreType.DMA
    tile = (devices, 8, 128)
    outs = [
        shape((seqs * 64, width), BF16),
        shape((seqs * 64, width), BF16),
        shape((hidden_rows, width), F32),
        shape((hidden_rows, width), F32),
        shape((chans, width), F32),
        shape((3 * chans, width), F32),
        shape(tile[1:], F32),
        shape(tile, F32),
        shape((chans, 128), F32),
        shape((chans, order), F32),
    ]
    parts = [
        shape((devices, hidden_rows, width), BF16),
        shape((devices, hidden_rows, width), BF16),
        shape((devices, chans, width), BF16),
        shape((devices, 3 * chans, width), BF16),
        shape(tile, F32),
    ]
    scratch = [
        pltpu.VMEM(full_in.shape, BF16),
        pltpu.VMEM(full_out.shape, BF16),
        pltpu.VMEM((2, shards, hidden_rows, width), BF16),
        pltpu.VMEM((2, shards, hidden_rows, width), BF16),
        pltpu.VMEM((width, width), BF16),
        dma((6,)),
    ]
    scratch += [pltpu.VMEM(p.shape, p.dtype) for p in parts]
    scratch += [
        pltpu.VMEM((seqs * 64, width), F32),
        pltpu.VMEM((seqs * 64, width), F32),
        pltpu.VMEM((seqs * 64, width), F32),
        pltpu.VMEM((devices, chans, 128), BF16),
        pltpu.VMEM((devices, chans, 128), BF16),
        pltpu.VMEM((rows, block), F32),
        pltpu.VMEM((rows, 2 * block), F32),
        pltpu.VMEM((rows, 2 * block), F32),
        pltpu.VMEM((3, seqs, chans, block * blocks), F32),
        pltpu.VMEM((blocks * chans, 2 * block), F32),
        pltpu.VMEM((devices, 3, chans, 128), BF16),
        pltpu.VMEM((devices, 3, chans, 128), BF16),
        pltpu.VMEM((devices * full_in.shape[1], 128), F32),
        pltpu.VMEM((4 * devices, 128), F32),
    ]
    scratch += [
        dma((5, 7, line * 4)),
        dma((5, 7, line * 4)),
        dma((devices,)),
        dma((devices,)),
        dma,
        dma((devices,)),
        dma((devices,)),
        dma((devices,)),
        dma((devices,)),
    ]
    scratch += [buffer for part in parts for buffer in reduce_scratch(line, part)]
    return pl.pallas_call(
        functools.partial(back_kernel, dims),
        name="back",
        out_shape=outs,
        in_specs=[pl.BlockSpec(memory_space=pl.ANY)] * 4 + [vmem] * len(operands),
        out_specs=[vmem] * len(outs),
        scratch_shapes=scratch,
        compiler_params=pltpu.CompilerParams(collective_id=1, has_side_effects=True, vmem_limit_bytes=KERNEL_VMEM),
    )(*fulls, *operands)


def finish_kernel(emb, order, *refs):
    (result, grad_hidden, up, down, out, inp, tile, everyone, chan_grads, filter_grad) = refs[:10]
    outs, desk = refs[10:-1], refs[-1]
    chans = chan_grads.shape[0]
    for target, source in zip(outs[:7], (result, grad_hidden, up, down, out, inp, filter_grad)):
        target[...] = source[...]
    taps, bias, skip, *gains = outs[7:14]
    desk[...] = jnp.zeros_like(desk)
    desk[:chans, :] = chan_grads[...]
    turned = desk[...].T
    for i in range(3):
        taps[i] = turned[3 * i : 3 * i + 3, :chans]
    bias[...] = turned[9:12, :chans]
    skip[...] = turned[12:13, :chans]
    for i, gain in enumerate(gains):
        gain[...] = tile[i : i + 1, :chans]
    for j in range(everyone.shape[0]):
        desk[4 * j : 4 * j + 4, :] = everyone[j, 4:8, :]
    pos, pos_bias, mid, mid_bias, rate = outs[14:]
    after = emb + 1 + -(emb + 1) % 8
    pos[...] = desk[:emb, :order]
    pos_bias[...] = desk[emb : emb + 1, :order]
    mid[...] = desk[after : after + order, :order]
    mid_bias[...] = desk[after + order : after + order + 1, :order]
    rate[...] = desk[after + order + 1 : after + order + 2, :order]


def finish(parts, pos_shape):
    emb, order = pos_shape
    chans = parts[8].shape[0]
    shape = jax.ShapeDtypeStruct
    vmem = pl.BlockSpec(memory_space=pltpu.VMEM)
    outs = [shape(p.shape, p.dtype) for p in parts[:6]] + [shape(parts[9].shape, F32)]
    outs += [shape((3, 3, chans), F32), shape((3, chans), F32)] + [shape((1, chans), F32)] * 5
    outs += [shape((emb, order), F32), shape((1, order), F32), shape((order, order), F32)]
    outs += [shape((1, order), F32)] * 2
    return pl.pallas_call(
        functools.partial(finish_kernel, emb, order),
        name="finish",
        out_shape=outs,
        in_specs=[vmem] * len(parts),
        out_specs=[vmem] * len(outs),
        scratch_shapes=[pltpu.VMEM((128, 128), F32)],
    )(*parts)


def shards_paired(
    hidden_in,
    cotangent,
    mixer_input_weight,
    mixer_output_weight,
    feedforward_up,
    feedforward_down,
    first_gain,
    first_shift,
    second_gain,
    second_shift,
    short_taps,
    short_bias,
    skip_scale,
    filter_out,
    pos_weight,
    pos_bias,
    mid_weight,
    mid_bias,
    sine_freq,
    decay_rate,
):
    devices = lax.axis_size(AXES)
    micro, seq_count, tok, width = hidden_in.shape
    seqs = micro * seq_count
    tokens = seqs * tok
    length = tok * devices
    chans = width // devices
    block = tok * lax.axis_size("chan")
    blocks = length // block

    line = devices // 8
    def row(vector):
        return vector.reshape(1, -1)

    shards = [mixer_input_weight.T, mixer_output_weight.T, feedforward_up.T, feedforward_down]
    raw = [row(v) for v in (first_gain, first_shift, second_gain, second_shift)]
    raw += [short_taps, short_bias, row(skip_scale), row(decay_rate), filter_out.T]
    raw += [pos_weight, row(pos_bias), mid_weight, row(sine_freq), row(mid_bias)]
    hidden = hidden_in.reshape(tokens, width)
    features, table = jnp.asarray(feature_blocks(length, block)), jnp.asarray(fixed_table(block))
    dims = (line, devices, chans, seqs, block, blocks, width)
    made = front(shards, hidden, features, table, raw, dims)
    fulls, kept, (params, pos_t, mid_t, fil_t, cols) = made[:4], made[4:17], made[17:]
    operands = [hidden, cotangent.reshape(tokens, width), *kept, params, features, pos_t, mid_t, fil_t, cols, table]
    outs = finish(back(fulls, operands, dims), pos_weight.shape)
    result, grad_hidden, up, down, out, inp, filter_grad, taps, bias, skip, *rest = outs
    gains, (pos, pos_bias, mid, mid_bias, rate) = rest[:4], rest[4:]
    return (
        result.reshape(hidden_in.shape),
        grad_hidden.reshape(hidden_in.shape),
        inp.T,
        out.T,
        up.T,
        down,
        *[g.reshape(-1) for g in gains],
        taps,
        bias,
        skip.reshape(-1),
        filter_grad.T,
        pos,
        pos_bias.reshape(-1),
        mid,
        mid_bias.reshape(-1),
        rate.reshape(-1),
    )


def shards(
    hidden_in,
    cotangent,
    mixer_input_weight,
    mixer_output_weight,
    feedforward_up,
    feedforward_down,
    first_gain,
    first_shift,
    second_gain,
    second_shift,
    short_taps,
    short_bias,
    skip_scale,
    filter_out,
    pos_weight,
    pos_bias,
    mid_weight,
    mid_bias,
    sine_freq,
    decay_rate,
):
    devices = lax.axis_size(AXES)
    micro, seq_count, tok, width = hidden_in.shape
    seqs = micro * seq_count
    tokens = seqs * tok
    length = tok * devices
    chans = width // devices
    block = tok * lax.axis_size("chan")
    blocks = length // block

    norms = jnp.stack([first_gain, first_shift, second_gain, second_shift])
    own = [mixer_input_weight.T, feedforward_up.T, feedforward_down, mixer_output_weight.T]
    full = [lax.all_gather(shard, AXES, axis=0, tiled=True) for shard in own]
    norms = lax.all_gather(norms, AXES, axis=1, tiled=True)
    weight_in, weight_up, weight_down, weight_out = full
    norms = norms.astype(F32)
    gain_one, shift_one, gain_two, shift_two = norms[0], norms[1], norms[2], norms[3]

    freq = sine_freq.astype(F32)
    w_pos, w_mid, w_fil = pos_weight.astype(F32), mid_weight.astype(F32), filter_out.astype(F32)
    lags, features, first_sum, first_act, second_sum, second_act = filter_hidden(
        length, w_pos, pos_bias.astype(F32), w_mid, mid_bias.astype(F32), freq
    )
    decay = jnp.exp(-lags[None, :] * decay_rate.astype(F32)[:, None])
    kernel = contract(w_fil, second_act, 0, 0, EXACT) * decay
    table = block_table(block)
    sign = 1.0 - 2.0 * (lax.iota(jnp.int32, block) % 2).astype(F32)
    ker_re, ker_im = to_spectrum(kernel.reshape(chans, blocks, block), table)

    def with_previous(spec):
        before = jnp.concatenate([jnp.zeros_like(spec[:, :1]), spec[:, :-1]], 1)
        return spec + sign * before

    k_re, k_alt, k_im = packed_kernel(with_previous(ker_re), with_previous(ker_im))

    values = hidden_in.reshape(tokens, width).astype(F32)
    normed, normal_one, inv_one = layer_norm(values, gain_one, shift_one)
    normed = normed.astype(BF16)
    projected = contract(weight_in, normed, 1, 1).astype(BF16)
    projected = projected.reshape(3, devices, chans, tokens).transpose(1, 0, 2, 3)
    arrived = exchange(projected)

    def by_sequence(values):
        parts = values.shape[1]
        values = values.reshape(devices, parts, chans, seqs, tok)
        return values.transpose(1, 3, 2, 0, 4).reshape(parts, seqs, chans, length)

    def by_device(values):
        parts = values.shape[0]
        values = values.reshape(parts, seqs, chans, devices, tok)
        return values.transpose(3, 0, 2, 1, 4).reshape(devices, parts, chans, tokens)

    steps = by_sequence(arrived).astype(F32)
    taps = short_taps.astype(F32)[:, :, None, :, None]
    conv = short_bias.astype(F32)[:, None, :, None]
    for i in range(3):
        conv = conv + taps[i] * delayed(steps, i)
    gate_out, gate_in, signal = conv[0], conv[1], conv[2]
    gated = signal * gate_in
    sig_re, sig_im = to_spectrum(gated.reshape(seqs, chans, blocks, block), table)

    def shifted_sum(make):
        total = None
        for d in range(blocks):
            term = make(d)
            total = term if total is None else tuple(a + b for a, b in zip(total, term))
        return total

    def ahead(x, d):
        return x if d == 0 else jnp.pad(x[:, :, :-d], ((0, 0), (0, 0), (d, 0), (0, 0)))

    def back(x, d):
        return x if d == 0 else jnp.pad(x[:, :, d:], ((0, 0), (0, 0), (0, d), (0, 0)))

    def forward_term(d):
        re, im = ahead(sig_re, d), ahead(sig_im, d)
        kr, ka, ki = k_re[:, d : d + 1], k_alt[:, d : d + 1], k_im[:, d : d + 1]
        return re * kr - im * ki, re * ki + im * ka

    out_re, out_im = shifted_sum(forward_term)
    long_out = from_spectrum(out_re, out_im, table).reshape(seqs, chans, length)
    skip = skip_scale.astype(F32)[None, :, None]
    long_total = long_out + skip * gated
    mixed = (long_total * gate_out).astype(BF16)
    mixed = exchange(by_device(mixed[None])).reshape(width, tokens)

    resid = values + contract(mixed, weight_out, 0, 1)
    second, normal_two, inv_two = layer_norm(resid, gain_two, shift_two)
    second = second.astype(BF16)
    upper = contract(second, weight_up, 1, 1)
    active, slope = gelu_parts(upper)
    active = active.astype(BF16)
    result = resid + contract(active, weight_down, 1, 0)

    cot = cotangent.reshape(tokens, width)
    grad_down = contract(active, cot, 0, 0)
    grad_upper = (contract(cot, weight_down, 1, 1) * slope).astype(BF16)
    grad_up = contract(grad_upper, second, 0, 0)
    grad_second = contract(grad_upper, weight_up, 1, 0)
    resid_term, grad_gain_two, grad_shift_two = layer_norm_back(grad_second, normal_two, inv_two, gain_two)
    grad_resid = cot.astype(F32) + resid_term
    grad_branch = grad_resid.astype(BF16)
    grad_out_w = contract(grad_branch, mixed, 0, 1)
    grad_mixed = contract(weight_out, grad_branch, 0, 1).astype(BF16)
    grad_mixed = exchange(grad_mixed.reshape(devices, 1, chans, tokens))
    grad_mixed = by_sequence(grad_mixed)[0].astype(F32)

    grad_gate_out = grad_mixed * long_total
    grad_long = grad_mixed * gate_out
    grad_skip = jnp.sum(grad_long * gated, (0, 2))
    gl_re, gl_im = to_spectrum(grad_long.reshape(seqs, chans, blocks, block), table)

    def signal_term(d):
        re, im = back(gl_re, d), back(gl_im, d)
        kr, ka, ki = k_re[:, d : d + 1], k_alt[:, d : d + 1], k_im[:, d : d + 1]
        return re * kr + im * ki, im * ka - re * ki

    gg_re, gg_im = shifted_sum(signal_term)
    grad_gated = from_spectrum(gg_re, gg_im, table).reshape(seqs, chans, length) + skip * grad_long

    first_slot = lax.iota(jnp.int32, block) == 0
    kg_re, kg_im = [], []
    for d in range(blocks):
        s_re, s_im = sig_re[:, :, : blocks - d], sig_im[:, :, : blocks - d]
        g_re, g_im = gl_re[:, :, d:], gl_im[:, :, d:]
        same, other = g_re * s_re, g_im * s_im
        kg_re.append(jnp.sum(jnp.where(first_slot, same, same + other), (0, 2)))
        kg_im.append(jnp.sum(jnp.where(first_slot, other, g_im * s_re - g_re * s_im), (0, 2)))
    kg_re, kg_im = jnp.stack(kg_re, 1), jnp.stack(kg_im, 1)

    def with_next(spec):
        after = jnp.concatenate([spec[:, 1:], jnp.zeros_like(spec[:, :1])], 1)
        return spec + sign * after

    grad_kernel = from_spectrum(with_next(kg_re), with_next(kg_im), table).reshape(chans, length)

    grad_conv = jnp.stack([grad_gate_out, grad_gated * signal, grad_gated * gate_in])
    grad_bias = jnp.sum(grad_conv, (1, 3))
    grad_taps = jnp.stack([jnp.sum(grad_conv * delayed(steps, i), (1, 3)) for i in range(3)])
    grad_steps = taps[0] * grad_conv
    for i in (1, 2):
        grad_steps = grad_steps + taps[i] * advanced(grad_conv, i)
    grad_proj = exchange(by_device(grad_steps.astype(BF16)))
    grad_proj = grad_proj.transpose(1, 0, 2, 3).reshape(3 * width, tokens)

    fade = grad_kernel * decay
    grad_filter = contract(second_act, fade, 1, 1, EXACT)
    grad_two = contract(w_fil, fade, 1, 0, EXACT) * jnp.cos(freq[:, None] * second_sum)
    grad_freq = jnp.sum(grad_two * second_sum, 1)
    grad_two = grad_two * freq[:, None]
    grad_mid = contract(first_act, grad_two, 1, 1, EXACT)
    grad_one = contract(w_mid, grad_two, 1, 0, EXACT) * jnp.cos(freq[:, None] * first_sum)
    grad_freq = grad_freq + jnp.sum(grad_one * first_sum, 1)
    grad_one = grad_one * freq[:, None]
    grad_pos = contract(features, grad_one, 1, 1, EXACT)
    small = jnp.concatenate(
        [grad_pos, jnp.sum(grad_one, 1)[None], grad_mid, jnp.sum(grad_two, 1)[None], grad_freq[None]]
    )
    emb, order = pos_weight.shape

    grad_in = contract(grad_proj, normed, 1, 0)
    grad_normed = contract(grad_proj, weight_in, 0, 0)
    input_term, grad_gain_one, grad_shift_one = layer_norm_back(grad_normed, normal_one, inv_one, gain_one)
    grad_hidden = (grad_resid + input_term).astype(BF16)

    norm_grads = jnp.stack([grad_gain_one, grad_shift_one, grad_gain_two, grad_shift_two])
    sums = [grad_in, grad_up, grad_down, grad_out_w]
    sums = [
        lax.psum_scatter(g.astype(BF16), AXES, scatter_dimension=0, tiled=True).astype(F32) for g in sums
    ]
    norm_grads = lax.psum_scatter(norm_grads, AXES, scatter_dimension=1, tiled=True)
    small = lax.psum(small, AXES)
    return (
        result.astype(BF16).reshape(hidden_in.shape),
        grad_hidden.reshape(hidden_in.shape),
        sums[0].T,
        sums[3].T,
        sums[1].T,
        sums[2],
        norm_grads[0],
        norm_grads[1],
        norm_grads[2],
        norm_grads[3],
        grad_taps,
        grad_bias,
        grad_skip,
        grad_filter,
        small[:emb],
        small[emb],
        small[emb + 1 : emb + 1 + order],
        small[emb + 1 + order],
        small[emb + 2 + order],
    )


def solution(mesh):
    paired = mesh.shape["chan"] == 4 and mesh.shape["blk"] == 8
    rows, spread, tokens = P(AXES), P(None, AXES), P(None, None, AXES, None)
    params = (rows, rows, rows, rows, P(None, None, AXES), spread, rows, spread, P(), P(), P(), P(), P())
    return jax.shard_map(
        shards_paired if paired else shards,
        mesh=mesh,
        in_specs=(tokens, tokens, spread, spread, spread, P(AXES, None)) + params + (rows,),
        out_specs=(tokens, tokens, spread, spread, spread, P(AXES, None)) + params,
        check_vma=False,
    )
```

```python
import functools
import math

import jax
import jax.numpy as jnp
import numpy as np
from jax import lax
from jax.experimental import pallas as pl
from jax.experimental.pallas import tpu as pltpu
from jax.sharding import PartitionSpec as P

EPS = 1e-05
BANDS = 16
EXACT = lax.Precision.HIGHEST
AXES = ("blk", "chan")
F32 = jnp.float32
BF16 = jnp.bfloat16
MESH = pl.DeviceIdType.MESH
KERNEL_VMEM = 62 << 20


def contract(a, b, dim_a, dim_b, precision=None):
    return lax.dot_general(
        a, b, (((dim_a,), (dim_b,)), ((), ())), precision=precision, preferred_element_type=F32
    )


def positions(length):
    lags = jnp.arange(length).astype(F32)
    band_freq = 0.0001 + (BANDS - 1 - 0.0001) * jnp.arange(BANDS).astype(F32) / (BANDS - 1)
    phase = 2.0 * math.pi / length * lags[None, :] * band_freq[:, None]
    return lags, jnp.concatenate([lags[None, :] / (length - 1), jnp.cos(phase), -jnp.sin(phase)], 0)


def feature_blocks(length, block):
    lags = np.arange(length).astype(np.float32)
    bands = np.arange(BANDS).astype(np.float32)
    band_freq = np.float32(0.0001) + np.float32(BANDS - 1 - 0.0001) * bands / np.float32(BANDS - 1)
    phase = np.float32(2.0 * math.pi / length) * lags[None, :] * band_freq[:, None]
    ramp = lags[None, :] / np.float32(length - 1)
    rows = np.concatenate([ramp, np.cos(phase), -np.sin(phase), np.ones_like(ramp)])
    rows = np.pad(rows, ((0, -len(rows) % 8), (0, 0))).astype(np.float32)
    return np.ascontiguousarray(rows.reshape(len(rows), -1, block).transpose(1, 0, 2))


def fixed_table(block):
    spot, freq = np.arange(block)[:, None], np.arange(block)[None, :]
    phase = (np.pi / block) * (spot * freq % (2 * block))
    imag = np.where(freq == 0, 1.0 - 2.0 * (spot % 2), -np.sin(phase))
    return np.concatenate([np.cos(phase), imag], 1).astype(np.float32)


def filter_hidden(length, pos_weight, pos_bias, mid_weight, mid_bias, sine_freq):
    lags, features = positions(length)
    freq = sine_freq[:, None]
    first_sum = contract(pos_weight, features, 0, 0, EXACT) + pos_bias[:, None]
    first = jnp.sin(freq * first_sum)
    second_sum = contract(mid_weight, first, 0, 0, EXACT) + mid_bias[:, None]
    second = jnp.sin(freq * second_sum)
    return lags, features, first_sum, first, second_sum, second


def block_table(block):
    spot = lax.broadcasted_iota(jnp.int32, (block, block), 0)
    freq = lax.broadcasted_iota(jnp.int32, (block, block), 1)
    phase = (math.pi / block) * (spot * freq % (2 * block)).astype(F32)
    parity = 1.0 - 2.0 * (spot % 2).astype(F32)
    imag = jnp.where(freq == 0, parity, -jnp.sin(phase))
    return jnp.concatenate([jnp.cos(phase), imag], 1)


def to_spectrum(blocks, table):
    spec = lax.dot_general(
        blocks, table, (((blocks.ndim - 1,), (0,)), ((), ())), precision=EXACT, preferred_element_type=F32
    )
    half = table.shape[0]
    return spec[..., :half], spec[..., half:]


def from_spectrum(real, imag, table):
    half = table.shape[0]
    weight = jnp.where(lax.iota(jnp.int32, half) == 0, 0.5 / half, 1.0 / half)
    spec = jnp.concatenate([real * weight, imag * weight], -1)
    return lax.dot_general(
        spec, table, (((spec.ndim - 1,), (1,)), ((), ())), precision=EXACT, preferred_element_type=F32
    )


def packed_kernel(real, imag):
    first = lax.iota(jnp.int32, real.shape[-1]) == 0
    return real, jnp.where(first, imag, real), jnp.where(first, 0.0, imag)


def layer_norm(values, gain, shift):
    center = values - jnp.mean(values, -1, keepdims=True)
    scale_inv = lax.rsqrt(jnp.mean(center * center, -1, keepdims=True) + EPS)
    normal = center * scale_inv
    return normal * gain + shift, normal, scale_inv


def layer_norm_back(grad_out, normal, scale_inv, gain):
    grad_normal = grad_out * gain
    inner = grad_normal - jnp.mean(grad_normal, -1, keepdims=True)
    inner = inner - normal * jnp.mean(grad_normal * normal, -1, keepdims=True)
    return inner * scale_inv, jnp.sum(grad_out * normal, 0), jnp.sum(grad_out, 0)


def gelu_parts(v):
    root = math.sqrt(2.0 / math.pi)
    inner = root * (v + 0.044715 * v * v * v)
    t = jnp.tanh(inner)
    value = 0.5 * v * (1.0 + t)
    slope = 0.5 * (1.0 + t) + 0.5 * v * (1.0 - t * t) * root * (1.0 + 3.0 * 0.044715 * v * v)
    return value, slope


def delayed(values, steps):
    if steps == 0:
        return values
    pad = jnp.zeros(values.shape[:-1] + (steps,), values.dtype)
    return jnp.concatenate([pad, values[..., :-steps]], -1)


def advanced(values, steps):
    if steps == 0:
        return values
    pad = jnp.zeros(values.shape[:-1] + (steps,), values.dtype)
    return jnp.concatenate([values[..., steps:], pad], -1)


def exchange(values):
    return lax.all_to_all(values, AXES, split_axis=0, concat_axis=0, tiled=True)


def spot():
    b, c = lax.axis_index("blk"), lax.axis_index("chan")
    return b // 2, b % 2, c // 2, c % 2


def at(z, y, x, k):
    return {"blk": z * 2 + y, "chan": x * 2 + k}


def flat(z, y, x, k):
    return ((z * 2 + y) * 2 + x) * 2 + k


def when(condition, act):
    pl.when(condition)(act)


def send(src, dst, send_sem, recv_sem, place):
    return pltpu.make_async_remote_copy(
        src_ref=src, dst_ref=dst, send_sem=send_sem, recv_sem=recv_sem, device_id=at(*place), device_id_type=MESH
    )


def greet_all(count):
    b, c = lax.axis_index("blk"), lax.axis_index("chan")
    chan = lax.axis_size("chan")
    me = b * chan + c
    barrier = pltpu.get_barrier_semaphore()

    def one(i, carry):
        other = lax.rem(me + i, count)
        pl.semaphore_signal(
            barrier, inc=1, device_id={"blk": other // chan, "chan": other % chan}, device_id_type=MESH
        )
        return carry

    lax.fori_loop(1, count, one, 0)
    pl.semaphore_wait(barrier, count - 1)


def low_rows(rows):
    return (rows + 16) // 32 * 16 if rows > 8 else rows


class Gather:
    def __init__(self, line, shard, full, sends, recvs, local):
        self.line, self.shard, self.full, self.s, self.r, self.local = line, shard, full, sends, recvs, local
        self.rows = shard.shape[0]
        self.low = low_rows(self.rows)
        self.z, self.y, self.x, self.k = spot()
        self.half = line // 2
        self.inward = 1 - 2 * (self.z // self.half)
        self.inner = self.z == self.half - 1 + self.z // self.half

    def copy(self, kind, index, shard, place, rows=None):
        ref = self.full.at[shard] if rows is None else self.full.at[shard, pl.ds(*rows)]
        return send(ref, ref, self.s.at[kind, index], self.r.at[kind, index], place)

    def up(self, zo):
        return self.copy(0, zo, flat(zo, self.y, self.x, self.k), (self.z + 1, self.y, self.x, self.k))

    def down(self, zo):
        return self.copy(1, zo, flat(zo, self.y, self.x, self.k), (self.z - 1, self.y, self.x, self.k))

    def to_x(self, zo):
        return self.copy(2, zo, flat(zo, self.y, self.x, self.k), (self.z, self.y, 1 - self.x, self.k))

    def to_y(self, zo):
        return self.copy(3, zo, flat(zo, self.y, self.x, self.k), (self.z, 1 - self.y, self.x, self.k))

    def low_y(self, zo, other_y=False):
        shard = flat(zo, 1 - self.y if other_y else self.y, 1 - self.x, self.k)
        return self.copy(4, zo, shard, (self.z, 1 - self.y, self.x, self.k), (0, self.low))

    def high_x(self, zo, other_x=False):
        shard = flat(zo, 1 - self.y, 1 - self.x if other_x else self.x, self.k)
        return self.copy(5, zo, shard, (self.z, self.y, 1 - self.x, self.k), (self.low, self.rows - self.low))

    def core(self, zo, yo, xo, k):
        return self.copy(6, (zo * 2 + yo) * 2 + xo, flat(zo, yo, xo, k), (self.z, self.y, self.x, 1 - self.k))

    def cross(self, zo, step):
        shard = flat(zo, 1 - self.y, 1 - self.x, self.k)
        return self.copy(7, zo, shard, (self.z + step, self.y, self.x, self.k))

    def same(self, zo):
        return zo // self.half == self.z // self.half

    def line_has(self, zo):
        self.to_x(zo).start()
        self.to_y(zo).start()
        self.core(zo, self.y, self.x, self.k).start()

    def begin(self):
        own = self.full.at[flat(self.z, self.y, self.x, self.k)]
        copy = pltpu.make_async_copy(self.shard, own, self.local)
        copy.start()
        copy.wait()
        when(self.z < self.line - 1, lambda: self.up(self.z).start())
        when(self.z > 0, lambda: self.down(self.z).start())
        self.line_has(self.z)

    def each(self, distance, act):
        if distance == 0:
            act(self.z)
        else:
            when(self.z - distance >= 0, lambda: act(self.z - distance))
            when(self.z + distance < self.line, lambda: act(self.z + distance))

    def along(self, distance):
        def from_below():
            zo = self.z - distance
            self.up(zo).wait_recv()
            when(self.z < self.line - 1, lambda: self.up(zo).start())
            self.line_has(zo)

        def from_above():
            zo = self.z + distance
            self.down(zo).wait_recv()
            when(self.z > 0, lambda: self.down(zo).start())
            self.line_has(zo)

        when(self.z - distance >= 0, from_below)
        when(self.z + distance < self.line, from_above)

    def plane(self, distance):
        def act(zo):
            self.to_x(zo).wait_recv()
            when(self.same(zo), lambda: self.low_y(zo).start())
            self.core(zo, self.y, 1 - self.x, self.k).start()
            self.to_y(zo).wait_recv()
            if self.low < self.rows:
                when(self.same(zo), lambda: self.high_x(zo).start())
            self.core(zo, 1 - self.y, self.x, self.k).start()

        self.each(distance, act)

    def corner(self, distance):
        def near(zo):
            self.low_y(zo, True).wait_recv()
            if self.low < self.rows:
                self.high_x(zo, True).wait_recv()
            when(self.inner, lambda: self.cross(zo, self.inward).start())

        def far(zo):
            self.cross(zo, self.inward).wait_recv()
            when(self.inner, lambda: self.cross(zo, -self.inward).start())

        def act(zo):
            when(self.same(zo), lambda: near(zo))
            when(jnp.logical_not(self.same(zo)), lambda: far(zo))
            self.core(zo, 1 - self.y, 1 - self.x, self.k).start()

        self.each(distance, act)

    def finish(self):
        for zo in range(self.line):
            for yo in range(2):
                for xo in range(2):
                    self.core(zo, yo, xo, 1 - self.k).wait_recv()

    def drain(self):
        def near(zo):
            self.low_y(zo).wait_send()
            if self.low < self.rows:
                self.high_x(zo).wait_send()

        for zo in range(self.line):
            when(jnp.logical_and(self.z < self.line - 1, zo <= self.z), lambda: self.up(zo).wait_send())
            when(jnp.logical_and(self.z > 0, zo >= self.z), lambda: self.down(zo).wait_send())
            self.to_x(zo).wait_send()
            self.to_y(zo).wait_send()
            when(self.same(zo), lambda: near(zo))
            when(self.inner, lambda: self.cross(zo, self.inward).wait_send())
            for yo in range(2):
                for xo in range(2):
                    self.core(zo, yo, xo, self.k).wait_send()


class Reduce:
    def __init__(self, line, part, out, chip, low_y, high_x, by_x, by_y, by_z, crossed, sends, recvs):
        self.line, self.part, self.out, self.chip = line, part, out, chip
        self.low_buf, self.high_buf, self.x_buf, self.y_buf, self.z_buf = low_y, high_x, by_x, by_y, by_z
        self.crossed = crossed
        self.s, self.r = sends, recvs
        self.rows = part.shape[1]
        self.low = low_rows(self.rows)
        self.z, self.y, self.x, self.k = spot()
        self.half = line // 2
        self.inward = 1 - 2 * (self.z // self.half)
        self.inner = self.z == self.half - 1 + self.z // self.half

    def index(self, zo, yo, xo):
        return (zo * 2 + yo) * 2 + xo

    def copy(self, kind, index, src, dst, place):
        return send(src, dst, self.s.at[kind, index], self.r.at[kind, index], place)

    def core(self, zo, yo, xo):
        i = self.index(zo, yo, xo)
        src = self.part.at[flat(zo, yo, xo, 1 - self.k)]
        return self.copy(6, i, src, self.chip.at[i], (self.z, self.y, self.x, 1 - self.k))

    def corner_of(self, zo):
        return self.index(zo, 1 - self.y, 1 - self.x)

    def low_y(self, zo):
        src = self.chip.at[self.corner_of(zo), pl.ds(0, self.low)]
        return self.copy(4, zo, src, self.low_buf.at[zo % self.half], (self.z, 1 - self.y, self.x, self.k))

    def high_x(self, zo):
        src = self.chip.at[self.corner_of(zo), pl.ds(self.low, self.rows - self.low)]
        return self.copy(5, zo, src, self.high_buf.at[zo % self.half], (self.z, self.y, 1 - self.x, self.k))

    def to_x(self, zo):
        src = self.chip.at[self.index(zo, self.y, 1 - self.x)]
        return self.copy(2, zo, src, self.x_buf.at[zo], (self.z, self.y, 1 - self.x, self.k))

    def to_y(self, zo):
        src = self.chip.at[self.index(zo, 1 - self.y, self.x)]
        return self.copy(3, zo, src, self.y_buf.at[zo], (self.z, 1 - self.y, self.x, self.k))

    def up(self, zo):
        src = self.chip.at[self.index(zo, self.y, self.x)]
        return self.copy(0, zo, src, self.z_buf.at[zo + 1], (self.z + 1, self.y, self.x, self.k))

    def down(self, zo):
        src = self.chip.at[self.index(zo, self.y, self.x)]
        return self.copy(1, zo, src, self.z_buf.at[zo], (self.z - 1, self.y, self.x, self.k))

    def cross(self, zo):
        src = self.chip.at[self.corner_of(zo)]
        return self.copy(7, zo, src, self.crossed.at[zo], (self.z + self.inward, self.y, self.x, self.k))

    def add(self, i, other, rows=None):
        if rows is None:
            self.chip[i] = self.chip[i] + other
        else:
            self.chip[i, pl.ds(*rows)] = self.chip[i, pl.ds(*rows)] + other

    def begin(self, zo):
        for yo, xo in ((1 - self.y, 1 - self.x), (self.y, 1 - self.x), (1 - self.y, self.x), (self.y, self.x)):
            self.core(zo, yo, xo).start()

    def corner(self, zo, near):
        def joined(yo, xo):
            self.core(zo, yo, xo).wait_recv()
            self.add(self.index(zo, yo, xo), self.part[flat(zo, yo, xo, self.k)])

        def crossing():
            self.cross(zo).wait_recv()
            self.add(self.corner_of(zo), self.crossed[zo])

        joined(1 - self.y, 1 - self.x)
        if not near:
            joined(self.y, 1 - self.x)
            self.to_x(zo).start()
            joined(1 - self.y, self.x)
            self.to_y(zo).start()
        when(self.inner, crossing)
        if near:
            self.low_y(zo).start()
            if self.low < self.rows:
                self.high_x(zo).start()
            joined(self.y, 1 - self.x)
            joined(1 - self.y, self.x)
        else:
            self.cross(zo).start()
        joined(self.y, self.x)

    def plane(self, zo):
        self.low_y(zo).wait_recv()
        self.add(self.index(zo, self.y, 1 - self.x), self.low_buf[zo % self.half], (0, self.low))
        self.to_x(zo).start()
        if self.low < self.rows:
            self.high_x(zo).wait_recv()
            high = (self.low, self.rows - self.low)
            self.add(self.index(zo, 1 - self.y, self.x), self.high_buf[zo % self.half], high)
        self.to_y(zo).start()

    def along(self, zo, own):
        i = self.index(zo, self.y, self.x)
        self.to_x(zo).wait_recv()
        self.to_y(zo).wait_recv()
        total = self.x_buf[zo].astype(F32) + self.y_buf[zo].astype(F32) + self.chip[i].astype(F32)

        def from_below():
            self.up(zo).wait_recv()
            self.add(i, self.z_buf[zo + 1])

        def from_above():
            self.down(zo).wait_recv()
            self.add(i, self.z_buf[zo])

        def rising():
            when(self.z > 0, from_below)
            self.up(zo).start()

        def falling():
            when(self.z < self.line - 1, from_above)
            self.down(zo).start()

        def last_below():
            self.up(zo).wait_recv()
            self.out[...] += self.z_buf[zo + 1].astype(F32)

        def last_above():
            self.down(zo).wait_recv()
            self.out[...] += self.z_buf[zo].astype(F32)

        if own:
            self.out[...] = total
            when(self.z > 0, last_below)
            when(self.z < self.line - 1, last_above)
        else:
            self.chip[i] = total.astype(self.chip.dtype)
            when(zo > self.z, rising)
            when(zo < self.z, falling)

    def drain(self):
        def near(zo):
            self.low_y(zo).wait_send()
            if self.low < self.rows:
                self.high_x(zo).wait_send()

        for zo in range(self.line):
            when(zo > self.z, lambda: self.up(zo).wait_send())
            when(zo < self.z, lambda: self.down(zo).wait_send())
            self.to_x(zo).wait_send()
            self.to_y(zo).wait_send()
            same = zo // self.half == self.z // self.half
            when(same, lambda: near(zo))
            when(jnp.logical_not(same), lambda: self.cross(zo).wait_send())
            for yo in range(2):
                for xo in range(2):
                    self.core(zo, yo, xo).wait_send()


BUFFERS = 7


def reduce_scratch(line, part):
    _, rows, width = part.shape
    low = low_rows(rows)
    high = max(rows - low, 8)
    half = line // 2
    sizes = [(line * 4, rows), (half, low), (half, high), (line, rows), (line, rows), (line + 1, rows), (line, rows)]
    return [pltpu.VMEM(s + (width,), part.dtype) for s in sizes]


def dot_rows(a, b, precision=None):
    return lax.dot_general(a, b, (((1,), (1,)), ((), ())), precision=precision, preferred_element_type=F32)


def dot_plain(a, b, precision=None):
    return lax.dot_general(a, b, (((1,), (0,)), ((), ())), precision=precision, preferred_element_type=F32)


def eighths(value):
    return pl.multiple_of(value, 8)


class Exchange:
    def __init__(self, src, dst, sends, recvs, devices):
        self.src, self.dst, self.s, self.r, self.devices = src, dst, sends, recvs, devices
        self.me = flat(*spot())

    def copy(self, i):
        other = lax.rem(self.me + i, self.devices)
        place = (other // 8, other // 4 % 2, other // 2 % 2, other % 2)
        return send(self.src.at[other], self.dst.at[self.me], self.s.at[i], self.r.at[i], place)

    def start(self):
        lax.fori_loop(1, self.devices, lambda i, c: (self.copy(i).start(), c)[1], 0)
        self.dst[self.me] = self.src[self.me]

    def arrive(self):
        lax.fori_loop(1, self.devices, lambda i, c: (self.copy(i).wait_recv(), c)[1], 0)

    def drain(self):
        lax.fori_loop(1, self.devices, lambda i, c: (self.copy(i).wait_send(), c)[1], 0)


def low_lanes(shape):
    return lax.broadcasted_iota(jnp.int32, shape, 1) < 64


def merge_halves(first, second):
    low = low_lanes(first.shape)
    return (
        jnp.where(low, first, pltpu.roll(second, 64, 1)),
        jnp.where(low, pltpu.roll(first, 64, 1), second),
    )


def lane_norm(values, gain, shift):
    center = values - jnp.mean(values, 1, keepdims=True)
    scale_inv = lax.rsqrt(jnp.mean(center * center, 1, keepdims=True) + EPS)
    normal = center * scale_inv
    return normal * gain + shift, normal, scale_inv


def slot_zero(shape):
    return lax.broadcasted_iota(jnp.int32, shape, 1) == 0


def slot_sign(shape):
    return 1.0 - 2.0 * (lax.broadcasted_iota(jnp.int32, shape, 1) % 2).astype(F32)


def slot_weight(shape):
    return jnp.where(slot_zero(shape), 0.5 / shape[1], 1.0 / shape[1])


def column(params, index):
    return params[:, index : index + 1]


def norm_rows(stack, count, chans, width):
    total = None
    for j in range(count):
        tile = stack(j).astype(F32)[:, :128]
        tile = jnp.where(lax.broadcasted_iota(jnp.int32, tile.shape, 1) < chans, tile, 0.0)
        wide = jnp.concatenate([tile, jnp.zeros((tile.shape[0], width - 128), F32)], 1)
        wide = pltpu.roll(wide, j * chans, 1) if j else wide
        total = wide if total is None else total + wide
    return total


RAW = 14


def prepare(in_t, raw, own_in, desk, params, pos_t, mid_t, fil_t, cols):
    gain_one, shift_one, gain_two, shift_two, taps, bias, skip, decay, fil, pos, pos_bias, mid, rate, mid_bias = raw
    chans, order, emb = fil.shape[0], mid.shape[0], pos.shape[0]

    def put(row, values, wide):
        desk[row : row + values.shape[0], :wide] = values.astype(F32)

    desk[...] = jnp.zeros_like(desk)
    for i, ref in enumerate((gain_one, shift_one, gain_two, shift_two)):
        put(i, ref[...], chans)
    norms = jnp.concatenate([desk[:8, :], jnp.zeros((8, in_t.shape[1] - 128), F32)], 1)
    own_in[...] = jnp.concatenate([in_t[...].astype(F32), norms], 0).astype(BF16)
    for i in range(3):
        put(3 * i, taps[i], chans)
    put(9, bias[...], chans)
    put(12, skip[...], chans)
    put(13, decay[...], chans)
    params[...] = desk[...].T[:chans]
    desk[...] = jnp.zeros_like(desk)
    put(0, pos[...], order)
    put(emb, pos_bias[...], order)
    pos_t[...] = desk[...].T[:order, : pos_t.shape[1]]
    desk[...] = jnp.zeros_like(desk)
    put(0, mid[...], order)
    mid_t[...] = desk[...].T[:order, :order]
    desk[...] = jnp.zeros_like(desk)
    put(0, rate[...], order)
    put(1, mid_bias[...], order)
    cols[...] = desk[...].T[:order]
    fil_t[...] = fil[...].astype(F32)


def lane_norm_back(grad_out, normal, scale_inv, gain):
    grad_normal = grad_out * gain
    inner = grad_normal - jnp.mean(grad_normal, 1, keepdims=True)
    inner = inner - normal * jnp.mean(grad_normal * normal, 1, keepdims=True)
    return inner * scale_inv, jnp.sum(grad_out * normal, 0, keepdims=True), jnp.sum(grad_out, 0, keepdims=True)


LATE = (0, 2, 3, 4)


def layer_kernel(dims, *refs):
    line, devices, chans, seqs, block, blocks, width = dims
    (in_t, own_out, own_up, own_down, hidden, cot, feats, table) = refs[:8]
    raw = refs[8 : 8 + RAW]
    refs = refs[8 + RAW :]
    (result, grad_hidden, sum_up, sum_down, sum_out, sum_in, sum_tile, everyone, chan_grads, filter_grad) = refs[:10]
    refs = refs[10:]
    (full_in, full_out, full_up, full_down, mixed_in, norms_ref, steps, conv, spec, total, k_re, k_alt, k_im) = refs[:13]
    (one, cos_one, two, cos_two, params, pos_t, mid_t, fil_t, cols) = refs[13:22]
    (own_in, desk, proj_send, proj_recv, mix_send, kernel_buf, gated, sums) = refs[22:30]
    (w_flat, g_out, g_in, g_tile, resid, value_sum, second_sum, mix_recv, g_spec, g_conv) = refs[30:40]
    (k_sums, g_proj, small) = refs[40:43]
    (gather_send, gather_recv, local, send_a, recv_a, send_b, recv_b, send_c, recv_c, send_d, recv_d) = refs[43:54]
    (sends, recvs, share_send, share_recv) = refs[54:58]
    buffers = refs[58:]
    shards = full_up.shape[0] // line
    hidden_rows = full_up.shape[1]
    chunk = shards * hidden_rows
    gated_grad, g_sums = gated, sums
    prepare(in_t, raw, own_in, desk, params, pos_t, mid_t, fil_t, cols)
    greet_all(devices)
    gathers = [
        Gather(line, shard, full, gather_send.at[p], gather_recv.at[p], local)
        for p, (shard, full) in enumerate(
            ((own_in, full_in), (own_out, full_out), (own_up, full_up), (own_down, full_down))
        )
    ]
    late = LATE

    def tick(now):
        for piece, offset in zip(gathers, late):
            step = now - offset
            if step == 0:
                piece.begin()
            if 1 <= step < line:
                piece.along(step)
            if 1 <= step <= line:
                piece.plane(step - 1)
            if 2 <= step <= line + 1:
                piece.corner(step - 2)

    def filter_part(n, carry):
        sum_one = dot_plain(pos_t[...], feats[n], EXACT)
        phase = column(cols[...], 0) * sum_one
        act_one = jnp.sin(phase)
        one[n] = act_one
        cos_one[n] = jnp.cos(phase)
        phase = column(cols[...], 0) * (dot_plain(mid_t[...], act_one, EXACT) + column(cols[...], 1))
        act_two = jnp.sin(phase)
        two[n] = act_two
        cos_two[n] = jnp.cos(phase)
        lag = lax.broadcasted_iota(jnp.int32, (chans, block), 1) + n * block
        fade = jnp.exp(-lag.astype(F32) * column(params[...], 13))
        kernel_buf[pl.ds(eighths(n * chans), chans), :] = dot_plain(fil_t[...], act_two, EXACT) * fade
        return carry

    def filters(first, last):
        lax.fori_loop(first, last, filter_part, 0)

    def kernel_spectrum():
        ker = dot_plain(kernel_buf[...], table[...], EXACT)
        before = jnp.concatenate([jnp.zeros((chans, 2 * block), F32), ker[:-chans]], 0)
        sign = slot_sign((chans * blocks, block))
        real = ker[:, :block] + sign * before[:, :block]
        imag = ker[:, block:] + sign * before[:, block:]
        zero = slot_zero(real.shape)
        k_re[...] = real
        k_alt[...] = jnp.where(zero, imag, real)
        k_im[...] = jnp.where(zero, 0.0, imag)

    tick(0)
    filters(0, blocks // 4)
    tick(1)
    filters(blocks // 4, blocks // 2)
    tick(2)
    filters(blocks // 2, 3 * blocks // 4)
    tick(3)
    filters(3 * blocks // 4, blocks)
    tick(4)
    kernel_spectrum()
    tick(5)
    gathers[0].finish()

    in_rows = full_in.shape[1]
    norms = norm_rows(lambda j: full_in[j, in_rows - 8 :], devices, chans, width)
    norms_ref[...] = norms
    normed, _, _ = lane_norm(hidden[...].astype(F32), norms[0:1], norms[1:2])
    projected = dot_rows(full_in[...].reshape(devices * in_rows, width), normed.astype(BF16))
    projected = projected.reshape(devices, in_rows, 128)
    for j in range(devices):
        for i in range(3):
            unit = 3 * j + i
            proj_send[unit % devices, unit // devices] = projected[j, i * chans : (i + 1) * chans].astype(BF16)
    moved = Exchange(proj_send, proj_recv, send_a, recv_a, devices)
    moved.start()
    tick(6)
    moved.arrive()

    def assemble(j, carry):
        lanes = pl.ds(pl.multiple_of(j * 128, 128), 128)
        for p in range(3):
            pair = merge_halves(proj_recv[2 * j, p].astype(F32), proj_recv[2 * j + 1, p].astype(F32))
            for s in range(seqs):
                steps[p, s, :, lanes] = pair[s]
        return carry

    lax.fori_loop(0, devices // 2, assemble, 0)
    length = block * blocks
    for s in range(seqs):
        for c in range(0, chans, 8):
            spots = lax.broadcasted_iota(jnp.int32, (8, length), 1)
            parts = []
            for p in range(3):
                x = steps[p, s, c : c + 8, :]
                local_params = params[c : c + 8, :]
                value = column(local_params, 9 + p) + column(local_params, p) * x
                for i in (1, 2):
                    value += column(local_params, 3 * i + p) * jnp.where(spots < i, 0.0, pltpu.roll(x, i, 1))
                parts.append(value)
            product = parts[1] * parts[2]
            for n in range(blocks):
                at_rows = (n * seqs + s) * chans + c
                lanes = slice(n * block, (n + 1) * block)
                gated[at_rows : at_rows + 8, :] = product[:, lanes]
                for p in range(3):
                    conv[p, at_rows : at_rows + 8, :] = parts[p][:, lanes]
    tick(7)

    spec[...] = dot_plain(gated[...], table[...], EXACT)
    weight = slot_weight((chans, block))

    def output_block(m, carry):
        def add(n, acc):
            at_kernel = pl.ds(eighths((m - n) * chans), chans)
            kr, ka, ki = k_re[at_kernel, :], k_alt[at_kernel, :], k_im[at_kernel, :]
            result = []
            for s in range(seqs):
                at_signal = pl.ds(eighths((n * seqs + s) * chans), chans)
                re, im = spec[at_signal, :block], spec[at_signal, block:]
                result.append(acc[2 * s] + re * kr - im * ki)
                result.append(acc[2 * s + 1] + re * ki + im * ka)
            return tuple(result)

        acc = lax.fori_loop(0, m + 1, add, tuple(jnp.zeros((chans, block), F32) for _ in range(2 * seqs)))
        for s in range(seqs):
            at_signal = pl.ds(eighths((m * seqs + s) * chans), chans)
            sums[at_signal, :block] = acc[2 * s] * weight
            sums[at_signal, block:] = acc[2 * s + 1] * weight
        return carry

    lax.fori_loop(0, blocks, output_block, 0)
    tick(8)
    total[...] = dot_rows(sums[...], table[...], EXACT)

    def mix(m, carry):
        mixed = []
        for s in range(seqs):
            at_signal = pl.ds(eighths((m * seqs + s) * chans), chans)
            value = total[at_signal, :] + column(params[...], 12) * gated[at_signal, :]
            total[at_signal, :] = value
            mixed.append(value * conv[0, at_signal, :])
        for h in range(block // 128):
            pair = merge_halves(*(v[:, h * 128 : (h + 1) * 128] for v in mixed))
            for q in range(2):
                mix_send[m * (block // 64) + 2 * h + q] = pair[q].astype(BF16)
        return carry

    lax.fori_loop(0, blocks, mix, 0)
    mix_home = Exchange(mix_send, mixed_in, send_b, recv_b, devices)
    mix_home.start()
    tick(9)
    for piece in gathers[1:]:
        piece.finish()
    mix_home.arrive()
    for piece in gathers:
        piece.drain()
    moved.drain()
    mix_home.drain()

    parts = (full_up, full_down, g_out, g_in, g_tile)
    outs = (sum_up, sum_down, sum_out, sum_in, sum_tile)
    pieces = [
        Reduce(line, parts[p], outs[p], *buffers[p * BUFFERS : (p + 1) * BUFFERS], sends.at[p], recvs.at[p])
        for p in range(5)
    ]

    z = lax.axis_index("blk") // 2
    half = line // 2
    flip = z // half
    mirror = z + flip * (line - 1 - 2 * z)

    def visit(i):
        near = half - 1 - mirror if i < line - 1 else mirror
        place = line - 1 - i if i < half else near
        return place + flip * (line - 1 - 2 * place)

    def fold(group, slot):
        for piece in group:
            if slot < line:
                piece.corner(visit(slot), slot >= half)
            if half < slot <= line:
                piece.plane(visit(slot - 1))
            if 2 <= slot <= line + 1:
                piece.along(visit(slot - 2), slot - 2 == line - 1)

    gain_two, shift_two = norms_ref[2:3], norms_ref[3:4]
    mixed = mixed_in[...].astype(F32).reshape(width, 128).T.astype(BF16)
    w_flat[...] = full_out[...].astype(F32).reshape(width, width).astype(BF16)
    resid[...] = hidden[...].astype(F32) + dot_rows(mixed, w_flat[...])
    second, normal_two, inv_two = lane_norm(resid[...], gain_two, shift_two)
    second = second.astype(BF16)
    value_sum[...] = jnp.zeros_like(value_sum)
    second_sum[...] = jnp.zeros_like(second_sum)

    for i in range(line):
        where_to = pl.ds(visit(i) * shards, shards)
        up = full_up[where_to].reshape(chunk, width)
        down = full_down[where_to].reshape(chunk, width)
        active, slope = gelu_parts(dot_rows(up, second))
        active = active.astype(BF16)
        grad_upper = (dot_rows(down, cot[...]) * slope).astype(BF16)
        value_sum[...] += dot_plain(active.astype(F32).T.astype(BF16), down)
        second_sum[...] += dot_plain(grad_upper.astype(F32).T.astype(BF16), up)
        full_down[where_to] = dot_plain(active, cot[...]).astype(BF16).reshape(shards, hidden_rows, width)
        full_up[where_to] = dot_plain(grad_upper, second).astype(BF16).reshape(shards, hidden_rows, width)
        for piece in pieces[:2]:
            piece.begin(visit(i))
        if i:
            fold(pieces[:2], i - 1)
    result[...] = (resid[...] + value_sum[...]).astype(BF16)
    resid_term, grad_gain_two, grad_shift_two = lane_norm_back(second_sum[...], normal_two, inv_two, gain_two)
    resid[...] = cot[...].astype(F32) + resid_term
    grad_mixed = dot_plain(resid[...].astype(BF16), w_flat[...])
    mix_send[...] = grad_mixed.T.reshape(devices, chans, 128).astype(BF16)
    grad_mix = Exchange(mix_send, mix_recv, send_c, recv_c, devices)
    grad_mix.start()
    grad_branch = resid[...].T.astype(BF16)
    g_out[...] = dot_plain(grad_branch, mixed).reshape(devices, chans, width).astype(BF16)
    for i in range(line):
        pieces[2].begin(visit(i))
    fold(pieces[:2], line - 1)
    fold(pieces[2:3], 0)
    grad_mix.arrive()

    weight = slot_weight((chans, block))
    skip = column(params[...], 12)
    per_block = block // 64

    def arrange(m, carry):
        for h in range(block // 128):
            source = m * per_block + 2 * h
            pair = merge_halves(mix_recv[source].astype(F32), mix_recv[source + 1].astype(F32))
            lanes = slice(h * 128, (h + 1) * 128)
            for s in range(seqs):
                at_rows = pl.ds(eighths((m * seqs + s) * chans), chans)
                place = pl.ds(pl.multiple_of(m * block + h * 128, 128), 128)
                g_conv[0, s, :, place] = pair[s] * total[at_rows, lanes]
                grad = pair[s] * conv[0, at_rows, lanes]
                gated_grad[at_rows, lanes] = grad
                carry = carry + grad * conv[1, at_rows, lanes] * conv[2, at_rows, lanes]
        return carry

    skip_sum = lax.fori_loop(0, blocks, arrange, jnp.zeros((chans, 128), F32))
    g_spec[...] = dot_plain(gated_grad[...], table[...], EXACT)
    fold(pieces[2:3], 1)

    def signal_block(n, carry):
        def add(m, acc):
            at_kernel = pl.ds(eighths((m - n) * chans), chans)
            kr, ka, ki = k_re[at_kernel, :], k_alt[at_kernel, :], k_im[at_kernel, :]
            out = []
            for s in range(seqs):
                at_rows = pl.ds(eighths((m * seqs + s) * chans), chans)
                re, im = g_spec[at_rows, :block], g_spec[at_rows, block:]
                out.append(acc[2 * s] + re * kr + im * ki)
                out.append(acc[2 * s + 1] + im * ka - re * ki)
            return tuple(out)

        acc = lax.fori_loop(n, blocks, add, tuple(jnp.zeros((chans, block), F32) for _ in range(2 * seqs)))
        for s in range(seqs):
            at_rows = pl.ds(eighths((n * seqs + s) * chans), chans)
            g_sums[at_rows, :block] = acc[2 * s] * weight
            g_sums[at_rows, block:] = acc[2 * s + 1] * weight
        return carry

    lax.fori_loop(0, blocks, signal_block, 0)
    g_sums[:, :block] = dot_rows(g_sums[...], table[...], EXACT)

    def gate_grads(m, carry):
        for s in range(seqs):
            at_rows = pl.ds(eighths((m * seqs + s) * chans), chans)
            place = pl.ds(pl.multiple_of(m * block, block), block)
            grad = g_sums[at_rows, :block] + skip * gated_grad[at_rows, :]
            g_conv[1, s, :, place] = grad * conv[2, at_rows, :]
            g_conv[2, s, :, place] = grad * conv[1, at_rows, :]
        return carry

    lax.fori_loop(0, blocks, gate_grads, 0)
    fold(pieces[:2], line)
    fold(pieces[2:3], 2)

    length = block * blocks
    for c in range(0, chans, 8):
        col = lax.broadcasted_iota(jnp.int32, (8, 128), 1)
        spots = lax.broadcasted_iota(jnp.int32, (8, length), 1)
        found = jnp.where(col == 12, jnp.sum(skip_sum[c : c + 8], 1, keepdims=True), 0.0)
        local_params = params[c : c + 8, :]
        for p in range(3):
            for s in range(seqs):
                grad = g_conv[p, s, c : c + 8, :]
                x = steps[p, s, c : c + 8, :]
                value = jnp.zeros_like(grad)
                for i in range(3):
                    later = jnp.where(spots < length - i, pltpu.roll(grad, length - i, 1), 0.0) if i else grad
                    value += column(local_params, 3 * i + p) * later
                    found += jnp.where(col == 3 * i + p, jnp.sum(later * x, 1, keepdims=True), 0.0)
                found += jnp.where(col == 9 + p, jnp.sum(grad, 1, keepdims=True), 0.0)
                g_conv[p, s, c : c + 8, :] = value
        chan_grads[c : c + 8, :] = found

    def pack(j, carry):
        lanes = pl.ds(pl.multiple_of(j * 128, 128), 128)
        for p in range(3):
            pair = merge_halves(g_conv[p, 0, :, lanes], g_conv[p, 1, :, lanes])
            proj_send[2 * j, p] = pair[0].astype(BF16)
            proj_send[2 * j + 1, p] = pair[1].astype(BF16)
        return carry

    lax.fori_loop(0, devices // 2, pack, 0)
    home = Exchange(proj_send, proj_recv, send_d, recv_d, devices)
    home.start()
    fold(pieces[:2], line + 1)
    fold(pieces[2:3], 3)

    def kernel_block(d, carry):
        def add(n, acc):
            real, imag = acc
            for s in range(seqs):
                at_signal = pl.ds(eighths((n * seqs + s) * chans), chans)
                at_grad = pl.ds(eighths(((n + d) * seqs + s) * chans), chans)
                s_re, s_im = spec[at_signal, :block], spec[at_signal, block:]
                g_re, g_im = g_spec[at_grad, :block], g_spec[at_grad, block:]
                zero = slot_zero((chans, block))
                same, other = g_re * s_re, g_im * s_im
                real = real + jnp.where(zero, same, same + other)
                imag = imag + jnp.where(zero, other, g_im * s_re - g_re * s_im)
            return real, imag

        empty = jnp.zeros((chans, block), F32)
        real, imag = lax.fori_loop(0, blocks - d, add, (empty, empty))
        at_kernel = pl.ds(eighths(d * chans), chans)
        k_sums[at_kernel, :block] = real
        k_sums[at_kernel, block:] = imag
        return carry

    lax.fori_loop(0, blocks, kernel_block, 0)
    after = jnp.concatenate([k_sums[chans:, :], jnp.zeros((chans, 2 * block), F32)], 0)
    shape = (chans * blocks, block)
    sign, scale = slot_sign(shape), slot_weight(shape)
    k_sums[:, :block] = (k_sums[:, :block] + sign * after[:, :block]) * scale
    k_sums[:, block:] = (k_sums[:, block:] + sign * after[:, block:]) * scale
    k_sums[:, :block] = dot_rows(k_sums[...], table[...], EXACT)
    fold(pieces[2:3], 4)

    order = pos_t.shape[0]
    emb = pos_t.shape[1]
    freq = column(cols[...], 0)

    def filter_block(n, carry):
        grad_fil, grad_pos, grad_mid, grad_bias = carry
        lag = lax.broadcasted_iota(jnp.int32, (chans, block), 1) + n * block
        fade = jnp.exp(-lag.astype(F32) * column(params[...], 13))
        grad = k_sums[pl.ds(eighths(n * chans), chans), :block] * fade
        grad_fil = grad_fil + dot_rows(grad, two[n], EXACT)
        grad_two = dot_plain(fil_t[...].T, grad, EXACT) * cos_two[n] * freq
        grad_mid = grad_mid + dot_rows(one[n], grad_two, EXACT)
        grad_bias = grad_bias + dot_rows(jnp.ones((8, block), F32), grad_two, EXACT)
        grad_one = dot_plain(mid_t[...].T, grad_two, EXACT) * cos_one[n] * freq
        grad_pos = grad_pos + dot_rows(feats[n], grad_one, EXACT)
        return grad_fil, grad_pos, grad_mid, grad_bias

    zeros = [jnp.zeros(s, F32) for s in ((chans, order), (emb, order), (order, order), (8, order))]
    grad_fil, grad_pos, grad_mid, grad_bias = lax.fori_loop(0, blocks, filter_block, tuple(zeros))
    filter_grad[...] = grad_fil
    rate_bias = cols[...].T
    grad_rate = jnp.sum(pos_t[...].T * grad_pos, 0, keepdims=True) + jnp.sum(mid_t[...].T * grad_mid, 0, keepdims=True)
    grad_rate = (grad_rate + rate_bias[1:2] * grad_bias[:1]) / rate_bias[0:1]
    small[...] = jnp.zeros_like(small)
    small[:emb, :order] = grad_pos
    small[emb : emb + order, :order] = grad_mid
    picked = lax.broadcasted_iota(jnp.int32, (8, order), 0)
    small[emb + order : emb + order + 8, :order] = jnp.where(
        picked == 0, grad_bias, jnp.where(picked == 1, grad_rate, 0.0)
    )
    fold(pieces[2:3], 5)

    gain_one, shift_one = norms_ref[0:1], norms_ref[1:2]
    normed, normal_one, inv_one = lane_norm(hidden[...].astype(F32), gain_one, shift_one)
    normed = normed.astype(BF16)
    g_proj[...] = jnp.zeros_like(g_proj)
    home.arrive()
    for j in range(devices):
        for i in range(3):
            unit = 3 * j + i
            at_rows = slice(j * in_rows + i * chans, j * in_rows + (i + 1) * chans)
            g_proj[at_rows, :] = proj_recv[unit % devices, unit // devices].astype(F32)
    for i in range(line):
        zo = visit(i)
        group = shards * in_rows
        grads = dot_plain(g_proj[pl.ds(eighths(zo * group), group), :].astype(BF16), normed)
        g_in[pl.ds(zo * shards, shards)] = grads.reshape(shards, in_rows, width)[:, : 3 * chans].astype(BF16)
        pieces[3].begin(zo)
    fold(pieces[3:4], 0)
    grad_normed = dot_plain(g_proj[...].T.astype(BF16), full_in[...].reshape(devices * in_rows, width))
    input_term, grad_gain_one, grad_shift_one = lane_norm_back(grad_normed, normal_one, inv_one, gain_one)
    grad_hidden[...] = (resid[...] + input_term).astype(BF16)
    norm_grads = jnp.concatenate(
        [grad_gain_one, grad_shift_one, grad_gain_two, grad_shift_two, jnp.zeros((4, width), F32)], 0
    )
    for j in range(devices):
        turned = pltpu.roll(norm_grads, width - j * chans, 1) if j else norm_grads
        g_tile[j, 0:4, :] = turned[0:4, :128]
        g_tile[j, 4:8, :] = small[4 * j : 4 * j + 4, :]
    for i in range(line):
        pieces[4].begin(visit(i))
    fold(pieces[4:5], 0)
    for step in range(1, line + 2):
        fold(pieces[3:], step)

    mine = flat(*spot())

    def share(i):
        other = lax.rem(mine + i, devices)
        place = (other // 8, other // 4 % 2, other // 2 % 2, other % 2)
        return send(sum_tile, everyone.at[mine], share_send.at[i], share_recv.at[i], place)

    keep = pltpu.make_async_copy(sum_tile, everyone.at[mine], local)
    keep.start()
    lax.fori_loop(1, devices, lambda i, c: (share(i).start(), c)[1], 0)
    for piece in pieces:
        piece.drain()
    grad_mix.drain()
    home.drain()
    keep.wait()

    def settle(i, carry):
        share(i).wait_recv()
        share(i).wait_send()
        return carry

    lax.fori_loop(1, devices, settle, 0)


def layer(shards, hidden, cot, feats, table, raw, dims):
    line, devices, chans, seqs, block, blocks, width = dims
    order = raw[-1].shape[1]
    rows, tokens = blocks * seqs * chans, hidden.shape[0]
    in_rows, hidden_rows = shards[0].shape[0] + 8, shards[2].shape[0]
    shape, buffer, dma = jax.ShapeDtypeStruct, pltpu.VMEM, pltpu.SemaphoreType.DMA
    vmem = pl.BlockSpec(memory_space=pltpu.VMEM)
    tile = (devices, 8, 128)
    outs = [
        shape((tokens, width), BF16),
        shape((tokens, width), BF16),
        shape((hidden_rows, width), F32),
        shape((hidden_rows, width), F32),
        shape((chans, width), F32),
        shape((3 * chans, width), F32),
        shape(tile[1:], F32),
        shape(tile, F32),
        shape((chans, 128), F32),
        shape((chans, order), F32),
    ]
    scratch = [buffer((devices, r, width), BF16) for r in (in_rows, chans, hidden_rows, hidden_rows)]
    scratch += [
        buffer((devices, chans, 128), BF16),
        buffer((8, width), F32),
        buffer((3, seqs, chans, block * blocks), F32),
        buffer((3, rows, block), F32),
        buffer((rows, 2 * block), F32),
        buffer((rows, block), F32),
    ]
    scratch += [buffer((blocks * chans, block), F32)] * 3 + [buffer((blocks, order, block), F32)] * 4
    scratch += [buffer((chans, 128), F32), buffer((order, feats.shape[1]), F32), buffer((order, order), F32)]
    scratch += [buffer((chans, order), F32), buffer((order, 128), F32)]
    scratch += [
        buffer((in_rows, width), BF16),
        buffer((128, 128), F32),
        buffer((devices, 3, chans, 128), BF16),
        buffer((devices, 3, chans, 128), BF16),
        buffer((devices, chans, 128), BF16),
        buffer((blocks * chans, block), F32),
        buffer((rows, block), F32),
        buffer((rows, 2 * block), F32),
        buffer((width, width), BF16),
        buffer((devices, chans, width), BF16),
        buffer((devices, 3 * chans, width), BF16),
        buffer(tile, F32),
        buffer((tokens, width), F32),
        buffer((tokens, width), F32),
        buffer((tokens, width), F32),
        buffer((devices, chans, 128), BF16),
        buffer((rows, 2 * block), F32),
        buffer((3, seqs, chans, block * blocks), F32),
        buffer((blocks * chans, 2 * block), F32),
        buffer((devices * in_rows, 128), F32),
        buffer((4 * devices, 128), F32),
    ]
    scratch += [dma((4, 8, line * 4)), dma((4, 8, line * 4)), dma] + [dma((devices,))] * 8
    scratch += [dma((5, 8, line * 4)), dma((5, 8, line * 4)), dma((devices,)), dma((devices,))]
    parts = [shape((devices, r, width), BF16) for r in (hidden_rows, hidden_rows, chans, 3 * chans)] + [shape(tile, F32)]
    scratch += [b for part in parts for b in reduce_scratch(line, part)]
    operands = [*shards, hidden, cot, feats, table, *raw]
    return pl.pallas_call(
        functools.partial(layer_kernel, dims),
        name="layer",
        out_shape=outs,
        in_specs=[vmem] * len(operands),
        out_specs=[vmem] * len(outs),
        scratch_shapes=scratch,
        compiler_params=pltpu.CompilerParams(collective_id=0, has_side_effects=True, vmem_limit_bytes=KERNEL_VMEM),
    )(*operands)


def finish_kernel(emb, order, *refs):
    (result, grad_hidden, up, down, out, inp, tile, everyone, chan_grads, filter_grad) = refs[:10]
    outs, desk = refs[10:-1], refs[-1]
    chans = chan_grads.shape[0]
    for target, source in zip(outs[:7], (result, grad_hidden, up, down, out, inp, filter_grad)):
        target[...] = source[...]
    taps, bias, skip, *gains = outs[7:14]
    desk[...] = jnp.zeros_like(desk)
    desk[:chans, :] = chan_grads[...]
    turned = desk[...].T
    for i in range(3):
        taps[i] = turned[3 * i : 3 * i + 3, :chans]
    bias[...] = turned[9:12, :chans]
    skip[...] = turned[12:13, :chans]
    for i, gain in enumerate(gains):
        gain[...] = tile[i : i + 1, :chans]
    for j in range(everyone.shape[0]):
        desk[4 * j : 4 * j + 4, :] = everyone[j, 4:8, :]
    pos, pos_bias, mid, mid_bias, rate = outs[14:]
    after = emb + 1 + -(emb + 1) % 8
    pos[...] = desk[:emb, :order]
    pos_bias[...] = desk[emb : emb + 1, :order]
    mid[...] = desk[after : after + order, :order]
    mid_bias[...] = desk[after + order : after + order + 1, :order]
    rate[...] = desk[after + order + 1 : after + order + 2, :order]


def finish(parts, pos_shape):
    emb, order = pos_shape
    chans = parts[8].shape[0]
    shape = jax.ShapeDtypeStruct
    vmem = pl.BlockSpec(memory_space=pltpu.VMEM)
    outs = [shape(p.shape, p.dtype) for p in parts[:6]] + [shape(parts[9].shape, F32)]
    outs += [shape((3, 3, chans), F32), shape((3, chans), F32)] + [shape((1, chans), F32)] * 5
    outs += [shape((emb, order), F32), shape((1, order), F32), shape((order, order), F32)]
    outs += [shape((1, order), F32)] * 2
    return pl.pallas_call(
        functools.partial(finish_kernel, emb, order),
        name="finish",
        out_shape=outs,
        in_specs=[vmem] * len(parts),
        out_specs=[vmem] * len(outs),
        scratch_shapes=[pltpu.VMEM((128, 128), F32)],
    )(*parts)


def shards_paired(
    hidden_in,
    cotangent,
    mixer_input_weight,
    mixer_output_weight,
    feedforward_up,
    feedforward_down,
    first_gain,
    first_shift,
    second_gain,
    second_shift,
    short_taps,
    short_bias,
    skip_scale,
    filter_out,
    pos_weight,
    pos_bias,
    mid_weight,
    mid_bias,
    sine_freq,
    decay_rate,
):
    devices = lax.axis_size(AXES)
    micro, seq_count, tok, width = hidden_in.shape
    seqs = micro * seq_count
    tokens = seqs * tok
    length = tok * devices
    chans = width // devices
    block = tok * lax.axis_size("chan")
    blocks = length // block

    line = devices // 8
    def row(vector):
        return vector.reshape(1, -1)

    shards = [mixer_input_weight.T, mixer_output_weight.T, feedforward_up.T, feedforward_down]
    raw = [row(v) for v in (first_gain, first_shift, second_gain, second_shift)]
    raw += [short_taps, short_bias, row(skip_scale), row(decay_rate), filter_out.T]
    raw += [pos_weight, row(pos_bias), mid_weight, row(sine_freq), row(mid_bias)]
    hidden = hidden_in.reshape(tokens, width)
    features, table = jnp.asarray(feature_blocks(length, block)), jnp.asarray(fixed_table(block))
    dims = (line, devices, chans, seqs, block, blocks, width)
    parts = layer(shards, hidden, cotangent.reshape(tokens, width), features, table, raw, dims)
    outs = finish(parts, pos_weight.shape)
    result, grad_hidden, up, down, out, inp, filter_grad, taps, bias, skip, *rest = outs
    gains, (pos, pos_bias, mid, mid_bias, rate) = rest[:4], rest[4:]
    return (
        result.reshape(hidden_in.shape),
        grad_hidden.reshape(hidden_in.shape),
        inp.T,
        out.T,
        up.T,
        down,
        *[g.reshape(-1) for g in gains],
        taps,
        bias,
        skip.reshape(-1),
        filter_grad.T,
        pos,
        pos_bias.reshape(-1),
        mid,
        mid_bias.reshape(-1),
        rate.reshape(-1),
    )


def shards(
    hidden_in,
    cotangent,
    mixer_input_weight,
    mixer_output_weight,
    feedforward_up,
    feedforward_down,
    first_gain,
    first_shift,
    second_gain,
    second_shift,
    short_taps,
    short_bias,
    skip_scale,
    filter_out,
    pos_weight,
    pos_bias,
    mid_weight,
    mid_bias,
    sine_freq,
    decay_rate,
):
    devices = lax.axis_size(AXES)
    micro, seq_count, tok, width = hidden_in.shape
    seqs = micro * seq_count
    tokens = seqs * tok
    length = tok * devices
    chans = width // devices
    block = tok * lax.axis_size("chan")
    blocks = length // block

    norms = jnp.stack([first_gain, first_shift, second_gain, second_shift])
    own = [mixer_input_weight.T, feedforward_up.T, feedforward_down, mixer_output_weight.T]
    full = [lax.all_gather(shard, AXES, axis=0, tiled=True) for shard in own]
    norms = lax.all_gather(norms, AXES, axis=1, tiled=True)
    weight_in, weight_up, weight_down, weight_out = full
    norms = norms.astype(F32)
    gain_one, shift_one, gain_two, shift_two = norms[0], norms[1], norms[2], norms[3]

    freq = sine_freq.astype(F32)
    w_pos, w_mid, w_fil = pos_weight.astype(F32), mid_weight.astype(F32), filter_out.astype(F32)
    lags, features, first_sum, first_act, second_sum, second_act = filter_hidden(
        length, w_pos, pos_bias.astype(F32), w_mid, mid_bias.astype(F32), freq
    )
    decay = jnp.exp(-lags[None, :] * decay_rate.astype(F32)[:, None])
    kernel = contract(w_fil, second_act, 0, 0, EXACT) * decay
    table = block_table(block)
    sign = 1.0 - 2.0 * (lax.iota(jnp.int32, block) % 2).astype(F32)
    ker_re, ker_im = to_spectrum(kernel.reshape(chans, blocks, block), table)

    def with_previous(spec):
        before = jnp.concatenate([jnp.zeros_like(spec[:, :1]), spec[:, :-1]], 1)
        return spec + sign * before

    k_re, k_alt, k_im = packed_kernel(with_previous(ker_re), with_previous(ker_im))

    values = hidden_in.reshape(tokens, width).astype(F32)
    normed, normal_one, inv_one = layer_norm(values, gain_one, shift_one)
    normed = normed.astype(BF16)
    projected = contract(weight_in, normed, 1, 1).astype(BF16)
    projected = projected.reshape(3, devices, chans, tokens).transpose(1, 0, 2, 3)
    arrived = exchange(projected)

    def by_sequence(values):
        parts = values.shape[1]
        values = values.reshape(devices, parts, chans, seqs, tok)
        return values.transpose(1, 3, 2, 0, 4).reshape(parts, seqs, chans, length)

    def by_device(values):
        parts = values.shape[0]
        values = values.reshape(parts, seqs, chans, devices, tok)
        return values.transpose(3, 0, 2, 1, 4).reshape(devices, parts, chans, tokens)

    steps = by_sequence(arrived).astype(F32)
    taps = short_taps.astype(F32)[:, :, None, :, None]
    conv = short_bias.astype(F32)[:, None, :, None]
    for i in range(3):
        conv = conv + taps[i] * delayed(steps, i)
    gate_out, gate_in, signal = conv[0], conv[1], conv[2]
    gated = signal * gate_in
    sig_re, sig_im = to_spectrum(gated.reshape(seqs, chans, blocks, block), table)

    def shifted_sum(make):
        total = None
        for d in range(blocks):
            term = make(d)
            total = term if total is None else tuple(a + b for a, b in zip(total, term))
        return total

    def ahead(x, d):
        return x if d == 0 else jnp.pad(x[:, :, :-d], ((0, 0), (0, 0), (d, 0), (0, 0)))

    def back(x, d):
        return x if d == 0 else jnp.pad(x[:, :, d:], ((0, 0), (0, 0), (0, d), (0, 0)))

    def forward_term(d):
        re, im = ahead(sig_re, d), ahead(sig_im, d)
        kr, ka, ki = k_re[:, d : d + 1], k_alt[:, d : d + 1], k_im[:, d : d + 1]
        return re * kr - im * ki, re * ki + im * ka

    out_re, out_im = shifted_sum(forward_term)
    long_out = from_spectrum(out_re, out_im, table).reshape(seqs, chans, length)
    skip = skip_scale.astype(F32)[None, :, None]
    long_total = long_out + skip * gated
    mixed = (long_total * gate_out).astype(BF16)
    mixed = exchange(by_device(mixed[None])).reshape(width, tokens)

    resid = values + contract(mixed, weight_out, 0, 1)
    second, normal_two, inv_two = layer_norm(resid, gain_two, shift_two)
    second = second.astype(BF16)
    upper = contract(second, weight_up, 1, 1)
    active, slope = gelu_parts(upper)
    active = active.astype(BF16)
    result = resid + contract(active, weight_down, 1, 0)

    cot = cotangent.reshape(tokens, width)
    grad_down = contract(active, cot, 0, 0)
    grad_upper = (contract(cot, weight_down, 1, 1) * slope).astype(BF16)
    grad_up = contract(grad_upper, second, 0, 0)
    grad_second = contract(grad_upper, weight_up, 1, 0)
    resid_term, grad_gain_two, grad_shift_two = layer_norm_back(grad_second, normal_two, inv_two, gain_two)
    grad_resid = cot.astype(F32) + resid_term
    grad_branch = grad_resid.astype(BF16)
    grad_out_w = contract(grad_branch, mixed, 0, 1)
    grad_mixed = contract(weight_out, grad_branch, 0, 1).astype(BF16)
    grad_mixed = exchange(grad_mixed.reshape(devices, 1, chans, tokens))
    grad_mixed = by_sequence(grad_mixed)[0].astype(F32)

    grad_gate_out = grad_mixed * long_total
    grad_long = grad_mixed * gate_out
    grad_skip = jnp.sum(grad_long * gated, (0, 2))
    gl_re, gl_im = to_spectrum(grad_long.reshape(seqs, chans, blocks, block), table)

    def signal_term(d):
        re, im = back(gl_re, d), back(gl_im, d)
        kr, ka, ki = k_re[:, d : d + 1], k_alt[:, d : d + 1], k_im[:, d : d + 1]
        return re * kr + im * ki, im * ka - re * ki

    gg_re, gg_im = shifted_sum(signal_term)
    grad_gated = from_spectrum(gg_re, gg_im, table).reshape(seqs, chans, length) + skip * grad_long

    first_slot = lax.iota(jnp.int32, block) == 0
    kg_re, kg_im = [], []
    for d in range(blocks):
        s_re, s_im = sig_re[:, :, : blocks - d], sig_im[:, :, : blocks - d]
        g_re, g_im = gl_re[:, :, d:], gl_im[:, :, d:]
        same, other = g_re * s_re, g_im * s_im
        kg_re.append(jnp.sum(jnp.where(first_slot, same, same + other), (0, 2)))
        kg_im.append(jnp.sum(jnp.where(first_slot, other, g_im * s_re - g_re * s_im), (0, 2)))
    kg_re, kg_im = jnp.stack(kg_re, 1), jnp.stack(kg_im, 1)

    def with_next(spec):
        after = jnp.concatenate([spec[:, 1:], jnp.zeros_like(spec[:, :1])], 1)
        return spec + sign * after

    grad_kernel = from_spectrum(with_next(kg_re), with_next(kg_im), table).reshape(chans, length)

    grad_conv = jnp.stack([grad_gate_out, grad_gated * signal, grad_gated * gate_in])
    grad_bias = jnp.sum(grad_conv, (1, 3))
    grad_taps = jnp.stack([jnp.sum(grad_conv * delayed(steps, i), (1, 3)) for i in range(3)])
    grad_steps = taps[0] * grad_conv
    for i in (1, 2):
        grad_steps = grad_steps + taps[i] * advanced(grad_conv, i)
    grad_proj = exchange(by_device(grad_steps.astype(BF16)))
    grad_proj = grad_proj.transpose(1, 0, 2, 3).reshape(3 * width, tokens)

    fade = grad_kernel * decay
    grad_filter = contract(second_act, fade, 1, 1, EXACT)
    grad_two = contract(w_fil, fade, 1, 0, EXACT) * jnp.cos(freq[:, None] * second_sum)
    grad_freq = jnp.sum(grad_two * second_sum, 1)
    grad_two = grad_two * freq[:, None]
    grad_mid = contract(first_act, grad_two, 1, 1, EXACT)
    grad_one = contract(w_mid, grad_two, 1, 0, EXACT) * jnp.cos(freq[:, None] * first_sum)
    grad_freq = grad_freq + jnp.sum(grad_one * first_sum, 1)
    grad_one = grad_one * freq[:, None]
    grad_pos = contract(features, grad_one, 1, 1, EXACT)
    small = jnp.concatenate(
        [grad_pos, jnp.sum(grad_one, 1)[None], grad_mid, jnp.sum(grad_two, 1)[None], grad_freq[None]]
    )
    emb, order = pos_weight.shape

    grad_in = contract(grad_proj, normed, 1, 0)
    grad_normed = contract(grad_proj, weight_in, 0, 0)
    input_term, grad_gain_one, grad_shift_one = layer_norm_back(grad_normed, normal_one, inv_one, gain_one)
    grad_hidden = (grad_resid + input_term).astype(BF16)

    norm_grads = jnp.stack([grad_gain_one, grad_shift_one, grad_gain_two, grad_shift_two])
    sums = [grad_in, grad_up, grad_down, grad_out_w]
    sums = [
        lax.psum_scatter(g.astype(BF16), AXES, scatter_dimension=0, tiled=True).astype(F32) for g in sums
    ]
    norm_grads = lax.psum_scatter(norm_grads, AXES, scatter_dimension=1, tiled=True)
    small = lax.psum(small, AXES)
    return (
        result.astype(BF16).reshape(hidden_in.shape),
        grad_hidden.reshape(hidden_in.shape),
        sums[0].T,
        sums[3].T,
        sums[1].T,
        sums[2],
        norm_grads[0],
        norm_grads[1],
        norm_grads[2],
        norm_grads[3],
        grad_taps,
        grad_bias,
        grad_skip,
        grad_filter,
        small[:emb],
        small[emb],
        small[emb + 1 : emb + 1 + order],
        small[emb + 1 + order],
        small[emb + 2 + order],
    )


def solution(mesh):
    paired = mesh.shape["chan"] == 4 and mesh.shape["blk"] == 8
    rows, spread, tokens = P(AXES), P(None, AXES), P(None, None, AXES, None)
    params = (rows, rows, rows, rows, P(None, None, AXES), spread, rows, spread, P(), P(), P(), P(), P())
    return jax.shard_map(
        shards_paired if paired else shards,
        mesh=mesh,
        in_specs=(tokens, tokens, spread, spread, spread, P(AXES, None)) + params + (rows,),
        out_specs=(tokens, tokens, spread, spread, spread, P(AXES, None)) + params,
        check_vma=False,
    )
```

```python
import functools
import math

import jax
import jax.numpy as jnp
import numpy as np
from jax import lax
from jax.experimental import pallas as pl
from jax.experimental.pallas import tpu as pltpu
from jax.sharding import PartitionSpec as P

EPS = 1e-05
BANDS = 16
EXACT = lax.Precision.HIGHEST
AXES = ("blk", "chan")
F32 = jnp.float32
BF16 = jnp.bfloat16
MESH = pl.DeviceIdType.MESH
KERNEL_VMEM = 62 << 20


def contract(a, b, dim_a, dim_b, precision=None):
    return lax.dot_general(
        a, b, (((dim_a,), (dim_b,)), ((), ())), precision=precision, preferred_element_type=F32
    )


def positions(length):
    lags = jnp.arange(length).astype(F32)
    band_freq = 0.0001 + (BANDS - 1 - 0.0001) * jnp.arange(BANDS).astype(F32) / (BANDS - 1)
    phase = 2.0 * math.pi / length * lags[None, :] * band_freq[:, None]
    return lags, jnp.concatenate([lags[None, :] / (length - 1), jnp.cos(phase), -jnp.sin(phase)], 0)


def feature_blocks(length, block):
    lags = np.arange(length).astype(np.float32)
    bands = np.arange(BANDS).astype(np.float32)
    band_freq = np.float32(0.0001) + np.float32(BANDS - 1 - 0.0001) * bands / np.float32(BANDS - 1)
    phase = np.float32(2.0 * math.pi / length) * lags[None, :] * band_freq[:, None]
    ramp = lags[None, :] / np.float32(length - 1)
    rows = np.concatenate([ramp, np.cos(phase), -np.sin(phase), np.ones_like(ramp)])
    rows = np.pad(rows, ((0, -len(rows) % 8), (0, 0))).astype(np.float32)
    return np.ascontiguousarray(rows.reshape(len(rows), -1, block).transpose(1, 0, 2))


def fixed_table(block):
    spot, freq = np.arange(block)[:, None], np.arange(block)[None, :]
    phase = (np.pi / block) * (spot * freq % (2 * block))
    imag = np.where(freq == 0, 1.0 - 2.0 * (spot % 2), -np.sin(phase))
    return np.concatenate([np.cos(phase), imag], 1).astype(np.float32)


def filter_hidden(length, pos_weight, pos_bias, mid_weight, mid_bias, sine_freq):
    lags, features = positions(length)
    freq = sine_freq[:, None]
    first_sum = contract(pos_weight, features, 0, 0, EXACT) + pos_bias[:, None]
    first = jnp.sin(freq * first_sum)
    second_sum = contract(mid_weight, first, 0, 0, EXACT) + mid_bias[:, None]
    second = jnp.sin(freq * second_sum)
    return lags, features, first_sum, first, second_sum, second


def block_table(block):
    spot = lax.broadcasted_iota(jnp.int32, (block, block), 0)
    freq = lax.broadcasted_iota(jnp.int32, (block, block), 1)
    phase = (math.pi / block) * (spot * freq % (2 * block)).astype(F32)
    parity = 1.0 - 2.0 * (spot % 2).astype(F32)
    imag = jnp.where(freq == 0, parity, -jnp.sin(phase))
    return jnp.concatenate([jnp.cos(phase), imag], 1)


def to_spectrum(blocks, table):
    spec = lax.dot_general(
        blocks, table, (((blocks.ndim - 1,), (0,)), ((), ())), precision=EXACT, preferred_element_type=F32
    )
    half = table.shape[0]
    return spec[..., :half], spec[..., half:]


def from_spectrum(real, imag, table):
    half = table.shape[0]
    weight = jnp.where(lax.iota(jnp.int32, half) == 0, 0.5 / half, 1.0 / half)
    spec = jnp.concatenate([real * weight, imag * weight], -1)
    return lax.dot_general(
        spec, table, (((spec.ndim - 1,), (1,)), ((), ())), precision=EXACT, preferred_element_type=F32
    )


def packed_kernel(real, imag):
    first = lax.iota(jnp.int32, real.shape[-1]) == 0
    return real, jnp.where(first, imag, real), jnp.where(first, 0.0, imag)


def layer_norm(values, gain, shift):
    center = values - jnp.mean(values, -1, keepdims=True)
    scale_inv = lax.rsqrt(jnp.mean(center * center, -1, keepdims=True) + EPS)
    normal = center * scale_inv
    return normal * gain + shift, normal, scale_inv


def layer_norm_back(grad_out, normal, scale_inv, gain):
    grad_normal = grad_out * gain
    inner = grad_normal - jnp.mean(grad_normal, -1, keepdims=True)
    inner = inner - normal * jnp.mean(grad_normal * normal, -1, keepdims=True)
    return inner * scale_inv, jnp.sum(grad_out * normal, 0), jnp.sum(grad_out, 0)


def gelu_parts(v):
    root = math.sqrt(2.0 / math.pi)
    inner = root * (v + 0.044715 * v * v * v)
    t = jnp.tanh(inner)
    value = 0.5 * v * (1.0 + t)
    slope = 0.5 * (1.0 + t) + 0.5 * v * (1.0 - t * t) * root * (1.0 + 3.0 * 0.044715 * v * v)
    return value, slope


def delayed(values, steps):
    if steps == 0:
        return values
    pad = jnp.zeros(values.shape[:-1] + (steps,), values.dtype)
    return jnp.concatenate([pad, values[..., :-steps]], -1)


def advanced(values, steps):
    if steps == 0:
        return values
    pad = jnp.zeros(values.shape[:-1] + (steps,), values.dtype)
    return jnp.concatenate([values[..., steps:], pad], -1)


def exchange(values):
    return lax.all_to_all(values, AXES, split_axis=0, concat_axis=0, tiled=True)


def spot():
    b, c = lax.axis_index("blk"), lax.axis_index("chan")
    return b // 2, b % 2, c // 2, c % 2


def at(z, y, x, k):
    return {"blk": z * 2 + y, "chan": x * 2 + k}


def flat(z, y, x, k):
    return ((z * 2 + y) * 2 + x) * 2 + k


def when(condition, act):
    pl.when(condition)(act)


def send(src, dst, send_sem, recv_sem, place):
    return pltpu.make_async_remote_copy(
        src_ref=src, dst_ref=dst, send_sem=send_sem, recv_sem=recv_sem, device_id=at(*place), device_id_type=MESH
    )


def greet_all(count):
    b, c = lax.axis_index("blk"), lax.axis_index("chan")
    chan = lax.axis_size("chan")
    me = b * chan + c
    barrier = pltpu.get_barrier_semaphore()

    def one(i, carry):
        other = lax.rem(me + i, count)
        pl.semaphore_signal(
            barrier, inc=1, device_id={"blk": other // chan, "chan": other % chan}, device_id_type=MESH
        )
        return carry

    lax.fori_loop(1, count, one, 0)
    pl.semaphore_wait(barrier, count - 1)


def low_rows(rows):
    return (rows + 16) // 32 * 16 if rows > 8 else rows


class Gather:
    def __init__(self, line, shard, full, sends, recvs, local):
        self.line, self.shard, self.full, self.s, self.r, self.local = line, shard, full, sends, recvs, local
        self.rows = shard.shape[0]
        self.low = low_rows(self.rows)
        self.z, self.y, self.x, self.k = spot()
        self.half = line // 2
        self.inward = 1 - 2 * (self.z // self.half)
        self.inner = self.z == self.half - 1 + self.z // self.half

    def copy(self, send_at, recv_at, shard, place, rows=None):
        ref = self.full.at[shard] if rows is None else self.full.at[shard, pl.ds(*rows)]
        return send(ref, ref, self.s.at[send_at], self.r.at[recv_at], place)

    def together(self, send_at, recv_at, count, rows=None):
        return self.copy(send_at, recv_at, pl.ds(0, count), (self.z, self.y, self.x, 1 - self.k), rows)

    def up(self, zo):
        return self.copy(zo, zo, flat(zo, self.y, self.x, self.k), (self.z + 1, self.y, self.x, self.k))

    def down(self, zo):
        return self.copy(self.line + zo, self.line + zo, flat(zo, self.y, self.x, self.k), (self.z - 1, self.y, self.x, self.k))

    def to_x(self, zo):
        return self.copy(2 * self.line, 2 * self.line + zo, flat(zo, self.y, self.x, self.k), (self.z, self.y, 1 - self.x, self.k))

    def to_y(self, zo):
        return self.copy(2 * self.line + 1, 3 * self.line + zo, flat(zo, self.y, self.x, self.k), (self.z, 1 - self.y, self.x, self.k))

    def low_y(self, zo, other_y=False):
        shard = flat(zo, 1 - self.y if other_y else self.y, 1 - self.x, self.k)
        return self.copy(2 * self.line + 2, 5 * self.line + zo % self.half, shard, (self.z, 1 - self.y, self.x, self.k), (0, self.low))

    def high_x(self, zo, other_x=False):
        shard = flat(zo, 1 - self.y, 1 - self.x if other_x else self.x, self.k)
        rows = (self.low, self.rows - self.low)
        recv_at = 5 * self.line + self.half + zo % self.half
        return self.copy(2 * self.line + 3, recv_at, shard, (self.z, self.y, 1 - self.x, self.k), rows)

    def core(self, zo, yo, xo, k):
        return self.copy(2 * self.line + 4, 6 * self.line, flat(zo, yo, xo, k), (self.z, self.y, self.x, 1 - self.k))

    def cross(self, zo, step):
        shard = flat(zo, 1 - self.y, 1 - self.x, self.k)
        return self.copy(2 * self.line + 5, 4 * self.line + zo, shard, (self.z + step, self.y, self.x, self.k))

    def same(self, zo):
        return zo // self.half == self.z // self.half

    def line_has(self, zo):
        self.to_x(zo).start()
        self.to_y(zo).start()
        self.core(zo, self.y, self.x, self.k).start()

    def begin(self):
        own = self.full.at[flat(self.z, self.y, self.x, self.k)]
        copy = pltpu.make_async_copy(self.shard, own, self.local)
        copy.start()
        copy.wait()
        when(self.z < self.line - 1, lambda: self.up(self.z).start())
        when(self.z > 0, lambda: self.down(self.z).start())
        self.line_has(self.z)

    def each(self, distance, act):
        if distance == 0:
            act(self.z)
        else:
            when(self.z - distance >= 0, lambda: act(self.z - distance))
            when(self.z + distance < self.line, lambda: act(self.z + distance))

    def along(self, distance):
        def from_below():
            zo = self.z - distance
            self.up(zo).wait_recv()
            when(self.z < self.line - 1, lambda: self.up(zo).start())
            self.line_has(zo)

        def from_above():
            zo = self.z + distance
            self.down(zo).wait_recv()
            when(self.z > 0, lambda: self.down(zo).start())
            self.line_has(zo)

        when(self.z - distance >= 0, from_below)
        when(self.z + distance < self.line, from_above)

    def plane(self, distance):
        def act(zo):
            self.to_x(zo).wait_recv()
            when(self.same(zo), lambda: self.low_y(zo).start())
            self.core(zo, self.y, 1 - self.x, self.k).start()
            self.to_y(zo).wait_recv()
            if self.low < self.rows:
                when(self.same(zo), lambda: self.high_x(zo).start())
            self.core(zo, 1 - self.y, self.x, self.k).start()

        self.each(distance, act)

    def corner(self, distance):
        def near(zo):
            self.low_y(zo, True).wait_recv()
            if self.low < self.rows:
                self.high_x(zo, True).wait_recv()
            when(self.inner, lambda: self.cross(zo, self.inward).start())

        def far(zo):
            self.cross(zo, self.inward).wait_recv()
            when(self.inner, lambda: self.cross(zo, -self.inward).start())

        def act(zo):
            when(self.same(zo), lambda: near(zo))
            when(jnp.logical_not(self.same(zo)), lambda: far(zo))
            self.core(zo, 1 - self.y, 1 - self.x, self.k).start()

        self.each(distance, act)

    def finish(self):
        self.together(2 * self.line + 4, 6 * self.line, 4 * self.line).wait_recv()

    def drain(self):
        line, high = self.line, self.rows - self.low
        for zo in range(line):
            when(jnp.logical_and(self.z < line - 1, zo <= self.z), lambda: self.up(zo).wait_send())
            when(jnp.logical_and(self.z > 0, zo >= self.z), lambda: self.down(zo).wait_send())
        self.together(2 * line, 0, line).wait_send()
        self.together(2 * line + 1, 0, line).wait_send()
        self.together(2 * line + 2, 0, self.half, (0, self.low)).wait_send()
        if high:
            self.together(2 * line + 3, 0, self.half, (self.low, high)).wait_send()
        self.together(2 * line + 4, 0, 4 * line).wait_send()
        when(self.inner, lambda: self.together(2 * line + 5, 0, line).wait_send())


class Reduce:
    def __init__(self, line, part, out, chip, low_y, high_x, by_x, by_y, by_z, crossed, sends, recvs):
        self.line, self.part, self.out, self.chip = line, part, out, chip
        self.low_buf, self.high_buf, self.x_buf, self.y_buf, self.z_buf = low_y, high_x, by_x, by_y, by_z
        self.crossed = crossed
        self.s, self.r = sends, recvs
        self.rows = part.shape[1]
        self.low = low_rows(self.rows)
        self.z, self.y, self.x, self.k = spot()
        self.half = line // 2
        self.inward = 1 - 2 * (self.z // self.half)
        self.inner = self.z == self.half - 1 + self.z // self.half

    def index(self, zo, yo, xo):
        return (zo * 2 + yo) * 2 + xo

    def copy(self, send_at, recv_at, src, dst, place):
        return send(src, dst, self.s.at[send_at], self.r.at[recv_at], place)

    def together(self, send_at, recv_at, ref):
        return self.copy(send_at, recv_at, ref, ref, (self.z, self.y, self.x, 1 - self.k))

    def core(self, zo, yo, xo):
        i = self.index(zo, yo, xo)
        src = self.part.at[flat(zo, yo, xo, 1 - self.k)]
        return self.copy(2 * self.line + 4, 5 * self.line + zo, src, self.chip.at[i], (self.z, self.y, self.x, 1 - self.k))

    def corner_of(self, zo):
        return self.index(zo, 1 - self.y, 1 - self.x)

    def low_y(self, zo):
        src = self.chip.at[self.corner_of(zo), pl.ds(0, self.low)]
        slot = zo % self.half
        place = (self.z, 1 - self.y, self.x, self.k)
        return self.copy(2 * self.line + 2, 6 * self.line + slot, src, self.low_buf.at[slot], place)

    def high_x(self, zo):
        src = self.chip.at[self.corner_of(zo), pl.ds(self.low, self.rows - self.low)]
        slot = zo % self.half
        place = (self.z, self.y, 1 - self.x, self.k)
        return self.copy(2 * self.line + 3, 6 * self.line + self.half + slot, src, self.high_buf.at[slot], place)

    def to_x(self, zo):
        src = self.chip.at[self.index(zo, self.y, 1 - self.x)]
        return self.copy(2 * self.line, 2 * self.line + zo, src, self.x_buf.at[zo], (self.z, self.y, 1 - self.x, self.k))

    def to_y(self, zo):
        src = self.chip.at[self.index(zo, 1 - self.y, self.x)]
        return self.copy(2 * self.line + 1, 3 * self.line + zo, src, self.y_buf.at[zo], (self.z, 1 - self.y, self.x, self.k))

    def up(self, zo):
        src = self.chip.at[self.index(zo, self.y, self.x)]
        return self.copy(zo, zo, src, self.z_buf.at[zo + 1], (self.z + 1, self.y, self.x, self.k))

    def down(self, zo):
        src = self.chip.at[self.index(zo, self.y, self.x)]
        return self.copy(self.line + zo, self.line + zo, src, self.z_buf.at[zo], (self.z - 1, self.y, self.x, self.k))

    def cross(self, zo):
        src = self.chip.at[self.corner_of(zo)]
        place = (self.z + self.inward, self.y, self.x, self.k)
        return self.copy(2 * self.line + 5, 4 * self.line + zo, src, self.crossed.at[zo], place)

    def add(self, i, other, rows=None):
        if rows is None:
            self.chip[i] = self.chip[i] + other
        else:
            self.chip[i, pl.ds(*rows)] = self.chip[i, pl.ds(*rows)] + other

    def begin(self, zo):
        for yo, xo in ((1 - self.y, 1 - self.x), (self.y, 1 - self.x), (1 - self.y, self.x), (self.y, self.x)):
            self.core(zo, yo, xo).start()

    def corner(self, zo, near):
        def joined(yo, xo):
            self.add(self.index(zo, yo, xo), self.part[flat(zo, yo, xo, self.k)])

        def crossing():
            self.cross(zo).wait_recv()
            self.add(self.corner_of(zo), self.crossed[zo])

        arrived = self.chip.at[pl.ds(4 * zo, 4)]
        self.together(2 * self.line + 4, 5 * self.line + zo, arrived).wait_recv()
        joined(1 - self.y, 1 - self.x)
        if not near:
            joined(self.y, 1 - self.x)
            self.to_x(zo).start()
            joined(1 - self.y, self.x)
            self.to_y(zo).start()
        when(self.inner, crossing)
        if near:
            self.low_y(zo).start()
            if self.low < self.rows:
                self.high_x(zo).start()
            joined(self.y, 1 - self.x)
            joined(1 - self.y, self.x)
        else:
            self.cross(zo).start()
        joined(self.y, self.x)

    def plane(self, zo):
        self.low_y(zo).wait_recv()
        self.add(self.index(zo, self.y, 1 - self.x), self.low_buf[zo % self.half], (0, self.low))
        self.to_x(zo).start()
        if self.low < self.rows:
            self.high_x(zo).wait_recv()
            high = (self.low, self.rows - self.low)
            self.add(self.index(zo, 1 - self.y, self.x), self.high_buf[zo % self.half], high)
        self.to_y(zo).start()

    def along(self, zo, own):
        i = self.index(zo, self.y, self.x)
        self.to_x(zo).wait_recv()
        self.to_y(zo).wait_recv()
        total = self.x_buf[zo].astype(F32) + self.y_buf[zo].astype(F32) + self.chip[i].astype(F32)

        def from_below():
            self.up(zo).wait_recv()
            self.add(i, self.z_buf[zo + 1])

        def from_above():
            self.down(zo).wait_recv()
            self.add(i, self.z_buf[zo])

        def rising():
            when(self.z > 0, from_below)
            self.up(zo).start()

        def falling():
            when(self.z < self.line - 1, from_above)
            self.down(zo).start()

        def last_below():
            self.up(zo).wait_recv()
            self.out[...] += self.z_buf[zo + 1].astype(F32)

        def last_above():
            self.down(zo).wait_recv()
            self.out[...] += self.z_buf[zo].astype(F32)

        if own:
            self.out[...] = total
            when(self.z > 0, last_below)
            when(self.z < self.line - 1, last_above)
        else:
            self.chip[i] = total.astype(self.chip.dtype)
            when(zo > self.z, rising)
            when(zo < self.z, falling)

    def drain(self):
        line, low, high = self.line, self.low, self.rows - self.low
        shards, halves = self.chip.at[pl.ds(0, line)], pl.ds(0, self.half)
        for zo in range(line):
            when(zo > self.z, lambda: self.up(zo).wait_send())
            when(zo < self.z, lambda: self.down(zo).wait_send())
        self.together(2 * line, 0, shards).wait_send()
        self.together(2 * line + 1, 0, shards).wait_send()
        self.together(2 * line + 2, 0, self.chip.at[halves, pl.ds(0, low)]).wait_send()
        if high:
            self.together(2 * line + 3, 0, self.chip.at[halves, pl.ds(low, high)]).wait_send()
        self.together(2 * line + 4, 0, self.part.at[pl.ds(0, 4 * line)]).wait_send()
        self.together(2 * line + 5, 0, self.chip.at[halves]).wait_send()


BUFFERS = 7


def reduce_scratch(line, part):
    _, rows, width = part.shape
    low = low_rows(rows)
    high = max(rows - low, 8)
    half = line // 2
    sizes = [(line * 4, rows), (half, low), (half, high), (line, rows), (line, rows), (line + 1, rows), (line, rows)]
    return [pltpu.VMEM(s + (width,), part.dtype) for s in sizes]


def dot_rows(a, b, precision=None):
    return lax.dot_general(a, b, (((1,), (1,)), ((), ())), precision=precision, preferred_element_type=F32)


def dot_plain(a, b, precision=None):
    return lax.dot_general(a, b, (((1,), (0,)), ((), ())), precision=precision, preferred_element_type=F32)


def eighths(value):
    return pl.multiple_of(value, 8)


class Exchange:
    def __init__(self, src, dst, send_sem, recv_sem, devices):
        self.src, self.dst, self.s, self.r, self.devices = src, dst, send_sem, recv_sem, devices
        self.me = flat(*spot())

    def copy(self, i):
        other = lax.rem(self.me + i, self.devices)
        place = (other // 8, other // 4 % 2, other // 2 % 2, other % 2)
        return send(self.src.at[other], self.dst.at[self.me], self.s, self.r, place)

    def together(self, ref):
        z, y, x, k = spot()
        ref = ref.at[pl.ds(0, self.devices - 1)]
        return send(ref, ref, self.s, self.r, (z, y, x, 1 - k))

    def start(self):
        lax.fori_loop(1, self.devices, lambda i, c: (self.copy(i).start(), c)[1], 0)
        self.dst[self.me] = self.src[self.me]

    def arrive(self):
        self.together(self.dst).wait_recv()

    def drain(self):
        self.together(self.src).wait_send()


def low_lanes(shape):
    return lax.broadcasted_iota(jnp.int32, shape, 1) < 64


def merge_halves(first, second):
    low = low_lanes(first.shape)
    return (
        jnp.where(low, first, pltpu.roll(second, 64, 1)),
        jnp.where(low, pltpu.roll(first, 64, 1), second),
    )


def lane_norm(values, gain, shift):
    center = values - jnp.mean(values, 1, keepdims=True)
    scale_inv = lax.rsqrt(jnp.mean(center * center, 1, keepdims=True) + EPS)
    normal = center * scale_inv
    return normal * gain + shift, normal, scale_inv


def slot_zero(shape):
    return lax.broadcasted_iota(jnp.int32, shape, 1) == 0


def slot_sign(shape):
    return 1.0 - 2.0 * (lax.broadcasted_iota(jnp.int32, shape, 1) % 2).astype(F32)


def slot_weight(shape):
    return jnp.where(slot_zero(shape), 0.5 / shape[1], 1.0 / shape[1])


def column(params, index):
    return params[:, index : index + 1]


def norm_rows(stack, count, chans, width):
    total = None
    for j in range(count):
        tile = stack(j).astype(F32)[:, :128]
        tile = jnp.where(lax.broadcasted_iota(jnp.int32, tile.shape, 1) < chans, tile, 0.0)
        wide = jnp.concatenate([tile, jnp.zeros((tile.shape[0], width - 128), F32)], 1)
        wide = pltpu.roll(wide, j * chans, 1) if j else wide
        total = wide if total is None else total + wide
    return total


RAW = 14


def prepare(in_t, raw, own_in, desk, params, pos_t, mid_t, fil_t, cols):
    gain_one, shift_one, gain_two, shift_two, taps, bias, skip, decay, fil, pos, pos_bias, mid, rate, mid_bias = raw
    chans, order, emb = fil.shape[0], mid.shape[0], pos.shape[0]

    def put(row, values, wide):
        desk[row : row + values.shape[0], :wide] = values.astype(F32)

    desk[...] = jnp.zeros_like(desk)
    for i, ref in enumerate((gain_one, shift_one, gain_two, shift_two)):
        put(i, ref[...], chans)
    norms = jnp.concatenate([desk[:8, :], jnp.zeros((8, in_t.shape[1] - 128), F32)], 1)
    own_in[...] = jnp.concatenate([in_t[...].astype(F32), norms], 0).astype(BF16)
    for i in range(3):
        put(3 * i, taps[i], chans)
    put(9, bias[...], chans)
    put(12, skip[...], chans)
    put(13, decay[...], chans)
    params[...] = desk[...].T[:chans]
    desk[...] = jnp.zeros_like(desk)
    put(0, pos[...], order)
    put(emb, pos_bias[...], order)
    pos_t[...] = desk[...].T[:order, : pos_t.shape[1]]
    desk[...] = jnp.zeros_like(desk)
    put(0, mid[...], order)
    mid_t[...] = desk[...].T[:order, :order]
    desk[...] = jnp.zeros_like(desk)
    put(0, rate[...], order)
    put(1, mid_bias[...], order)
    cols[...] = desk[...].T[:order]
    fil_t[...] = fil[...].astype(F32)


def lane_norm_back(grad_out, normal, scale_inv, gain):
    grad_normal = grad_out * gain
    inner = grad_normal - jnp.mean(grad_normal, 1, keepdims=True)
    inner = inner - normal * jnp.mean(grad_normal * normal, 1, keepdims=True)
    return inner * scale_inv, jnp.sum(grad_out * normal, 0, keepdims=True), jnp.sum(grad_out, 0, keepdims=True)


LATE = (0, 2, 3, 4)


def layer_kernel(dims, *refs):
    line, devices, chans, seqs, block, blocks, width = dims
    (in_t, own_out, own_up, own_down, hidden, cot, feats, table) = refs[:8]
    raw = refs[8 : 8 + RAW]
    refs = refs[8 + RAW :]
    (result, grad_hidden, sum_up, sum_down, sum_out, sum_in, sum_tile, everyone, chan_grads, filter_grad) = refs[:10]
    refs = refs[10:]
    (full_in, full_out, full_up, full_down, mixed_in, norms_ref, steps, conv, spec, total, k_re, k_alt, k_im) = refs[:13]
    (one, cos_one, two, cos_two, params, pos_t, mid_t, fil_t, cols) = refs[13:22]
    (own_in, desk, proj_send, proj_recv, mix_send, kernel_buf, gated, sums) = refs[22:30]
    (w_flat, g_out, g_in, g_tile, resid, value_sum, second_sum, mix_recv, g_spec, g_conv) = refs[30:40]
    (k_sums, g_proj, small) = refs[40:43]
    (gather_send, gather_recv, sends, recvs, local, exchange) = refs[43:49]
    buffers = refs[49:]
    shards = full_up.shape[0] // line
    hidden_rows = full_up.shape[1]
    chunk = shards * hidden_rows
    gated_grad, g_sums = gated, sums
    prepare(in_t, raw, own_in, desk, params, pos_t, mid_t, fil_t, cols)
    greet_all(devices)
    gathers = [
        Gather(line, shard, full, gather_send.at[p], gather_recv.at[p], local)
        for p, (shard, full) in enumerate(
            ((own_in, full_in), (own_out, full_out), (own_up, full_up), (own_down, full_down))
        )
    ]
    late = LATE

    def tick(now):
        for piece, offset in zip(gathers, late):
            step = now - offset
            if step == 0:
                piece.begin()
            if 1 <= step < line:
                piece.along(step)
            if 1 <= step <= line:
                piece.plane(step - 1)
            if 2 <= step <= line + 1:
                piece.corner(step - 2)

    def filter_part(n, carry):
        sum_one = dot_plain(pos_t[...], feats[n], EXACT)
        phase = column(cols[...], 0) * sum_one
        act_one = jnp.sin(phase)
        one[n] = act_one
        cos_one[n] = jnp.cos(phase)
        phase = column(cols[...], 0) * (dot_plain(mid_t[...], act_one, EXACT) + column(cols[...], 1))
        act_two = jnp.sin(phase)
        two[n] = act_two
        cos_two[n] = jnp.cos(phase)
        lag = lax.broadcasted_iota(jnp.int32, (chans, block), 1) + n * block
        fade = jnp.exp(-lag.astype(F32) * column(params[...], 13))
        kernel_buf[pl.ds(eighths(n * chans), chans), :] = dot_plain(fil_t[...], act_two, EXACT) * fade
        return carry

    def filters(first, last):
        lax.fori_loop(first, last, filter_part, 0)

    def kernel_spectrum():
        ker = dot_plain(kernel_buf[...], table[...], EXACT)
        before = jnp.concatenate([jnp.zeros((chans, 2 * block), F32), ker[:-chans]], 0)
        sign = slot_sign((chans * blocks, block))
        real = ker[:, :block] + sign * before[:, :block]
        imag = ker[:, block:] + sign * before[:, block:]
        zero = slot_zero(real.shape)
        k_re[...] = real
        k_alt[...] = jnp.where(zero, imag, real)
        k_im[...] = jnp.where(zero, 0.0, imag)

    tick(0)
    filters(0, blocks // 4)
    tick(1)
    filters(blocks // 4, blocks // 2)
    tick(2)
    filters(blocks // 2, 3 * blocks // 4)
    tick(3)
    filters(3 * blocks // 4, blocks)
    tick(4)
    kernel_spectrum()
    tick(5)
    gathers[0].finish()

    in_rows = full_in.shape[1]
    norms = norm_rows(lambda j: full_in[j, in_rows - 8 :], devices, chans, width)
    norms_ref[...] = norms
    normed, _, _ = lane_norm(hidden[...].astype(F32), norms[0:1], norms[1:2])
    projected = dot_rows(full_in[...].reshape(devices * in_rows, width), normed.astype(BF16))
    projected = projected.reshape(devices, in_rows, 128)
    for j in range(devices):
        for i in range(3):
            unit = 3 * j + i
            proj_send[unit % devices, unit // devices] = projected[j, i * chans : (i + 1) * chans].astype(BF16)
    moved = Exchange(proj_send, proj_recv, exchange.at[0], exchange.at[1], devices)
    moved.start()
    tick(6)
    moved.arrive()

    def assemble(j, carry):
        lanes = pl.ds(pl.multiple_of(j * 128, 128), 128)
        for p in range(3):
            pair = merge_halves(proj_recv[2 * j, p].astype(F32), proj_recv[2 * j + 1, p].astype(F32))
            for s in range(seqs):
                steps[p, s, :, lanes] = pair[s]
        return carry

    lax.fori_loop(0, devices // 2, assemble, 0)
    length = block * blocks
    for s in range(seqs):
        for c in range(0, chans, 8):
            spots = lax.broadcasted_iota(jnp.int32, (8, length), 1)
            parts = []
            for p in range(3):
                x = steps[p, s, c : c + 8, :]
                local_params = params[c : c + 8, :]
                value = column(local_params, 9 + p) + column(local_params, p) * x
                for i in (1, 2):
                    value += column(local_params, 3 * i + p) * jnp.where(spots < i, 0.0, pltpu.roll(x, i, 1))
                parts.append(value)
            product = parts[1] * parts[2]
            for n in range(blocks):
                at_rows = (n * seqs + s) * chans + c
                lanes = slice(n * block, (n + 1) * block)
                gated[at_rows : at_rows + 8, :] = product[:, lanes]
                for p in range(3):
                    conv[p, at_rows : at_rows + 8, :] = parts[p][:, lanes]
    tick(7)

    spec[...] = dot_plain(gated[...], table[...], EXACT)
    weight = slot_weight((chans, block))

    def output_block(m, carry):
        def add(n, acc):
            at_kernel = pl.ds(eighths((m - n) * chans), chans)
            kr, ka, ki = k_re[at_kernel, :], k_alt[at_kernel, :], k_im[at_kernel, :]
            result = []
            for s in range(seqs):
                at_signal = pl.ds(eighths((n * seqs + s) * chans), chans)
                re, im = spec[at_signal, :block], spec[at_signal, block:]
                result.append(acc[2 * s] + re * kr - im * ki)
                result.append(acc[2 * s + 1] + re * ki + im * ka)
            return tuple(result)

        acc = lax.fori_loop(0, m + 1, add, tuple(jnp.zeros((chans, block), F32) for _ in range(2 * seqs)))
        for s in range(seqs):
            at_signal = pl.ds(eighths((m * seqs + s) * chans), chans)
            sums[at_signal, :block] = acc[2 * s] * weight
            sums[at_signal, block:] = acc[2 * s + 1] * weight
        return carry

    lax.fori_loop(0, blocks, output_block, 0)
    tick(8)
    total[...] = dot_rows(sums[...], table[...], EXACT)

    def mix(m, carry):
        mixed = []
        for s in range(seqs):
            at_signal = pl.ds(eighths((m * seqs + s) * chans), chans)
            value = total[at_signal, :] + column(params[...], 12) * gated[at_signal, :]
            total[at_signal, :] = value
            mixed.append(value * conv[0, at_signal, :])
        for h in range(block // 128):
            pair = merge_halves(*(v[:, h * 128 : (h + 1) * 128] for v in mixed))
            for q in range(2):
                mix_send[m * (block // 64) + 2 * h + q] = pair[q].astype(BF16)
        return carry

    lax.fori_loop(0, blocks, mix, 0)
    mix_home = Exchange(mix_send, mixed_in, exchange.at[2], exchange.at[3], devices)
    mix_home.start()
    tick(9)
    for piece in gathers[1:]:
        piece.finish()
    mix_home.arrive()
    for piece in gathers:
        piece.drain()
    moved.drain()
    mix_home.drain()

    parts = (full_up, full_down, g_out, g_in, g_tile)
    outs = (sum_up, sum_down, sum_out, sum_in, sum_tile)
    pieces = [
        Reduce(line, parts[p], outs[p], *buffers[p * BUFFERS : (p + 1) * BUFFERS], sends.at[p], recvs.at[p])
        for p in range(5)
    ]

    z = lax.axis_index("blk") // 2
    half = line // 2
    flip = z // half
    mirror = z + flip * (line - 1 - 2 * z)

    def visit(i):
        near = half - 1 - mirror if i < line - 1 else mirror
        place = line - 1 - i if i < half else near
        return place + flip * (line - 1 - 2 * place)

    def fold(group, slot):
        for piece in group:
            if slot < line:
                piece.corner(visit(slot), slot >= half)
            if half < slot <= line:
                piece.plane(visit(slot - 1))
            if 2 <= slot <= line + 1:
                piece.along(visit(slot - 2), slot - 2 == line - 1)

    gain_two, shift_two = norms_ref[2:3], norms_ref[3:4]
    mixed = mixed_in[...].astype(F32).reshape(width, 128).T.astype(BF16)
    w_flat[...] = full_out[...].astype(F32).reshape(width, width).astype(BF16)
    resid[...] = hidden[...].astype(F32) + dot_rows(mixed, w_flat[...])
    second, normal_two, inv_two = lane_norm(resid[...], gain_two, shift_two)
    second = second.astype(BF16)
    value_sum[...] = jnp.zeros_like(value_sum)
    second_sum[...] = jnp.zeros_like(second_sum)

    for i in range(line):
        where_to = pl.ds(visit(i) * shards, shards)
        up = full_up[where_to].reshape(chunk, width)
        down = full_down[where_to].reshape(chunk, width)
        active, slope = gelu_parts(dot_rows(up, second))
        active = active.astype(BF16)
        grad_upper = (dot_rows(down, cot[...]) * slope).astype(BF16)
        value_sum[...] += dot_plain(active.astype(F32).T.astype(BF16), down)
        second_sum[...] += dot_plain(grad_upper.astype(F32).T.astype(BF16), up)
        full_down[where_to] = dot_plain(active, cot[...]).astype(BF16).reshape(shards, hidden_rows, width)
        full_up[where_to] = dot_plain(grad_upper, second).astype(BF16).reshape(shards, hidden_rows, width)
        for piece in pieces[:2]:
            piece.begin(visit(i))
        if i:
            fold(pieces[:2], i - 1)
    result[...] = (resid[...] + value_sum[...]).astype(BF16)
    resid_term, grad_gain_two, grad_shift_two = lane_norm_back(second_sum[...], normal_two, inv_two, gain_two)
    resid[...] = cot[...].astype(F32) + resid_term
    grad_mixed = dot_plain(resid[...].astype(BF16), w_flat[...])
    mix_send[...] = grad_mixed.T.reshape(devices, chans, 128).astype(BF16)
    grad_mix = Exchange(mix_send, mix_recv, exchange.at[4], exchange.at[5], devices)
    grad_mix.start()
    grad_branch = resid[...].T.astype(BF16)
    g_out[...] = dot_plain(grad_branch, mixed).reshape(devices, chans, width).astype(BF16)
    for i in range(line):
        pieces[2].begin(visit(i))
    fold(pieces[:2], line - 1)
    fold(pieces[2:3], 0)
    grad_mix.arrive()

    weight = slot_weight((chans, block))
    skip = column(params[...], 12)
    per_block = block // 64

    def arrange(m, carry):
        for h in range(block // 128):
            source = m * per_block + 2 * h
            pair = merge_halves(mix_recv[source].astype(F32), mix_recv[source + 1].astype(F32))
            lanes = slice(h * 128, (h + 1) * 128)
            for s in range(seqs):
                at_rows = pl.ds(eighths((m * seqs + s) * chans), chans)
                place = pl.ds(pl.multiple_of(m * block + h * 128, 128), 128)
                g_conv[0, s, :, place] = pair[s] * total[at_rows, lanes]
                grad = pair[s] * conv[0, at_rows, lanes]
                gated_grad[at_rows, lanes] = grad
                carry = carry + grad * conv[1, at_rows, lanes] * conv[2, at_rows, lanes]
        return carry

    skip_sum = lax.fori_loop(0, blocks, arrange, jnp.zeros((chans, 128), F32))
    g_spec[...] = dot_plain(gated_grad[...], table[...], EXACT)
    fold(pieces[2:3], 1)

    def signal_block(n, carry):
        def add(m, acc):
            at_kernel = pl.ds(eighths((m - n) * chans), chans)
            kr, ka, ki = k_re[at_kernel, :], k_alt[at_kernel, :], k_im[at_kernel, :]
            out = []
            for s in range(seqs):
                at_rows = pl.ds(eighths((m * seqs + s) * chans), chans)
                re, im = g_spec[at_rows, :block], g_spec[at_rows, block:]
                out.append(acc[2 * s] + re * kr + im * ki)
                out.append(acc[2 * s + 1] + im * ka - re * ki)
            return tuple(out)

        acc = lax.fori_loop(n, blocks, add, tuple(jnp.zeros((chans, block), F32) for _ in range(2 * seqs)))
        for s in range(seqs):
            at_rows = pl.ds(eighths((n * seqs + s) * chans), chans)
            g_sums[at_rows, :block] = acc[2 * s] * weight
            g_sums[at_rows, block:] = acc[2 * s + 1] * weight
        return carry

    lax.fori_loop(0, blocks, signal_block, 0)
    g_sums[:, :block] = dot_rows(g_sums[...], table[...], EXACT)

    def gate_grads(m, carry):
        for s in range(seqs):
            at_rows = pl.ds(eighths((m * seqs + s) * chans), chans)
            place = pl.ds(pl.multiple_of(m * block, block), block)
            grad = g_sums[at_rows, :block] + skip * gated_grad[at_rows, :]
            g_conv[1, s, :, place] = grad * conv[2, at_rows, :]
            g_conv[2, s, :, place] = grad * conv[1, at_rows, :]
        return carry

    lax.fori_loop(0, blocks, gate_grads, 0)
    fold(pieces[:2], line)
    fold(pieces[2:3], 2)

    length = block * blocks
    for c in range(0, chans, 8):
        col = lax.broadcasted_iota(jnp.int32, (8, 128), 1)
        spots = lax.broadcasted_iota(jnp.int32, (8, length), 1)
        found = jnp.where(col == 12, jnp.sum(skip_sum[c : c + 8], 1, keepdims=True), 0.0)
        local_params = params[c : c + 8, :]
        for p in range(3):
            for s in range(seqs):
                grad = g_conv[p, s, c : c + 8, :]
                x = steps[p, s, c : c + 8, :]
                value = jnp.zeros_like(grad)
                for i in range(3):
                    later = jnp.where(spots < length - i, pltpu.roll(grad, length - i, 1), 0.0) if i else grad
                    value += column(local_params, 3 * i + p) * later
                    found += jnp.where(col == 3 * i + p, jnp.sum(later * x, 1, keepdims=True), 0.0)
                found += jnp.where(col == 9 + p, jnp.sum(grad, 1, keepdims=True), 0.0)
                g_conv[p, s, c : c + 8, :] = value
        chan_grads[c : c + 8, :] = found

    def pack(j, carry):
        lanes = pl.ds(pl.multiple_of(j * 128, 128), 128)
        for p in range(3):
            pair = merge_halves(g_conv[p, 0, :, lanes], g_conv[p, 1, :, lanes])
            proj_send[2 * j, p] = pair[0].astype(BF16)
            proj_send[2 * j + 1, p] = pair[1].astype(BF16)
        return carry

    lax.fori_loop(0, devices // 2, pack, 0)
    home = Exchange(proj_send, proj_recv, exchange.at[6], exchange.at[7], devices)
    home.start()
    fold(pieces[:2], line + 1)
    fold(pieces[2:3], 3)

    def kernel_block(d, carry):
        def add(n, acc):
            real, imag = acc
            for s in range(seqs):
                at_signal = pl.ds(eighths((n * seqs + s) * chans), chans)
                at_grad = pl.ds(eighths(((n + d) * seqs + s) * chans), chans)
                s_re, s_im = spec[at_signal, :block], spec[at_signal, block:]
                g_re, g_im = g_spec[at_grad, :block], g_spec[at_grad, block:]
                zero = slot_zero((chans, block))
                same, other = g_re * s_re, g_im * s_im
                real = real + jnp.where(zero, same, same + other)
                imag = imag + jnp.where(zero, other, g_im * s_re - g_re * s_im)
            return real, imag

        empty = jnp.zeros((chans, block), F32)
        real, imag = lax.fori_loop(0, blocks - d, add, (empty, empty))
        at_kernel = pl.ds(eighths(d * chans), chans)
        k_sums[at_kernel, :block] = real
        k_sums[at_kernel, block:] = imag
        return carry

    lax.fori_loop(0, blocks, kernel_block, 0)
    after = jnp.concatenate([k_sums[chans:, :], jnp.zeros((chans, 2 * block), F32)], 0)
    shape = (chans * blocks, block)
    sign, scale = slot_sign(shape), slot_weight(shape)
    k_sums[:, :block] = (k_sums[:, :block] + sign * after[:, :block]) * scale
    k_sums[:, block:] = (k_sums[:, block:] + sign * after[:, block:]) * scale
    k_sums[:, :block] = dot_rows(k_sums[...], table[...], EXACT)
    fold(pieces[2:3], 4)

    order = pos_t.shape[0]
    emb = pos_t.shape[1]
    freq = column(cols[...], 0)

    def filter_block(n, carry):
        grad_fil, grad_pos, grad_mid, grad_bias = carry
        lag = lax.broadcasted_iota(jnp.int32, (chans, block), 1) + n * block
        fade = jnp.exp(-lag.astype(F32) * column(params[...], 13))
        grad = k_sums[pl.ds(eighths(n * chans), chans), :block] * fade
        grad_fil = grad_fil + dot_rows(grad, two[n], EXACT)
        grad_two = dot_plain(fil_t[...].T, grad, EXACT) * cos_two[n] * freq
        grad_mid = grad_mid + dot_rows(one[n], grad_two, EXACT)
        grad_bias = grad_bias + dot_rows(jnp.ones((8, block), F32), grad_two, EXACT)
        grad_one = dot_plain(mid_t[...].T, grad_two, EXACT) * cos_one[n] * freq
        grad_pos = grad_pos + dot_rows(feats[n], grad_one, EXACT)
        return grad_fil, grad_pos, grad_mid, grad_bias

    zeros = [jnp.zeros(s, F32) for s in ((chans, order), (emb, order), (order, order), (8, order))]
    grad_fil, grad_pos, grad_mid, grad_bias = lax.fori_loop(0, blocks, filter_block, tuple(zeros))
    filter_grad[...] = grad_fil
    rate_bias = cols[...].T
    grad_rate = jnp.sum(pos_t[...].T * grad_pos, 0, keepdims=True) + jnp.sum(mid_t[...].T * grad_mid, 0, keepdims=True)
    grad_rate = (grad_rate + rate_bias[1:2] * grad_bias[:1]) / rate_bias[0:1]
    small[...] = jnp.zeros_like(small)
    small[:emb, :order] = grad_pos
    small[emb : emb + order, :order] = grad_mid
    picked = lax.broadcasted_iota(jnp.int32, (8, order), 0)
    small[emb + order : emb + order + 8, :order] = jnp.where(
        picked == 0, grad_bias, jnp.where(picked == 1, grad_rate, 0.0)
    )
    fold(pieces[2:3], 5)

    gain_one, shift_one = norms_ref[0:1], norms_ref[1:2]
    normed, normal_one, inv_one = lane_norm(hidden[...].astype(F32), gain_one, shift_one)
    normed = normed.astype(BF16)
    g_proj[...] = jnp.zeros_like(g_proj)
    home.arrive()
    for j in range(devices):
        for i in range(3):
            unit = 3 * j + i
            at_rows = slice(j * in_rows + i * chans, j * in_rows + (i + 1) * chans)
            g_proj[at_rows, :] = proj_recv[unit % devices, unit // devices].astype(F32)
    for i in range(line):
        zo = visit(i)
        group = shards * in_rows
        grads = dot_plain(g_proj[pl.ds(eighths(zo * group), group), :].astype(BF16), normed)
        g_in[pl.ds(zo * shards, shards)] = grads.reshape(shards, in_rows, width)[:, : 3 * chans].astype(BF16)
        pieces[3].begin(zo)
    fold(pieces[3:4], 0)
    grad_normed = dot_plain(g_proj[...].T.astype(BF16), full_in[...].reshape(devices * in_rows, width))
    input_term, grad_gain_one, grad_shift_one = lane_norm_back(grad_normed, normal_one, inv_one, gain_one)
    grad_hidden[...] = (resid[...] + input_term).astype(BF16)
    norm_grads = jnp.concatenate(
        [grad_gain_one, grad_shift_one, grad_gain_two, grad_shift_two, jnp.zeros((4, width), F32)], 0
    )
    for j in range(devices):
        turned = pltpu.roll(norm_grads, width - j * chans, 1) if j else norm_grads
        g_tile[j, 0:4, :] = turned[0:4, :128]
        g_tile[j, 4:8, :] = small[4 * j : 4 * j + 4, :]
    for i in range(line):
        pieces[4].begin(visit(i))
    fold(pieces[4:5], 0)
    for step in range(1, line + 2):
        fold(pieces[3:], step)

    mine = flat(*spot())

    def share(i):
        other = lax.rem(mine + i, devices)
        place = (other // 8, other // 4 % 2, other // 2 % 2, other % 2)
        return send(sum_tile, everyone.at[mine], exchange.at[8], exchange.at[9], place)

    keep = pltpu.make_async_copy(sum_tile, everyone.at[mine], local)
    keep.start()
    lax.fori_loop(1, devices, lambda i, c: (share(i).start(), c)[1], 0)
    for piece in pieces:
        piece.drain()
    grad_mix.drain()
    home.drain()
    keep.wait()

    arrived = everyone.at[pl.ds(0, devices - 1)]
    shared = send(arrived, arrived, exchange.at[8], exchange.at[9], (*spot()[:3], 1 - spot()[3]))
    shared.wait_recv()
    shared.wait_send()


def layer(shards, hidden, cot, feats, table, raw, dims):
    line, devices, chans, seqs, block, blocks, width = dims
    order = raw[-1].shape[1]
    rows, tokens = blocks * seqs * chans, hidden.shape[0]
    in_rows, hidden_rows = shards[0].shape[0] + 8, shards[2].shape[0]
    shape, buffer, dma = jax.ShapeDtypeStruct, pltpu.VMEM, pltpu.SemaphoreType.DMA
    vmem = pl.BlockSpec(memory_space=pltpu.VMEM)
    tile = (devices, 8, 128)
    outs = [
        shape((tokens, width), BF16),
        shape((tokens, width), BF16),
        shape((hidden_rows, width), F32),
        shape((hidden_rows, width), F32),
        shape((chans, width), F32),
        shape((3 * chans, width), F32),
        shape(tile[1:], F32),
        shape(tile, F32),
        shape((chans, 128), F32),
        shape((chans, order), F32),
    ]
    scratch = [buffer((devices, r, width), BF16) for r in (in_rows, chans, hidden_rows, hidden_rows)]
    scratch += [
        buffer((devices, chans, 128), BF16),
        buffer((8, width), F32),
        buffer((3, seqs, chans, block * blocks), F32),
        buffer((3, rows, block), F32),
        buffer((rows, 2 * block), F32),
        buffer((rows, block), F32),
    ]
    scratch += [buffer((blocks * chans, block), F32)] * 3 + [buffer((blocks, order, block), F32)] * 4
    scratch += [buffer((chans, 128), F32), buffer((order, feats.shape[1]), F32), buffer((order, order), F32)]
    scratch += [buffer((chans, order), F32), buffer((order, 128), F32)]
    scratch += [
        buffer((in_rows, width), BF16),
        buffer((128, 128), F32),
        buffer((devices, 3, chans, 128), BF16),
        buffer((devices, 3, chans, 128), BF16),
        buffer((devices, chans, 128), BF16),
        buffer((blocks * chans, block), F32),
        buffer((rows, block), F32),
        buffer((rows, 2 * block), F32),
        buffer((width, width), BF16),
        buffer((devices, chans, width), BF16),
        buffer((devices, 3 * chans, width), BF16),
        buffer(tile, F32),
        buffer((tokens, width), F32),
        buffer((tokens, width), F32),
        buffer((tokens, width), F32),
        buffer((devices, chans, 128), BF16),
        buffer((rows, 2 * block), F32),
        buffer((3, seqs, chans, block * blocks), F32),
        buffer((blocks * chans, 2 * block), F32),
        buffer((devices * in_rows, 128), F32),
        buffer((4 * devices, 128), F32),
    ]
    scratch += [dma((4, 2 * line + 6)), dma((4, 6 * line + 1)), dma((5, 2 * line + 6)), dma((5, 7 * line))]
    scratch += [dma, dma((10,))]
    parts = [shape((devices, r, width), BF16) for r in (hidden_rows, hidden_rows, chans, 3 * chans)] + [shape(tile, F32)]
    scratch += [b for part in parts for b in reduce_scratch(line, part)]
    operands = [*shards, hidden, cot, feats, table, *raw]
    return pl.pallas_call(
        functools.partial(layer_kernel, dims),
        name="layer",
        out_shape=outs,
        in_specs=[vmem] * len(operands),
        out_specs=[vmem] * len(outs),
        scratch_shapes=scratch,
        compiler_params=pltpu.CompilerParams(collective_id=0, has_side_effects=True, vmem_limit_bytes=KERNEL_VMEM),
    )(*operands)


def finish_kernel(emb, order, *refs):
    (result, grad_hidden, up, down, out, inp, tile, everyone, chan_grads, filter_grad) = refs[:10]
    outs, desk = refs[10:-1], refs[-1]
    chans = chan_grads.shape[0]
    for target, source in zip(outs[:7], (result, grad_hidden, up, down, out, inp, filter_grad)):
        target[...] = source[...]
    taps, bias, skip, *gains = outs[7:14]
    desk[...] = jnp.zeros_like(desk)
    desk[:chans, :] = chan_grads[...]
    turned = desk[...].T
    for i in range(3):
        taps[i] = turned[3 * i : 3 * i + 3, :chans]
    bias[...] = turned[9:12, :chans]
    skip[...] = turned[12:13, :chans]
    for i, gain in enumerate(gains):
        gain[...] = tile[i : i + 1, :chans]
    for j in range(everyone.shape[0]):
        desk[4 * j : 4 * j + 4, :] = everyone[j, 4:8, :]
    pos, pos_bias, mid, mid_bias, rate = outs[14:]
    after = emb + 1 + -(emb + 1) % 8
    pos[...] = desk[:emb, :order]
    pos_bias[...] = desk[emb : emb + 1, :order]
    mid[...] = desk[after : after + order, :order]
    mid_bias[...] = desk[after + order : after + order + 1, :order]
    rate[...] = desk[after + order + 1 : after + order + 2, :order]


def finish(parts, pos_shape):
    emb, order = pos_shape
    chans = parts[8].shape[0]
    shape = jax.ShapeDtypeStruct
    vmem = pl.BlockSpec(memory_space=pltpu.VMEM)
    outs = [shape(p.shape, p.dtype) for p in parts[:6]] + [shape(parts[9].shape, F32)]
    outs += [shape((3, 3, chans), F32), shape((3, chans), F32)] + [shape((1, chans), F32)] * 5
    outs += [shape((emb, order), F32), shape((1, order), F32), shape((order, order), F32)]
    outs += [shape((1, order), F32)] * 2
    return pl.pallas_call(
        functools.partial(finish_kernel, emb, order),
        name="finish",
        out_shape=outs,
        in_specs=[vmem] * len(parts),
        out_specs=[vmem] * len(outs),
        scratch_shapes=[pltpu.VMEM((128, 128), F32)],
    )(*parts)


def shards_paired(
    hidden_in,
    cotangent,
    mixer_input_weight,
    mixer_output_weight,
    feedforward_up,
    feedforward_down,
    first_gain,
    first_shift,
    second_gain,
    second_shift,
    short_taps,
    short_bias,
    skip_scale,
    filter_out,
    pos_weight,
    pos_bias,
    mid_weight,
    mid_bias,
    sine_freq,
    decay_rate,
):
    devices = lax.axis_size(AXES)
    micro, seq_count, tok, width = hidden_in.shape
    seqs = micro * seq_count
    tokens = seqs * tok
    length = tok * devices
    chans = width // devices
    block = tok * lax.axis_size("chan")
    blocks = length // block

    line = devices // 8
    def row(vector):
        return vector.reshape(1, -1)

    shards = [mixer_input_weight.T, mixer_output_weight.T, feedforward_up.T, feedforward_down]
    raw = [row(v) for v in (first_gain, first_shift, second_gain, second_shift)]
    raw += [short_taps, short_bias, row(skip_scale), row(decay_rate), filter_out.T]
    raw += [pos_weight, row(pos_bias), mid_weight, row(sine_freq), row(mid_bias)]
    hidden = hidden_in.reshape(tokens, width)
    features, table = jnp.asarray(feature_blocks(length, block)), jnp.asarray(fixed_table(block))
    dims = (line, devices, chans, seqs, block, blocks, width)
    parts = layer(shards, hidden, cotangent.reshape(tokens, width), features, table, raw, dims)
    outs = finish(parts, pos_weight.shape)
    result, grad_hidden, up, down, out, inp, filter_grad, taps, bias, skip, *rest = outs
    gains, (pos, pos_bias, mid, mid_bias, rate) = rest[:4], rest[4:]
    return (
        result.reshape(hidden_in.shape),
        grad_hidden.reshape(hidden_in.shape),
        inp.T,
        out.T,
        up.T,
        down,
        *[g.reshape(-1) for g in gains],
        taps,
        bias,
        skip.reshape(-1),
        filter_grad.T,
        pos,
        pos_bias.reshape(-1),
        mid,
        mid_bias.reshape(-1),
        rate.reshape(-1),
    )


def shards(
    hidden_in,
    cotangent,
    mixer_input_weight,
    mixer_output_weight,
    feedforward_up,
    feedforward_down,
    first_gain,
    first_shift,
    second_gain,
    second_shift,
    short_taps,
    short_bias,
    skip_scale,
    filter_out,
    pos_weight,
    pos_bias,
    mid_weight,
    mid_bias,
    sine_freq,
    decay_rate,
):
    devices = lax.axis_size(AXES)
    micro, seq_count, tok, width = hidden_in.shape
    seqs = micro * seq_count
    tokens = seqs * tok
    length = tok * devices
    chans = width // devices
    block = tok * lax.axis_size("chan")
    blocks = length // block

    norms = jnp.stack([first_gain, first_shift, second_gain, second_shift])
    own = [mixer_input_weight.T, feedforward_up.T, feedforward_down, mixer_output_weight.T]
    full = [lax.all_gather(shard, AXES, axis=0, tiled=True) for shard in own]
    norms = lax.all_gather(norms, AXES, axis=1, tiled=True)
    weight_in, weight_up, weight_down, weight_out = full
    norms = norms.astype(F32)
    gain_one, shift_one, gain_two, shift_two = norms[0], norms[1], norms[2], norms[3]

    freq = sine_freq.astype(F32)
    w_pos, w_mid, w_fil = pos_weight.astype(F32), mid_weight.astype(F32), filter_out.astype(F32)
    lags, features, first_sum, first_act, second_sum, second_act = filter_hidden(
        length, w_pos, pos_bias.astype(F32), w_mid, mid_bias.astype(F32), freq
    )
    decay = jnp.exp(-lags[None, :] * decay_rate.astype(F32)[:, None])
    kernel = contract(w_fil, second_act, 0, 0, EXACT) * decay
    table = block_table(block)
    sign = 1.0 - 2.0 * (lax.iota(jnp.int32, block) % 2).astype(F32)
    ker_re, ker_im = to_spectrum(kernel.reshape(chans, blocks, block), table)

    def with_previous(spec):
        before = jnp.concatenate([jnp.zeros_like(spec[:, :1]), spec[:, :-1]], 1)
        return spec + sign * before

    k_re, k_alt, k_im = packed_kernel(with_previous(ker_re), with_previous(ker_im))

    values = hidden_in.reshape(tokens, width).astype(F32)
    normed, normal_one, inv_one = layer_norm(values, gain_one, shift_one)
    normed = normed.astype(BF16)
    projected = contract(weight_in, normed, 1, 1).astype(BF16)
    projected = projected.reshape(3, devices, chans, tokens).transpose(1, 0, 2, 3)
    arrived = exchange(projected)

    def by_sequence(values):
        parts = values.shape[1]
        values = values.reshape(devices, parts, chans, seqs, tok)
        return values.transpose(1, 3, 2, 0, 4).reshape(parts, seqs, chans, length)

    def by_device(values):
        parts = values.shape[0]
        values = values.reshape(parts, seqs, chans, devices, tok)
        return values.transpose(3, 0, 2, 1, 4).reshape(devices, parts, chans, tokens)

    steps = by_sequence(arrived).astype(F32)
    taps = short_taps.astype(F32)[:, :, None, :, None]
    conv = short_bias.astype(F32)[:, None, :, None]
    for i in range(3):
        conv = conv + taps[i] * delayed(steps, i)
    gate_out, gate_in, signal = conv[0], conv[1], conv[2]
    gated = signal * gate_in
    sig_re, sig_im = to_spectrum(gated.reshape(seqs, chans, blocks, block), table)

    def shifted_sum(make):
        total = None
        for d in range(blocks):
            term = make(d)
            total = term if total is None else tuple(a + b for a, b in zip(total, term))
        return total

    def ahead(x, d):
        return x if d == 0 else jnp.pad(x[:, :, :-d], ((0, 0), (0, 0), (d, 0), (0, 0)))

    def back(x, d):
        return x if d == 0 else jnp.pad(x[:, :, d:], ((0, 0), (0, 0), (0, d), (0, 0)))

    def forward_term(d):
        re, im = ahead(sig_re, d), ahead(sig_im, d)
        kr, ka, ki = k_re[:, d : d + 1], k_alt[:, d : d + 1], k_im[:, d : d + 1]
        return re * kr - im * ki, re * ki + im * ka

    out_re, out_im = shifted_sum(forward_term)
    long_out = from_spectrum(out_re, out_im, table).reshape(seqs, chans, length)
    skip = skip_scale.astype(F32)[None, :, None]
    long_total = long_out + skip * gated
    mixed = (long_total * gate_out).astype(BF16)
    mixed = exchange(by_device(mixed[None])).reshape(width, tokens)

    resid = values + contract(mixed, weight_out, 0, 1)
    second, normal_two, inv_two = layer_norm(resid, gain_two, shift_two)
    second = second.astype(BF16)
    upper = contract(second, weight_up, 1, 1)
    active, slope = gelu_parts(upper)
    active = active.astype(BF16)
    result = resid + contract(active, weight_down, 1, 0)

    cot = cotangent.reshape(tokens, width)
    grad_down = contract(active, cot, 0, 0)
    grad_upper = (contract(cot, weight_down, 1, 1) * slope).astype(BF16)
    grad_up = contract(grad_upper, second, 0, 0)
    grad_second = contract(grad_upper, weight_up, 1, 0)
    resid_term, grad_gain_two, grad_shift_two = layer_norm_back(grad_second, normal_two, inv_two, gain_two)
    grad_resid = cot.astype(F32) + resid_term
    grad_branch = grad_resid.astype(BF16)
    grad_out_w = contract(grad_branch, mixed, 0, 1)
    grad_mixed = contract(weight_out, grad_branch, 0, 1).astype(BF16)
    grad_mixed = exchange(grad_mixed.reshape(devices, 1, chans, tokens))
    grad_mixed = by_sequence(grad_mixed)[0].astype(F32)

    grad_gate_out = grad_mixed * long_total
    grad_long = grad_mixed * gate_out
    grad_skip = jnp.sum(grad_long * gated, (0, 2))
    gl_re, gl_im = to_spectrum(grad_long.reshape(seqs, chans, blocks, block), table)

    def signal_term(d):
        re, im = back(gl_re, d), back(gl_im, d)
        kr, ka, ki = k_re[:, d : d + 1], k_alt[:, d : d + 1], k_im[:, d : d + 1]
        return re * kr + im * ki, im * ka - re * ki

    gg_re, gg_im = shifted_sum(signal_term)
    grad_gated = from_spectrum(gg_re, gg_im, table).reshape(seqs, chans, length) + skip * grad_long

    first_slot = lax.iota(jnp.int32, block) == 0
    kg_re, kg_im = [], []
    for d in range(blocks):
        s_re, s_im = sig_re[:, :, : blocks - d], sig_im[:, :, : blocks - d]
        g_re, g_im = gl_re[:, :, d:], gl_im[:, :, d:]
        same, other = g_re * s_re, g_im * s_im
        kg_re.append(jnp.sum(jnp.where(first_slot, same, same + other), (0, 2)))
        kg_im.append(jnp.sum(jnp.where(first_slot, other, g_im * s_re - g_re * s_im), (0, 2)))
    kg_re, kg_im = jnp.stack(kg_re, 1), jnp.stack(kg_im, 1)

    def with_next(spec):
        after = jnp.concatenate([spec[:, 1:], jnp.zeros_like(spec[:, :1])], 1)
        return spec + sign * after

    grad_kernel = from_spectrum(with_next(kg_re), with_next(kg_im), table).reshape(chans, length)

    grad_conv = jnp.stack([grad_gate_out, grad_gated * signal, grad_gated * gate_in])
    grad_bias = jnp.sum(grad_conv, (1, 3))
    grad_taps = jnp.stack([jnp.sum(grad_conv * delayed(steps, i), (1, 3)) for i in range(3)])
    grad_steps = taps[0] * grad_conv
    for i in (1, 2):
        grad_steps = grad_steps + taps[i] * advanced(grad_conv, i)
    grad_proj = exchange(by_device(grad_steps.astype(BF16)))
    grad_proj = grad_proj.transpose(1, 0, 2, 3).reshape(3 * width, tokens)

    fade = grad_kernel * decay
    grad_filter = contract(second_act, fade, 1, 1, EXACT)
    grad_two = contract(w_fil, fade, 1, 0, EXACT) * jnp.cos(freq[:, None] * second_sum)
    grad_freq = jnp.sum(grad_two * second_sum, 1)
    grad_two = grad_two * freq[:, None]
    grad_mid = contract(first_act, grad_two, 1, 1, EXACT)
    grad_one = contract(w_mid, grad_two, 1, 0, EXACT) * jnp.cos(freq[:, None] * first_sum)
    grad_freq = grad_freq + jnp.sum(grad_one * first_sum, 1)
    grad_one = grad_one * freq[:, None]
    grad_pos = contract(features, grad_one, 1, 1, EXACT)
    small = jnp.concatenate(
        [grad_pos, jnp.sum(grad_one, 1)[None], grad_mid, jnp.sum(grad_two, 1)[None], grad_freq[None]]
    )
    emb, order = pos_weight.shape

    grad_in = contract(grad_proj, normed, 1, 0)
    grad_normed = contract(grad_proj, weight_in, 0, 0)
    input_term, grad_gain_one, grad_shift_one = layer_norm_back(grad_normed, normal_one, inv_one, gain_one)
    grad_hidden = (grad_resid + input_term).astype(BF16)

    norm_grads = jnp.stack([grad_gain_one, grad_shift_one, grad_gain_two, grad_shift_two])
    sums = [grad_in, grad_up, grad_down, grad_out_w]
    sums = [
        lax.psum_scatter(g.astype(BF16), AXES, scatter_dimension=0, tiled=True).astype(F32) for g in sums
    ]
    norm_grads = lax.psum_scatter(norm_grads, AXES, scatter_dimension=1, tiled=True)
    small = lax.psum(small, AXES)
    return (
        result.astype(BF16).reshape(hidden_in.shape),
        grad_hidden.reshape(hidden_in.shape),
        sums[0].T,
        sums[3].T,
        sums[1].T,
        sums[2],
        norm_grads[0],
        norm_grads[1],
        norm_grads[2],
        norm_grads[3],
        grad_taps,
        grad_bias,
        grad_skip,
        grad_filter,
        small[:emb],
        small[emb],
        small[emb + 1 : emb + 1 + order],
        small[emb + 1 + order],
        small[emb + 2 + order],
    )


def solution(mesh):
    paired = mesh.shape["chan"] == 4 and mesh.shape["blk"] == 8
    rows, spread, tokens = P(AXES), P(None, AXES), P(None, None, AXES, None)
    params = (rows, rows, rows, rows, P(None, None, AXES), spread, rows, spread, P(), P(), P(), P(), P())
    return jax.shard_map(
        shards_paired if paired else shards,
        mesh=mesh,
        in_specs=(tokens, tokens, spread, spread, spread, P(AXES, None)) + params + (rows,),
        out_specs=(tokens, tokens, spread, spread, spread, P(AXES, None)) + params,
        check_vma=False,
    )
```

```python
import functools
import math

import jax
import jax.numpy as jnp
import numpy as np
from jax import lax
from jax.experimental import pallas as pl
from jax.experimental.pallas import tpu as pltpu
from jax.sharding import PartitionSpec as P

EPS = 1e-05
BANDS = 16
EXACT = lax.Precision.HIGHEST
AXES = ("blk", "chan")
F32 = jnp.float32
BF16 = jnp.bfloat16
MESH = pl.DeviceIdType.MESH
KERNEL_VMEM = 62 << 20


def contract(a, b, dim_a, dim_b, precision=None):
    return lax.dot_general(
        a, b, (((dim_a,), (dim_b,)), ((), ())), precision=precision, preferred_element_type=F32
    )


def positions(length):
    lags = jnp.arange(length).astype(F32)
    band_freq = 0.0001 + (BANDS - 1 - 0.0001) * jnp.arange(BANDS).astype(F32) / (BANDS - 1)
    phase = 2.0 * math.pi / length * lags[None, :] * band_freq[:, None]
    return lags, jnp.concatenate([lags[None, :] / (length - 1), jnp.cos(phase), -jnp.sin(phase)], 0)


def feature_blocks(length, block):
    lags = np.arange(length).astype(np.float32)
    bands = np.arange(BANDS).astype(np.float32)
    band_freq = np.float32(0.0001) + np.float32(BANDS - 1 - 0.0001) * bands / np.float32(BANDS - 1)
    phase = np.float32(2.0 * math.pi / length) * lags[None, :] * band_freq[:, None]
    ramp = lags[None, :] / np.float32(length - 1)
    rows = np.concatenate([ramp, np.cos(phase), -np.sin(phase), np.ones_like(ramp)])
    rows = np.pad(rows, ((0, -len(rows) % 8), (0, 0))).astype(np.float32)
    return np.ascontiguousarray(rows.reshape(len(rows), -1, block).transpose(1, 0, 2))


def fixed_table(block):
    spot, freq = np.arange(block)[:, None], np.arange(block)[None, :]
    phase = (np.pi / block) * (spot * freq % (2 * block))
    imag = np.where(freq == 0, 1.0 - 2.0 * (spot % 2), -np.sin(phase))
    return np.concatenate([np.cos(phase), imag], 1).astype(np.float32)


def filter_hidden(length, pos_weight, pos_bias, mid_weight, mid_bias, sine_freq):
    lags, features = positions(length)
    freq = sine_freq[:, None]
    first_sum = contract(pos_weight, features, 0, 0, EXACT) + pos_bias[:, None]
    first = jnp.sin(freq * first_sum)
    second_sum = contract(mid_weight, first, 0, 0, EXACT) + mid_bias[:, None]
    second = jnp.sin(freq * second_sum)
    return lags, features, first_sum, first, second_sum, second


def block_table(block):
    spot = lax.broadcasted_iota(jnp.int32, (block, block), 0)
    freq = lax.broadcasted_iota(jnp.int32, (block, block), 1)
    phase = (math.pi / block) * (spot * freq % (2 * block)).astype(F32)
    parity = 1.0 - 2.0 * (spot % 2).astype(F32)
    imag = jnp.where(freq == 0, parity, -jnp.sin(phase))
    return jnp.concatenate([jnp.cos(phase), imag], 1)


def to_spectrum(blocks, table):
    spec = lax.dot_general(
        blocks, table, (((blocks.ndim - 1,), (0,)), ((), ())), precision=EXACT, preferred_element_type=F32
    )
    half = table.shape[0]
    return spec[..., :half], spec[..., half:]


def from_spectrum(real, imag, table):
    half = table.shape[0]
    weight = jnp.where(lax.iota(jnp.int32, half) == 0, 0.5 / half, 1.0 / half)
    spec = jnp.concatenate([real * weight, imag * weight], -1)
    return lax.dot_general(
        spec, table, (((spec.ndim - 1,), (1,)), ((), ())), precision=EXACT, preferred_element_type=F32
    )


def packed_kernel(real, imag):
    first = lax.iota(jnp.int32, real.shape[-1]) == 0
    return real, jnp.where(first, imag, real), jnp.where(first, 0.0, imag)


def layer_norm(values, gain, shift):
    center = values - jnp.mean(values, -1, keepdims=True)
    scale_inv = lax.rsqrt(jnp.mean(center * center, -1, keepdims=True) + EPS)
    normal = center * scale_inv
    return normal * gain + shift, normal, scale_inv


def layer_norm_back(grad_out, normal, scale_inv, gain):
    grad_normal = grad_out * gain
    inner = grad_normal - jnp.mean(grad_normal, -1, keepdims=True)
    inner = inner - normal * jnp.mean(grad_normal * normal, -1, keepdims=True)
    return inner * scale_inv, jnp.sum(grad_out * normal, 0), jnp.sum(grad_out, 0)


def gelu_parts(v):
    root = math.sqrt(2.0 / math.pi)
    inner = root * (v + 0.044715 * v * v * v)
    t = jnp.tanh(inner)
    value = 0.5 * v * (1.0 + t)
    slope = 0.5 * (1.0 + t) + 0.5 * v * (1.0 - t * t) * root * (1.0 + 3.0 * 0.044715 * v * v)
    return value, slope


def delayed(values, steps):
    if steps == 0:
        return values
    pad = jnp.zeros(values.shape[:-1] + (steps,), values.dtype)
    return jnp.concatenate([pad, values[..., :-steps]], -1)


def advanced(values, steps):
    if steps == 0:
        return values
    pad = jnp.zeros(values.shape[:-1] + (steps,), values.dtype)
    return jnp.concatenate([values[..., steps:], pad], -1)


def exchange(values):
    return lax.all_to_all(values, AXES, split_axis=0, concat_axis=0, tiled=True)


def spot():
    b, c = lax.axis_index("blk"), lax.axis_index("chan")
    return b // 2, b % 2, c // 2, c % 2


def at(z, y, x, k):
    return {"blk": z * 2 + y, "chan": x * 2 + k}


def flat(z, y, x, k):
    return ((z * 2 + y) * 2 + x) * 2 + k


def when(condition, act):
    pl.when(condition)(act)


def send(src, dst, send_sem, recv_sem, place):
    return pltpu.make_async_remote_copy(
        src_ref=src, dst_ref=dst, send_sem=send_sem, recv_sem=recv_sem, device_id=at(*place), device_id_type=MESH
    )


def greet_near(line):
    z, y, x, k = spot()
    barrier = pltpu.get_barrier_semaphore()

    def hello(*place):
        pl.semaphore_signal(barrier, inc=1, device_id=at(*place), device_id_type=MESH)

    hello(z, 1 - y, x, k)
    hello(z, y, 1 - x, k)
    hello(z, y, x, 1 - k)
    when(z > 0, lambda: hello(z - 1, y, x, k))
    when(z < line - 1, lambda: hello(z + 1, y, x, k))
    pl.semaphore_wait(barrier, 3 + jnp.minimum(z, 1) + jnp.minimum(line - 1 - z, 1))


def low_rows(rows):
    return (rows + 16) // 32 * 16 if rows > 8 else rows


class Gather:
    def __init__(self, line, shard, full, sends, recvs, local):
        self.line, self.shard, self.full, self.s, self.r, self.local = line, shard, full, sends, recvs, local
        self.rows = shard.shape[0]
        self.low = low_rows(self.rows)
        self.z, self.y, self.x, self.k = spot()
        self.half = line // 2
        self.inward = 1 - 2 * (self.z // self.half)
        self.inner = self.z == self.half - 1 + self.z // self.half

    def copy(self, send_at, recv_at, shard, place, rows=None):
        ref = self.full.at[shard] if rows is None else self.full.at[shard, pl.ds(*rows)]
        return send(ref, ref, self.s.at[send_at], self.r.at[recv_at], place)

    def together(self, send_at, recv_at, count, rows=None):
        return self.copy(send_at, recv_at, pl.ds(0, count), (self.z, self.y, self.x, 1 - self.k), rows)

    def up(self, zo):
        return self.copy(zo, zo, flat(zo, self.y, self.x, self.k), (self.z + 1, self.y, self.x, self.k))

    def down(self, zo):
        return self.copy(self.line + zo, self.line + zo, flat(zo, self.y, self.x, self.k), (self.z - 1, self.y, self.x, self.k))

    def to_x(self, zo):
        return self.copy(2 * self.line, 2 * self.line + zo, flat(zo, self.y, self.x, self.k), (self.z, self.y, 1 - self.x, self.k))

    def to_y(self, zo):
        return self.copy(2 * self.line + 1, 3 * self.line + zo, flat(zo, self.y, self.x, self.k), (self.z, 1 - self.y, self.x, self.k))

    def low_y(self, zo, other_y=False):
        shard = flat(zo, 1 - self.y if other_y else self.y, 1 - self.x, self.k)
        return self.copy(2 * self.line + 2, 5 * self.line + zo % self.half, shard, (self.z, 1 - self.y, self.x, self.k), (0, self.low))

    def high_x(self, zo, other_x=False):
        shard = flat(zo, 1 - self.y, 1 - self.x if other_x else self.x, self.k)
        rows = (self.low, self.rows - self.low)
        recv_at = 5 * self.line + self.half + zo % self.half
        return self.copy(2 * self.line + 3, recv_at, shard, (self.z, self.y, 1 - self.x, self.k), rows)

    def core(self, zo, yo, xo, k):
        return self.copy(2 * self.line + 4, 6 * self.line, flat(zo, yo, xo, k), (self.z, self.y, self.x, 1 - self.k))

    def cross(self, zo, step):
        shard = flat(zo, 1 - self.y, 1 - self.x, self.k)
        return self.copy(2 * self.line + 5, 4 * self.line + zo, shard, (self.z + step, self.y, self.x, self.k))

    def same(self, zo):
        return zo // self.half == self.z // self.half

    def line_has(self, zo):
        self.to_x(zo).start()
        self.to_y(zo).start()
        self.core(zo, self.y, self.x, self.k).start()

    def begin(self):
        own = self.full.at[flat(self.z, self.y, self.x, self.k)]
        copy = pltpu.make_async_copy(self.shard, own, self.local)
        copy.start()
        copy.wait()
        when(self.z < self.line - 1, lambda: self.up(self.z).start())
        when(self.z > 0, lambda: self.down(self.z).start())
        self.line_has(self.z)

    def each(self, distance, act):
        if distance == 0:
            act(self.z)
        else:
            when(self.z - distance >= 0, lambda: act(self.z - distance))
            when(self.z + distance < self.line, lambda: act(self.z + distance))

    def along(self, distance):
        def from_below():
            zo = self.z - distance
            self.up(zo).wait_recv()
            when(self.z < self.line - 1, lambda: self.up(zo).start())
            self.line_has(zo)

        def from_above():
            zo = self.z + distance
            self.down(zo).wait_recv()
            when(self.z > 0, lambda: self.down(zo).start())
            self.line_has(zo)

        when(self.z - distance >= 0, from_below)
        when(self.z + distance < self.line, from_above)

    def plane(self, distance):
        def act(zo):
            self.to_x(zo).wait_recv()
            when(self.same(zo), lambda: self.low_y(zo).start())
            self.core(zo, self.y, 1 - self.x, self.k).start()
            self.to_y(zo).wait_recv()
            if self.low < self.rows:
                when(self.same(zo), lambda: self.high_x(zo).start())
            self.core(zo, 1 - self.y, self.x, self.k).start()

        self.each(distance, act)

    def corner(self, distance):
        def near(zo):
            self.low_y(zo, True).wait_recv()
            if self.low < self.rows:
                self.high_x(zo, True).wait_recv()
            when(self.inner, lambda: self.cross(zo, self.inward).start())

        def far(zo):
            self.cross(zo, self.inward).wait_recv()
            when(self.inner, lambda: self.cross(zo, -self.inward).start())

        def act(zo):
            when(self.same(zo), lambda: near(zo))
            when(jnp.logical_not(self.same(zo)), lambda: far(zo))
            self.core(zo, 1 - self.y, 1 - self.x, self.k).start()

        self.each(distance, act)

    def finish(self):
        self.together(2 * self.line + 4, 6 * self.line, 4 * self.line).wait_recv()

    def drain(self):
        line, high = self.line, self.rows - self.low
        for zo in range(line):
            when(jnp.logical_and(self.z < line - 1, zo <= self.z), lambda: self.up(zo).wait_send())
            when(jnp.logical_and(self.z > 0, zo >= self.z), lambda: self.down(zo).wait_send())
        self.together(2 * line, 0, line).wait_send()
        self.together(2 * line + 1, 0, line).wait_send()
        self.together(2 * line + 2, 0, self.half, (0, self.low)).wait_send()
        if high:
            self.together(2 * line + 3, 0, self.half, (self.low, high)).wait_send()
        self.together(2 * line + 4, 0, 4 * line).wait_send()
        when(self.inner, lambda: self.together(2 * line + 5, 0, line).wait_send())


class Reduce:
    def __init__(self, line, part, out, chip, low_y, high_x, by_x, by_y, by_z, crossed, sends, recvs):
        self.line, self.part, self.out, self.chip = line, part, out, chip
        self.low_buf, self.high_buf, self.x_buf, self.y_buf, self.z_buf = low_y, high_x, by_x, by_y, by_z
        self.crossed = crossed
        self.s, self.r = sends, recvs
        self.rows = part.shape[1]
        self.low = low_rows(self.rows)
        self.z, self.y, self.x, self.k = spot()
        self.half = line // 2
        self.inward = 1 - 2 * (self.z // self.half)
        self.inner = self.z == self.half - 1 + self.z // self.half

    def index(self, zo, yo, xo):
        return (zo * 2 + yo) * 2 + xo

    def copy(self, send_at, recv_at, src, dst, place):
        return send(src, dst, self.s.at[send_at], self.r.at[recv_at], place)

    def together(self, send_at, recv_at, ref):
        return self.copy(send_at, recv_at, ref, ref, (self.z, self.y, self.x, 1 - self.k))

    def core(self, zo, yo, xo):
        i = self.index(zo, yo, xo)
        src = self.part.at[flat(zo, yo, xo, 1 - self.k)]
        return self.copy(2 * self.line + 4, 5 * self.line + zo, src, self.chip.at[i], (self.z, self.y, self.x, 1 - self.k))

    def corner_of(self, zo):
        return self.index(zo, 1 - self.y, 1 - self.x)

    def low_y(self, zo):
        src = self.chip.at[self.corner_of(zo), pl.ds(0, self.low)]
        slot = zo % self.half
        place = (self.z, 1 - self.y, self.x, self.k)
        return self.copy(2 * self.line + 2, 6 * self.line + slot, src, self.low_buf.at[slot], place)

    def high_x(self, zo):
        src = self.chip.at[self.corner_of(zo), pl.ds(self.low, self.rows - self.low)]
        slot = zo % self.half
        place = (self.z, self.y, 1 - self.x, self.k)
        return self.copy(2 * self.line + 3, 6 * self.line + self.half + slot, src, self.high_buf.at[slot], place)

    def to_x(self, zo):
        src = self.chip.at[self.index(zo, self.y, 1 - self.x)]
        return self.copy(2 * self.line, 2 * self.line + zo, src, self.x_buf.at[zo], (self.z, self.y, 1 - self.x, self.k))

    def to_y(self, zo):
        src = self.chip.at[self.index(zo, 1 - self.y, self.x)]
        return self.copy(2 * self.line + 1, 3 * self.line + zo, src, self.y_buf.at[zo], (self.z, 1 - self.y, self.x, self.k))

    def up(self, zo):
        src = self.chip.at[self.index(zo, self.y, self.x)]
        return self.copy(zo, zo, src, self.z_buf.at[zo + 1], (self.z + 1, self.y, self.x, self.k))

    def down(self, zo):
        src = self.chip.at[self.index(zo, self.y, self.x)]
        return self.copy(self.line + zo, self.line + zo, src, self.z_buf.at[zo], (self.z - 1, self.y, self.x, self.k))

    def cross(self, zo):
        src = self.chip.at[self.corner_of(zo)]
        place = (self.z + self.inward, self.y, self.x, self.k)
        return self.copy(2 * self.line + 5, 4 * self.line + zo, src, self.crossed.at[zo], place)

    def add(self, i, other, rows=None):
        if rows is None:
            self.chip[i] = self.chip[i] + other
        else:
            self.chip[i, pl.ds(*rows)] = self.chip[i, pl.ds(*rows)] + other

    def begin(self, zo):
        for yo, xo in ((1 - self.y, 1 - self.x), (self.y, 1 - self.x), (1 - self.y, self.x), (self.y, self.x)):
            self.core(zo, yo, xo).start()

    def corner(self, zo, near):
        def joined(yo, xo):
            self.add(self.index(zo, yo, xo), self.part[flat(zo, yo, xo, self.k)])

        def crossing():
            self.cross(zo).wait_recv()
            self.add(self.corner_of(zo), self.crossed[zo])

        arrived = self.chip.at[pl.ds(4 * zo, 4)]
        self.together(2 * self.line + 4, 5 * self.line + zo, arrived).wait_recv()
        joined(1 - self.y, 1 - self.x)
        if not near:
            joined(self.y, 1 - self.x)
            self.to_x(zo).start()
            joined(1 - self.y, self.x)
            self.to_y(zo).start()
        when(self.inner, crossing)
        if near:
            self.low_y(zo).start()
            if self.low < self.rows:
                self.high_x(zo).start()
            joined(self.y, 1 - self.x)
            joined(1 - self.y, self.x)
        else:
            self.cross(zo).start()
        joined(self.y, self.x)

    def plane(self, zo):
        self.low_y(zo).wait_recv()
        self.add(self.index(zo, self.y, 1 - self.x), self.low_buf[zo % self.half], (0, self.low))
        self.to_x(zo).start()
        if self.low < self.rows:
            self.high_x(zo).wait_recv()
            high = (self.low, self.rows - self.low)
            self.add(self.index(zo, 1 - self.y, self.x), self.high_buf[zo % self.half], high)
        self.to_y(zo).start()

    def along(self, zo, own):
        i = self.index(zo, self.y, self.x)
        self.to_x(zo).wait_recv()
        self.to_y(zo).wait_recv()
        total = self.x_buf[zo].astype(F32) + self.y_buf[zo].astype(F32) + self.chip[i].astype(F32)

        def from_below():
            self.up(zo).wait_recv()
            self.add(i, self.z_buf[zo + 1])

        def from_above():
            self.down(zo).wait_recv()
            self.add(i, self.z_buf[zo])

        def rising():
            when(self.z > 0, from_below)
            self.up(zo).start()

        def falling():
            when(self.z < self.line - 1, from_above)
            self.down(zo).start()

        def last_below():
            self.up(zo).wait_recv()
            self.out[...] += self.z_buf[zo + 1].astype(F32)

        def last_above():
            self.down(zo).wait_recv()
            self.out[...] += self.z_buf[zo].astype(F32)

        if own:
            self.out[...] = total
            when(self.z > 0, last_below)
            when(self.z < self.line - 1, last_above)
        else:
            self.chip[i] = total.astype(self.chip.dtype)
            when(zo > self.z, rising)
            when(zo < self.z, falling)

    def drain(self):
        line, low, high = self.line, self.low, self.rows - self.low
        shards, halves = self.chip.at[pl.ds(0, line)], pl.ds(0, self.half)
        for zo in range(line):
            when(zo > self.z, lambda: self.up(zo).wait_send())
            when(zo < self.z, lambda: self.down(zo).wait_send())
        self.together(2 * line, 0, shards).wait_send()
        self.together(2 * line + 1, 0, shards).wait_send()
        self.together(2 * line + 2, 0, self.chip.at[halves, pl.ds(0, low)]).wait_send()
        if high:
            self.together(2 * line + 3, 0, self.chip.at[halves, pl.ds(low, high)]).wait_send()
        self.together(2 * line + 4, 0, self.part.at[pl.ds(0, 4 * line)]).wait_send()
        self.together(2 * line + 5, 0, self.chip.at[halves]).wait_send()


BUFFERS = 7


def reduce_scratch(line, part):
    _, rows, width = part.shape
    low = low_rows(rows)
    high = max(rows - low, 8)
    half = line // 2
    sizes = [(line * 4, rows), (half, low), (half, high), (line, rows), (line, rows), (line + 1, rows), (line, rows)]
    return [pltpu.VMEM(s + (width,), part.dtype) for s in sizes]


def dot_rows(a, b, precision=None):
    return lax.dot_general(a, b, (((1,), (1,)), ((), ())), precision=precision, preferred_element_type=F32)


def dot_plain(a, b, precision=None):
    return lax.dot_general(a, b, (((1,), (0,)), ((), ())), precision=precision, preferred_element_type=F32)


def eighths(value):
    return pl.multiple_of(value, 8)


class Exchange:
    def __init__(self, src, dst, send_sem, recv_sem, devices):
        self.src, self.dst, self.s, self.r, self.devices = src, dst, send_sem, recv_sem, devices
        self.me = flat(*spot())

    def copy(self, i):
        other = lax.rem(self.me + i, self.devices)
        place = (other // 8, other // 4 % 2, other // 2 % 2, other % 2)
        return send(self.src.at[other], self.dst.at[self.me], self.s, self.r, place)

    def together(self, ref):
        z, y, x, k = spot()
        ref = ref.at[pl.ds(0, self.devices - 1)]
        return send(ref, ref, self.s, self.r, (z, y, x, 1 - k))

    def start(self):
        lax.fori_loop(1, self.devices, lambda i, c: (self.copy(i).start(), c)[1], 0)
        self.dst[self.me] = self.src[self.me]

    def arrive(self):
        self.together(self.dst).wait_recv()

    def drain(self):
        self.together(self.src).wait_send()


def low_lanes(shape):
    return lax.broadcasted_iota(jnp.int32, shape, 1) < 64


def merge_halves(first, second):
    low = low_lanes(first.shape)
    return (
        jnp.where(low, first, pltpu.roll(second, 64, 1)),
        jnp.where(low, pltpu.roll(first, 64, 1), second),
    )


def lane_norm(values, gain, shift):
    center = values - jnp.mean(values, 1, keepdims=True)
    scale_inv = lax.rsqrt(jnp.mean(center * center, 1, keepdims=True) + EPS)
    normal = center * scale_inv
    return normal * gain + shift, normal, scale_inv


def slot_zero(shape):
    return lax.broadcasted_iota(jnp.int32, shape, 1) == 0


def slot_sign(shape):
    return 1.0 - 2.0 * (lax.broadcasted_iota(jnp.int32, shape, 1) % 2).astype(F32)


def slot_weight(shape):
    return jnp.where(slot_zero(shape), 0.5 / shape[1], 1.0 / shape[1])


def column(params, index):
    return params[:, index : index + 1]


def norm_rows(stack, count, chans, width):
    total = None
    for j in range(count):
        tile = stack(j).astype(F32)[:, :128]
        tile = jnp.where(lax.broadcasted_iota(jnp.int32, tile.shape, 1) < chans, tile, 0.0)
        wide = jnp.concatenate([tile, jnp.zeros((tile.shape[0], width - 128), F32)], 1)
        wide = pltpu.roll(wide, j * chans, 1) if j else wide
        total = wide if total is None else total + wide
    return total


RAW = 14


def prepare(in_t, raw, own_in, desk, params, pos_t, mid_t, fil_t, cols):
    gain_one, shift_one, gain_two, shift_two, taps, bias, skip, decay, fil, pos, pos_bias, mid, rate, mid_bias = raw
    chans, order, emb = fil.shape[0], mid.shape[0], pos.shape[0]

    def put(row, values, wide):
        desk[row : row + values.shape[0], :wide] = values.astype(F32)

    desk[...] = jnp.zeros_like(desk)
    for i, ref in enumerate((gain_one, shift_one, gain_two, shift_two)):
        put(i, ref[...], chans)
    norms = jnp.concatenate([desk[:8, :], jnp.zeros((8, in_t.shape[1] - 128), F32)], 1)
    own_in[...] = jnp.concatenate([in_t[...].astype(F32), norms], 0).astype(BF16)
    for i in range(3):
        put(3 * i, taps[i], chans)
    put(9, bias[...], chans)
    put(12, skip[...], chans)
    put(13, decay[...], chans)
    params[...] = desk[...].T[:chans]
    desk[...] = jnp.zeros_like(desk)
    put(0, pos[...], order)
    put(emb, pos_bias[...], order)
    pos_t[...] = desk[...].T[:order, : pos_t.shape[1]]
    desk[...] = jnp.zeros_like(desk)
    put(0, mid[...], order)
    mid_t[...] = desk[...].T[:order, :order]
    desk[...] = jnp.zeros_like(desk)
    put(0, rate[...], order)
    put(1, mid_bias[...], order)
    cols[...] = desk[...].T[:order]
    fil_t[...] = fil[...].astype(F32)


def lane_norm_back(grad_out, normal, scale_inv, gain):
    grad_normal = grad_out * gain
    inner = grad_normal - jnp.mean(grad_normal, 1, keepdims=True)
    inner = inner - normal * jnp.mean(grad_normal * normal, 1, keepdims=True)
    return inner * scale_inv, jnp.sum(grad_out * normal, 0, keepdims=True), jnp.sum(grad_out, 0, keepdims=True)


LATE = (0, 3, 4, 5)


def layer_kernel(dims, *refs):
    line, devices, chans, seqs, block, blocks, width = dims
    (in_t, own_out, own_up, own_down, hidden, cot, feats, table) = refs[:8]
    raw = refs[8 : 8 + RAW]
    refs = refs[8 + RAW :]
    (result, grad_hidden, sum_up, sum_down, sum_out, sum_in, sum_tile, everyone, chan_grads, filter_grad) = refs[:10]
    refs = refs[10:]
    (full_in, full_out, full_up, full_down, mixed_in, norms_ref, steps, conv, spec, total, k_re, k_alt, k_im) = refs[:13]
    (one, cos_one, two, cos_two, params, pos_t, mid_t, fil_t, cols) = refs[13:22]
    (own_in, desk, proj_send, proj_recv, mix_send, kernel_buf, gated, sums) = refs[22:30]
    (w_flat, g_out, g_in, g_tile, resid, value_sum, second_sum, mix_recv, g_spec, g_conv) = refs[30:40]
    (k_sums, g_proj, small) = refs[40:43]
    (gather_send, gather_recv, sends, recvs, local, exchange) = refs[43:49]
    buffers = refs[49:]
    shards = full_up.shape[0] // line
    hidden_rows = full_up.shape[1]
    chunk = shards * hidden_rows
    gated_grad, g_sums = gated, sums
    prepare(in_t, raw, own_in, desk, params, pos_t, mid_t, fil_t, cols)
    greet_near(line)
    gathers = [
        Gather(line, shard, full, gather_send.at[p], gather_recv.at[p], local)
        for p, (shard, full) in enumerate(
            ((own_in, full_in), (own_out, full_out), (own_up, full_up), (own_down, full_down))
        )
    ]
    late = LATE

    def tick(now):
        for piece, offset in zip(gathers, late):
            step = now - offset
            if step == 0:
                piece.begin()
            if 1 <= step < line:
                piece.along(step)
            if 1 <= step <= line:
                piece.plane(step - 1)
            if 2 <= step <= line + 1:
                piece.corner(step - 2)

    def filter_part(n, carry):
        sum_one = dot_plain(pos_t[...], feats[n], EXACT)
        phase = column(cols[...], 0) * sum_one
        act_one = jnp.sin(phase)
        one[n] = act_one
        cos_one[n] = jnp.cos(phase)
        phase = column(cols[...], 0) * (dot_plain(mid_t[...], act_one, EXACT) + column(cols[...], 1))
        act_two = jnp.sin(phase)
        two[n] = act_two
        cos_two[n] = jnp.cos(phase)
        lag = lax.broadcasted_iota(jnp.int32, (chans, block), 1) + n * block
        fade = jnp.exp(-lag.astype(F32) * column(params[...], 13))
        kernel_buf[pl.ds(eighths(n * chans), chans), :] = dot_plain(fil_t[...], act_two, EXACT) * fade
        return carry

    def filters(first, last):
        lax.fori_loop(first, last, filter_part, 0)

    def kernel_spectrum():
        ker = dot_plain(kernel_buf[...], table[...], EXACT)
        before = jnp.concatenate([jnp.zeros((chans, 2 * block), F32), ker[:-chans]], 0)
        sign = slot_sign((chans * blocks, block))
        real = ker[:, :block] + sign * before[:, :block]
        imag = ker[:, block:] + sign * before[:, block:]
        zero = slot_zero(real.shape)
        k_re[...] = real
        k_alt[...] = jnp.where(zero, imag, real)
        k_im[...] = jnp.where(zero, 0.0, imag)

    tick(0)
    filters(0, blocks // 4)
    tick(1)
    filters(blocks // 4, blocks // 2)
    tick(2)
    filters(blocks // 2, 3 * blocks // 4)
    tick(3)
    filters(3 * blocks // 4, blocks)
    tick(4)
    kernel_spectrum()
    tick(5)
    gathers[0].finish()

    in_rows = full_in.shape[1]
    norms = norm_rows(lambda j: full_in[j, in_rows - 8 :], devices, chans, width)
    norms_ref[...] = norms
    normed, _, _ = lane_norm(hidden[...].astype(F32), norms[0:1], norms[1:2])
    projected = dot_rows(full_in[...].reshape(devices * in_rows, width), normed.astype(BF16))
    projected = projected.reshape(devices, in_rows, 128)
    for j in range(devices):
        for i in range(3):
            unit = 3 * j + i
            proj_send[unit % devices, unit // devices] = projected[j, i * chans : (i + 1) * chans].astype(BF16)
    moved = Exchange(proj_send, proj_recv, exchange.at[0], exchange.at[1], devices)
    moved.start()
    tick(6)
    moved.arrive()

    def assemble(j, carry):
        lanes = pl.ds(pl.multiple_of(j * 128, 128), 128)
        for p in range(3):
            pair = merge_halves(proj_recv[2 * j, p].astype(F32), proj_recv[2 * j + 1, p].astype(F32))
            for s in range(seqs):
                steps[p, s, :, lanes] = pair[s]
        return carry

    lax.fori_loop(0, devices // 2, assemble, 0)
    length = block * blocks
    for s in range(seqs):
        for c in range(0, chans, 8):
            spots = lax.broadcasted_iota(jnp.int32, (8, length), 1)
            parts = []
            for p in range(3):
                x = steps[p, s, c : c + 8, :]
                local_params = params[c : c + 8, :]
                value = column(local_params, 9 + p) + column(local_params, p) * x
                for i in (1, 2):
                    value += column(local_params, 3 * i + p) * jnp.where(spots < i, 0.0, pltpu.roll(x, i, 1))
                parts.append(value)
            product = parts[1] * parts[2]
            for n in range(blocks):
                at_rows = (n * seqs + s) * chans + c
                lanes = slice(n * block, (n + 1) * block)
                gated[at_rows : at_rows + 8, :] = product[:, lanes]
                for p in range(3):
                    conv[p, at_rows : at_rows + 8, :] = parts[p][:, lanes]
    tick(7)

    spec[...] = dot_plain(gated[...], table[...], EXACT)
    weight = slot_weight((chans, block))

    def output_block(m, carry):
        def add(n, acc):
            at_kernel = pl.ds(eighths((m - n) * chans), chans)
            kr, ka, ki = k_re[at_kernel, :], k_alt[at_kernel, :], k_im[at_kernel, :]
            result = []
            for s in range(seqs):
                at_signal = pl.ds(eighths((n * seqs + s) * chans), chans)
                re, im = spec[at_signal, :block], spec[at_signal, block:]
                result.append(acc[2 * s] + re * kr - im * ki)
                result.append(acc[2 * s + 1] + re * ki + im * ka)
            return tuple(result)

        acc = lax.fori_loop(0, m + 1, add, tuple(jnp.zeros((chans, block), F32) for _ in range(2 * seqs)))
        for s in range(seqs):
            at_signal = pl.ds(eighths((m * seqs + s) * chans), chans)
            sums[at_signal, :block] = acc[2 * s] * weight
            sums[at_signal, block:] = acc[2 * s + 1] * weight
        return carry

    lax.fori_loop(0, blocks, output_block, 0)
    tick(8)
    total[...] = dot_rows(sums[...], table[...], EXACT)

    def mix(m, carry):
        mixed = []
        for s in range(seqs):
            at_signal = pl.ds(eighths((m * seqs + s) * chans), chans)
            value = total[at_signal, :] + column(params[...], 12) * gated[at_signal, :]
            total[at_signal, :] = value
            mixed.append(value * conv[0, at_signal, :])
        for h in range(block // 128):
            pair = merge_halves(*(v[:, h * 128 : (h + 1) * 128] for v in mixed))
            for q in range(2):
                mix_send[m * (block // 64) + 2 * h + q] = pair[q].astype(BF16)
        return carry

    lax.fori_loop(0, blocks, mix, 0)
    mix_home = Exchange(mix_send, mixed_in, exchange.at[2], exchange.at[3], devices)
    mix_home.start()
    tick(9)
    tick(10)
    for piece in gathers[1:]:
        piece.finish()
    mix_home.arrive()
    for piece in gathers:
        piece.drain()
    moved.drain()
    mix_home.drain()

    parts = (full_up, full_down, g_out, g_in, g_tile)
    outs = (sum_up, sum_down, sum_out, sum_in, sum_tile)
    pieces = [
        Reduce(line, parts[p], outs[p], *buffers[p * BUFFERS : (p + 1) * BUFFERS], sends.at[p], recvs.at[p])
        for p in range(5)
    ]

    z = lax.axis_index("blk") // 2
    half = line // 2
    flip = z // half
    mirror = z + flip * (line - 1 - 2 * z)

    def visit(i):
        near = half - 1 - mirror if i < line - 1 else mirror
        place = line - 1 - i if i < half else near
        return place + flip * (line - 1 - 2 * place)

    def fold(group, slot):
        for piece in group:
            if slot < line:
                piece.corner(visit(slot), slot >= half)
            if half < slot <= line:
                piece.plane(visit(slot - 1))
            if 2 <= slot <= line + 1:
                piece.along(visit(slot - 2), slot - 2 == line - 1)

    gain_two, shift_two = norms_ref[2:3], norms_ref[3:4]
    mixed = mixed_in[...].astype(F32).reshape(width, 128).T.astype(BF16)
    w_flat[...] = full_out[...].astype(F32).reshape(width, width).astype(BF16)
    resid[...] = hidden[...].astype(F32) + dot_rows(mixed, w_flat[...])
    second, normal_two, inv_two = lane_norm(resid[...], gain_two, shift_two)
    second = second.astype(BF16)
    value_sum[...] = jnp.zeros_like(value_sum)
    second_sum[...] = jnp.zeros_like(second_sum)

    for i in range(line):
        where_to = pl.ds(visit(i) * shards, shards)
        up = full_up[where_to].reshape(chunk, width)
        down = full_down[where_to].reshape(chunk, width)
        active, slope = gelu_parts(dot_rows(up, second))
        active = active.astype(BF16)
        grad_upper = (dot_rows(down, cot[...]) * slope).astype(BF16)
        value_sum[...] += dot_plain(active.astype(F32).T.astype(BF16), down)
        second_sum[...] += dot_plain(grad_upper.astype(F32).T.astype(BF16), up)
        full_down[where_to] = dot_plain(active, cot[...]).astype(BF16).reshape(shards, hidden_rows, width)
        full_up[where_to] = dot_plain(grad_upper, second).astype(BF16).reshape(shards, hidden_rows, width)
        for piece in pieces[:2]:
            piece.begin(visit(i))
    result[...] = (resid[...] + value_sum[...]).astype(BF16)
    resid_term, grad_gain_two, grad_shift_two = lane_norm_back(second_sum[...], normal_two, inv_two, gain_two)
    resid[...] = cot[...].astype(F32) + resid_term
    grad_mixed = dot_plain(resid[...].astype(BF16), w_flat[...])
    mix_send[...] = grad_mixed.T.reshape(devices, chans, 128).astype(BF16)
    grad_mix = Exchange(mix_send, mix_recv, exchange.at[4], exchange.at[5], devices)
    grad_mix.start()
    fold(pieces[:2], 0)
    grad_branch = resid[...].T.astype(BF16)
    g_out[...] = dot_plain(grad_branch, mixed).reshape(devices, chans, width).astype(BF16)
    for i in range(line):
        pieces[2].begin(visit(i))
    grad_mix.arrive()

    weight = slot_weight((chans, block))
    skip = column(params[...], 12)
    per_block = block // 64

    def arrange(m, carry):
        for h in range(block // 128):
            source = m * per_block + 2 * h
            pair = merge_halves(mix_recv[source].astype(F32), mix_recv[source + 1].astype(F32))
            lanes = slice(h * 128, (h + 1) * 128)
            for s in range(seqs):
                at_rows = pl.ds(eighths((m * seqs + s) * chans), chans)
                place = pl.ds(pl.multiple_of(m * block + h * 128, 128), 128)
                g_conv[0, s, :, place] = pair[s] * total[at_rows, lanes]
                grad = pair[s] * conv[0, at_rows, lanes]
                gated_grad[at_rows, lanes] = grad
                carry = carry + grad * conv[1, at_rows, lanes] * conv[2, at_rows, lanes]
        return carry

    skip_sum = lax.fori_loop(0, blocks, arrange, jnp.zeros((chans, 128), F32))
    g_spec[...] = dot_plain(gated_grad[...], table[...], EXACT)
    fold(pieces[:2], 1)

    def signal_block(n, carry):
        def add(m, acc):
            at_kernel = pl.ds(eighths((m - n) * chans), chans)
            kr, ka, ki = k_re[at_kernel, :], k_alt[at_kernel, :], k_im[at_kernel, :]
            out = []
            for s in range(seqs):
                at_rows = pl.ds(eighths((m * seqs + s) * chans), chans)
                re, im = g_spec[at_rows, :block], g_spec[at_rows, block:]
                out.append(acc[2 * s] + re * kr + im * ki)
                out.append(acc[2 * s + 1] + im * ka - re * ki)
            return tuple(out)

        acc = lax.fori_loop(n, blocks, add, tuple(jnp.zeros((chans, block), F32) for _ in range(2 * seqs)))
        for s in range(seqs):
            at_rows = pl.ds(eighths((n * seqs + s) * chans), chans)
            g_sums[at_rows, :block] = acc[2 * s] * weight
            g_sums[at_rows, block:] = acc[2 * s + 1] * weight
        return carry

    lax.fori_loop(0, blocks, signal_block, 0)
    g_sums[:, :block] = dot_rows(g_sums[...], table[...], EXACT)

    def gate_grads(m, carry):
        for s in range(seqs):
            at_rows = pl.ds(eighths((m * seqs + s) * chans), chans)
            place = pl.ds(pl.multiple_of(m * block, block), block)
            grad = g_sums[at_rows, :block] + skip * gated_grad[at_rows, :]
            g_conv[1, s, :, place] = grad * conv[2, at_rows, :]
            g_conv[2, s, :, place] = grad * conv[1, at_rows, :]
        return carry

    lax.fori_loop(0, blocks, gate_grads, 0)

    length = block * blocks
    for c in range(0, chans, 8):
        col = lax.broadcasted_iota(jnp.int32, (8, 128), 1)
        spots = lax.broadcasted_iota(jnp.int32, (8, length), 1)
        found = jnp.where(col == 12, jnp.sum(skip_sum[c : c + 8], 1, keepdims=True), 0.0)
        local_params = params[c : c + 8, :]
        for p in range(3):
            for s in range(seqs):
                grad = g_conv[p, s, c : c + 8, :]
                x = steps[p, s, c : c + 8, :]
                value = jnp.zeros_like(grad)
                for i in range(3):
                    later = jnp.where(spots < length - i, pltpu.roll(grad, length - i, 1), 0.0) if i else grad
                    value += column(local_params, 3 * i + p) * later
                    found += jnp.where(col == 3 * i + p, jnp.sum(later * x, 1, keepdims=True), 0.0)
                found += jnp.where(col == 9 + p, jnp.sum(grad, 1, keepdims=True), 0.0)
                g_conv[p, s, c : c + 8, :] = value
        chan_grads[c : c + 8, :] = found

    def pack(j, carry):
        lanes = pl.ds(pl.multiple_of(j * 128, 128), 128)
        for p in range(3):
            pair = merge_halves(g_conv[p, 0, :, lanes], g_conv[p, 1, :, lanes])
            proj_send[2 * j, p] = pair[0].astype(BF16)
            proj_send[2 * j + 1, p] = pair[1].astype(BF16)
        return carry

    lax.fori_loop(0, devices // 2, pack, 0)
    home = Exchange(proj_send, proj_recv, exchange.at[6], exchange.at[7], devices)
    home.start()
    fold(pieces[:2], 2)

    def kernel_block(d, carry):
        def add(n, acc):
            real, imag = acc
            for s in range(seqs):
                at_signal = pl.ds(eighths((n * seqs + s) * chans), chans)
                at_grad = pl.ds(eighths(((n + d) * seqs + s) * chans), chans)
                s_re, s_im = spec[at_signal, :block], spec[at_signal, block:]
                g_re, g_im = g_spec[at_grad, :block], g_spec[at_grad, block:]
                zero = slot_zero((chans, block))
                same, other = g_re * s_re, g_im * s_im
                real = real + jnp.where(zero, same, same + other)
                imag = imag + jnp.where(zero, other, g_im * s_re - g_re * s_im)
            return real, imag

        empty = jnp.zeros((chans, block), F32)
        real, imag = lax.fori_loop(0, blocks - d, add, (empty, empty))
        at_kernel = pl.ds(eighths(d * chans), chans)
        k_sums[at_kernel, :block] = real
        k_sums[at_kernel, block:] = imag
        return carry

    lax.fori_loop(0, blocks, kernel_block, 0)
    after = jnp.concatenate([k_sums[chans:, :], jnp.zeros((chans, 2 * block), F32)], 0)
    shape = (chans * blocks, block)
    sign, scale = slot_sign(shape), slot_weight(shape)
    k_sums[:, :block] = (k_sums[:, :block] + sign * after[:, :block]) * scale
    k_sums[:, block:] = (k_sums[:, block:] + sign * after[:, block:]) * scale
    k_sums[:, :block] = dot_rows(k_sums[...], table[...], EXACT)
    fold(pieces[:2], 3)
    fold(pieces[2:3], 0)

    order = pos_t.shape[0]
    emb = pos_t.shape[1]
    freq = column(cols[...], 0)

    def filter_block(n, carry):
        grad_fil, grad_pos, grad_mid, grad_bias = carry
        lag = lax.broadcasted_iota(jnp.int32, (chans, block), 1) + n * block
        fade = jnp.exp(-lag.astype(F32) * column(params[...], 13))
        grad = k_sums[pl.ds(eighths(n * chans), chans), :block] * fade
        grad_fil = grad_fil + dot_rows(grad, two[n], EXACT)
        grad_two = dot_plain(fil_t[...].T, grad, EXACT) * cos_two[n] * freq
        grad_mid = grad_mid + dot_rows(one[n], grad_two, EXACT)
        grad_bias = grad_bias + dot_rows(jnp.ones((8, block), F32), grad_two, EXACT)
        grad_one = dot_plain(mid_t[...].T, grad_two, EXACT) * cos_one[n] * freq
        grad_pos = grad_pos + dot_rows(feats[n], grad_one, EXACT)
        return grad_fil, grad_pos, grad_mid, grad_bias

    zeros = [jnp.zeros(s, F32) for s in ((chans, order), (emb, order), (order, order), (8, order))]
    grad_fil, grad_pos, grad_mid, grad_bias = lax.fori_loop(0, blocks, filter_block, tuple(zeros))
    filter_grad[...] = grad_fil
    rate_bias = cols[...].T
    grad_rate = jnp.sum(pos_t[...].T * grad_pos, 0, keepdims=True) + jnp.sum(mid_t[...].T * grad_mid, 0, keepdims=True)
    grad_rate = (grad_rate + rate_bias[1:2] * grad_bias[:1]) / rate_bias[0:1]
    small[...] = jnp.zeros_like(small)
    small[:emb, :order] = grad_pos
    small[emb : emb + order, :order] = grad_mid
    picked = lax.broadcasted_iota(jnp.int32, (8, order), 0)
    small[emb + order : emb + order + 8, :order] = jnp.where(
        picked == 0, grad_bias, jnp.where(picked == 1, grad_rate, 0.0)
    )
    fold(pieces[:2], 4)
    fold(pieces[2:3], 1)

    gain_one, shift_one = norms_ref[0:1], norms_ref[1:2]
    normed, normal_one, inv_one = lane_norm(hidden[...].astype(F32), gain_one, shift_one)
    normed = normed.astype(BF16)
    g_proj[...] = jnp.zeros_like(g_proj)
    home.arrive()
    for j in range(devices):
        for i in range(3):
            unit = 3 * j + i
            at_rows = slice(j * in_rows + i * chans, j * in_rows + (i + 1) * chans)
            g_proj[at_rows, :] = proj_recv[unit % devices, unit // devices].astype(F32)
    for i in range(line):
        zo = visit(i)
        group = shards * in_rows
        grads = dot_plain(g_proj[pl.ds(eighths(zo * group), group), :].astype(BF16), normed)
        g_in[pl.ds(zo * shards, shards)] = grads.reshape(shards, in_rows, width)[:, : 3 * chans].astype(BF16)
        pieces[3].begin(zo)
    fold(pieces[3:4], 0)
    fold(pieces[:2], 5)
    fold(pieces[2:3], 2)
    grad_normed = dot_plain(g_proj[...].T.astype(BF16), full_in[...].reshape(devices * in_rows, width))
    input_term, grad_gain_one, grad_shift_one = lane_norm_back(grad_normed, normal_one, inv_one, gain_one)
    grad_hidden[...] = (resid[...] + input_term).astype(BF16)
    norm_grads = jnp.concatenate(
        [grad_gain_one, grad_shift_one, grad_gain_two, grad_shift_two, jnp.zeros((4, width), F32)], 0
    )
    for j in range(devices):
        turned = pltpu.roll(norm_grads, width - j * chans, 1) if j else norm_grads
        g_tile[j, 0:4, :] = turned[0:4, :128]
        g_tile[j, 4:8, :] = small[4 * j : 4 * j + 4, :]
    for i in range(line):
        pieces[4].begin(visit(i))
    fold(pieces[4:5], 0)
    fold(pieces[3:], 1)
    fold(pieces[2:3], 3)
    fold(pieces[3:], 2)
    fold(pieces[2:3], 4)
    fold(pieces[3:], 3)
    fold(pieces[2:3], 5)
    fold(pieces[3:], 4)
    fold(pieces[3:], 5)

    mine = flat(*spot())

    def share(i):
        other = lax.rem(mine + i, devices)
        place = (other // 8, other // 4 % 2, other // 2 % 2, other % 2)
        return send(sum_tile, everyone.at[mine], exchange.at[8], exchange.at[9], place)

    keep = pltpu.make_async_copy(sum_tile, everyone.at[mine], local)
    keep.start()
    lax.fori_loop(1, devices, lambda i, c: (share(i).start(), c)[1], 0)
    for piece in pieces:
        piece.drain()
    grad_mix.drain()
    home.drain()
    keep.wait()

    arrived = everyone.at[pl.ds(0, devices - 1)]
    shared = send(arrived, arrived, exchange.at[8], exchange.at[9], (*spot()[:3], 1 - spot()[3]))
    shared.wait_recv()
    shared.wait_send()


def layer(shards, hidden, cot, feats, table, raw, dims):
    line, devices, chans, seqs, block, blocks, width = dims
    order = raw[-1].shape[1]
    rows, tokens = blocks * seqs * chans, hidden.shape[0]
    in_rows, hidden_rows = shards[0].shape[0] + 8, shards[2].shape[0]
    shape, buffer, dma = jax.ShapeDtypeStruct, pltpu.VMEM, pltpu.SemaphoreType.DMA
    vmem = pl.BlockSpec(memory_space=pltpu.VMEM)
    tile = (devices, 8, 128)
    outs = [
        shape((tokens, width), BF16),
        shape((tokens, width), BF16),
        shape((hidden_rows, width), F32),
        shape((hidden_rows, width), F32),
        shape((chans, width), F32),
        shape((3 * chans, width), F32),
        shape(tile[1:], F32),
        shape(tile, F32),
        shape((chans, 128), F32),
        shape((chans, order), F32),
    ]
    scratch = [buffer((devices, r, width), BF16) for r in (in_rows, chans, hidden_rows, hidden_rows)]
    scratch += [
        buffer((devices, chans, 128), BF16),
        buffer((8, width), F32),
        buffer((3, seqs, chans, block * blocks), F32),
        buffer((3, rows, block), F32),
        buffer((rows, 2 * block), F32),
        buffer((rows, block), F32),
    ]
    scratch += [buffer((blocks * chans, block), F32)] * 3 + [buffer((blocks, order, block), F32)] * 4
    scratch += [buffer((chans, 128), F32), buffer((order, feats.shape[1]), F32), buffer((order, order), F32)]
    scratch += [buffer((chans, order), F32), buffer((order, 128), F32)]
    scratch += [
        buffer((in_rows, width), BF16),
        buffer((128, 128), F32),
        buffer((devices, 3, chans, 128), BF16),
        buffer((devices, 3, chans, 128), BF16),
        buffer((devices, chans, 128), BF16),
        buffer((blocks * chans, block), F32),
        buffer((rows, block), F32),
        buffer((rows, 2 * block), F32),
        buffer((width, width), BF16),
        buffer((devices, chans, width), BF16),
        buffer((devices, 3 * chans, width), BF16),
        buffer(tile, F32),
        buffer((tokens, width), F32),
        buffer((tokens, width), F32),
        buffer((tokens, width), F32),
        buffer((devices, chans, 128), BF16),
        buffer((rows, 2 * block), F32),
        buffer((3, seqs, chans, block * blocks), F32),
        buffer((blocks * chans, 2 * block), F32),
        buffer((devices * in_rows, 128), F32),
        buffer((4 * devices, 128), F32),
    ]
    scratch += [dma((4, 2 * line + 6)), dma((4, 6 * line + 1)), dma((5, 2 * line + 6)), dma((5, 7 * line))]
    scratch += [dma, dma((10,))]
    parts = [shape((devices, r, width), BF16) for r in (hidden_rows, hidden_rows, chans, 3 * chans)] + [shape(tile, F32)]
    scratch += [b for part in parts for b in reduce_scratch(line, part)]
    operands = [*shards, hidden, cot, feats, table, *raw]
    return pl.pallas_call(
        functools.partial(layer_kernel, dims),
        name="layer",
        out_shape=outs,
        in_specs=[vmem] * len(operands),
        out_specs=[vmem] * len(outs),
        scratch_shapes=scratch,
        compiler_params=pltpu.CompilerParams(collective_id=0, has_side_effects=True, vmem_limit_bytes=KERNEL_VMEM),
    )(*operands)


def finish_kernel(emb, order, *refs):
    (result, grad_hidden, up, down, out, inp, tile, everyone, chan_grads, filter_grad) = refs[:10]
    outs, desk = refs[10:-1], refs[-1]
    chans = chan_grads.shape[0]
    for target, source in zip(outs[:7], (result, grad_hidden, up, down, out, inp, filter_grad)):
        target[...] = source[...]
    taps, bias, skip, *gains = outs[7:14]
    desk[...] = jnp.zeros_like(desk)
    desk[:chans, :] = chan_grads[...]
    turned = desk[...].T
    for i in range(3):
        taps[i] = turned[3 * i : 3 * i + 3, :chans]
    bias[...] = turned[9:12, :chans]
    skip[...] = turned[12:13, :chans]
    for i, gain in enumerate(gains):
        gain[...] = tile[i : i + 1, :chans]
    for j in range(everyone.shape[0]):
        desk[4 * j : 4 * j + 4, :] = everyone[j, 4:8, :]
    pos, pos_bias, mid, mid_bias, rate = outs[14:]
    after = emb + 1 + -(emb + 1) % 8
    pos[...] = desk[:emb, :order]
    pos_bias[...] = desk[emb : emb + 1, :order]
    mid[...] = desk[after : after + order, :order]
    mid_bias[...] = desk[after + order : after + order + 1, :order]
    rate[...] = desk[after + order + 1 : after + order + 2, :order]


def finish(parts, pos_shape):
    emb, order = pos_shape
    chans = parts[8].shape[0]
    shape = jax.ShapeDtypeStruct
    vmem = pl.BlockSpec(memory_space=pltpu.VMEM)
    outs = [shape(p.shape, p.dtype) for p in parts[:6]] + [shape(parts[9].shape, F32)]
    outs += [shape((3, 3, chans), F32), shape((3, chans), F32)] + [shape((1, chans), F32)] * 5
    outs += [shape((emb, order), F32), shape((1, order), F32), shape((order, order), F32)]
    outs += [shape((1, order), F32)] * 2
    return pl.pallas_call(
        functools.partial(finish_kernel, emb, order),
        name="finish",
        out_shape=outs,
        in_specs=[vmem] * len(parts),
        out_specs=[vmem] * len(outs),
        scratch_shapes=[pltpu.VMEM((128, 128), F32)],
    )(*parts)


def shards_paired(
    hidden_in,
    cotangent,
    mixer_input_weight,
    mixer_output_weight,
    feedforward_up,
    feedforward_down,
    first_gain,
    first_shift,
    second_gain,
    second_shift,
    short_taps,
    short_bias,
    skip_scale,
    filter_out,
    pos_weight,
    pos_bias,
    mid_weight,
    mid_bias,
    sine_freq,
    decay_rate,
):
    devices = lax.axis_size(AXES)
    micro, seq_count, tok, width = hidden_in.shape
    seqs = micro * seq_count
    tokens = seqs * tok
    length = tok * devices
    chans = width // devices
    block = tok * lax.axis_size("chan")
    blocks = length // block

    line = devices // 8
    def row(vector):
        return vector.reshape(1, -1)

    shards = [mixer_input_weight.T, mixer_output_weight.T, feedforward_up.T, feedforward_down]
    raw = [row(v) for v in (first_gain, first_shift, second_gain, second_shift)]
    raw += [short_taps, short_bias, row(skip_scale), row(decay_rate), filter_out.T]
    raw += [pos_weight, row(pos_bias), mid_weight, row(sine_freq), row(mid_bias)]
    hidden = hidden_in.reshape(tokens, width)
    features, table = jnp.asarray(feature_blocks(length, block)), jnp.asarray(fixed_table(block))
    dims = (line, devices, chans, seqs, block, blocks, width)
    parts = layer(shards, hidden, cotangent.reshape(tokens, width), features, table, raw, dims)
    outs = finish(parts, pos_weight.shape)
    result, grad_hidden, up, down, out, inp, filter_grad, taps, bias, skip, *rest = outs
    gains, (pos, pos_bias, mid, mid_bias, rate) = rest[:4], rest[4:]
    return (
        result.reshape(hidden_in.shape),
        grad_hidden.reshape(hidden_in.shape),
        inp.T,
        out.T,
        up.T,
        down,
        *[g.reshape(-1) for g in gains],
        taps,
        bias,
        skip.reshape(-1),
        filter_grad.T,
        pos,
        pos_bias.reshape(-1),
        mid,
        mid_bias.reshape(-1),
        rate.reshape(-1),
    )


def shards(
    hidden_in,
    cotangent,
    mixer_input_weight,
    mixer_output_weight,
    feedforward_up,
    feedforward_down,
    first_gain,
    first_shift,
    second_gain,
    second_shift,
    short_taps,
    short_bias,
    skip_scale,
    filter_out,
    pos_weight,
    pos_bias,
    mid_weight,
    mid_bias,
    sine_freq,
    decay_rate,
):
    devices = lax.axis_size(AXES)
    micro, seq_count, tok, width = hidden_in.shape
    seqs = micro * seq_count
    tokens = seqs * tok
    length = tok * devices
    chans = width // devices
    block = tok * lax.axis_size("chan")
    blocks = length // block

    norms = jnp.stack([first_gain, first_shift, second_gain, second_shift])
    own = [mixer_input_weight.T, feedforward_up.T, feedforward_down, mixer_output_weight.T]
    full = [lax.all_gather(shard, AXES, axis=0, tiled=True) for shard in own]
    norms = lax.all_gather(norms, AXES, axis=1, tiled=True)
    weight_in, weight_up, weight_down, weight_out = full
    norms = norms.astype(F32)
    gain_one, shift_one, gain_two, shift_two = norms[0], norms[1], norms[2], norms[3]

    freq = sine_freq.astype(F32)
    w_pos, w_mid, w_fil = pos_weight.astype(F32), mid_weight.astype(F32), filter_out.astype(F32)
    lags, features, first_sum, first_act, second_sum, second_act = filter_hidden(
        length, w_pos, pos_bias.astype(F32), w_mid, mid_bias.astype(F32), freq
    )
    decay = jnp.exp(-lags[None, :] * decay_rate.astype(F32)[:, None])
    kernel = contract(w_fil, second_act, 0, 0, EXACT) * decay
    table = block_table(block)
    sign = 1.0 - 2.0 * (lax.iota(jnp.int32, block) % 2).astype(F32)
    ker_re, ker_im = to_spectrum(kernel.reshape(chans, blocks, block), table)

    def with_previous(spec):
        before = jnp.concatenate([jnp.zeros_like(spec[:, :1]), spec[:, :-1]], 1)
        return spec + sign * before

    k_re, k_alt, k_im = packed_kernel(with_previous(ker_re), with_previous(ker_im))

    values = hidden_in.reshape(tokens, width).astype(F32)
    normed, normal_one, inv_one = layer_norm(values, gain_one, shift_one)
    normed = normed.astype(BF16)
    projected = contract(weight_in, normed, 1, 1).astype(BF16)
    projected = projected.reshape(3, devices, chans, tokens).transpose(1, 0, 2, 3)
    arrived = exchange(projected)

    def by_sequence(values):
        parts = values.shape[1]
        values = values.reshape(devices, parts, chans, seqs, tok)
        return values.transpose(1, 3, 2, 0, 4).reshape(parts, seqs, chans, length)

    def by_device(values):
        parts = values.shape[0]
        values = values.reshape(parts, seqs, chans, devices, tok)
        return values.transpose(3, 0, 2, 1, 4).reshape(devices, parts, chans, tokens)

    steps = by_sequence(arrived).astype(F32)
    taps = short_taps.astype(F32)[:, :, None, :, None]
    conv = short_bias.astype(F32)[:, None, :, None]
    for i in range(3):
        conv = conv + taps[i] * delayed(steps, i)
    gate_out, gate_in, signal = conv[0], conv[1], conv[2]
    gated = signal * gate_in
    sig_re, sig_im = to_spectrum(gated.reshape(seqs, chans, blocks, block), table)

    def shifted_sum(make):
        total = None
        for d in range(blocks):
            term = make(d)
            total = term if total is None else tuple(a + b for a, b in zip(total, term))
        return total

    def ahead(x, d):
        return x if d == 0 else jnp.pad(x[:, :, :-d], ((0, 0), (0, 0), (d, 0), (0, 0)))

    def back(x, d):
        return x if d == 0 else jnp.pad(x[:, :, d:], ((0, 0), (0, 0), (0, d), (0, 0)))

    def forward_term(d):
        re, im = ahead(sig_re, d), ahead(sig_im, d)
        kr, ka, ki = k_re[:, d : d + 1], k_alt[:, d : d + 1], k_im[:, d : d + 1]
        return re * kr - im * ki, re * ki + im * ka

    out_re, out_im = shifted_sum(forward_term)
    long_out = from_spectrum(out_re, out_im, table).reshape(seqs, chans, length)
    skip = skip_scale.astype(F32)[None, :, None]
    long_total = long_out + skip * gated
    mixed = (long_total * gate_out).astype(BF16)
    mixed = exchange(by_device(mixed[None])).reshape(width, tokens)

    resid = values + contract(mixed, weight_out, 0, 1)
    second, normal_two, inv_two = layer_norm(resid, gain_two, shift_two)
    second = second.astype(BF16)
    upper = contract(second, weight_up, 1, 1)
    active, slope = gelu_parts(upper)
    active = active.astype(BF16)
    result = resid + contract(active, weight_down, 1, 0)

    cot = cotangent.reshape(tokens, width)
    grad_down = contract(active, cot, 0, 0)
    grad_upper = (contract(cot, weight_down, 1, 1) * slope).astype(BF16)
    grad_up = contract(grad_upper, second, 0, 0)
    grad_second = contract(grad_upper, weight_up, 1, 0)
    resid_term, grad_gain_two, grad_shift_two = layer_norm_back(grad_second, normal_two, inv_two, gain_two)
    grad_resid = cot.astype(F32) + resid_term
    grad_branch = grad_resid.astype(BF16)
    grad_out_w = contract(grad_branch, mixed, 0, 1)
    grad_mixed = contract(weight_out, grad_branch, 0, 1).astype(BF16)
    grad_mixed = exchange(grad_mixed.reshape(devices, 1, chans, tokens))
    grad_mixed = by_sequence(grad_mixed)[0].astype(F32)

    grad_gate_out = grad_mixed * long_total
    grad_long = grad_mixed * gate_out
    grad_skip = jnp.sum(grad_long * gated, (0, 2))
    gl_re, gl_im = to_spectrum(grad_long.reshape(seqs, chans, blocks, block), table)

    def signal_term(d):
        re, im = back(gl_re, d), back(gl_im, d)
        kr, ka, ki = k_re[:, d : d + 1], k_alt[:, d : d + 1], k_im[:, d : d + 1]
        return re * kr + im * ki, im * ka - re * ki

    gg_re, gg_im = shifted_sum(signal_term)
    grad_gated = from_spectrum(gg_re, gg_im, table).reshape(seqs, chans, length) + skip * grad_long

    first_slot = lax.iota(jnp.int32, block) == 0
    kg_re, kg_im = [], []
    for d in range(blocks):
        s_re, s_im = sig_re[:, :, : blocks - d], sig_im[:, :, : blocks - d]
        g_re, g_im = gl_re[:, :, d:], gl_im[:, :, d:]
        same, other = g_re * s_re, g_im * s_im
        kg_re.append(jnp.sum(jnp.where(first_slot, same, same + other), (0, 2)))
        kg_im.append(jnp.sum(jnp.where(first_slot, other, g_im * s_re - g_re * s_im), (0, 2)))
    kg_re, kg_im = jnp.stack(kg_re, 1), jnp.stack(kg_im, 1)

    def with_next(spec):
        after = jnp.concatenate([spec[:, 1:], jnp.zeros_like(spec[:, :1])], 1)
        return spec + sign * after

    grad_kernel = from_spectrum(with_next(kg_re), with_next(kg_im), table).reshape(chans, length)

    grad_conv = jnp.stack([grad_gate_out, grad_gated * signal, grad_gated * gate_in])
    grad_bias = jnp.sum(grad_conv, (1, 3))
    grad_taps = jnp.stack([jnp.sum(grad_conv * delayed(steps, i), (1, 3)) for i in range(3)])
    grad_steps = taps[0] * grad_conv
    for i in (1, 2):
        grad_steps = grad_steps + taps[i] * advanced(grad_conv, i)
    grad_proj = exchange(by_device(grad_steps.astype(BF16)))
    grad_proj = grad_proj.transpose(1, 0, 2, 3).reshape(3 * width, tokens)

    fade = grad_kernel * decay
    grad_filter = contract(second_act, fade, 1, 1, EXACT)
    grad_two = contract(w_fil, fade, 1, 0, EXACT) * jnp.cos(freq[:, None] * second_sum)
    grad_freq = jnp.sum(grad_two * second_sum, 1)
    grad_two = grad_two * freq[:, None]
    grad_mid = contract(first_act, grad_two, 1, 1, EXACT)
    grad_one = contract(w_mid, grad_two, 1, 0, EXACT) * jnp.cos(freq[:, None] * first_sum)
    grad_freq = grad_freq + jnp.sum(grad_one * first_sum, 1)
    grad_one = grad_one * freq[:, None]
    grad_pos = contract(features, grad_one, 1, 1, EXACT)
    small = jnp.concatenate(
        [grad_pos, jnp.sum(grad_one, 1)[None], grad_mid, jnp.sum(grad_two, 1)[None], grad_freq[None]]
    )
    emb, order = pos_weight.shape

    grad_in = contract(grad_proj, normed, 1, 0)
    grad_normed = contract(grad_proj, weight_in, 0, 0)
    input_term, grad_gain_one, grad_shift_one = layer_norm_back(grad_normed, normal_one, inv_one, gain_one)
    grad_hidden = (grad_resid + input_term).astype(BF16)

    norm_grads = jnp.stack([grad_gain_one, grad_shift_one, grad_gain_two, grad_shift_two])
    sums = [grad_in, grad_up, grad_down, grad_out_w]
    sums = [
        lax.psum_scatter(g.astype(BF16), AXES, scatter_dimension=0, tiled=True).astype(F32) for g in sums
    ]
    norm_grads = lax.psum_scatter(norm_grads, AXES, scatter_dimension=1, tiled=True)
    small = lax.psum(small, AXES)
    return (
        result.astype(BF16).reshape(hidden_in.shape),
        grad_hidden.reshape(hidden_in.shape),
        sums[0].T,
        sums[3].T,
        sums[1].T,
        sums[2],
        norm_grads[0],
        norm_grads[1],
        norm_grads[2],
        norm_grads[3],
        grad_taps,
        grad_bias,
        grad_skip,
        grad_filter,
        small[:emb],
        small[emb],
        small[emb + 1 : emb + 1 + order],
        small[emb + 1 + order],
        small[emb + 2 + order],
    )


def solution(mesh):
    paired = mesh.shape["chan"] == 4 and mesh.shape["blk"] == 8
    rows, spread, tokens = P(AXES), P(None, AXES), P(None, None, AXES, None)
    params = (rows, rows, rows, rows, P(None, None, AXES), spread, rows, spread, P(), P(), P(), P(), P())
    return jax.shard_map(
        shards_paired if paired else shards,
        mesh=mesh,
        in_specs=(tokens, tokens, spread, spread, spread, P(AXES, None)) + params + (rows,),
        out_specs=(tokens, tokens, spread, spread, spread, P(AXES, None)) + params,
        check_vma=False,
    )
```

```python
import functools
import math

import jax
import jax.numpy as jnp
import numpy as np
from jax import lax
from jax.experimental import pallas as pl
from jax.experimental.pallas import tpu as pltpu
from jax.sharding import PartitionSpec as P

EPS = 1e-05
BANDS = 16
EXACT = lax.Precision.HIGHEST
AXES = ("blk", "chan")
F32 = jnp.float32
BF16 = jnp.bfloat16
MESH = pl.DeviceIdType.MESH
KERNEL_VMEM = 62 << 20


def contract(a, b, dim_a, dim_b, precision=None):
    return lax.dot_general(
        a, b, (((dim_a,), (dim_b,)), ((), ())), precision=precision, preferred_element_type=F32
    )


def positions(length):
    lags = jnp.arange(length).astype(F32)
    band_freq = 0.0001 + (BANDS - 1 - 0.0001) * jnp.arange(BANDS).astype(F32) / (BANDS - 1)
    phase = 2.0 * math.pi / length * lags[None, :] * band_freq[:, None]
    return lags, jnp.concatenate([lags[None, :] / (length - 1), jnp.cos(phase), -jnp.sin(phase)], 0)


def feature_blocks(length, block):
    lags = np.arange(length).astype(np.float32)
    bands = np.arange(BANDS).astype(np.float32)
    band_freq = np.float32(0.0001) + np.float32(BANDS - 1 - 0.0001) * bands / np.float32(BANDS - 1)
    phase = np.float32(2.0 * math.pi / length) * lags[None, :] * band_freq[:, None]
    ramp = lags[None, :] / np.float32(length - 1)
    rows = np.concatenate([ramp, np.cos(phase), -np.sin(phase), np.ones_like(ramp)])
    rows = np.pad(rows, ((0, -len(rows) % 8), (0, 0))).astype(np.float32)
    return np.ascontiguousarray(rows.reshape(len(rows), -1, block).transpose(1, 0, 2))


def fixed_table(block):
    spot, freq = np.arange(block)[:, None], np.arange(block)[None, :]
    phase = (np.pi / block) * (spot * freq % (2 * block))
    imag = np.where(freq == 0, 1.0 - 2.0 * (spot % 2), -np.sin(phase))
    return np.concatenate([np.cos(phase), imag], 1).astype(np.float32)


def filter_hidden(length, pos_weight, pos_bias, mid_weight, mid_bias, sine_freq):
    lags, features = positions(length)
    freq = sine_freq[:, None]
    first_sum = contract(pos_weight, features, 0, 0, EXACT) + pos_bias[:, None]
    first = jnp.sin(freq * first_sum)
    second_sum = contract(mid_weight, first, 0, 0, EXACT) + mid_bias[:, None]
    second = jnp.sin(freq * second_sum)
    return lags, features, first_sum, first, second_sum, second


def block_table(block):
    spot = lax.broadcasted_iota(jnp.int32, (block, block), 0)
    freq = lax.broadcasted_iota(jnp.int32, (block, block), 1)
    phase = (math.pi / block) * (spot * freq % (2 * block)).astype(F32)
    parity = 1.0 - 2.0 * (spot % 2).astype(F32)
    imag = jnp.where(freq == 0, parity, -jnp.sin(phase))
    return jnp.concatenate([jnp.cos(phase), imag], 1)


def to_spectrum(blocks, table):
    spec = lax.dot_general(
        blocks, table, (((blocks.ndim - 1,), (0,)), ((), ())), precision=EXACT, preferred_element_type=F32
    )
    half = table.shape[0]
    return spec[..., :half], spec[..., half:]


def from_spectrum(real, imag, table):
    half = table.shape[0]
    weight = jnp.where(lax.iota(jnp.int32, half) == 0, 0.5 / half, 1.0 / half)
    spec = jnp.concatenate([real * weight, imag * weight], -1)
    return lax.dot_general(
        spec, table, (((spec.ndim - 1,), (1,)), ((), ())), precision=EXACT, preferred_element_type=F32
    )


def packed_kernel(real, imag):
    first = lax.iota(jnp.int32, real.shape[-1]) == 0
    return real, jnp.where(first, imag, real), jnp.where(first, 0.0, imag)


def layer_norm(values, gain, shift):
    center = values - jnp.mean(values, -1, keepdims=True)
    scale_inv = lax.rsqrt(jnp.mean(center * center, -1, keepdims=True) + EPS)
    normal = center * scale_inv
    return normal * gain + shift, normal, scale_inv


def layer_norm_back(grad_out, normal, scale_inv, gain):
    grad_normal = grad_out * gain
    inner = grad_normal - jnp.mean(grad_normal, -1, keepdims=True)
    inner = inner - normal * jnp.mean(grad_normal * normal, -1, keepdims=True)
    return inner * scale_inv, jnp.sum(grad_out * normal, 0), jnp.sum(grad_out, 0)


def gelu_parts(v):
    root = math.sqrt(2.0 / math.pi)
    inner = root * (v + 0.044715 * v * v * v)
    t = jnp.tanh(inner)
    value = 0.5 * v * (1.0 + t)
    slope = 0.5 * (1.0 + t) + 0.5 * v * (1.0 - t * t) * root * (1.0 + 3.0 * 0.044715 * v * v)
    return value, slope


def delayed(values, steps):
    if steps == 0:
        return values
    pad = jnp.zeros(values.shape[:-1] + (steps,), values.dtype)
    return jnp.concatenate([pad, values[..., :-steps]], -1)


def advanced(values, steps):
    if steps == 0:
        return values
    pad = jnp.zeros(values.shape[:-1] + (steps,), values.dtype)
    return jnp.concatenate([values[..., steps:], pad], -1)


def exchange(values):
    return lax.all_to_all(values, AXES, split_axis=0, concat_axis=0, tiled=True)


def spot():
    b, c = lax.axis_index("blk"), lax.axis_index("chan")
    return b // 2, b % 2, c // 2, c % 2


def at(z, y, x, k):
    return {"blk": z * 2 + y, "chan": x * 2 + k}


def flat(z, y, x, k):
    return ((z * 2 + y) * 2 + x) * 2 + k


def when(condition, act):
    pl.when(condition)(act)


def send(src, dst, send_sem, recv_sem, place):
    return pltpu.make_async_remote_copy(
        src_ref=src, dst_ref=dst, send_sem=send_sem, recv_sem=recv_sem, device_id=at(*place), device_id_type=MESH
    )


def greet_near(line):
    z, y, x, k = spot()
    barrier = pltpu.get_barrier_semaphore()

    def hello(*place):
        pl.semaphore_signal(barrier, inc=1, device_id=at(*place), device_id_type=MESH)

    hello(z, 1 - y, x, k)
    hello(z, y, 1 - x, k)
    hello(z, y, x, 1 - k)
    when(z > 0, lambda: hello(z - 1, y, x, k))
    when(z < line - 1, lambda: hello(z + 1, y, x, k))
    pl.semaphore_wait(barrier, 3 + jnp.minimum(z, 1) + jnp.minimum(line - 1 - z, 1))


def low_rows(rows):
    return (rows + 16) // 32 * 16 if rows > 8 else rows


class Gather:
    def __init__(self, line, shard, full, sends, recvs, local):
        self.line, self.shard, self.full, self.s, self.r, self.local = line, shard, full, sends, recvs, local
        self.rows = shard.shape[0]
        self.low = low_rows(self.rows)
        self.z, self.y, self.x, self.k = spot()
        self.half = line // 2
        self.inward = 1 - 2 * (self.z // self.half)
        self.inner = self.z == self.half - 1 + self.z // self.half

    def copy(self, send_at, recv_at, shard, place, rows=None):
        ref = self.full.at[shard] if rows is None else self.full.at[shard, pl.ds(*rows)]
        return send(ref, ref, self.s.at[send_at], self.r.at[recv_at], place)

    def together(self, send_at, recv_at, count, rows=None):
        return self.copy(send_at, recv_at, pl.ds(0, count), (self.z, self.y, self.x, 1 - self.k), rows)

    def up(self, zo):
        return self.copy(zo, zo, flat(zo, self.y, self.x, self.k), (self.z + 1, self.y, self.x, self.k))

    def down(self, zo):
        return self.copy(self.line + zo, self.line + zo, flat(zo, self.y, self.x, self.k), (self.z - 1, self.y, self.x, self.k))

    def to_x(self, zo):
        return self.copy(2 * self.line, 2 * self.line + zo, flat(zo, self.y, self.x, self.k), (self.z, self.y, 1 - self.x, self.k))

    def to_y(self, zo):
        return self.copy(2 * self.line + 1, 3 * self.line + zo, flat(zo, self.y, self.x, self.k), (self.z, 1 - self.y, self.x, self.k))

    def low_y(self, zo, other_y=False):
        shard = flat(zo, 1 - self.y if other_y else self.y, 1 - self.x, self.k)
        return self.copy(2 * self.line + 2, 5 * self.line + zo % self.half, shard, (self.z, 1 - self.y, self.x, self.k), (0, self.low))

    def high_x(self, zo, other_x=False):
        shard = flat(zo, 1 - self.y, 1 - self.x if other_x else self.x, self.k)
        rows = (self.low, self.rows - self.low)
        recv_at = 5 * self.line + self.half + zo % self.half
        return self.copy(2 * self.line + 3, recv_at, shard, (self.z, self.y, 1 - self.x, self.k), rows)

    def core(self, zo, yo, xo, k):
        return self.copy(2 * self.line + 4, 6 * self.line, flat(zo, yo, xo, k), (self.z, self.y, self.x, 1 - self.k))

    def cross(self, zo, step):
        shard = flat(zo, 1 - self.y, 1 - self.x, self.k)
        return self.copy(2 * self.line + 5, 4 * self.line + zo, shard, (self.z + step, self.y, self.x, self.k))

    def same(self, zo):
        return zo // self.half == self.z // self.half

    def line_has(self, zo):
        self.to_x(zo).start()
        self.to_y(zo).start()
        self.core(zo, self.y, self.x, self.k).start()

    def begin(self):
        own = self.full.at[flat(self.z, self.y, self.x, self.k)]
        copy = pltpu.make_async_copy(self.shard, own, self.local)
        copy.start()
        copy.wait()
        when(self.z < self.line - 1, lambda: self.up(self.z).start())
        when(self.z > 0, lambda: self.down(self.z).start())
        self.line_has(self.z)

    def each(self, distance, act):
        if distance == 0:
            act(self.z)
        else:
            when(self.z - distance >= 0, lambda: act(self.z - distance))
            when(self.z + distance < self.line, lambda: act(self.z + distance))

    def along(self, distance):
        def from_below():
            zo = self.z - distance
            self.up(zo).wait_recv()
            when(self.z < self.line - 1, lambda: self.up(zo).start())
            self.line_has(zo)

        def from_above():
            zo = self.z + distance
            self.down(zo).wait_recv()
            when(self.z > 0, lambda: self.down(zo).start())
            self.line_has(zo)

        when(self.z - distance >= 0, from_below)
        when(self.z + distance < self.line, from_above)

    def plane(self, distance):
        def act(zo):
            self.to_x(zo).wait_recv()
            when(self.same(zo), lambda: self.low_y(zo).start())
            self.core(zo, self.y, 1 - self.x, self.k).start()
            self.to_y(zo).wait_recv()
            if self.low < self.rows:
                when(self.same(zo), lambda: self.high_x(zo).start())
            self.core(zo, 1 - self.y, self.x, self.k).start()

        self.each(distance, act)

    def corner(self, distance):
        def near(zo):
            self.low_y(zo, True).wait_recv()
            if self.low < self.rows:
                self.high_x(zo, True).wait_recv()
            when(self.inner, lambda: self.cross(zo, self.inward).start())

        def far(zo):
            self.cross(zo, self.inward).wait_recv()
            when(self.inner, lambda: self.cross(zo, -self.inward).start())

        def act(zo):
            when(self.same(zo), lambda: near(zo))
            when(jnp.logical_not(self.same(zo)), lambda: far(zo))
            self.core(zo, 1 - self.y, 1 - self.x, self.k).start()

        self.each(distance, act)

    def finish(self):
        self.together(2 * self.line + 4, 6 * self.line, 4 * self.line).wait_recv()

    def drain(self):
        line, high = self.line, self.rows - self.low
        for zo in range(line):
            when(jnp.logical_and(self.z < line - 1, zo <= self.z), lambda: self.up(zo).wait_send())
            when(jnp.logical_and(self.z > 0, zo >= self.z), lambda: self.down(zo).wait_send())
        self.together(2 * line, 0, line).wait_send()
        self.together(2 * line + 1, 0, line).wait_send()
        self.together(2 * line + 2, 0, self.half, (0, self.low)).wait_send()
        if high:
            self.together(2 * line + 3, 0, self.half, (self.low, high)).wait_send()
        self.together(2 * line + 4, 0, 4 * line).wait_send()
        when(self.inner, lambda: self.together(2 * line + 5, 0, line).wait_send())


class Reduce:
    def __init__(self, line, part, out, chip, low_y, high_x, by_x, by_y, by_z, crossed, sends, recvs):
        self.line, self.part, self.out, self.chip = line, part, out, chip
        self.low_buf, self.high_buf, self.x_buf, self.y_buf, self.z_buf = low_y, high_x, by_x, by_y, by_z
        self.crossed = crossed
        self.s, self.r = sends, recvs
        self.rows = part.shape[1]
        self.low = low_rows(self.rows)
        self.z, self.y, self.x, self.k = spot()
        self.half = line // 2
        self.inward = 1 - 2 * (self.z // self.half)
        self.inner = self.z == self.half - 1 + self.z // self.half

    def index(self, zo, yo, xo):
        return (zo * 2 + yo) * 2 + xo

    def copy(self, send_at, recv_at, src, dst, place):
        return send(src, dst, self.s.at[send_at], self.r.at[recv_at], place)

    def together(self, send_at, recv_at, ref):
        return self.copy(send_at, recv_at, ref, ref, (self.z, self.y, self.x, 1 - self.k))

    def core(self, zo, yo, xo):
        i = self.index(zo, yo, xo)
        src = self.part.at[flat(zo, yo, xo, 1 - self.k)]
        return self.copy(2 * self.line + 4, 5 * self.line + zo, src, self.chip.at[i], (self.z, self.y, self.x, 1 - self.k))

    def corner_of(self, zo):
        return self.index(zo, 1 - self.y, 1 - self.x)

    def low_y(self, zo):
        src = self.chip.at[self.corner_of(zo), pl.ds(0, self.low)]
        slot = zo % self.half
        place = (self.z, 1 - self.y, self.x, self.k)
        return self.copy(2 * self.line + 2, 6 * self.line + slot, src, self.low_buf.at[slot], place)

    def high_x(self, zo):
        src = self.chip.at[self.corner_of(zo), pl.ds(self.low, self.rows - self.low)]
        slot = zo % self.half
        place = (self.z, self.y, 1 - self.x, self.k)
        return self.copy(2 * self.line + 3, 6 * self.line + self.half + slot, src, self.high_buf.at[slot], place)

    def to_x(self, zo):
        src = self.chip.at[self.index(zo, self.y, 1 - self.x)]
        return self.copy(2 * self.line, 2 * self.line + zo, src, self.x_buf.at[zo], (self.z, self.y, 1 - self.x, self.k))

    def to_y(self, zo):
        src = self.chip.at[self.index(zo, 1 - self.y, self.x)]
        return self.copy(2 * self.line + 1, 3 * self.line + zo, src, self.y_buf.at[zo], (self.z, 1 - self.y, self.x, self.k))

    def up(self, zo):
        src = self.chip.at[self.index(zo, self.y, self.x)]
        return self.copy(zo, zo, src, self.z_buf.at[zo + 1], (self.z + 1, self.y, self.x, self.k))

    def down(self, zo):
        src = self.chip.at[self.index(zo, self.y, self.x)]
        return self.copy(self.line + zo, self.line + zo, src, self.z_buf.at[zo], (self.z - 1, self.y, self.x, self.k))

    def cross(self, zo):
        src = self.chip.at[self.corner_of(zo)]
        place = (self.z + self.inward, self.y, self.x, self.k)
        return self.copy(2 * self.line + 5, 4 * self.line + zo, src, self.crossed.at[zo], place)

    def add(self, i, other, rows=None):
        if rows is None:
            self.chip[i] = self.chip[i] + other
        else:
            self.chip[i, pl.ds(*rows)] = self.chip[i, pl.ds(*rows)] + other

    def begin(self, zo):
        for yo, xo in ((1 - self.y, 1 - self.x), (self.y, 1 - self.x), (1 - self.y, self.x), (self.y, self.x)):
            self.core(zo, yo, xo).start()

    def corner(self, zo, near):
        def joined(yo, xo):
            self.add(self.index(zo, yo, xo), self.part[flat(zo, yo, xo, self.k)])

        def crossing():
            self.cross(zo).wait_recv()
            self.add(self.corner_of(zo), self.crossed[zo])

        arrived = self.chip.at[pl.ds(4 * zo, 4)]
        self.together(2 * self.line + 4, 5 * self.line + zo, arrived).wait_recv()
        joined(1 - self.y, 1 - self.x)
        if not near:
            joined(self.y, 1 - self.x)
            self.to_x(zo).start()
            joined(1 - self.y, self.x)
            self.to_y(zo).start()
        when(self.inner, crossing)
        if near:
            self.low_y(zo).start()
            if self.low < self.rows:
                self.high_x(zo).start()
            joined(self.y, 1 - self.x)
            joined(1 - self.y, self.x)
        else:
            self.cross(zo).start()
        joined(self.y, self.x)

    def plane(self, zo):
        self.low_y(zo).wait_recv()
        self.add(self.index(zo, self.y, 1 - self.x), self.low_buf[zo % self.half], (0, self.low))
        self.to_x(zo).start()
        if self.low < self.rows:
            self.high_x(zo).wait_recv()
            high = (self.low, self.rows - self.low)
            self.add(self.index(zo, 1 - self.y, self.x), self.high_buf[zo % self.half], high)
        self.to_y(zo).start()

    def along(self, zo, own):
        i = self.index(zo, self.y, self.x)
        self.to_x(zo).wait_recv()
        self.to_y(zo).wait_recv()
        total = self.x_buf[zo].astype(F32) + self.y_buf[zo].astype(F32) + self.chip[i].astype(F32)

        def from_below():
            self.up(zo).wait_recv()
            self.add(i, self.z_buf[zo + 1])

        def from_above():
            self.down(zo).wait_recv()
            self.add(i, self.z_buf[zo])

        def rising():
            when(self.z > 0, from_below)
            self.up(zo).start()

        def falling():
            when(self.z < self.line - 1, from_above)
            self.down(zo).start()

        def last_below():
            self.up(zo).wait_recv()
            self.out[...] += self.z_buf[zo + 1].astype(F32)

        def last_above():
            self.down(zo).wait_recv()
            self.out[...] += self.z_buf[zo].astype(F32)

        if own:
            self.out[...] = total
            when(self.z > 0, last_below)
            when(self.z < self.line - 1, last_above)
        else:
            self.chip[i] = total.astype(self.chip.dtype)
            when(zo > self.z, rising)
            when(zo < self.z, falling)

    def drain(self):
        line, low, high = self.line, self.low, self.rows - self.low
        shards, halves = self.chip.at[pl.ds(0, line)], pl.ds(0, self.half)
        for zo in range(line):
            when(zo > self.z, lambda: self.up(zo).wait_send())
            when(zo < self.z, lambda: self.down(zo).wait_send())
        self.together(2 * line, 0, shards).wait_send()
        self.together(2 * line + 1, 0, shards).wait_send()
        self.together(2 * line + 2, 0, self.chip.at[halves, pl.ds(0, low)]).wait_send()
        if high:
            self.together(2 * line + 3, 0, self.chip.at[halves, pl.ds(low, high)]).wait_send()
        self.together(2 * line + 4, 0, self.part.at[pl.ds(0, 4 * line)]).wait_send()
        self.together(2 * line + 5, 0, self.chip.at[halves]).wait_send()


BUFFERS = 7


def reduce_scratch(line, part):
    _, rows, width = part.shape
    low = low_rows(rows)
    high = max(rows - low, 8)
    half = line // 2
    sizes = [(line * 4, rows), (half, low), (half, high), (line, rows), (line, rows), (line + 1, rows), (line, rows)]
    return [pltpu.VMEM(s + (width,), part.dtype) for s in sizes]


def dot_rows(a, b, precision=None):
    return lax.dot_general(a, b, (((1,), (1,)), ((), ())), precision=precision, preferred_element_type=F32)


def dot_plain(a, b, precision=None):
    return lax.dot_general(a, b, (((1,), (0,)), ((), ())), precision=precision, preferred_element_type=F32)


def eighths(value):
    return pl.multiple_of(value, 8)


class Exchange:
    def __init__(self, src, dst, send_sem, recv_sem, devices):
        self.src, self.dst, self.s, self.r, self.devices = src, dst, send_sem, recv_sem, devices
        self.me = flat(*spot())

    def copy(self, i):
        other = lax.rem(self.me + i, self.devices)
        place = (other // 8, other // 4 % 2, other // 2 % 2, other % 2)
        return send(self.src.at[other], self.dst.at[self.me], self.s, self.r, place)

    def together(self, ref):
        z, y, x, k = spot()
        ref = ref.at[pl.ds(0, self.devices - 1)]
        return send(ref, ref, self.s, self.r, (z, y, x, 1 - k))

    def start(self):
        lax.fori_loop(1, self.devices, lambda i, c: (self.copy(i).start(), c)[1], 0)
        self.dst[self.me] = self.src[self.me]

    def arrive(self):
        self.together(self.dst).wait_recv()

    def drain(self):
        self.together(self.src).wait_send()


def low_lanes(shape):
    return lax.broadcasted_iota(jnp.int32, shape, 1) < 64


def merge_halves(first, second):
    low = low_lanes(first.shape)
    return (
        jnp.where(low, first, pltpu.roll(second, 64, 1)),
        jnp.where(low, pltpu.roll(first, 64, 1), second),
    )


def lane_norm(values, gain, shift):
    center = values - jnp.mean(values, 1, keepdims=True)
    scale_inv = lax.rsqrt(jnp.mean(center * center, 1, keepdims=True) + EPS)
    normal = center * scale_inv
    return normal * gain + shift, normal, scale_inv


def slot_zero(shape):
    return lax.broadcasted_iota(jnp.int32, shape, 1) == 0


def slot_sign(shape):
    return 1.0 - 2.0 * (lax.broadcasted_iota(jnp.int32, shape, 1) % 2).astype(F32)


def slot_weight(shape):
    return jnp.where(slot_zero(shape), 0.5 / shape[1], 1.0 / shape[1])


def column(params, index):
    return params[:, index : index + 1]


def norm_rows(stack, count, chans, width):
    total = None
    for j in range(count):
        tile = stack(j).astype(F32)[:, :128]
        tile = jnp.where(lax.broadcasted_iota(jnp.int32, tile.shape, 1) < chans, tile, 0.0)
        wide = jnp.concatenate([tile, jnp.zeros((tile.shape[0], width - 128), F32)], 1)
        wide = pltpu.roll(wide, j * chans, 1) if j else wide
        total = wide if total is None else total + wide
    return total


RAW = 14


def prepare(in_t, raw, own_in, desk, params, pos_t, mid_t, fil_t, cols):
    gain_one, shift_one, gain_two, shift_two, taps, bias, skip, decay, fil, pos, pos_bias, mid, rate, mid_bias = raw
    chans, order, emb = fil.shape[0], mid.shape[0], pos.shape[0]

    def put(row, values, wide):
        desk[row : row + values.shape[0], :wide] = values.astype(F32)

    desk[...] = jnp.zeros_like(desk)
    for i, ref in enumerate((gain_one, shift_one, gain_two, shift_two)):
        put(i, ref[...], chans)
    norms = jnp.concatenate([desk[:8, :], jnp.zeros((8, in_t.shape[1] - 128), F32)], 1)
    own_in[...] = jnp.concatenate([in_t[...].astype(F32), norms], 0).astype(BF16)
    for i in range(3):
        put(3 * i, taps[i], chans)
    put(9, bias[...], chans)
    put(12, skip[...], chans)
    put(13, decay[...], chans)
    params[...] = desk[...].T[:chans]
    desk[...] = jnp.zeros_like(desk)
    put(0, pos[...], order)
    put(emb, pos_bias[...], order)
    pos_t[...] = desk[...].T[:order, : pos_t.shape[1]]
    desk[...] = jnp.zeros_like(desk)
    put(0, mid[...], order)
    mid_t[...] = desk[...].T[:order, :order]
    desk[...] = jnp.zeros_like(desk)
    put(0, rate[...], order)
    put(1, mid_bias[...], order)
    cols[...] = desk[...].T[:order]
    fil_t[...] = fil[...].astype(F32)


def lane_norm_back(grad_out, normal, scale_inv, gain):
    grad_normal = grad_out * gain
    inner = grad_normal - jnp.mean(grad_normal, 1, keepdims=True)
    inner = inner - normal * jnp.mean(grad_normal * normal, 1, keepdims=True)
    return inner * scale_inv, jnp.sum(grad_out * normal, 0, keepdims=True), jnp.sum(grad_out, 0, keepdims=True)


LATE = (0, 3, 4, 5)


def layer_kernel(dims, *refs):
    line, devices, chans, seqs, block, blocks, width = dims
    (in_t, own_out, own_up, own_down, hidden, cot, feats, table) = refs[:8]
    raw = refs[8 : 8 + RAW]
    refs = refs[8 + RAW :]
    (result, grad_hidden, sum_up, sum_down, sum_out, sum_in, sum_tile, everyone, chan_grads, filter_grad) = refs[:10]
    refs = refs[10:]
    (full_in, full_out, full_up, full_down, mixed_in, norms_ref, steps, conv, spec, total, k_re, k_alt, k_im) = refs[:13]
    (one, cos_one, two, cos_two, params, pos_t, mid_t, fil_t, cols) = refs[13:22]
    (own_in, desk, proj_send, proj_recv, mix_send, kernel_buf, gated, sums) = refs[22:30]
    (w_flat, g_out, g_in, g_tile, resid, value_sum, second_sum, mix_recv, g_spec, g_conv) = refs[30:40]
    (k_sums, g_proj, small, g_rates, sum_rates) = refs[40:45]
    (gather_send, gather_recv, sends, recvs, local, exchange) = refs[45:51]
    buffers = refs[51:]
    shards = full_up.shape[0] // line
    hidden_rows = full_up.shape[1]
    chunk = shards * hidden_rows
    gated_grad, g_sums = gated, sums
    prepare(in_t, raw, own_in, desk, params, pos_t, mid_t, fil_t, cols)
    greet_near(line)
    gathers = [
        Gather(line, shard, full, gather_send.at[p], gather_recv.at[p], local)
        for p, (shard, full) in enumerate(
            ((own_in, full_in), (own_out, full_out), (own_up, full_up), (own_down, full_down))
        )
    ]
    late = LATE

    def tick(now):
        for piece, offset in zip(gathers, late):
            step = now - offset
            if step == 0:
                piece.begin()
            if 1 <= step < line:
                piece.along(step)
            if 1 <= step <= line:
                piece.plane(step - 1)
            if 2 <= step <= line + 1:
                piece.corner(step - 2)

    def filter_part(n, carry):
        sum_one = dot_plain(pos_t[...], feats[n], EXACT)
        phase = column(cols[...], 0) * sum_one
        act_one = jnp.sin(phase)
        one[n] = act_one
        cos_one[n] = jnp.cos(phase)
        phase = column(cols[...], 0) * (dot_plain(mid_t[...], act_one, EXACT) + column(cols[...], 1))
        act_two = jnp.sin(phase)
        two[n] = act_two
        cos_two[n] = jnp.cos(phase)
        lag = lax.broadcasted_iota(jnp.int32, (chans, block), 1) + n * block
        fade = jnp.exp(-lag.astype(F32) * column(params[...], 13))
        kernel_buf[pl.ds(eighths(n * chans), chans), :] = dot_plain(fil_t[...], act_two, EXACT) * fade
        return carry

    def filters(first, last):
        lax.fori_loop(first, last, filter_part, 0)

    def kernel_spectrum():
        ker = dot_plain(kernel_buf[...], table[...], EXACT)
        before = jnp.concatenate([jnp.zeros((chans, 2 * block), F32), ker[:-chans]], 0)
        sign = slot_sign((chans * blocks, block))
        real = ker[:, :block] + sign * before[:, :block]
        imag = ker[:, block:] + sign * before[:, block:]
        zero = slot_zero(real.shape)
        k_re[...] = real
        k_alt[...] = jnp.where(zero, imag, real)
        k_im[...] = jnp.where(zero, 0.0, imag)

    tick(0)
    filters(0, blocks // 4)
    tick(1)
    filters(blocks // 4, blocks // 2)
    tick(2)
    filters(blocks // 2, 3 * blocks // 4)
    tick(3)
    filters(3 * blocks // 4, blocks)
    tick(4)
    kernel_spectrum()
    tick(5)
    gathers[0].finish()

    in_rows = full_in.shape[1]
    norms = norm_rows(lambda j: full_in[j, in_rows - 8 :], devices, chans, width)
    norms_ref[...] = norms
    normed, _, _ = lane_norm(hidden[...].astype(F32), norms[0:1], norms[1:2])
    projected = dot_rows(full_in[...].reshape(devices * in_rows, width), normed.astype(BF16))
    projected = projected.reshape(devices, in_rows, 128)
    for j in range(devices):
        for i in range(3):
            unit = 3 * j + i
            proj_send[unit % devices, unit // devices] = projected[j, i * chans : (i + 1) * chans].astype(BF16)
    moved = Exchange(proj_send, proj_recv, exchange.at[0], exchange.at[1], devices)
    moved.start()
    tick(6)
    moved.arrive()

    def assemble(j, carry):
        lanes = pl.ds(pl.multiple_of(j * 128, 128), 128)
        for p in range(3):
            pair = merge_halves(proj_recv[2 * j, p].astype(F32), proj_recv[2 * j + 1, p].astype(F32))
            for s in range(seqs):
                steps[p, s, :, lanes] = pair[s]
        return carry

    lax.fori_loop(0, devices // 2, assemble, 0)
    length = block * blocks
    for s in range(seqs):
        for c in range(0, chans, 8):
            spots = lax.broadcasted_iota(jnp.int32, (8, length), 1)
            parts = []
            for p in range(3):
                x = steps[p, s, c : c + 8, :]
                local_params = params[c : c + 8, :]
                value = column(local_params, 9 + p) + column(local_params, p) * x
                for i in (1, 2):
                    value += column(local_params, 3 * i + p) * jnp.where(spots < i, 0.0, pltpu.roll(x, i, 1))
                parts.append(value)
            product = parts[1] * parts[2]
            for n in range(blocks):
                at_rows = (n * seqs + s) * chans + c
                lanes = slice(n * block, (n + 1) * block)
                gated[at_rows : at_rows + 8, :] = product[:, lanes]
                for p in range(3):
                    conv[p, at_rows : at_rows + 8, :] = parts[p][:, lanes]
    tick(7)

    spec[...] = dot_plain(gated[...], table[...], EXACT)
    weight = slot_weight((chans, block))

    def output_block(m, carry):
        def add(n, acc):
            at_kernel = pl.ds(eighths((m - n) * chans), chans)
            kr, ka, ki = k_re[at_kernel, :], k_alt[at_kernel, :], k_im[at_kernel, :]
            result = []
            for s in range(seqs):
                at_signal = pl.ds(eighths((n * seqs + s) * chans), chans)
                re, im = spec[at_signal, :block], spec[at_signal, block:]
                result.append(acc[2 * s] + re * kr - im * ki)
                result.append(acc[2 * s + 1] + re * ki + im * ka)
            return tuple(result)

        acc = lax.fori_loop(0, m + 1, add, tuple(jnp.zeros((chans, block), F32) for _ in range(2 * seqs)))
        for s in range(seqs):
            at_signal = pl.ds(eighths((m * seqs + s) * chans), chans)
            sums[at_signal, :block] = acc[2 * s] * weight
            sums[at_signal, block:] = acc[2 * s + 1] * weight
        return carry

    lax.fori_loop(0, blocks, output_block, 0)
    tick(8)
    total[...] = dot_rows(sums[...], table[...], EXACT)

    def mix(m, carry):
        mixed = []
        for s in range(seqs):
            at_signal = pl.ds(eighths((m * seqs + s) * chans), chans)
            value = total[at_signal, :] + column(params[...], 12) * gated[at_signal, :]
            total[at_signal, :] = value
            mixed.append(value * conv[0, at_signal, :])
        for h in range(block // 128):
            pair = merge_halves(*(v[:, h * 128 : (h + 1) * 128] for v in mixed))
            for q in range(2):
                mix_send[m * (block // 64) + 2 * h + q] = pair[q].astype(BF16)
        return carry

    lax.fori_loop(0, blocks, mix, 0)
    mix_home = Exchange(mix_send, mixed_in, exchange.at[2], exchange.at[3], devices)
    mix_home.start()
    tick(9)
    tick(10)
    for piece in gathers[1:]:
        piece.finish()
    mix_home.arrive()
    for piece in gathers:
        piece.drain()
    moved.drain()
    mix_home.drain()

    parts = (full_up, full_down, g_out, g_in, g_tile, g_rates)
    outs = (sum_up, sum_down, sum_out, sum_in, sum_tile, sum_rates)
    pieces = [
        Reduce(line, parts[p], outs[p], *buffers[p * BUFFERS : (p + 1) * BUFFERS], sends.at[p], recvs.at[p])
        for p in range(6)
    ]

    z = lax.axis_index("blk") // 2
    half = line // 2
    flip = z // half
    mirror = z + flip * (line - 1 - 2 * z)

    def visit(i):
        near = half - 1 - mirror if i < line - 1 else mirror
        place = line - 1 - i if i < half else near
        return place + flip * (line - 1 - 2 * place)

    def fold(group, slot):
        for piece in group:
            if slot < line:
                piece.corner(visit(slot), slot >= half)
            if half < slot <= line:
                piece.plane(visit(slot - 1))
            if 2 <= slot <= line + 1:
                piece.along(visit(slot - 2), slot - 2 == line - 1)

    gain_two, shift_two = norms_ref[2:3], norms_ref[3:4]
    mixed = mixed_in[...].astype(F32).reshape(width, 128).T.astype(BF16)
    w_flat[...] = full_out[...].astype(F32).reshape(width, width).astype(BF16)
    resid[...] = hidden[...].astype(F32) + dot_rows(mixed, w_flat[...])
    second, normal_two, inv_two = lane_norm(resid[...], gain_two, shift_two)
    second = second.astype(BF16)
    value_sum[...] = jnp.zeros_like(value_sum)
    second_sum[...] = jnp.zeros_like(second_sum)

    for i in range(line):
        where_to = pl.ds(visit(i) * shards, shards)
        up = full_up[where_to].reshape(chunk, width)
        down = full_down[where_to].reshape(chunk, width)
        active, slope = gelu_parts(dot_rows(up, second))
        active = active.astype(BF16)
        grad_upper = (dot_rows(down, cot[...]) * slope).astype(BF16)
        value_sum[...] += dot_plain(active.astype(F32).T.astype(BF16), down)
        second_sum[...] += dot_plain(grad_upper.astype(F32).T.astype(BF16), up)
        full_down[where_to] = dot_plain(active, cot[...]).astype(BF16).reshape(shards, hidden_rows, width)
        full_up[where_to] = dot_plain(grad_upper, second).astype(BF16).reshape(shards, hidden_rows, width)
        for piece in pieces[:2]:
            piece.begin(visit(i))
    result[...] = (resid[...] + value_sum[...]).astype(BF16)
    resid_term, grad_gain_two, grad_shift_two = lane_norm_back(second_sum[...], normal_two, inv_two, gain_two)
    resid[...] = cot[...].astype(F32) + resid_term
    grad_mixed = dot_plain(resid[...].astype(BF16), w_flat[...])
    mix_send[...] = grad_mixed.T.reshape(devices, chans, 128).astype(BF16)
    grad_mix = Exchange(mix_send, mix_recv, exchange.at[4], exchange.at[5], devices)
    grad_mix.start()
    fold(pieces[:2], 0)
    grad_branch = resid[...].T.astype(BF16)
    g_out[...] = dot_plain(grad_branch, mixed).reshape(devices, chans, width).astype(BF16)
    for i in range(line):
        pieces[2].begin(visit(i))
    grad_mix.arrive()

    weight = slot_weight((chans, block))
    skip = column(params[...], 12)
    per_block = block // 64

    def arrange(m, carry):
        for h in range(block // 128):
            source = m * per_block + 2 * h
            pair = merge_halves(mix_recv[source].astype(F32), mix_recv[source + 1].astype(F32))
            lanes = slice(h * 128, (h + 1) * 128)
            for s in range(seqs):
                at_rows = pl.ds(eighths((m * seqs + s) * chans), chans)
                place = pl.ds(pl.multiple_of(m * block + h * 128, 128), 128)
                g_conv[0, s, :, place] = pair[s] * total[at_rows, lanes]
                grad = pair[s] * conv[0, at_rows, lanes]
                gated_grad[at_rows, lanes] = grad
                carry = carry + grad * conv[1, at_rows, lanes] * conv[2, at_rows, lanes]
        return carry

    skip_sum = lax.fori_loop(0, blocks, arrange, jnp.zeros((chans, 128), F32))
    g_spec[...] = dot_plain(gated_grad[...], table[...], EXACT)
    fold(pieces[:2], 1)

    def signal_block(n, carry):
        def add(m, acc):
            at_kernel = pl.ds(eighths((m - n) * chans), chans)
            kr, ka, ki = k_re[at_kernel, :], k_alt[at_kernel, :], k_im[at_kernel, :]
            out = []
            for s in range(seqs):
                at_rows = pl.ds(eighths((m * seqs + s) * chans), chans)
                re, im = g_spec[at_rows, :block], g_spec[at_rows, block:]
                out.append(acc[2 * s] + re * kr + im * ki)
                out.append(acc[2 * s + 1] + im * ka - re * ki)
            return tuple(out)

        acc = lax.fori_loop(n, blocks, add, tuple(jnp.zeros((chans, block), F32) for _ in range(2 * seqs)))
        for s in range(seqs):
            at_rows = pl.ds(eighths((n * seqs + s) * chans), chans)
            g_sums[at_rows, :block] = acc[2 * s] * weight
            g_sums[at_rows, block:] = acc[2 * s + 1] * weight
        return carry

    lax.fori_loop(0, blocks, signal_block, 0)
    g_sums[:, :block] = dot_rows(g_sums[...], table[...], EXACT)

    def gate_grads(m, carry):
        for s in range(seqs):
            at_rows = pl.ds(eighths((m * seqs + s) * chans), chans)
            place = pl.ds(pl.multiple_of(m * block, block), block)
            grad = g_sums[at_rows, :block] + skip * gated_grad[at_rows, :]
            g_conv[1, s, :, place] = grad * conv[2, at_rows, :]
            g_conv[2, s, :, place] = grad * conv[1, at_rows, :]
        return carry

    lax.fori_loop(0, blocks, gate_grads, 0)

    length = block * blocks
    for c in range(0, chans, 8):
        col = lax.broadcasted_iota(jnp.int32, (8, 128), 1)
        spots = lax.broadcasted_iota(jnp.int32, (8, length), 1)
        found = jnp.where(col == 12, jnp.sum(skip_sum[c : c + 8], 1, keepdims=True), 0.0)
        local_params = params[c : c + 8, :]
        for p in range(3):
            for s in range(seqs):
                grad = g_conv[p, s, c : c + 8, :]
                x = steps[p, s, c : c + 8, :]
                value = jnp.zeros_like(grad)
                for i in range(3):
                    later = jnp.where(spots < length - i, pltpu.roll(grad, length - i, 1), 0.0) if i else grad
                    value += column(local_params, 3 * i + p) * later
                    found += jnp.where(col == 3 * i + p, jnp.sum(later * x, 1, keepdims=True), 0.0)
                found += jnp.where(col == 9 + p, jnp.sum(grad, 1, keepdims=True), 0.0)
                g_conv[p, s, c : c + 8, :] = value
        chan_grads[c : c + 8, :] = found

    def pack(j, carry):
        lanes = pl.ds(pl.multiple_of(j * 128, 128), 128)
        for p in range(3):
            pair = merge_halves(g_conv[p, 0, :, lanes], g_conv[p, 1, :, lanes])
            proj_send[2 * j, p] = pair[0].astype(BF16)
            proj_send[2 * j + 1, p] = pair[1].astype(BF16)
        return carry

    lax.fori_loop(0, devices // 2, pack, 0)
    home = Exchange(proj_send, proj_recv, exchange.at[6], exchange.at[7], devices)
    home.start()
    fold(pieces[:2], 2)

    def kernel_block(d, carry):
        def add(n, acc):
            real, imag = acc
            for s in range(seqs):
                at_signal = pl.ds(eighths((n * seqs + s) * chans), chans)
                at_grad = pl.ds(eighths(((n + d) * seqs + s) * chans), chans)
                s_re, s_im = spec[at_signal, :block], spec[at_signal, block:]
                g_re, g_im = g_spec[at_grad, :block], g_spec[at_grad, block:]
                zero = slot_zero((chans, block))
                same, other = g_re * s_re, g_im * s_im
                real = real + jnp.where(zero, same, same + other)
                imag = imag + jnp.where(zero, other, g_im * s_re - g_re * s_im)
            return real, imag

        empty = jnp.zeros((chans, block), F32)
        real, imag = lax.fori_loop(0, blocks - d, add, (empty, empty))
        at_kernel = pl.ds(eighths(d * chans), chans)
        k_sums[at_kernel, :block] = real
        k_sums[at_kernel, block:] = imag
        return carry

    lax.fori_loop(0, blocks, kernel_block, 0)
    after = jnp.concatenate([k_sums[chans:, :], jnp.zeros((chans, 2 * block), F32)], 0)
    shape = (chans * blocks, block)
    sign, scale = slot_sign(shape), slot_weight(shape)
    k_sums[:, :block] = (k_sums[:, :block] + sign * after[:, :block]) * scale
    k_sums[:, block:] = (k_sums[:, block:] + sign * after[:, block:]) * scale
    k_sums[:, :block] = dot_rows(k_sums[...], table[...], EXACT)
    fold(pieces[:2], 3)
    fold(pieces[2:3], 0)

    order = pos_t.shape[0]
    emb = pos_t.shape[1]
    freq = column(cols[...], 0)

    def filter_block(n, carry):
        grad_fil, grad_pos, grad_mid, grad_bias = carry
        lag = lax.broadcasted_iota(jnp.int32, (chans, block), 1) + n * block
        fade = jnp.exp(-lag.astype(F32) * column(params[...], 13))
        grad = k_sums[pl.ds(eighths(n * chans), chans), :block] * fade
        grad_fil = grad_fil + dot_rows(grad, two[n], EXACT)
        grad_two = dot_plain(fil_t[...].T, grad, EXACT) * cos_two[n] * freq
        grad_mid = grad_mid + dot_rows(one[n], grad_two, EXACT)
        grad_bias = grad_bias + dot_rows(jnp.ones((8, block), F32), grad_two, EXACT)
        grad_one = dot_plain(mid_t[...].T, grad_two, EXACT) * cos_one[n] * freq
        grad_pos = grad_pos + dot_rows(feats[n], grad_one, EXACT)
        return grad_fil, grad_pos, grad_mid, grad_bias

    zeros = [jnp.zeros(s, F32) for s in ((chans, order), (emb, order), (order, order), (8, order))]
    grad_fil, grad_pos, grad_mid, grad_bias = lax.fori_loop(0, blocks, filter_block, tuple(zeros))
    filter_grad[...] = grad_fil
    rate_bias = cols[...].T
    grad_rate = jnp.sum(pos_t[...].T * grad_pos, 0, keepdims=True) + jnp.sum(mid_t[...].T * grad_mid, 0, keepdims=True)
    grad_rate = (grad_rate + rate_bias[1:2] * grad_bias[:1]) / rate_bias[0:1]
    small[...] = jnp.zeros_like(small)
    small[:emb, :order] = grad_pos
    small[emb : emb + order, :order] = grad_mid
    picked = lax.broadcasted_iota(jnp.int32, (8, order), 0)
    small[emb + order : emb + order + 8, :order] = jnp.where(
        picked == 0, grad_bias, jnp.where(picked == 1, grad_rate, 0.0)
    )
    g_rates[...] = jnp.zeros_like(g_rates)
    for j in range(devices):
        g_rates[j, 4:8, :] = small[4 * j : 4 * j + 4, :]
    for i in range(line):
        pieces[5].begin(visit(i))
    fold(pieces[:2], 4)
    fold(pieces[2:3], 1)
    fold(pieces[5:6], 0)

    gain_one, shift_one = norms_ref[0:1], norms_ref[1:2]
    normed, normal_one, inv_one = lane_norm(hidden[...].astype(F32), gain_one, shift_one)
    normed = normed.astype(BF16)
    g_proj[...] = jnp.zeros_like(g_proj)
    home.arrive()
    for j in range(devices):
        for i in range(3):
            unit = 3 * j + i
            at_rows = slice(j * in_rows + i * chans, j * in_rows + (i + 1) * chans)
            g_proj[at_rows, :] = proj_recv[unit % devices, unit // devices].astype(F32)
    for i in range(line):
        zo = visit(i)
        group = shards * in_rows
        grads = dot_plain(g_proj[pl.ds(eighths(zo * group), group), :].astype(BF16), normed)
        g_in[pl.ds(zo * shards, shards)] = grads.reshape(shards, in_rows, width)[:, : 3 * chans].astype(BF16)
        pieces[3].begin(zo)
    fold(pieces[3:4], 0)
    fold(pieces[5:6], 1)
    fold(pieces[2:3], 2)
    grad_normed = dot_plain(g_proj[...].T.astype(BF16), full_in[...].reshape(devices * in_rows, width))
    input_term, grad_gain_one, grad_shift_one = lane_norm_back(grad_normed, normal_one, inv_one, gain_one)
    grad_hidden[...] = (resid[...] + input_term).astype(BF16)
    norm_grads = jnp.concatenate(
        [grad_gain_one, grad_shift_one, grad_gain_two, grad_shift_two, jnp.zeros((4, width), F32)], 0
    )
    for j in range(devices):
        turned = pltpu.roll(norm_grads, width - j * chans, 1) if j else norm_grads
        g_tile[j, 0:4, :] = turned[0:4, :128]
        g_tile[j, 4:8, :] = jnp.zeros((4, 128), F32)
    for i in range(line):
        pieces[4].begin(visit(i))
    fold(pieces[4:5], 0)
    fold(pieces[3:5], 1)
    fold(pieces[2:3], 3)
    fold(pieces[5:6], 2)
    fold(pieces[3:5], 2)
    fold(pieces[2:3], 4)
    fold(pieces[5:6], 3)
    fold(pieces[3:5], 3)
    fold(pieces[:2], 5)
    fold(pieces[5:6], 4)
    fold(pieces[2:3], 5)
    fold(pieces[5:6], 5)
    mine = flat(*spot())

    def share(i):
        other = lax.rem(mine + i, devices)
        place = (other // 8, other // 4 % 2, other // 2 % 2, other % 2)
        return send(sum_rates, everyone.at[mine], exchange.at[8], exchange.at[9], place)

    keep = pltpu.make_async_copy(sum_rates, everyone.at[mine], local)
    keep.start()
    lax.fori_loop(1, devices, lambda i, c: (share(i).start(), c)[1], 0)
    fold(pieces[3:5], 4)
    fold(pieces[3:5], 5)

    for piece in pieces:
        piece.drain()
    grad_mix.drain()
    home.drain()
    keep.wait()

    arrived = everyone.at[pl.ds(0, devices - 1)]
    shared = send(arrived, arrived, exchange.at[8], exchange.at[9], (*spot()[:3], 1 - spot()[3]))
    shared.wait_recv()
    shared.wait_send()


def layer(shards, hidden, cot, feats, table, raw, dims):
    line, devices, chans, seqs, block, blocks, width = dims
    order = raw[-1].shape[1]
    rows, tokens = blocks * seqs * chans, hidden.shape[0]
    in_rows, hidden_rows = shards[0].shape[0] + 8, shards[2].shape[0]
    shape, buffer, dma = jax.ShapeDtypeStruct, pltpu.VMEM, pltpu.SemaphoreType.DMA
    vmem = pl.BlockSpec(memory_space=pltpu.VMEM)
    tile = (devices, 8, 128)
    outs = [
        shape((tokens, width), BF16),
        shape((tokens, width), BF16),
        shape((hidden_rows, width), F32),
        shape((hidden_rows, width), F32),
        shape((chans, width), F32),
        shape((3 * chans, width), F32),
        shape(tile[1:], F32),
        shape(tile, F32),
        shape((chans, 128), F32),
        shape((chans, order), F32),
    ]
    scratch = [buffer((devices, r, width), BF16) for r in (in_rows, chans, hidden_rows, hidden_rows)]
    scratch += [
        buffer((devices, chans, 128), BF16),
        buffer((8, width), F32),
        buffer((3, seqs, chans, block * blocks), F32),
        buffer((3, rows, block), F32),
        buffer((rows, 2 * block), F32),
        buffer((rows, block), F32),
    ]
    scratch += [buffer((blocks * chans, block), F32)] * 3 + [buffer((blocks, order, block), F32)] * 4
    scratch += [buffer((chans, 128), F32), buffer((order, feats.shape[1]), F32), buffer((order, order), F32)]
    scratch += [buffer((chans, order), F32), buffer((order, 128), F32)]
    scratch += [
        buffer((in_rows, width), BF16),
        buffer((128, 128), F32),
        buffer((devices, 3, chans, 128), BF16),
        buffer((devices, 3, chans, 128), BF16),
        buffer((devices, chans, 128), BF16),
        buffer((blocks * chans, block), F32),
        buffer((rows, block), F32),
        buffer((rows, 2 * block), F32),
        buffer((width, width), BF16),
        buffer((devices, chans, width), BF16),
        buffer((devices, 3 * chans, width), BF16),
        buffer(tile, F32),
        buffer((tokens, width), F32),
        buffer((tokens, width), F32),
        buffer((tokens, width), F32),
        buffer((devices, chans, 128), BF16),
        buffer((rows, 2 * block), F32),
        buffer((3, seqs, chans, block * blocks), F32),
        buffer((blocks * chans, 2 * block), F32),
        buffer((devices * in_rows, 128), F32),
        buffer((4 * devices, 128), F32),
        buffer(tile, F32),
        buffer(tile[1:], F32),
    ]
    scratch += [dma((4, 2 * line + 6)), dma((4, 6 * line + 1)), dma((6, 2 * line + 6)), dma((6, 7 * line))]
    scratch += [dma, dma((10,))]
    parts = [shape((devices, r, width), BF16) for r in (hidden_rows, hidden_rows, chans, 3 * chans)] + [shape(tile, F32)] * 2
    scratch += [b for part in parts for b in reduce_scratch(line, part)]
    operands = [*shards, hidden, cot, feats, table, *raw]
    return pl.pallas_call(
        functools.partial(layer_kernel, dims),
        name="layer",
        out_shape=outs,
        in_specs=[vmem] * len(operands),
        out_specs=[vmem] * len(outs),
        scratch_shapes=scratch,
        compiler_params=pltpu.CompilerParams(collective_id=0, has_side_effects=True, vmem_limit_bytes=KERNEL_VMEM),
    )(*operands)


def finish_kernel(emb, order, *refs):
    (result, grad_hidden, up, down, out, inp, tile, everyone, chan_grads, filter_grad) = refs[:10]
    outs, desk = refs[10:-1], refs[-1]
    chans = chan_grads.shape[0]
    for target, source in zip(outs[:7], (result, grad_hidden, up, down, out, inp, filter_grad)):
        target[...] = source[...]
    taps, bias, skip, *gains = outs[7:14]
    desk[...] = jnp.zeros_like(desk)
    desk[:chans, :] = chan_grads[...]
    turned = desk[...].T
    for i in range(3):
        taps[i] = turned[3 * i : 3 * i + 3, :chans]
    bias[...] = turned[9:12, :chans]
    skip[...] = turned[12:13, :chans]
    for i, gain in enumerate(gains):
        gain[...] = tile[i : i + 1, :chans]
    for j in range(everyone.shape[0]):
        desk[4 * j : 4 * j + 4, :] = everyone[j, 4:8, :]
    pos, pos_bias, mid, mid_bias, rate = outs[14:]
    after = emb + 1 + -(emb + 1) % 8
    pos[...] = desk[:emb, :order]
    pos_bias[...] = desk[emb : emb + 1, :order]
    mid[...] = desk[after : after + order, :order]
    mid_bias[...] = desk[after + order : after + order + 1, :order]
    rate[...] = desk[after + order + 1 : after + order + 2, :order]


def finish(parts, pos_shape):
    emb, order = pos_shape
    chans = parts[8].shape[0]
    shape = jax.ShapeDtypeStruct
    vmem = pl.BlockSpec(memory_space=pltpu.VMEM)
    outs = [shape(p.shape, p.dtype) for p in parts[:6]] + [shape(parts[9].shape, F32)]
    outs += [shape((3, 3, chans), F32), shape((3, chans), F32)] + [shape((1, chans), F32)] * 5
    outs += [shape((emb, order), F32), shape((1, order), F32), shape((order, order), F32)]
    outs += [shape((1, order), F32)] * 2
    return pl.pallas_call(
        functools.partial(finish_kernel, emb, order),
        name="finish",
        out_shape=outs,
        in_specs=[vmem] * len(parts),
        out_specs=[vmem] * len(outs),
        scratch_shapes=[pltpu.VMEM((128, 128), F32)],
    )(*parts)


def shards_paired(
    hidden_in,
    cotangent,
    mixer_input_weight,
    mixer_output_weight,
    feedforward_up,
    feedforward_down,
    first_gain,
    first_shift,
    second_gain,
    second_shift,
    short_taps,
    short_bias,
    skip_scale,
    filter_out,
    pos_weight,
    pos_bias,
    mid_weight,
    mid_bias,
    sine_freq,
    decay_rate,
):
    devices = lax.axis_size(AXES)
    micro, seq_count, tok, width = hidden_in.shape
    seqs = micro * seq_count
    tokens = seqs * tok
    length = tok * devices
    chans = width // devices
    block = tok * lax.axis_size("chan")
    blocks = length // block

    line = devices // 8
    def row(vector):
        return vector.reshape(1, -1)

    shards = [mixer_input_weight.T, mixer_output_weight.T, feedforward_up.T, feedforward_down]
    raw = [row(v) for v in (first_gain, first_shift, second_gain, second_shift)]
    raw += [short_taps, short_bias, row(skip_scale), row(decay_rate), filter_out.T]
    raw += [pos_weight, row(pos_bias), mid_weight, row(sine_freq), row(mid_bias)]
    hidden = hidden_in.reshape(tokens, width)
    features, table = jnp.asarray(feature_blocks(length, block)), jnp.asarray(fixed_table(block))
    dims = (line, devices, chans, seqs, block, blocks, width)
    parts = layer(shards, hidden, cotangent.reshape(tokens, width), features, table, raw, dims)
    outs = finish(parts, pos_weight.shape)
    result, grad_hidden, up, down, out, inp, filter_grad, taps, bias, skip, *rest = outs
    gains, (pos, pos_bias, mid, mid_bias, rate) = rest[:4], rest[4:]
    return (
        result.reshape(hidden_in.shape),
        grad_hidden.reshape(hidden_in.shape),
        inp.T,
        out.T,
        up.T,
        down,
        *[g.reshape(-1) for g in gains],
        taps,
        bias,
        skip.reshape(-1),
        filter_grad.T,
        pos,
        pos_bias.reshape(-1),
        mid,
        mid_bias.reshape(-1),
        rate.reshape(-1),
    )


def shards(
    hidden_in,
    cotangent,
    mixer_input_weight,
    mixer_output_weight,
    feedforward_up,
    feedforward_down,
    first_gain,
    first_shift,
    second_gain,
    second_shift,
    short_taps,
    short_bias,
    skip_scale,
    filter_out,
    pos_weight,
    pos_bias,
    mid_weight,
    mid_bias,
    sine_freq,
    decay_rate,
):
    devices = lax.axis_size(AXES)
    micro, seq_count, tok, width = hidden_in.shape
    seqs = micro * seq_count
    tokens = seqs * tok
    length = tok * devices
    chans = width // devices
    block = tok * lax.axis_size("chan")
    blocks = length // block

    norms = jnp.stack([first_gain, first_shift, second_gain, second_shift])
    own = [mixer_input_weight.T, feedforward_up.T, feedforward_down, mixer_output_weight.T]
    full = [lax.all_gather(shard, AXES, axis=0, tiled=True) for shard in own]
    norms = lax.all_gather(norms, AXES, axis=1, tiled=True)
    weight_in, weight_up, weight_down, weight_out = full
    norms = norms.astype(F32)
    gain_one, shift_one, gain_two, shift_two = norms[0], norms[1], norms[2], norms[3]

    freq = sine_freq.astype(F32)
    w_pos, w_mid, w_fil = pos_weight.astype(F32), mid_weight.astype(F32), filter_out.astype(F32)
    lags, features, first_sum, first_act, second_sum, second_act = filter_hidden(
        length, w_pos, pos_bias.astype(F32), w_mid, mid_bias.astype(F32), freq
    )
    decay = jnp.exp(-lags[None, :] * decay_rate.astype(F32)[:, None])
    kernel = contract(w_fil, second_act, 0, 0, EXACT) * decay
    table = block_table(block)
    sign = 1.0 - 2.0 * (lax.iota(jnp.int32, block) % 2).astype(F32)
    ker_re, ker_im = to_spectrum(kernel.reshape(chans, blocks, block), table)

    def with_previous(spec):
        before = jnp.concatenate([jnp.zeros_like(spec[:, :1]), spec[:, :-1]], 1)
        return spec + sign * before

    k_re, k_alt, k_im = packed_kernel(with_previous(ker_re), with_previous(ker_im))

    values = hidden_in.reshape(tokens, width).astype(F32)
    normed, normal_one, inv_one = layer_norm(values, gain_one, shift_one)
    normed = normed.astype(BF16)
    projected = contract(weight_in, normed, 1, 1).astype(BF16)
    projected = projected.reshape(3, devices, chans, tokens).transpose(1, 0, 2, 3)
    arrived = exchange(projected)

    def by_sequence(values):
        parts = values.shape[1]
        values = values.reshape(devices, parts, chans, seqs, tok)
        return values.transpose(1, 3, 2, 0, 4).reshape(parts, seqs, chans, length)

    def by_device(values):
        parts = values.shape[0]
        values = values.reshape(parts, seqs, chans, devices, tok)
        return values.transpose(3, 0, 2, 1, 4).reshape(devices, parts, chans, tokens)

    steps = by_sequence(arrived).astype(F32)
    taps = short_taps.astype(F32)[:, :, None, :, None]
    conv = short_bias.astype(F32)[:, None, :, None]
    for i in range(3):
        conv = conv + taps[i] * delayed(steps, i)
    gate_out, gate_in, signal = conv[0], conv[1], conv[2]
    gated = signal * gate_in
    sig_re, sig_im = to_spectrum(gated.reshape(seqs, chans, blocks, block), table)

    def shifted_sum(make):
        total = None
        for d in range(blocks):
            term = make(d)
            total = term if total is None else tuple(a + b for a, b in zip(total, term))
        return total

    def ahead(x, d):
        return x if d == 0 else jnp.pad(x[:, :, :-d], ((0, 0), (0, 0), (d, 0), (0, 0)))

    def back(x, d):
        return x if d == 0 else jnp.pad(x[:, :, d:], ((0, 0), (0, 0), (0, d), (0, 0)))

    def forward_term(d):
        re, im = ahead(sig_re, d), ahead(sig_im, d)
        kr, ka, ki = k_re[:, d : d + 1], k_alt[:, d : d + 1], k_im[:, d : d + 1]
        return re * kr - im * ki, re * ki + im * ka

    out_re, out_im = shifted_sum(forward_term)
    long_out = from_spectrum(out_re, out_im, table).reshape(seqs, chans, length)
    skip = skip_scale.astype(F32)[None, :, None]
    long_total = long_out + skip * gated
    mixed = (long_total * gate_out).astype(BF16)
    mixed = exchange(by_device(mixed[None])).reshape(width, tokens)

    resid = values + contract(mixed, weight_out, 0, 1)
    second, normal_two, inv_two = layer_norm(resid, gain_two, shift_two)
    second = second.astype(BF16)
    upper = contract(second, weight_up, 1, 1)
    active, slope = gelu_parts(upper)
    active = active.astype(BF16)
    result = resid + contract(active, weight_down, 1, 0)

    cot = cotangent.reshape(tokens, width)
    grad_down = contract(active, cot, 0, 0)
    grad_upper = (contract(cot, weight_down, 1, 1) * slope).astype(BF16)
    grad_up = contract(grad_upper, second, 0, 0)
    grad_second = contract(grad_upper, weight_up, 1, 0)
    resid_term, grad_gain_two, grad_shift_two = layer_norm_back(grad_second, normal_two, inv_two, gain_two)
    grad_resid = cot.astype(F32) + resid_term
    grad_branch = grad_resid.astype(BF16)
    grad_out_w = contract(grad_branch, mixed, 0, 1)
    grad_mixed = contract(weight_out, grad_branch, 0, 1).astype(BF16)
    grad_mixed = exchange(grad_mixed.reshape(devices, 1, chans, tokens))
    grad_mixed = by_sequence(grad_mixed)[0].astype(F32)

    grad_gate_out = grad_mixed * long_total
    grad_long = grad_mixed * gate_out
    grad_skip = jnp.sum(grad_long * gated, (0, 2))
    gl_re, gl_im = to_spectrum(grad_long.reshape(seqs, chans, blocks, block), table)

    def signal_term(d):
        re, im = back(gl_re, d), back(gl_im, d)
        kr, ka, ki = k_re[:, d : d + 1], k_alt[:, d : d + 1], k_im[:, d : d + 1]
        return re * kr + im * ki, im * ka - re * ki

    gg_re, gg_im = shifted_sum(signal_term)
    grad_gated = from_spectrum(gg_re, gg_im, table).reshape(seqs, chans, length) + skip * grad_long

    first_slot = lax.iota(jnp.int32, block) == 0
    kg_re, kg_im = [], []
    for d in range(blocks):
        s_re, s_im = sig_re[:, :, : blocks - d], sig_im[:, :, : blocks - d]
        g_re, g_im = gl_re[:, :, d:], gl_im[:, :, d:]
        same, other = g_re * s_re, g_im * s_im
        kg_re.append(jnp.sum(jnp.where(first_slot, same, same + other), (0, 2)))
        kg_im.append(jnp.sum(jnp.where(first_slot, other, g_im * s_re - g_re * s_im), (0, 2)))
    kg_re, kg_im = jnp.stack(kg_re, 1), jnp.stack(kg_im, 1)

    def with_next(spec):
        after = jnp.concatenate([spec[:, 1:], jnp.zeros_like(spec[:, :1])], 1)
        return spec + sign * after

    grad_kernel = from_spectrum(with_next(kg_re), with_next(kg_im), table).reshape(chans, length)

    grad_conv = jnp.stack([grad_gate_out, grad_gated * signal, grad_gated * gate_in])
    grad_bias = jnp.sum(grad_conv, (1, 3))
    grad_taps = jnp.stack([jnp.sum(grad_conv * delayed(steps, i), (1, 3)) for i in range(3)])
    grad_steps = taps[0] * grad_conv
    for i in (1, 2):
        grad_steps = grad_steps + taps[i] * advanced(grad_conv, i)
    grad_proj = exchange(by_device(grad_steps.astype(BF16)))
    grad_proj = grad_proj.transpose(1, 0, 2, 3).reshape(3 * width, tokens)

    fade = grad_kernel * decay
    grad_filter = contract(second_act, fade, 1, 1, EXACT)
    grad_two = contract(w_fil, fade, 1, 0, EXACT) * jnp.cos(freq[:, None] * second_sum)
    grad_freq = jnp.sum(grad_two * second_sum, 1)
    grad_two = grad_two * freq[:, None]
    grad_mid = contract(first_act, grad_two, 1, 1, EXACT)
    grad_one = contract(w_mid, grad_two, 1, 0, EXACT) * jnp.cos(freq[:, None] * first_sum)
    grad_freq = grad_freq + jnp.sum(grad_one * first_sum, 1)
    grad_one = grad_one * freq[:, None]
    grad_pos = contract(features, grad_one, 1, 1, EXACT)
    small = jnp.concatenate(
        [grad_pos, jnp.sum(grad_one, 1)[None], grad_mid, jnp.sum(grad_two, 1)[None], grad_freq[None]]
    )
    emb, order = pos_weight.shape

    grad_in = contract(grad_proj, normed, 1, 0)
    grad_normed = contract(grad_proj, weight_in, 0, 0)
    input_term, grad_gain_one, grad_shift_one = layer_norm_back(grad_normed, normal_one, inv_one, gain_one)
    grad_hidden = (grad_resid + input_term).astype(BF16)

    norm_grads = jnp.stack([grad_gain_one, grad_shift_one, grad_gain_two, grad_shift_two])
    sums = [grad_in, grad_up, grad_down, grad_out_w]
    sums = [
        lax.psum_scatter(g.astype(BF16), AXES, scatter_dimension=0, tiled=True).astype(F32) for g in sums
    ]
    norm_grads = lax.psum_scatter(norm_grads, AXES, scatter_dimension=1, tiled=True)
    small = lax.psum(small, AXES)
    return (
        result.astype(BF16).reshape(hidden_in.shape),
        grad_hidden.reshape(hidden_in.shape),
        sums[0].T,
        sums[3].T,
        sums[1].T,
        sums[2],
        norm_grads[0],
        norm_grads[1],
        norm_grads[2],
        norm_grads[3],
        grad_taps,
        grad_bias,
        grad_skip,
        grad_filter,
        small[:emb],
        small[emb],
        small[emb + 1 : emb + 1 + order],
        small[emb + 1 + order],
        small[emb + 2 + order],
    )


def solution(mesh):
    paired = mesh.shape["chan"] == 4 and mesh.shape["blk"] == 8
    rows, spread, tokens = P(AXES), P(None, AXES), P(None, None, AXES, None)
    params = (rows, rows, rows, rows, P(None, None, AXES), spread, rows, spread, P(), P(), P(), P(), P())
    return jax.shard_map(
        shards_paired if paired else shards,
        mesh=mesh,
        in_specs=(tokens, tokens, spread, spread, spread, P(AXES, None)) + params + (rows,),
        out_specs=(tokens, tokens, spread, spread, spread, P(AXES, None)) + params,
        check_vma=False,
    )
```
